32 devices in a mesh: shard: 4 (over z), ctx: 4 (over x, core), tensor: 2 (over y).
Axes of the slice: x: 2, y: 2, z: 4, core: 2. Of those that a mesh axis runs over, the one named last changes fastest.
Arguments:
- tokens_in: bfloat16 [8192, 1024], P(('shard', 'ctx')), may hold values from -6 to 6
- cotangent: bfloat16 [8192, 1024], P(('shard', 'ctx')), may hold values from -6 to 6
- segment_ids: int32 [4, 2048], P('shard', 'ctx'), may hold values from 0 to 7, never falling along the last dimension, each value on 1 to 1024 neighbouring positions
- live_blocks: int32 [4, 4, 4], P('shard'), may hold values from 0 to 1, as said below
- routes: int32 [8192, 2], P(('shard', 'ctx')), may hold values from 0 to 3, all different within a row; in each aligned block of 512 rows (0 to 511, 512 to 1023, ...) at most 384 rows name the same one
- w_query: float32 [1024, 1024], P(('shard', 'ctx'), 'tensor'), may hold values from -0.1875 to 0.1875
- w_key: float32 [1024, 1024], P(('shard', 'ctx'), 'tensor'), may hold values from -0.1875 to 0.1875
- w_value: float32 [1024, 1024], P(('shard', 'ctx'), 'tensor'), may hold values from -0.1875 to 0.1875
- w_out: float32 [1024, 1024], P(('shard', 'ctx'), 'tensor'), may hold values from -0.75 to 0.75
- rel_bias: float32 [32, 16], P(None, 'tensor'), may hold values from -4 to 4
- attn_gain: float32 [1024], P(('shard', 'ctx')), may hold values from 0.5 to 1.5
- ffn_gain: float32 [1024], P(('shard', 'ctx')), may hold values from 0.5 to 1.5
- router: float32 [1024, 4], P(('shard', 'ctx')), may hold values from -0.125 to 0.125
- w_gate: float32 [4, 1024, 2816], P('shard', 'ctx', 'tensor'), may hold values from -0.1875 to 0.1875
- w_up: float32 [4, 1024, 2816], P('shard', 'ctx', 'tensor'), may hold values from -0.1875 to 0.1875
- w_down: float32 [4, 1024, 2816], P('shard', 'ctx', 'tensor'), may hold values from -0.109375 to 0.109375
Outputs:
- mixed: bfloat16 [8192, 1024], P(('shard', 'ctx'))
- grad_input: bfloat16 [8192, 1024], P(('shard', 'ctx'))
- grad_query: float32 [1024, 1024], P(('shard', 'ctx'), 'tensor')
- grad_key: float32 [1024, 1024], P(('shard', 'ctx'), 'tensor')
- grad_value: float32 [1024, 1024], P(('shard', 'ctx'), 'tensor')
- grad_out: float32 [1024, 1024], P(('shard', 'ctx'), 'tensor')
- grad_bias: float32 [32, 16], P(None, 'tensor')
- grad_attn_gain: float32 [1024], P(('shard', 'ctx'))
- grad_ffn_gain: float32 [1024], P(('shard', 'ctx'))
- grad_router: float32 [1024, 4], P(('shard', 'ctx'))
- grad_gate: float32 [4, 1024, 2816], P('shard', 'ctx', 'tensor')
- grad_up: float32 [4, 1024, 2816], P('shard', 'ctx', 'tensor')
- grad_down: float32 [4, 1024, 2816], P('shard', 'ctx', 'tensor')
The draws below stay inside these ranges and needn't reach their ends.
Inputs may be any that keep to these rules, and one draw needn't show every extreme that they name: `segment_ids`: ids never fall along a sequence; each document has 1 to 1024 positions and one has exactly 1024. live_blocks[s, b, b] = 1 for every sequence s and block b. `routes`: the experts of a row differ; in the rows of one device (aligned blocks of 512 rows) no expert is named more than 384 times, and in some blocks one is named exactly 384 times.
All inputs are finite; a program needn't handle non-finite values.
Results may differ from the reference program's by a relative error of at most 0.025.
Values may be sent and summed in bfloat16 or wider, within the bound.
A program may use at most 192 MiB of HBM per device.

```python
import math
import jax
import jax.numpy as jnp
import numpy as np
from jax import lax

D = 1024
HEADS = 16
HEAD = 64
FF = 2816
NBUCK = 32
TOP = 2
ATT_BLK = 512
SEQ_LEN = 2048
SEQS = 4
TOK_DEV = 512
TOKENS = 8192
EXPERTS = 4
CAP = 384
NBLK = 4
DOCS = 8
DOC_MOST = 1024


def draw_live_blocks(key, part):
    bits = jax.random.randint(key, (SEQS, NBLK, NBLK), 0, 2).astype(jnp.int32)
    diagonal = (jnp.arange(NBLK)[:, None] == jnp.arange(NBLK)[None, :]).astype(jnp.int32)
    return jnp.maximum(bits, diagonal[None]).astype(jnp.int32)


def block_levels(rng, shape, cuts, least, high):
    def one(position, blocks):
        steps = jax.random.uniform(jax.random.fold_in(jax.random.fold_in(rng, 6), position), (blocks,), jnp.float32, least / len(cuts), high / len(cuts))
        return jnp.repeat(jnp.exp(steps), shape[position] // blocks).reshape((-1,) + (1,) * (len(shape) - position - 1))

    level = one(*cuts[0])
    for cut in cuts[1:]:
        level = level * one(*cut)
    return level


def split_up(number_of, total, reach, skew):
    loads = [(1 << 20) // math.isqrt(rank ** skew) + 1 for rank in range(2, number_of + 1)]
    rest, counts = total - reach - (number_of - 1), [1] * (number_of - 1)
    while rest > 0:
        free = [i for i in range(number_of - 1) if counts[i] < reach]
        whole, left = sum([loads[i] for i in free]), rest
        for i in free:
            more = min(reach - counts[i], max(1, left * loads[i] // whole), rest)
            counts[i] = counts[i] + more
            rest = rest - more
    return np.array([reach] + counts)


def ragged_sizes(own_key, number_of, total, reach, lean):
    if number_of == 2:
        one = jax.random.randint(own_key, (), max(1, total - reach), min(reach, total - 1) + 1)
        return jnp.stack([one, total - one])
    tallies = jnp.asarray(split_up(number_of, total, reach, lean), jnp.int32)
    couples = (number_of - 1) // 2
    giver, taker = tallies[1:1 + 2 * couples:2], tallies[2:2 + 2 * couples:2]
    room = jnp.minimum(giver - 1, reach - taker)
    moved = jax.random.randint(jax.random.fold_in(own_key, 1), (couples,), 0, 1 << 20) % (room + 1)
    tallies = tallies.at[1:1 + 2 * couples:2].set(giver - moved).at[2:2 + 2 * couples:2].set(taker + moved)
    return tallies[jax.random.permutation(jax.random.fold_in(own_key, 2), number_of)]


def deal_out(own_key, own, number, rows, amount, top, reach, lean):
    order = jax.random.permutation(own_key, amount)
    heavy_load, ordinary = shares(amount, rows * top, reach, lean, True), shares(amount, rows * top, reach, lean, False)
    places = jnp.arange(amount)

    def named(tallies, rotation):
        used = int((tallies > 0).sum())
        fixed = max(1, used // 4)
        moved = fixed + (places - fixed + rotation * (used - fixed)) % max(1, amount - fixed)
        return jnp.zeros((amount,), jnp.int32).at[order[jnp.where(places < fixed, places, moved)]].set(jnp.asarray(tallies, jnp.int32))

    tallies = jnp.where(number % 4 == 0, named(heavy_load, number // 4), named(ordinary, number - number // 4 - 1))
    mixed = jax.random.permutation(jax.random.fold_in(own, 3), amount)
    donor, taker = mixed[0:amount // 2 * 2:2], mixed[1:amount // 2 * 2:2]
    slack = jnp.minimum(tallies[donor] - 1, reach - tallies[taker]) // 2
    slack = jnp.where((donor == order[0]) | (taker == order[0]) | (tallies[taker] == 0), 0, jnp.maximum(slack, 0))
    moved = jax.random.randint(jax.random.fold_in(own, 4), (amount // 2,), 0, 1 << 20) % (slack + 1)
    tallies = tallies.at[donor].add(-moved).at[taker].add(moved)
    members = jnp.searchsorted(jnp.cumsum(tallies), jnp.arange(rows * top), side="right").astype(jnp.int32)
    listing = members.reshape(top, rows).T
    listing = listing[jax.random.permutation(jax.random.fold_in(own, 1), rows)]
    rotation = jax.random.randint(jax.random.fold_in(own, 2), (rows, 1), 0, top)
    return jnp.take_along_axis(listing, (jnp.arange(top)[None, :] + rotation) % top, axis=1)


def shares(amount, total, most, lean, full):
    weights = [(1 << 20) // math.isqrt(grade ** lean) + 1 for grade in range(1, amount + 1)]
    largest = most if full else min(most, max(-(-total // amount), total * weights[0] // sum(weights)))
    least = 1 if total - largest >= amount - 1 else 0
    holding, surplus = [largest] + [least] * (amount - 1), total - largest - least * (amount - 1)
    while surplus > 0:
        candidates = [i for i in range(1, amount) if holding[i] < largest] or [i for i in range(1, amount) if holding[i] < most]
        pool, remaining = sum([weights[i] for i in candidates]), surplus
        for i in candidates:
            more = min(most - holding[i], max(1, remaining * weights[i] // pool), surplus)
            holding[i] = holding[i] + more
            surplus = surplus - more
    return np.array(holding)


def scatter_about(stream_key, shape, scale, most, shards=(), kind=jnp.bfloat16):
    values = scale * jax.random.normal(stream_key, shape, jnp.float32)
    if shards:
        values = values * block_levels(stream_key, shape, shards, -0.22, 0.18)
    return jnp.clip(values, -most, most).astype(kind)


def setup_inputs(seed: int = 0) -> dict:
    streams_of = jax.random.split(jax.random.key(seed), 17)
    tokens_in = scatter_about(streams_of[0], (TOKENS, D), 1.0, 6.0, ((0, 16),))
    cotangent = scatter_about(streams_of[1], (TOKENS, D), 1.0, 6.0, ((0, 16),))
    segment_ids = jax.vmap(lambda own: jnp.searchsorted(jnp.cumsum(ragged_sizes(own, DOCS, SEQ_LEN, DOC_MOST, 2)), jnp.arange(SEQ_LEN), side="right"))(jax.random.split(streams_of[2], SEQS)).reshape((SEQS, SEQ_LEN)).astype(jnp.int32)
    live_blocks = draw_live_blocks(jax.random.fold_in(streams_of[16], 71), 0)
    routes_keys = jax.random.split(jax.random.fold_in(streams_of[4], 1), TOKENS // TOK_DEV)
    routes_turns = jax.random.permutation(jax.random.fold_in(streams_of[4], 3), TOKENS // TOK_DEV)
    routes = jax.vmap(lambda own, number: deal_out(jax.random.fold_in(streams_of[4], 2), own, number, TOK_DEV, EXPERTS, TOP, CAP, 2))(routes_keys, routes_turns).reshape((TOKENS, TOP))
    w_query = scatter_about(streams_of[5], (D, HEADS * HEAD), D ** -0.5, 0.1875, ((0, 16), (1, 2)), jnp.float32)
    w_key = scatter_about(streams_of[6], (D, HEADS * HEAD), D ** -0.5, 0.1875, ((0, 16), (1, 2)), jnp.float32)
    w_value = scatter_about(streams_of[7], (D, HEADS * HEAD), D ** -0.5, 0.1875, ((0, 16), (1, 2)), jnp.float32)
    w_out = scatter_about(streams_of[8], (D, HEADS * HEAD), HEAD ** -0.5, 0.75, ((0, 16), (1, 2)), jnp.float32)
    rel_bias = scatter_about(streams_of[9], (NBUCK, HEADS), 1.0, 4.0, ((1, 2),), jnp.float32)
    attn_gain = jnp.clip(1.0 + 0.1 * jax.random.normal(streams_of[10], (D,), jnp.float32), 0.5, 1.5)
    ffn_gain = jnp.clip(1.0 + 0.1 * jax.random.normal(streams_of[11], (D,), jnp.float32), 0.5, 1.5)
    router = scatter_about(streams_of[12], (D, EXPERTS), (2 * D) ** -0.5, 0.125, ((0, 16),), jnp.float32)
    w_gate = scatter_about(streams_of[13], (EXPERTS, D, FF), D ** -0.5, 0.1875, ((0, 4), (1, 4), (2, 2)), jnp.float32)
    w_up = scatter_about(streams_of[14], (EXPERTS, D, FF), D ** -0.5, 0.1875, ((0, 4), (1, 4), (2, 2)), jnp.float32)
    w_down = scatter_about(streams_of[15], (EXPERTS, D, FF), FF ** -0.5, 0.109375, ((0, 4), (1, 4), (2, 2)), jnp.float32)
    return dict(tokens_in=tokens_in, cotangent=cotangent, segment_ids=segment_ids, live_blocks=live_blocks, routes=routes, w_query=w_query, w_key=w_key, w_value=w_value, w_out=w_out, rel_bias=rel_bias, attn_gain=attn_gain, ffn_gain=ffn_gain, router=router, w_gate=w_gate, w_up=w_up, w_down=w_down)


@jax.custom_vjp
def low(v):
    return lax.optimization_barrier(v.astype(jnp.bfloat16)).astype(jnp.float32)

@jax.custom_vjp
def low_back(v):
    return v

def low_keep(v):
    return (low(v), None)

def low_pass(kept, grad):
    return (grad,)

def back_keep(v):
    return (v, None)

def back_low(kept, grad):
    return (low(grad),)
low.defvjp(low_keep, low_pass)
low_back.defvjp(back_keep, back_low)
FAR_STEPS = (12, 16, 23, 32, 46, 64, 91)

def exact_dot(left, right):
    return jnp.dot(left, right, precision=lax.Precision.HIGHEST, preferred_element_type=jnp.float32)

def bucket_ids(relative):
    distance = jnp.abs(relative)
    far = jnp.full(distance.shape, 8, jnp.int32)
    for bound in FAR_STEPS:
        far = far + (distance >= bound).astype(jnp.int32)
    near = jnp.where(distance < 8, distance, far)
    return (near + jnp.where(relative > 0, NBUCK // 2, 0)).astype(jnp.int32)

def rms_parts(values, gain):
    scale = lax.rsqrt(lax.optimization_barrier(jnp.mean(values * values, axis=-1, keepdims=True)) + 1e-06)
    return values * scale * gain

def attend_block(query, keys, values, places, segments, live_rows, key_segments, table):
    key_places = jnp.arange(keys.shape[0], dtype=jnp.int32)
    scores = jnp.einsum('qhd,khd->hqk', query, keys, precision=lax.Precision.HIGHEST) * 0.125
    index = bucket_ids(key_places[None, :] - places[:, None])
    scores = scores + jnp.transpose(jnp.take(table, index, axis=0), (2, 0, 1))
    scores = low_back(scores)
    allowed = (segments[:, None] == key_segments[None, :]) & (jnp.take(live_rows, key_places // ATT_BLK, axis=1) == 1)
    scores = jnp.where(allowed[None], scores, -1e+30)
    weights = low(jax.nn.softmax(scores, axis=-1))
    return jnp.einsum('hqk,khd->qhd', weights, values, precision=lax.Precision.HIGHEST)

def attend_sequence(table, query, keys, values, segments, live):
    places = jnp.arange(SEQ_LEN, dtype=jnp.int32)
    blocks = SEQ_LEN // ATT_BLK
    live_rows = jnp.take(live, places // ATT_BLK, axis=0)
    block_fn = jax.checkpoint(lambda arrays: attend_block(arrays[0], keys, values, arrays[1], arrays[2], arrays[3], segments, table))
    outputs = lax.map(block_fn, (query.reshape(blocks, ATT_BLK, HEADS, HEAD), places.reshape(blocks, ATT_BLK), segments.reshape(blocks, ATT_BLK), live_rows.reshape(blocks, ATT_BLK, blocks)))
    return outputs.reshape(SEQ_LEN, HEADS, HEAD)

def expert_rows(arrays):
    rows, gate_weight, up_weight, down_weight = arrays
    gate_pre = low_back(exact_dot(rows, gate_weight))
    up_pre = low_back(exact_dot(rows, up_weight))
    inner = low(jax.nn.gelu(gate_pre, approximate=True) * up_pre)
    return low_back(exact_dot(inner, down_weight.T))

def layer(tokens, w_query, w_key, w_value, w_out, rel_bias, attn_gain, ffn_gain, router, w_gate, w_up, w_down, segments, live, routes, token_of, choice_of, valid):
    norm_one = low(rms_parts(tokens, low(attn_gain)))

    def project(weight):
        return low_back(low(exact_dot(norm_one, low(weight)))).reshape(SEQS, SEQ_LEN, HEADS, HEAD)
    query = project(w_query)
    keys = project(w_key)
    values = project(w_value)
    attended = lax.map(lambda arrays: attend_sequence(rel_bias, arrays[0], arrays[1], arrays[2], arrays[3], arrays[4]), (query, keys, values, segments, live))
    attended = low_back(low(attended.reshape(TOKENS, HEADS * HEAD)))
    branch = low_back(exact_dot(attended, low(w_out).T))
    hidden_one = tokens + branch
    norm_two = low(rms_parts(hidden_one, low(ffn_gain)))
    logits = exact_dot(norm_two, low(router))
    gates = jax.nn.softmax(jnp.take_along_axis(logits, routes, axis=1), axis=1)
    rows = jnp.take(norm_two, token_of, axis=0)
    outputs = lax.map(jax.checkpoint(expert_rows), (rows, low(w_gate), low(w_up), low(w_down)))
    weight = gates[token_of, choice_of] * valid
    mixture = jnp.zeros_like(tokens).at[token_of.reshape(-1)].add((outputs * weight[..., None]).reshape(-1, D))
    return hidden_one + mixture

def reference(tokens_in, cotangent, segment_ids, live_blocks, routes, w_query, w_key, w_value, w_out, rel_bias, attn_gain, ffn_gain, router, w_gate, w_up, w_down):
    flat = routes.reshape(-1).astype(jnp.int32)
    total = flat.shape[0]
    positions = jnp.arange(total, dtype=jnp.int32)
    experts_range = jnp.arange(EXPERTS, dtype=jnp.int32)
    order_keys = jnp.where(flat[None, :] == experts_range[:, None], positions[None, :], total)
    bound = TOKENS // TOK_DEV * CAP
    picked = jnp.sort(order_keys, axis=1)[:, :bound].astype(jnp.int32)
    valid = (picked < total).astype(jnp.float32)
    picked = jnp.minimum(picked, total - 1).astype(jnp.int32)
    token_of = (picked // TOP).astype(jnp.int32)
    choice_of = (picked % TOP).astype(jnp.int32)
    floats = (tokens_in.astype(jnp.float32), w_query.astype(jnp.float32), w_key.astype(jnp.float32), w_value.astype(jnp.float32), w_out.astype(jnp.float32), rel_bias.astype(jnp.float32), attn_gain.astype(jnp.float32), ffn_gain.astype(jnp.float32), router.astype(jnp.float32), w_gate.astype(jnp.float32), w_up.astype(jnp.float32), w_down.astype(jnp.float32))

    def wrapped(*values):
        return layer(*values, segment_ids, live_blocks, routes, token_of, choice_of, valid)
    result, pullback = jax.vjp(wrapped, *floats)
    grads = pullback(cotangent.astype(jnp.float32))
    return (result.astype(jnp.bfloat16), grads[0].astype(jnp.bfloat16), grads[1], grads[2], grads[3], grads[4], grads[5], grads[6], grads[7], grads[8], grads[9], grads[10], grads[11])
```

```python
from functools import partial

import jax
import jax.numpy as jnp
from jax import lax
from jax.experimental import pallas as pl
from jax.experimental.pallas import tpu as pltpu
from jax.sharding import PartitionSpec as P

HEAD = 64
NBUCK = 32
TOP = 2
ATT_BLK = 512


FAR_STEPS = (12, 16, 23, 32, 46, 64, 91)


def bucket_ids(relative):
    distance = jnp.abs(relative)
    far = jnp.full(distance.shape, 8, jnp.int32)
    for bound in FAR_STEPS:
        far = far + (distance >= bound).astype(jnp.int32)
    near = jnp.where(distance < 8, distance, far)
    return near + jnp.where(relative > 0, NBUCK // 2, 0)


TILE = 256
BIG = 2.0**100
SPAN = 4 * TILE


def place_mask(segment_row):
    rows = lax.broadcasted_iota(jnp.int32, (128, segment_row.shape[1]), 0).astype(jnp.float32)
    apart = jnp.where(rows == segment_row, 0.0, -BIG)
    return jnp.where(rows < 8.0, apart, jnp.where(rows < 11.0, 1.0, 0.0))


def seat_rows(segment_row, extra):
    rows = lax.broadcasted_iota(jnp.int32, (128, segment_row.shape[1]), 0).astype(jnp.float32)
    own = jnp.where((rows == segment_row) & (rows < 8.0), 1.0, 0.0)
    if extra is None:
        return own.astype(jnp.bfloat16)
    high = extra.astype(jnp.bfloat16).astype(jnp.float32)
    rest = extra - high
    middle = rest.astype(jnp.bfloat16).astype(jnp.float32)
    low = rest - middle
    own = jnp.where(rows == 8.0, high, own)
    own = jnp.where(rows == 9.0, middle, own)
    return jnp.where(rows == 10.0, low, own).astype(jnp.bfloat16)


def fill_bias(line_ref, bias_ref):
    for head in range(2):
        line = line_ref[head : head + 1, :]
        turned = pltpu.roll(
            jnp.broadcast_to(line, (TILE, SPAN)), 0, axis=1, stride=1, stride_axis=0
        )
        bias_ref[head, 1] = turned[:, TILE : 2 * TILE]
        bias_ref[head, 2] = turned[:, :TILE]
        bias_ref[head, 3] = turned[:, 3 * TILE :]
        bias_ref[head, 0] = jnp.broadcast_to(line[:, 511:512], (TILE, TILE))
        bias_ref[head, 4] = jnp.broadcast_to(line[:, 513:514], (TILE, TILE))


def tile_at(index):
    return pl.ds(pl.multiple_of(index * TILE, TILE), TILE)


def dot32(left, right):
    return jnp.dot(left, right, preferred_element_type=jnp.float32)


def attention_forward(
    alive, packed, segment, line, out, out_t, log_sum, key_side, query_side, value_t, bias, top, acc
):
    length = packed.shape[0]
    tiles = length // TILE
    fill_bias(line, bias)

    def prepare(index, unused):
        spot = tile_at(index)
        seg = segment[0:1, spot]
        block = packed[spot, :].astype(jnp.float32)
        key_side[spot, :128] = packed[spot, 128:256]
        key_side[spot, 128:] = jnp.transpose(place_mask(seg)).astype(jnp.bfloat16)
        query_t = jnp.transpose(block[:, :128]) * 0.125
        seats = seat_rows(seg, None)
        half = lax.broadcasted_iota(jnp.int32, (128, TILE), 0) // HEAD
        values = jnp.transpose(block[:, 256:]).astype(jnp.bfloat16)
        ones = jnp.where(lax.broadcasted_iota(jnp.int32, (16, TILE), 0) == 0, 1.0, 0.0)
        for head in range(2):
            query_side[head, :128, spot] = jnp.where(half == head, query_t, 0.0).astype(
                jnp.bfloat16
            )
            query_side[head, 128:, spot] = seats
            value_t[head, :HEAD, spot] = values[HEAD * head : HEAD * (head + 1)]
            value_t[head, HEAD:, spot] = ones.astype(jnp.bfloat16)
        return unused

    lax.fori_loop(0, tiles, prepare, 0)

    def query_tile(query_index, unused):
        query_spot = tile_at(query_index)
        top[...] = jnp.full(top.shape, -3e38, jnp.float32)
        acc[...] = jnp.zeros(acc.shape, jnp.float32)

        def key_tile(key_index, carried):
            @pl.when(alive[query_index * tiles + key_index] == 1)
            def _():
                key_spot = tile_at(key_index)
                slot = jnp.clip(key_index - query_index, -2, 2) + 2
                keys = key_side[key_spot, :]
                for head in range(2):
                    scores = dot32(keys, query_side[head, :, query_spot]) + bias[head, slot]
                    before = top[head : head + 1, :]
                    now = jnp.maximum(before, jnp.max(scores, axis=0, keepdims=True))
                    weights = jnp.exp(scores - now).astype(jnp.bfloat16)
                    top[head : head + 1, :] = now
                    acc[head] = acc[head] * jnp.exp(before - now) + dot32(
                        value_t[head, :, key_spot], weights
                    )

            return carried

        lax.fori_loop(0, tiles, key_tile, 0)
        parts = []
        for head in range(2):
            total = acc[head, HEAD : HEAD + 1, :]
            part = acc[head, :HEAD, :] / total
            out_t[HEAD * head : HEAD * (head + 1), query_spot] = part
            log_sum[head : head + 1, query_spot] = top[head : head + 1, :] + jnp.log(total)
            parts.append(part)
        out[query_spot, :] = jnp.transpose(jnp.concatenate(parts, axis=0)).astype(jnp.bfloat16)
        return unused

    lax.fori_loop(0, tiles, query_tile, 0)


def attention_backward(
    alive,
    packed,
    segment,
    line,
    grads,
    out_t,
    log_sum,
    packed_grad,
    bias_grad,
    key_side,
    value_side,
    query_side,
    grad_side,
    key_t,
    query_pair,
    grad_pair,
    bias,
    bias_acc,
    query_acc,
    key_acc,
    value_acc,
):
    length = packed.shape[0]
    tiles = length // TILE
    fill_bias(line, bias)
    bias_acc[...] = jnp.zeros(bias_acc.shape, jnp.float32)

    def prepare(index, unused):
        spot = tile_at(index)
        seg = segment[0:1, spot]
        block = packed[spot, :].astype(jnp.float32)
        grad = grads[spot, :].astype(jnp.float32)
        seats = jnp.transpose(place_mask(seg)).astype(jnp.bfloat16)
        key_side[spot, :128] = packed[spot, 128:256]
        key_side[spot, 128:] = seats
        value_side[spot, :128] = packed[spot, 256:]
        value_side[spot, 128:] = seats
        key_t[:, spot] = jnp.transpose(block[:, 128:256]).astype(jnp.bfloat16)
        query_t = jnp.transpose(block[:, :128]) * 0.125
        grad_t = jnp.transpose(grad)
        half = lax.broadcasted_iota(jnp.int32, (128, TILE), 0) // HEAD
        side = lax.broadcasted_iota(jnp.int32, (TILE, 128), 1) // HEAD
        products = grad_t * out_t[:, spot]
        query_acc[:, spot] = jnp.zeros((128, TILE), jnp.float32)
        for head in range(2):
            query_side[head, :128, spot] = jnp.where(half == head, query_t, 0.0).astype(
                jnp.bfloat16
            )
            query_side[head, 128:, spot] = seat_rows(seg, -log_sum[head : head + 1, spot])
            delta = jnp.sum(products[HEAD * head : HEAD * (head + 1)], axis=0, keepdims=True)
            grad_side[head, :128, spot] = jnp.where(half == head, grad_t, 0.0).astype(jnp.bfloat16)
            grad_side[head, 128:, spot] = seat_rows(jnp.full_like(seg, -1.0), -delta)
            query_pair[index, TILE * head : TILE * (head + 1), :] = jnp.where(
                side == head, block[:, :128] * 0.125, 0.0
            ).astype(jnp.bfloat16)
            grad_pair[index, TILE * head : TILE * (head + 1), :] = jnp.where(
                side == head, grad, 0.0
            ).astype(jnp.bfloat16)
        return unused

    lax.fori_loop(0, tiles, prepare, 0)

    def key_tile(key_index, unused):
        key_spot = tile_at(key_index)
        key_acc[...] = jnp.zeros(key_acc.shape, jnp.float32)
        value_acc[...] = jnp.zeros(value_acc.shape, jnp.float32)

        def query_tile(query_index, carried):
            @pl.when(alive[query_index * tiles + key_index] == 1)
            def _():
                query_spot = tile_at(query_index)
                slot = jnp.clip(key_index - query_index, -2, 2) + 2
                keys = key_side[key_spot, :]
                values = value_side[key_spot, :]
                probs, score_grads = [], []
                for head in range(2):
                    scores = dot32(keys, query_side[head, :, query_spot]) + bias[head, slot]
                    prob = jnp.exp(scores)
                    score_grad = prob * dot32(values, grad_side[head, :, query_spot])
                    bias_acc[head, slot] += score_grad
                    score_grad = score_grad.astype(jnp.bfloat16)
                    probs.append(prob.astype(jnp.bfloat16))
                    score_grads.append(score_grad)
                    rows = slice(HEAD * head, HEAD * (head + 1))
                    query_acc[rows, query_spot] += dot32(key_t[rows, key_spot], score_grad)
                value_acc[...] += dot32(jnp.concatenate(probs, axis=1), grad_pair[query_index])
                key_acc[...] += dot32(jnp.concatenate(score_grads, axis=1), query_pair[query_index])

            return carried

        lax.fori_loop(0, tiles, query_tile, 0)
        packed_grad[key_spot, 128:256] = key_acc[...].astype(jnp.bfloat16)
        packed_grad[key_spot, 256:] = value_acc[...].astype(jnp.bfloat16)
        return unused

    lax.fori_loop(0, tiles, key_tile, 0)

    def finish(index, unused):
        spot = tile_at(index)
        packed_grad[spot, :128] = (jnp.transpose(query_acc[:, spot]) * 0.125).astype(jnp.bfloat16)
        return unused

    lax.fori_loop(0, tiles, finish, 0)
    rows = lax.broadcasted_iota(jnp.int32, (TILE, TILE), 0)
    columns = lax.broadcasted_iota(jnp.int32, (TILE, TILE), 1)
    flip = jnp.where(rows + columns == TILE - 1, 1.0, 0.0)
    bias_grad[...] = jnp.zeros(bias_grad.shape, jnp.float32)
    for head in range(2):
        spread = jnp.concatenate(
            [
                bias_acc[head, 2],
                bias_acc[head, 1],
                jnp.zeros((TILE, TILE), jnp.float32),
                bias_acc[head, 3],
            ],
            axis=1,
        )
        flipped = jnp.dot(
            flip, spread, precision=lax.Precision.HIGHEST, preferred_element_type=jnp.float32
        )
        turned = pltpu.roll(flipped, SPAN - TILE + 1, axis=1, stride=1, stride_axis=0)
        bias_grad[head : head + 1, :] = jnp.sum(turned, axis=0, keepdims=True)
        bias_grad[2 + head : 3 + head, :TILE] = jnp.sum(bias_acc[head, 0], axis=0, keepdims=True)
        bias_grad[4 + head : 5 + head, :TILE] = jnp.sum(bias_acc[head, 4], axis=0, keepdims=True)


def in_vmem(count):
    return [pl.BlockSpec(memory_space=pltpu.VMEM)] * count


def run_forward(alive, packed, segment, line):
    length = packed.shape[0]
    return pl.pallas_call(
        attention_forward,
        out_shape=(
            jax.ShapeDtypeStruct((length, 128), jnp.bfloat16),
            jax.ShapeDtypeStruct((128, length), jnp.float32),
            jax.ShapeDtypeStruct((8, length), jnp.float32),
        ),
        in_specs=[pl.BlockSpec(memory_space=pltpu.SMEM)] + in_vmem(3),
        out_specs=tuple(in_vmem(3)),
        scratch_shapes=[
            pltpu.VMEM((length, 256), jnp.bfloat16),
            pltpu.VMEM((2, 256, length), jnp.bfloat16),
            pltpu.VMEM((2, HEAD + 16, length), jnp.bfloat16),
            pltpu.VMEM((2, 5, TILE, TILE), jnp.float32),
            pltpu.VMEM((8, TILE), jnp.float32),
            pltpu.VMEM((2, HEAD + 16, TILE), jnp.float32),
        ],
        compiler_params=pltpu.CompilerParams(vmem_limit_bytes=40 * 2**20),
        name="attention_forward",
    )(alive, packed, segment, line)


def run_backward(alive, packed, segment, line, grads, out_t, log_sum):
    length = packed.shape[0]
    tiles = length // TILE
    return pl.pallas_call(
        attention_backward,
        out_shape=(
            jax.ShapeDtypeStruct((length, 384), jnp.bfloat16),
            jax.ShapeDtypeStruct((8, SPAN), jnp.float32),
        ),
        in_specs=[pl.BlockSpec(memory_space=pltpu.SMEM)] + in_vmem(6),
        out_specs=tuple(in_vmem(2)),
        scratch_shapes=[
            pltpu.VMEM((length, 256), jnp.bfloat16),
            pltpu.VMEM((length, 256), jnp.bfloat16),
            pltpu.VMEM((2, 256, length), jnp.bfloat16),
            pltpu.VMEM((2, 256, length), jnp.bfloat16),
            pltpu.VMEM((128, length), jnp.bfloat16),
            pltpu.VMEM((tiles, 2 * TILE, 128), jnp.bfloat16),
            pltpu.VMEM((tiles, 2 * TILE, 128), jnp.bfloat16),
            pltpu.VMEM((2, 5, TILE, TILE), jnp.float32),
            pltpu.VMEM((2, 5, TILE, TILE), jnp.float32),
            pltpu.VMEM((128, length), jnp.float32),
            pltpu.VMEM((TILE, 128), jnp.float32),
            pltpu.VMEM((TILE, 128), jnp.float32),
        ],
        compiler_params=pltpu.CompilerParams(vmem_limit_bytes=48 * 2**20),
        name="attention_backward",
    )(alive, packed, segment, line, grads, out_t, log_sum)


def signed_span():
    places = jnp.arange(SPAN, dtype=jnp.int32)
    return jnp.where(places < SPAN // 2, -places, SPAN - places)


def span_buckets():
    return (bucket_ids(signed_span())[:, None] == jnp.arange(NBUCK)[None, :]).astype(jnp.float32)


def live_tiles(segments, live):
    tiles = segments.shape[0] // TILE
    grouped = segments.reshape(tiles, TILE)
    first, last = grouped[:, 0], grouped[:, -1]
    meets = (first[:, None] <= last[None, :]) & (first[None, :] <= last[:, None])
    spread = jnp.repeat(jnp.repeat(live, ATT_BLK // TILE, axis=0), ATT_BLK // TILE, axis=1)
    return (meets & (spread == 1)).astype(jnp.int32).reshape(-1)


def contract_rows(left, right):
    return lax.dot_general(
        left, right, (((0,), (0,)), ((), ())), preferred_element_type=jnp.float32
    )


def contract_cols(left, right):
    return lax.dot_general(
        left, right, (((1,), (1,)), ((), ())), preferred_element_type=jnp.float32
    )


def local(
    tokens_in,
    cotangent,
    segment_ids,
    live_blocks,
    routes,
    w_query,
    w_key,
    w_value,
    w_out,
    rel_bias,
    attn_gain,
    ffn_gain,
    router,
    w_gate,
    w_up,
    w_down,
):
    width = tokens_in.shape[1]
    rows_here = tokens_in.shape[0]
    ctx_size = lax.axis_size("ctx")
    ctx_index = lax.axis_index("ctx")
    heads_here = w_query.shape[1] // HEAD
    share = w_query.shape[1] // ctx_size

    def by_owner(member):
        return member.reshape(member.shape[0], ctx_size, share)

    packed_rows = jnp.stack([by_owner(w_query), by_owner(w_key), by_owner(w_value)], axis=2)
    experts = router.shape[1]
    gathered = lax.all_gather(
        jnp.concatenate(
            [
                packed_rows.reshape(w_query.shape[0], -1),
                w_out,
                attn_gain[:, None],
                ffn_gain[:, None],
                router,
            ],
            axis=1,
        ).astype(jnp.bfloat16),
        ("shard", "ctx"),
        axis=0,
        tiled=True,
    )
    head_cols = w_query.shape[1]
    packed_w = gathered[:, : 3 * head_cols]
    out_w = gathered[:, 3 * head_cols : 4 * head_cols]
    gain_one = gathered[:, 4 * head_cols]
    gain_two = gathered[:, 4 * head_cols + 1]
    router_w = gathered[:, 4 * head_cols + 2 :]
    inputs = tokens_in.astype(jnp.float32)
    scale_one = lax.rsqrt(jnp.mean(inputs * inputs, axis=1, keepdims=True) + 1e-06)
    normal_one = inputs * scale_one
    norm_one = (normal_one * gain_one.astype(jnp.float32)).astype(jnp.bfloat16)
    packed = jnp.dot(norm_one, packed_w, preferred_element_type=jnp.float32).astype(jnp.bfloat16)
    packed = jnp.transpose(packed.reshape(rows_here, ctx_size, 3 * share), (1, 0, 2))
    packed = lax.all_to_all(packed, "ctx", split_axis=0, concat_axis=0, tiled=True)
    packed = packed.reshape(ctx_size * rows_here, 3 * share)
    segments = lax.all_gather(segment_ids.reshape(-1), "ctx", axis=0, tiled=True)
    alive = live_tiles(segments, live_blocks[0])
    segment_row = segments.astype(jnp.float32)[None]
    pair_heads = share // HEAD
    own_bias = lax.dynamic_slice_in_dim(rel_bias, ctx_index * pair_heads, pair_heads, 1)
    buckets = span_buckets()
    line = jnp.dot(own_bias.T, buckets.T, precision=lax.Precision.HIGHEST)
    attended, attended_t, log_sum = run_forward(alive, packed, segment_row, line)
    attended_low = lax.all_to_all(
        attended.reshape(ctx_size, rows_here, share), "ctx", split_axis=0, concat_axis=0, tiled=True
    )
    attended_low = jnp.transpose(attended_low, (1, 0, 2)).reshape(rows_here, head_cols)
    branch = lax.psum(contract_cols(attended_low, out_w).astype(jnp.bfloat16), "tensor").astype(
        jnp.float32
    )
    hidden_one = inputs + branch
    scale_two = lax.rsqrt(jnp.mean(hidden_one * hidden_one, axis=1, keepdims=True) + 1e-06)
    normal_two = hidden_one * scale_two
    norm_two = (normal_two * gain_two.astype(jnp.float32)).astype(jnp.bfloat16)
    logits = jnp.dot(norm_two, router_w, preferred_element_type=jnp.float32)
    picks = routes[:, :, None] == jnp.arange(experts, dtype=jnp.int32)[None, None, :]
    chosen = jnp.sum(jnp.where(picks, logits[:, None, :], 0.0), axis=2)
    gates = jax.nn.softmax(chosen, axis=1)
    upstream = cotangent.astype(jnp.float32)
    flat_picks = picks.reshape(rows_here * TOP, experts).astype(jnp.int32)
    slot_of = jnp.sum(flat_picks * (jnp.cumsum(flat_picks, axis=0) - 1), axis=1)
    expert_of = routes.reshape(-1)
    capacity = max(2, 3 * rows_here // experts)
    shaped = (experts, capacity, width)
    send_rows = (
        jnp.zeros(shaped, jnp.bfloat16)
        .at[expert_of, slot_of]
        .set(jnp.repeat(norm_two, TOP, axis=0))
    )
    grad_rows = (
        (gates[:, :, None] * upstream[:, None, :])
        .reshape(rows_here * TOP, width)
        .astype(jnp.bfloat16)
    )
    send_grads = jnp.zeros(shaped, jnp.bfloat16).at[expert_of, slot_of].set(grad_rows)
    got_rows, got_grads = (
        lax.all_to_all(send_rows, "shard", split_axis=0, concat_axis=0, tiled=True),
        lax.all_to_all(send_grads, "shard", split_axis=0, concat_axis=0, tiled=True),
    )
    expert_gate, expert_up, expert_down = (
        lax.all_gather(w_gate.astype(jnp.bfloat16), "ctx", axis=1, tiled=True),
        lax.all_gather(w_up.astype(jnp.bfloat16), "ctx", axis=1, tiled=True),
        lax.all_gather(w_down.astype(jnp.bfloat16), "ctx", axis=1, tiled=True),
    )
    gate_mat = expert_gate[0]
    up_mat = expert_up[0]
    down_mat = expert_down[0]
    slot_rows = got_rows.reshape(-1, width)
    slot_grads = got_grads.reshape(-1, width)
    gate_pre = jnp.dot(slot_rows, gate_mat, preferred_element_type=jnp.float32)
    up_pre = jnp.dot(slot_rows, up_mat, preferred_element_type=jnp.float32)
    activated, gelu_back = jax.vjp(partial(jax.nn.gelu, approximate=True), gate_pre)
    inner = (activated * up_pre).astype(jnp.bfloat16)
    expert_out = contract_cols(inner, down_mat)
    inner_grad = jnp.dot(slot_grads, down_mat, preferred_element_type=jnp.float32)
    gate_grad = gelu_back(inner_grad * up_pre)[0].astype(jnp.bfloat16)
    up_grad = (inner_grad * activated).astype(jnp.bfloat16)
    rows_grad = contract_cols(gate_grad, gate_mat) + contract_cols(up_grad, up_mat)
    weight_grads = lax.psum_scatter(
        jnp.stack(
            [
                contract_rows(slot_rows, gate_grad),
                contract_rows(slot_rows, up_grad),
                contract_rows(slot_grads, inner),
            ],
            axis=1,
        ).astype(jnp.bfloat16),
        "ctx",
        scatter_dimension=0,
        tiled=True,
    ).astype(jnp.float32)
    expert_out, rows_grad = (
        lax.psum(expert_out.astype(jnp.bfloat16), "tensor").astype(jnp.float32),
        lax.psum(rows_grad.astype(jnp.bfloat16), "tensor").astype(jnp.float32),
    )
    back_out, back_grad = (
        lax.all_to_all(
            expert_out.reshape(shaped).astype(jnp.bfloat16),
            "shard",
            split_axis=0,
            concat_axis=0,
            tiled=True,
        ).astype(jnp.float32),
        lax.all_to_all(
            rows_grad.reshape(shaped).astype(jnp.bfloat16),
            "shard",
            split_axis=0,
            concat_axis=0,
            tiled=True,
        ).astype(jnp.float32),
    )
    per_choice = back_out[expert_of, slot_of].reshape(rows_here, TOP, width)
    mixture = jnp.sum(gates[:, :, None] * per_choice, axis=1)
    gate_dots = jnp.sum(per_choice * upstream[:, None, :], axis=2)
    norm_grad = jnp.sum(back_grad[expert_of, slot_of].reshape(rows_here, TOP, width), axis=1)
    mixed = (hidden_one + mixture).astype(jnp.bfloat16)
    gate_shift = gates * (gate_dots - jnp.sum(gates * gate_dots, axis=1, keepdims=True))
    logit_grad = jnp.sum(jnp.where(picks, gate_shift[:, :, None], 0.0), axis=1)
    router_f = router_w.astype(jnp.float32)
    norm_grad = norm_grad + jnp.dot(logit_grad, router_f.T, precision=lax.Precision.HIGHEST)
    spread_two = norm_grad * gain_two.astype(jnp.float32)
    hidden_grad = upstream + scale_two * (
        spread_two - normal_two * jnp.mean(spread_two * normal_two, axis=1, keepdims=True)
    )
    branch_grad = hidden_grad.astype(jnp.bfloat16)
    attended_grad = jnp.dot(branch_grad, out_w, preferred_element_type=jnp.float32).astype(
        jnp.bfloat16
    )
    grad_heads = jnp.transpose(attended_grad.reshape(rows_here, ctx_size, share), (1, 0, 2))
    grad_heads = lax.all_to_all(grad_heads, "ctx", split_axis=0, concat_axis=0, tiled=True)
    packed_grad, bias_line = run_backward(
        alive, packed, segment_row, line, grad_heads.reshape(-1, share), attended_t, log_sum
    )
    own_grad = jnp.dot(buckets.T, bias_line[:pair_heads].T, precision=lax.Precision.HIGHEST)
    far = jnp.sum(bias_line[pair_heads : 3 * pair_heads], axis=1)
    half = NBUCK // 2
    own_grad = own_grad.at[half - 1].add(far[:pair_heads]).at[NBUCK - 1].add(far[pair_heads:])
    bias_acc = lax.dynamic_update_slice_in_dim(
        jnp.zeros(rel_bias.shape, jnp.float32), own_grad, ctx_index * pair_heads, 1
    )
    packed_grad = lax.all_to_all(
        packed_grad.reshape(ctx_size, rows_here, 3 * share),
        "ctx",
        split_axis=0,
        concat_axis=0,
        tiled=True,
    )
    packed_grad = jnp.transpose(packed_grad, (1, 0, 2)).reshape(rows_here, 3 * head_cols)
    norm_one_grad = lax.psum(
        contract_cols(packed_grad, packed_w).astype(jnp.bfloat16), "tensor"
    ).astype(jnp.float32)
    spread_one = norm_one_grad * gain_one.astype(jnp.float32)
    input_grad = hidden_grad + scale_one * (
        spread_one - normal_one * jnp.mean(spread_one * normal_one, axis=1, keepdims=True)
    )
    gain_one_terms = norm_one_grad * normal_one
    gain_two_terms = norm_grad * normal_two
    cols_two = norm_two.astype(jnp.float32)
    first_gain = jnp.sum(gain_one_terms, axis=0)[:, None]
    second_gain = jnp.sum(gain_two_terms, axis=0)[:, None]
    router_part = jnp.dot(cols_two.T, logit_grad, precision=lax.Precision.HIGHEST)
    reduced = lax.psum_scatter(
        jnp.concatenate(
            [
                contract_rows(norm_one, packed_grad),
                contract_rows(branch_grad, attended_low),
                first_gain,
                second_gain,
                router_part,
            ],
            axis=1,
        ),
        ("shard", "ctx"),
        scatter_dimension=0,
        tiled=True,
    )
    grad_bias = lax.psum(bias_acc, ("shard", "ctx"))
    packed_rows = reduced[:, : 3 * head_cols].reshape(-1, ctx_size, 3, share)
    return (
        mixed,
        input_grad.astype(jnp.bfloat16),
        packed_rows[:, :, 0].reshape(-1, head_cols),
        packed_rows[:, :, 1].reshape(-1, head_cols),
        packed_rows[:, :, 2].reshape(-1, head_cols),
        reduced[:, 3 * head_cols : 4 * head_cols],
        grad_bias,
        reduced[:, 4 * head_cols],
        reduced[:, 4 * head_cols + 1],
        reduced[:, 4 * head_cols + 2 :],
        weight_grads[:, 0][None],
        weight_grads[:, 1][None],
        weight_grads[:, 2][None],
    )


def solution(mesh):
    placed = (
        P(("shard", "ctx"), None),
        P(("shard", "ctx"), None),
        P("shard", "ctx"),
        P("shard", None, None),
        P(("shard", "ctx"), None),
        P(("shard", "ctx"), "tensor"),
        P(("shard", "ctx"), "tensor"),
        P(("shard", "ctx"), "tensor"),
        P(("shard", "ctx"), "tensor"),
        P(None, "tensor"),
        P(("shard", "ctx")),
        P(("shard", "ctx")),
        P(("shard", "ctx"), None),
        P("shard", "ctx", "tensor"),
        P("shard", "ctx", "tensor"),
        P("shard", "ctx", "tensor"),
    )
    return jax.shard_map(
        local,
        mesh=mesh,
        in_specs=placed,
        out_specs=(
            P(("shard", "ctx"), None),
            P(("shard", "ctx"), None),
            P(("shard", "ctx"), "tensor"),
            P(("shard", "ctx"), "tensor"),
            P(("shard", "ctx"), "tensor"),
            P(("shard", "ctx"), "tensor"),
            P(None, "tensor"),
            P(("shard", "ctx")),
            P(("shard", "ctx")),
            P(("shard", "ctx"), None),
            P("shard", "ctx", "tensor"),
            P("shard", "ctx", "tensor"),
            P("shard", "ctx", "tensor"),
        ),
        check_vma=False,
    )
```

```python
import math
from functools import partial

import jax
import jax.numpy as jnp
from jax import lax
from jax.experimental import pallas as pl
from jax.experimental.pallas import tpu as pltpu
from jax.sharding import PartitionSpec as P

HEAD = 64
NBUCK = 32
TOP = 2
ATT_BLK = 512


FAR_STEPS = (12, 16, 23, 32, 46, 64, 91)


def bucket_ids(relative):
    distance = jnp.abs(relative)
    far = jnp.full(distance.shape, 8, jnp.int32)
    for bound in FAR_STEPS:
        far = far + (distance >= bound).astype(jnp.int32)
    near = jnp.where(distance < 8, distance, far)
    return near + jnp.where(relative > 0, NBUCK // 2, 0)


def contract_rows(left, right):
    return lax.dot_general(
        left, right, (((0,), (0,)), ((), ())), preferred_element_type=jnp.float32
    )


def contract_cols(left, right):
    return lax.dot_general(
        left, right, (((1,), (1,)), ((), ())), preferred_element_type=jnp.float32
    )


TILE = 256
BIG = 2.0**100
SPAN = 4 * TILE


def place_mask(segment_row):
    rows = lax.broadcasted_iota(jnp.int32, (128, segment_row.shape[1]), 0).astype(jnp.float32)
    apart = jnp.where(rows == segment_row, 0.0, -BIG)
    return jnp.where(rows < 8.0, apart, jnp.where(rows < 11.0, 1.0, 0.0))


def seat_rows(segment_row, extra):
    rows = lax.broadcasted_iota(jnp.int32, (128, segment_row.shape[1]), 0).astype(jnp.float32)
    own = jnp.where((rows == segment_row) & (rows < 8.0), 1.0, 0.0)
    if extra is None:
        return own.astype(jnp.bfloat16)
    high = extra.astype(jnp.bfloat16).astype(jnp.float32)
    rest = extra - high
    middle = rest.astype(jnp.bfloat16).astype(jnp.float32)
    low = rest - middle
    own = jnp.where(rows == 8.0, high, own)
    own = jnp.where(rows == 9.0, middle, own)
    return jnp.where(rows == 10.0, low, own).astype(jnp.bfloat16)


def fill_bias(line_ref, bias_ref):
    for head in range(2):
        line = line_ref[head : head + 1, :]
        turned = pltpu.roll(
            jnp.broadcast_to(line, (TILE, SPAN)), 0, axis=1, stride=1, stride_axis=0
        )
        bias_ref[head, 1] = turned[:, TILE : 2 * TILE]
        bias_ref[head, 2] = turned[:, :TILE]
        bias_ref[head, 3] = turned[:, 3 * TILE :]
        bias_ref[head, 0] = jnp.broadcast_to(line[:, 511:512], (TILE, TILE))
        bias_ref[head, 4] = jnp.broadcast_to(line[:, 513:514], (TILE, TILE))


def tile_at(index):
    return pl.ds(pl.multiple_of(index * TILE, TILE), TILE)


def dot32(left, right):
    return jnp.dot(left, right, preferred_element_type=jnp.float32)


def attention_forward(
    alive, packed, segment, line, out, out_t, log_sum, key_side, query_side, value_t, bias, top, acc
):
    length = packed.shape[0]
    tiles = length // TILE
    fill_bias(line, bias)

    def prepare(index, unused):
        spot = tile_at(index)
        seg = segment[0:1, spot]
        block = packed[spot, :].astype(jnp.float32)
        key_side[spot, :128] = packed[spot, 128:256]
        key_side[spot, 128:] = jnp.transpose(place_mask(seg)).astype(jnp.bfloat16)
        query_t = jnp.transpose(block[:, :128]) * 0.125
        seats = seat_rows(seg, None)
        half = lax.broadcasted_iota(jnp.int32, (128, TILE), 0) // HEAD
        values = jnp.transpose(block[:, 256:]).astype(jnp.bfloat16)
        ones = jnp.where(lax.broadcasted_iota(jnp.int32, (16, TILE), 0) == 0, 1.0, 0.0)
        for head in range(2):
            query_side[head, :128, spot] = jnp.where(half == head, query_t, 0.0).astype(
                jnp.bfloat16
            )
            query_side[head, 128:, spot] = seats
            value_t[head, :HEAD, spot] = values[HEAD * head : HEAD * (head + 1)]
            value_t[head, HEAD:, spot] = ones.astype(jnp.bfloat16)
        return unused

    lax.fori_loop(0, tiles, prepare, 0)

    def query_tile(query_index, unused):
        query_spot = tile_at(query_index)
        top[...] = jnp.full(top.shape, -3e38, jnp.float32)
        acc[...] = jnp.zeros(acc.shape, jnp.float32)

        def key_tile(key_index, carried):
            @pl.when(alive[query_index * tiles + key_index] == 1)
            def _():
                key_spot = tile_at(key_index)
                slot = jnp.clip(key_index - query_index, -2, 2) + 2
                keys = key_side[key_spot, :]
                for head in range(2):
                    scores = dot32(keys, query_side[head, :, query_spot]) + bias[head, slot]
                    before = top[head : head + 1, :]
                    now = jnp.maximum(before, jnp.max(scores, axis=0, keepdims=True))
                    weights = jnp.exp(scores - now).astype(jnp.bfloat16)
                    top[head : head + 1, :] = now
                    acc[head] = acc[head] * jnp.exp(before - now) + dot32(
                        value_t[head, :, key_spot], weights
                    )

            return carried

        lax.fori_loop(0, tiles, key_tile, 0)
        parts = []
        for head in range(2):
            total = acc[head, HEAD : HEAD + 1, :]
            part = acc[head, :HEAD, :] / total
            out_t[HEAD * head : HEAD * (head + 1), query_spot] = part
            log_sum[head : head + 1, query_spot] = top[head : head + 1, :] + jnp.log(total)
            parts.append(part)
        out[query_spot, :] = jnp.transpose(jnp.concatenate(parts, axis=0)).astype(jnp.bfloat16)
        return unused

    lax.fori_loop(0, tiles, query_tile, 0)


def attention_backward(
    alive,
    packed,
    segment,
    line,
    grads,
    out_t,
    log_sum,
    packed_grad,
    bias_grad,
    key_side,
    value_side,
    query_side,
    grad_side,
    key_t,
    query_pair,
    grad_pair,
    bias,
    bias_acc,
    query_acc,
    key_acc,
    value_acc,
):
    length = packed.shape[0]
    tiles = length // TILE
    fill_bias(line, bias)
    bias_acc[...] = jnp.zeros(bias_acc.shape, jnp.float32)

    def prepare(index, unused):
        spot = tile_at(index)
        seg = segment[0:1, spot]
        block = packed[spot, :].astype(jnp.float32)
        grad = grads[spot, :].astype(jnp.float32)
        seats = jnp.transpose(place_mask(seg)).astype(jnp.bfloat16)
        key_side[spot, :128] = packed[spot, 128:256]
        key_side[spot, 128:] = seats
        value_side[spot, :128] = packed[spot, 256:]
        value_side[spot, 128:] = seats
        key_t[:, spot] = jnp.transpose(block[:, 128:256]).astype(jnp.bfloat16)
        query_t = jnp.transpose(block[:, :128]) * 0.125
        grad_t = jnp.transpose(grad)
        half = lax.broadcasted_iota(jnp.int32, (128, TILE), 0) // HEAD
        side = lax.broadcasted_iota(jnp.int32, (TILE, 128), 1) // HEAD
        products = grad_t * out_t[:, spot]
        query_acc[:, spot] = jnp.zeros((128, TILE), jnp.float32)
        for head in range(2):
            query_side[head, :128, spot] = jnp.where(half == head, query_t, 0.0).astype(
                jnp.bfloat16
            )
            query_side[head, 128:, spot] = seat_rows(seg, -log_sum[head : head + 1, spot])
            delta = jnp.sum(products[HEAD * head : HEAD * (head + 1)], axis=0, keepdims=True)
            grad_side[head, :128, spot] = jnp.where(half == head, grad_t, 0.0).astype(jnp.bfloat16)
            grad_side[head, 128:, spot] = seat_rows(jnp.full_like(seg, -1.0), -delta)
            query_pair[index, TILE * head : TILE * (head + 1), :] = jnp.where(
                side == head, block[:, :128] * 0.125, 0.0
            ).astype(jnp.bfloat16)
            grad_pair[index, TILE * head : TILE * (head + 1), :] = jnp.where(
                side == head, grad, 0.0
            ).astype(jnp.bfloat16)
        return unused

    lax.fori_loop(0, tiles, prepare, 0)

    def key_tile(key_index, unused):
        key_spot = tile_at(key_index)
        key_acc[...] = jnp.zeros(key_acc.shape, jnp.float32)
        value_acc[...] = jnp.zeros(value_acc.shape, jnp.float32)

        def query_tile(query_index, carried):
            @pl.when(alive[query_index * tiles + key_index] == 1)
            def _():
                query_spot = tile_at(query_index)
                slot = jnp.clip(key_index - query_index, -2, 2) + 2
                keys = key_side[key_spot, :]
                values = value_side[key_spot, :]
                probs, score_grads = [], []
                for head in range(2):
                    scores = dot32(keys, query_side[head, :, query_spot]) + bias[head, slot]
                    prob = jnp.exp(scores)
                    score_grad = prob * dot32(values, grad_side[head, :, query_spot])
                    bias_acc[head, slot] += score_grad
                    score_grad = score_grad.astype(jnp.bfloat16)
                    probs.append(prob.astype(jnp.bfloat16))
                    score_grads.append(score_grad)
                    rows = slice(HEAD * head, HEAD * (head + 1))
                    query_acc[rows, query_spot] += dot32(key_t[rows, key_spot], score_grad)
                value_acc[...] += dot32(jnp.concatenate(probs, axis=1), grad_pair[query_index])
                key_acc[...] += dot32(jnp.concatenate(score_grads, axis=1), query_pair[query_index])

            return carried

        lax.fori_loop(0, tiles, query_tile, 0)
        packed_grad[key_spot, 128:256] = key_acc[...].astype(jnp.bfloat16)
        packed_grad[key_spot, 256:] = value_acc[...].astype(jnp.bfloat16)
        return unused

    lax.fori_loop(0, tiles, key_tile, 0)

    def finish(index, unused):
        spot = tile_at(index)
        packed_grad[spot, :128] = (jnp.transpose(query_acc[:, spot]) * 0.125).astype(jnp.bfloat16)
        return unused

    lax.fori_loop(0, tiles, finish, 0)
    rows = lax.broadcasted_iota(jnp.int32, (TILE, TILE), 0)
    columns = lax.broadcasted_iota(jnp.int32, (TILE, TILE), 1)
    flip = jnp.where(rows + columns == TILE - 1, 1.0, 0.0)
    bias_grad[...] = jnp.zeros(bias_grad.shape, jnp.float32)
    for head in range(2):
        spread = jnp.concatenate(
            [
                bias_acc[head, 2],
                bias_acc[head, 1],
                jnp.zeros((TILE, TILE), jnp.float32),
                bias_acc[head, 3],
            ],
            axis=1,
        )
        flipped = jnp.dot(
            flip, spread, precision=lax.Precision.HIGHEST, preferred_element_type=jnp.float32
        )
        turned = pltpu.roll(flipped, SPAN - TILE + 1, axis=1, stride=1, stride_axis=0)
        bias_grad[head : head + 1, :] = jnp.sum(turned, axis=0, keepdims=True)
        bias_grad[2 + head : 3 + head, :TILE] = jnp.sum(bias_acc[head, 0], axis=0, keepdims=True)
        bias_grad[4 + head : 5 + head, :TILE] = jnp.sum(bias_acc[head, 4], axis=0, keepdims=True)


def in_vmem(count):
    return [pl.BlockSpec(memory_space=pltpu.VMEM)] * count


def run_forward(alive, packed, segment, line):
    length = packed.shape[0]
    return pl.pallas_call(
        attention_forward,
        out_shape=(
            jax.ShapeDtypeStruct((length, 128), jnp.bfloat16),
            jax.ShapeDtypeStruct((128, length), jnp.float32),
            jax.ShapeDtypeStruct((8, length), jnp.float32),
        ),
        in_specs=[pl.BlockSpec(memory_space=pltpu.SMEM)] + in_vmem(3),
        out_specs=tuple(in_vmem(3)),
        scratch_shapes=[
            pltpu.VMEM((length, 256), jnp.bfloat16),
            pltpu.VMEM((2, 256, length), jnp.bfloat16),
            pltpu.VMEM((2, HEAD + 16, length), jnp.bfloat16),
            pltpu.VMEM((2, 5, TILE, TILE), jnp.float32),
            pltpu.VMEM((8, TILE), jnp.float32),
            pltpu.VMEM((2, HEAD + 16, TILE), jnp.float32),
        ],
        compiler_params=pltpu.CompilerParams(vmem_limit_bytes=40 * 2**20),
        name="attention_forward",
    )(alive, packed, segment, line)


def run_backward(alive, packed, segment, line, grads, out_t, log_sum):
    length = packed.shape[0]
    tiles = length // TILE
    return pl.pallas_call(
        attention_backward,
        out_shape=(
            jax.ShapeDtypeStruct((length, 384), jnp.bfloat16),
            jax.ShapeDtypeStruct((8, SPAN), jnp.float32),
        ),
        in_specs=[pl.BlockSpec(memory_space=pltpu.SMEM)] + in_vmem(6),
        out_specs=tuple(in_vmem(2)),
        scratch_shapes=[
            pltpu.VMEM((length, 256), jnp.bfloat16),
            pltpu.VMEM((length, 256), jnp.bfloat16),
            pltpu.VMEM((2, 256, length), jnp.bfloat16),
            pltpu.VMEM((2, 256, length), jnp.bfloat16),
            pltpu.VMEM((128, length), jnp.bfloat16),
            pltpu.VMEM((tiles, 2 * TILE, 128), jnp.bfloat16),
            pltpu.VMEM((tiles, 2 * TILE, 128), jnp.bfloat16),
            pltpu.VMEM((2, 5, TILE, TILE), jnp.float32),
            pltpu.VMEM((2, 5, TILE, TILE), jnp.float32),
            pltpu.VMEM((128, length), jnp.float32),
            pltpu.VMEM((TILE, 128), jnp.float32),
            pltpu.VMEM((TILE, 128), jnp.float32),
        ],
        compiler_params=pltpu.CompilerParams(vmem_limit_bytes=48 * 2**20),
        name="attention_backward",
    )(alive, packed, segment, line, grads, out_t, log_sum)


def signed_span():
    places = jnp.arange(SPAN, dtype=jnp.int32)
    return jnp.where(places < SPAN // 2, -places, SPAN - places)


def span_buckets():
    return (bucket_ids(signed_span())[:, None] == jnp.arange(NBUCK)[None, :]).astype(jnp.float32)


def live_tiles(segments, live):
    tiles = segments.shape[0] // TILE
    grouped = segments.reshape(tiles, TILE)
    first, last = grouped[:, 0], grouped[:, -1]
    meets = (first[:, None] <= last[None, :]) & (first[None, :] <= last[:, None])
    spread = jnp.repeat(jnp.repeat(live, ATT_BLK // TILE, axis=0), ATT_BLK // TILE, axis=1)
    return (meets & (spread == 1)).astype(jnp.int32).reshape(-1)


MESH = pl.DeviceIdType.MESH


def gelu_parts(value):
    root = math.sqrt(2.0 / math.pi)
    square = value * value
    bend = jnp.tanh(root * value * (1.0 + 0.044715 * square))
    half = 0.5 * (1.0 + bend)
    slope = half + 0.5 * value * (1.0 - bend * bend) * (root * (1.0 + 0.134145 * square))
    return value * half, slope


def dot_last(left, right):
    return lax.dot_general(
        left, right, (((1,), (1,)), ((), ())), preferred_element_type=jnp.float32
    )


def expert_exchange(
    count,
    norm,
    gates,
    code_rows,
    code_cols,
    upstream,
    gate_hbm,
    up_hbm,
    down_hbm,
    row_grad,
    dot_rows,
    rows_hbm,
    slot_hbm,
    inner_hbm,
    gate_grad_hbm,
    up_grad_hbm,
    out_hbm,
    gate_w,
    up_w,
    down_w,
    rows,
    sent,
    gates_in,
    gates_out,
    slot_grad,
    inner,
    gate_grad,
    up_grad,
    outs,
    partial,
    peer_part,
    summed,
    back,
    dots_out,
    dots_in,
    final_out,
    final_in,
    final_dots,
    load_sem,
    store_sem,
    rows_send,
    rows_recv,
    pass_send,
    pass_recv,
    gates_send,
    gates_recv,
    part_send,
    part_recv,
    back_send,
    back_recv,
    dots_send,
    dots_recv,
    final_send,
    final_recv,
):
    own = lax.axis_index("shard")
    ctx = lax.axis_index("ctx")
    side = lax.axis_index("tensor")
    tokens, width = norm.shape
    room = upstream.shape[1]
    half = room // 2
    hidden = gate_w.shape[1]
    peer = (own, ctx, 1 - side)

    def source(step):
        flip = own // (count // 2)
        place = flip * (count - 1 - own) + (1 - flip) * own
        turn = step - 1
        turn = turn + (turn - place + count) // count
        other = flip * (count - 1 - turn) + (1 - flip) * turn
        first = 1 - (step + count - 1) // count
        return first * own + (1 - first) * other

    barrier = pltpu.get_barrier_semaphore()
    for step in range(1, count):
        pl.semaphore_signal(barrier, 1, device_id=(source(step), ctx, side), device_id_type=MESH)
    pl.semaphore_signal(barrier, 1, device_id=peer, device_id_type=MESH)
    loads = [
        pltpu.make_async_copy(source_ref, target, load_sem.at[number])
        for number, (source_ref, target) in enumerate(
            ((gate_hbm, gate_w), (up_hbm, up_w), (down_hbm, down_w))
        )
    ]
    for load in loads:
        load.start()
    pl.semaphore_wait(barrier, count)

    my_half = pl.ds(pl.multiple_of(side * half, half), half)
    peer_half = pl.ds(pl.multiple_of((1 - side) * half, half), half)

    def picked(expert, start, amount):
        slots = lax.broadcasted_iota(jnp.int32, (amount, tokens), 0) + expert * room + start
        slots = slots.astype(jnp.float32)
        hit = (code_rows[0:1, :] == slots) | (code_rows[1:2, :] == slots)
        return jnp.where(hit, 1.0, 0.0).astype(jnp.bfloat16)

    def slot_gates(expert):
        slots = lax.broadcasted_iota(jnp.int32, (tokens, room), 1) + expert * room
        slots = slots.astype(jnp.float32)
        held = jnp.where(code_cols[:, 0:1] == slots, gates[:, 0:1], 0.0)
        held = held + jnp.where(code_cols[:, 1:2] == slots, gates[:, 1:2], 0.0)
        return jnp.broadcast_to(jnp.sum(held, axis=0, keepdims=True), (8, room))

    def rows_copy(step):
        target = source(step)
        return pltpu.make_async_remote_copy(
            sent.at[step - 1],
            rows.at[own, my_half],
            rows_send.at[step - 1],
            rows_recv.at[own],
            device_id=(target, ctx, side),
            device_id_type=MESH,
        )

    def gates_copy(step):
        return pltpu.make_async_remote_copy(
            gates_out.at[step - 1],
            gates_in.at[own],
            gates_send.at[step - 1],
            gates_recv.at[own],
            device_id=(source(step), ctx, side),
            device_id_type=MESH,
        )

    def send_rows(step, unused):
        target = source(step)
        sent[step - 1] = dot32(picked(target, side * half, half), norm[...]).astype(jnp.bfloat16)
        rows_copy(step).start()
        gates_out[step - 1] = slot_gates(target)
        gates_copy(step).start()
        return unused

    lax.fori_loop(1, count, send_rows, 0)
    rows[own] = dot32(picked(own, 0, room), norm[...]).astype(jnp.bfloat16)
    gates_in[own] = slot_gates(own)
    for load in loads:
        load.wait()

    def landed(buffer, send, recv, origin):
        return pltpu.make_async_remote_copy(
            buffer, buffer, send, recv, device_id=peer, device_id_type=MESH
        )

    def pass_copy(origin):
        return pltpu.make_async_remote_copy(
            rows.at[origin, my_half],
            rows.at[origin, my_half],
            pass_send.at[origin],
            pass_recv.at[origin],
            device_id=peer,
            device_id_type=MESH,
        )

    def part_copy(step):
        return pltpu.make_async_remote_copy(
            partial.at[step, peer_half],
            peer_part.at[step],
            part_send.at[step],
            part_recv.at[step],
            device_id=peer,
            device_id_type=MESH,
        )

    def back_copy(step):
        return pltpu.make_async_remote_copy(
            summed.at[step],
            back.at[own],
            back_send.at[step],
            back_recv.at[own],
            device_id=(source(step), ctx, side),
            device_id_type=MESH,
        )

    def dots_copy(step):
        return pltpu.make_async_remote_copy(
            dots_out.at[step],
            dots_in.at[own],
            dots_send.at[step],
            dots_recv.at[own],
            device_id=(source(step), ctx, side),
            device_id_type=MESH,
        )

    def send_back(step):
        part_copy(step).wait_recv()
        summed[step] = (
            partial[step, my_half].astype(jnp.float32) + peer_part[step].astype(jnp.float32)
        ).astype(jnp.bfloat16)
        back_copy(step).start()

    cut = (hidden // 256 + 1) // 2 * 256
    pieces = (slice(0, cut), slice(cut, hidden))

    def run_chunk(step, unused):
        origin = source(step)

        @pl.when(step > 0)
        def _():
            landed(rows.at[origin, peer_half], pass_send.at[origin], pass_recv.at[origin], 0).wait_recv()
            landed(gates_in.at[origin], gates_send.at[0], gates_recv.at[origin], 0).wait_recv()

        gate_column = jnp.transpose(gates_in[origin])[:, 0:1]
        slot_grad[origin] = (upstream[origin].astype(jnp.float32) * gate_column).astype(
            jnp.bfloat16
        )

        def inside(piece):
            block = rows[origin]
            gate_pre = dot32(block, gate_w[:, piece])
            up_pre = dot32(block, up_w[:, piece])
            inner_grad = dot32(slot_grad[origin], down_w[:, piece])
            active, slope = gelu_parts(gate_pre)
            held = (active * up_pre).astype(jnp.bfloat16)
            inner[origin, :, piece] = held
            gate_grad[origin, :, piece] = (inner_grad * up_pre * slope).astype(jnp.bfloat16)
            up_grad[origin, :, piece] = (inner_grad * active).astype(jnp.bfloat16)
            return jnp.sum(active * up_pre * inner_grad, axis=1, keepdims=True)

        dots = inside(pieces[0])

        @pl.when(step < count - 1)
        def _():
            following = source(step + 1)
            landed(
                rows.at[following, my_half], rows_send.at[0], rows_recv.at[following], 0
            ).wait_recv()
            pass_copy(following).start()

        dots = dots + inside(pieces[1])
        dots_out[step] = jnp.transpose(jnp.broadcast_to(dots, (room, 128)))[0:8, :]

        @pl.when(step > 1)
        def _():
            send_back(step - 1)

        partial[step] = (
            dot_last(gate_grad[origin], gate_w[...]) + dot_last(up_grad[origin], up_w[...])
        ).astype(jnp.bfloat16)

        @pl.when(step > 0)
        def _():
            part_copy(step).start()
            dots_copy(step).start()

        return unused

    lax.fori_loop(0, count, run_chunk, 0)
    stores = [
        pltpu.make_async_copy(source_ref, target, store_sem.at[number])
        for number, (source_ref, target) in enumerate(
            (
                (rows, rows_hbm),
                (slot_grad, slot_hbm),
                (inner, inner_hbm),
                (gate_grad, gate_grad_hbm),
                (up_grad, up_grad_hbm),
            )
        )
    ]
    for store in stores:
        store.start()

    def run_out(step, unused):
        outs[step] = dot_last(inner[step], down_w[...]).astype(jnp.bfloat16)
        return unused

    lax.fori_loop(0, 1, run_out, 0)
    send_back(count - 1)
    lax.fori_loop(1, count, run_out, 0)
    out_store = pltpu.make_async_copy(outs, out_hbm, store_sem.at[5])
    out_store.start()

    def dots_landed(step, unused):
        origin = source(step)
        landed(dots_in.at[origin], dots_send.at[0], dots_recv.at[origin], 0).wait_recv()
        return unused

    def back_landed(step, unused):
        origin = source(step)
        landed(back.at[origin], back_send.at[0], back_recv.at[origin], 0).wait_recv()
        return unused

    lax.fori_loop(1, count, dots_landed, 0)
    dots_in[own] = dots_out[0]
    final_dots[0] = jnp.zeros((8, tokens), jnp.float32)
    for expert in range(count):
        column = jnp.transpose(dots_in[expert])[:, 0:1]
        slots = lax.broadcasted_iota(jnp.int32, (room, tokens), 0) + expert * room
        slots = slots.astype(jnp.float32)
        for choice in range(2):
            final_dots[0, choice : choice + 1, :] += jnp.sum(
                jnp.where(code_rows[choice : choice + 1, :] == slots, column, 0.0),
                axis=0,
                keepdims=True,
            )
    lax.fori_loop(1, count, back_landed, 0)
    blocks = final_out.shape[0]
    span = tokens // blocks

    def final_copy(block):
        return pltpu.make_async_remote_copy(
            final_out.at[block],
            final_in.at[block],
            final_send.at[block],
            final_recv.at[block],
            device_id=peer,
            device_id_type=MESH,
        )

    dots_final = pltpu.make_async_remote_copy(
        final_dots.at[0],
        final_dots.at[1],
        final_send.at[blocks],
        final_recv.at[blocks],
        device_id=peer,
        device_id_type=MESH,
    )
    dots_final.start()

    def combine(block, unused):
        spot = pl.ds(pl.multiple_of(block * span, span), span)

        def chosen(start, amount):
            slots = lax.broadcasted_iota(jnp.int32, (span, amount), 1) + start
            slots = slots.astype(jnp.float32)
            hit = (code_cols[spot, 0:1] == slots) | (code_cols[spot, 1:2] == slots)
            return jnp.where(hit, 1.0, 0.0).astype(jnp.bfloat16)

        total = dot32(chosen(own * room, room), partial[0])
        for step in range(1, count):
            origin = source(step)
            total = total + dot32(chosen(origin * room + side * half, half), back[origin])
        final_out[block] = total.astype(jnp.bfloat16)
        final_copy(block).start()
        return unused

    lax.fori_loop(0, blocks, combine, 0)

    def finish(block, unused):
        spot = pl.ds(pl.multiple_of(block * span, span), span)
        final_copy(block).wait_recv()
        row_grad[spot, :] = final_out[block].astype(jnp.float32) + final_in[block].astype(
            jnp.float32
        )
        return unused

    lax.fori_loop(0, blocks, finish, 0)
    dots_final.wait_recv()
    dot_rows[...] = final_dots[0] + final_dots[1]

    def drain(step, unused):
        rows_copy(step).wait_send()
        gates_copy(step).wait_send()
        pass_copy(source(step)).wait_send()
        part_copy(step).wait_send()
        back_copy(step).wait_send()
        dots_copy(step).wait_send()
        return unused

    lax.fori_loop(1, count, drain, 0)

    def drain_final(block, unused):
        final_copy(block).wait_send()
        return unused

    lax.fori_loop(0, blocks, drain_final, 0)
    dots_final.wait_send()
    for store in stores:
        store.wait()
    out_store.wait()


def run_experts(count, norm, gates, code_rows, code_cols, upstream, gate_w, up_w, down_w):
    tokens, width = norm.shape
    room = upstream.shape[1]
    half = room // 2
    hidden = gate_w.shape[1]
    blocks = 4
    low = jnp.bfloat16
    full = jnp.float32
    dma = pltpu.SemaphoreType.DMA
    return pl.pallas_call(
        partial(expert_exchange, count),
        out_shape=(
            jax.ShapeDtypeStruct((tokens, width), full),
            jax.ShapeDtypeStruct((8, tokens), full),
            jax.ShapeDtypeStruct((count, room, width), low),
            jax.ShapeDtypeStruct((count, room, width), low),
            jax.ShapeDtypeStruct((count, room, hidden), low),
            jax.ShapeDtypeStruct((count, room, hidden), low),
            jax.ShapeDtypeStruct((count, room, hidden), low),
            jax.ShapeDtypeStruct((count, room, width), low),
        ),
        in_specs=in_vmem(5) + [pl.BlockSpec(memory_space=pl.ANY)] * 3,
        out_specs=tuple(in_vmem(2) + [pl.BlockSpec(memory_space=pl.ANY)] * 6),
        scratch_shapes=[
            pltpu.VMEM((width, hidden), low),
            pltpu.VMEM((width, hidden), low),
            pltpu.VMEM((width, hidden), low),
            pltpu.VMEM((count, room, width), low),
            pltpu.VMEM((count - 1, half, width), low),
            pltpu.VMEM((count, 8, room), full),
            pltpu.VMEM((count - 1, 8, room), full),
            pltpu.VMEM((count, room, width), low),
            pltpu.VMEM((count, room, hidden), low),
            pltpu.VMEM((count, room, hidden), low),
            pltpu.VMEM((count, room, hidden), low),
            pltpu.VMEM((count, room, width), low),
            pltpu.VMEM((count, room, width), low),
            pltpu.VMEM((count, half, width), low),
            pltpu.VMEM((count, half, width), low),
            pltpu.VMEM((count, half, width), low),
            pltpu.VMEM((count, 8, room), full),
            pltpu.VMEM((count, 8, room), full),
            pltpu.VMEM((blocks, tokens // blocks, width), low),
            pltpu.VMEM((blocks, tokens // blocks, width), low),
            pltpu.VMEM((2, 8, tokens), full),
            dma((3,)),
            dma((6,)),
            dma((count,)),
            dma((count,)),
            dma((count,)),
            dma((count,)),
            dma((count,)),
            dma((count,)),
            dma((count,)),
            dma((count,)),
            dma((count,)),
            dma((count,)),
            dma((count,)),
            dma((count,)),
            dma((blocks + 1,)),
            dma((blocks + 1,)),
        ],
        compiler_params=pltpu.CompilerParams(
            collective_id=3, has_side_effects=True, vmem_limit_bytes=63 * 2**20
        ),
        name="expert_exchange",
    )(norm, gates, code_rows, code_cols, upstream, gate_w, up_w, down_w)


def swap_sides(member):
    return lax.ppermute(member, "tensor", [(0, 1), (1, 0)])


def exchange(member, axis):
    return lax.all_to_all(member, axis, split_axis=0, concat_axis=0, tiled=True)


def slot_codes(routes, experts, room):
    tokens = routes.shape[0]
    picks = routes[:, :, None] == jnp.arange(experts, dtype=jnp.int32)[None, None, :]
    named = jnp.sum(picks, axis=1).astype(jnp.bfloat16)
    index = jnp.arange(tokens, dtype=jnp.int32)
    before = (index[:, None] > index[None, :]).astype(jnp.bfloat16)
    rank = jnp.dot(before, named, preferred_element_type=jnp.float32)
    slots = rank + room * jnp.arange(experts, dtype=jnp.float32)[None, :]
    return picks, jnp.sum(jnp.where(picks, slots[:, None, :], 0.0), axis=2)


def experts_apart(norm_two, upstream, gates, codes, room, count, weights):
    tokens, width = norm_two.shape
    codes = codes.astype(jnp.int32).reshape(-1)
    shaped = (count, room, width)

    def sent(member):
        slots = jnp.zeros((count * room, width), jnp.bfloat16).at[codes].set(member)
        return exchange(slots.reshape(shaped), "shard").reshape(-1, width)

    slot_rows = sent(jnp.repeat(norm_two, TOP, axis=0))
    slot_grads = sent(
        (gates[:, :, None] * upstream[:, None, :]).reshape(-1, width).astype(jnp.bfloat16)
    )
    gate_mat, up_mat, down_mat = weights
    gate_pre = dot32(slot_rows, gate_mat)
    up_pre = dot32(slot_rows, up_mat)
    activated, slope = gelu_parts(gate_pre)
    inner = (activated * up_pre).astype(jnp.bfloat16)
    expert_out = contract_cols(inner, down_mat)
    inner_grad = dot32(slot_grads, down_mat)
    gate_grad = (inner_grad * up_pre * slope).astype(jnp.bfloat16)
    up_grad = (inner_grad * activated).astype(jnp.bfloat16)
    rows_grad = contract_cols(gate_grad, gate_mat) + contract_cols(up_grad, up_mat)

    def returned(member):
        member = lax.psum(member.astype(jnp.bfloat16), "tensor").reshape(shaped)
        member = exchange(member, "shard").reshape(-1, width)[codes]
        return member.astype(jnp.float32).reshape(tokens, TOP, width)

    per_choice = returned(expert_out)
    mixture = jnp.sum(gates[:, :, None] * per_choice, axis=1)
    dots = gates * jnp.sum(per_choice * upstream[:, None, :], axis=2)
    norm_grad = jnp.sum(returned(rows_grad), axis=1)
    return mixture, dots, norm_grad, slot_rows, slot_grads, inner, gate_grad, up_grad


def experts_fused(norm_two, up_slots, gates, codes, code_rows, room, count, weights):
    width = norm_two.shape[1]
    half = room // 2
    side = lax.axis_index("tensor")
    norm_grad, dots, rows, grads, inner, gate_grad, up_grad, outs = run_experts(
        count, norm_two, gates, code_rows, codes, up_slots, *weights
    )
    theirs = lax.dynamic_slice_in_dim(outs, (1 - side) * half, half, 1)
    ours = lax.dynamic_slice_in_dim(outs, side * half, half, 1)
    ours = (ours.astype(jnp.float32) + swap_sides(theirs).astype(jnp.float32)).astype(jnp.bfloat16)
    ours = exchange(ours, "shard").reshape(-1, width)
    slots = jnp.arange(count * half, dtype=jnp.int32)
    slots = (slots // half * room + slots % half + side * half).astype(jnp.float32)
    mixing = sum(
        jnp.where(codes[:, k : k + 1] == slots[None, :], gates[:, k : k + 1], 0.0)
        for k in range(TOP)
    )
    mixture = dot32(mixing.astype(jnp.bfloat16), ours).astype(jnp.bfloat16)
    mixture = mixture.astype(jnp.float32) + swap_sides(mixture).astype(jnp.float32)
    flat = [member.reshape(-1, member.shape[2]) for member in (rows, grads, inner)]
    flat += [gate_grad.reshape(-1, inner.shape[2]), up_grad.reshape(-1, inner.shape[2])]
    return (mixture, jnp.transpose(dots[:TOP]), norm_grad, *flat)


def local(
    tokens_in,
    cotangent,
    segment_ids,
    live_blocks,
    routes,
    w_query,
    w_key,
    w_value,
    w_out,
    rel_bias,
    attn_gain,
    ffn_gain,
    router,
    w_gate,
    w_up,
    w_down,
):
    rows_here, width = tokens_in.shape
    shard_size = lax.axis_size("shard")
    ctx_size = lax.axis_size("ctx")
    side_count = lax.axis_size("tensor")
    ctx_index = lax.axis_index("ctx")
    side = lax.axis_index("tensor")
    head_cols = w_query.shape[1]
    share = head_cols // ctx_size
    experts = router.shape[1]
    room = max(2, 3 * rows_here // experts)
    fused = shard_size == 4 and experts == shard_size and side_count == 2

    picks, codes = slot_codes(routes, experts, room)
    code_rows = jnp.pad(jnp.transpose(codes), ((0, 8 - TOP), (0, 0)), constant_values=-1.0)
    up_slots = None
    if fused:
        slots = jnp.arange(experts * room, dtype=jnp.int32).astype(jnp.float32)[:, None]
        chosen = (code_rows[0:1] == slots) | (code_rows[1:2] == slots)
        up_slots = dot32(chosen.astype(jnp.bfloat16), cotangent).astype(jnp.bfloat16)
        up_slots = exchange(up_slots.reshape(experts, room, width), "shard")

    def by_owner(member):
        return member.reshape(member.shape[0], ctx_size, share)

    packed_rows = jnp.stack([by_owner(w_query), by_owner(w_key), by_owner(w_value)], axis=2)
    gathered = lax.all_gather(
        jnp.concatenate(
            [
                packed_rows.reshape(w_query.shape[0], -1),
                attn_gain[:, None],
                ffn_gain[:, None],
                router,
            ],
            axis=1,
        ).astype(jnp.bfloat16),
        ("shard", "ctx"),
        axis=0,
        tiled=True,
    )
    packed_w = gathered[:, : 3 * head_cols]
    gain_one = gathered[:, 3 * head_cols]
    gain_two = gathered[:, 3 * head_cols + 1]
    router_w = gathered[:, 3 * head_cols + 2 :]
    out_w = lax.all_gather(w_out.astype(jnp.bfloat16), ("shard", "ctx", "tensor"), axis=0)
    out_w = out_w.reshape(-1, side_count, w_out.shape[0], head_cols)
    out_w = jnp.transpose(out_w, (0, 2, 1, 3)).reshape(width, side_count * head_cols)
    expert_weights = tuple(
        lax.all_gather(member.astype(jnp.bfloat16), "ctx", axis=1, tiled=True)[0]
        for member in (w_gate, w_up, w_down)
    )

    inputs = tokens_in.astype(jnp.float32)
    scale_one = lax.rsqrt(jnp.mean(inputs * inputs, axis=1, keepdims=True) + 1e-06)
    normal_one = inputs * scale_one
    norm_one = (normal_one * gain_one.astype(jnp.float32)).astype(jnp.bfloat16)
    packed = dot32(norm_one, packed_w).astype(jnp.bfloat16)
    packed = jnp.transpose(packed.reshape(rows_here, ctx_size, 3 * share), (1, 0, 2))
    packed = exchange(packed, "ctx").reshape(ctx_size * rows_here, 3 * share)
    segments = lax.all_gather(segment_ids.reshape(-1), "ctx", axis=0, tiled=True)
    alive = live_tiles(segments, live_blocks[0])
    segment_row = segments.astype(jnp.float32)[None]
    pair_heads = share // HEAD
    own_bias = lax.dynamic_slice_in_dim(rel_bias, ctx_index * pair_heads, pair_heads, 1)
    buckets = span_buckets()
    line = jnp.dot(own_bias.T, buckets.T, precision=lax.Precision.HIGHEST)
    attended, attended_t, log_sum = run_forward(alive, packed, segment_row, line)
    attended = attended.reshape(ctx_size, 1, rows_here, share)
    attended = jnp.broadcast_to(attended, (ctx_size, side_count, rows_here, share))
    attended = exchange(attended.reshape(-1, rows_here, share), ("ctx", "tensor"))
    attended = attended.reshape(ctx_size, side_count, rows_here, share)
    attended = jnp.transpose(attended, (2, 1, 0, 3))
    attended_low = lax.dynamic_index_in_dim(attended, side, 1, False).reshape(rows_here, head_cols)
    attended = attended.reshape(rows_here, side_count * head_cols)
    hidden_one = inputs + contract_cols(attended, out_w)
    scale_two = lax.rsqrt(jnp.mean(hidden_one * hidden_one, axis=1, keepdims=True) + 1e-06)
    normal_two = hidden_one * scale_two
    norm_two = (normal_two * gain_two.astype(jnp.float32)).astype(jnp.bfloat16)
    logits = dot32(norm_two, router_w)
    chosen = jnp.sum(jnp.where(picks, logits[:, None, :], 0.0), axis=2)
    gates = jax.nn.softmax(chosen, axis=1)
    upstream = cotangent.astype(jnp.float32)
    if fused:
        results = experts_fused(
            norm_two, up_slots, gates, codes, code_rows, room, experts, expert_weights
        )
    else:
        results = experts_apart(norm_two, upstream, gates, codes, room, experts, expert_weights)
    mixture, gate_dots, norm_grad, slot_rows, slot_grads, inner, gate_grad, up_grad = results
    weight_grads = lax.psum_scatter(
        jnp.stack(
            [
                contract_rows(slot_rows, gate_grad),
                contract_rows(slot_rows, up_grad),
                contract_rows(slot_grads, inner),
            ],
            axis=1,
        ).astype(jnp.bfloat16),
        "ctx",
        scatter_dimension=0,
        tiled=True,
    ).astype(jnp.float32)
    mixed = (hidden_one + mixture).astype(jnp.bfloat16)
    gate_shift = gate_dots - gates * jnp.sum(gate_dots, axis=1, keepdims=True)
    logit_grad = jnp.sum(jnp.where(picks, gate_shift[:, :, None], 0.0), axis=1)
    router_f = router_w.astype(jnp.float32)
    norm_grad = norm_grad + jnp.dot(logit_grad, router_f.T, precision=lax.Precision.HIGHEST)
    spread_two = norm_grad * gain_two.astype(jnp.float32)
    hidden_grad = upstream + scale_two * (
        spread_two - normal_two * jnp.mean(spread_two * normal_two, axis=1, keepdims=True)
    )
    branch_grad = hidden_grad.astype(jnp.bfloat16)
    own_out_w = lax.dynamic_slice_in_dim(out_w, side * head_cols, head_cols, 1)
    grad_heads = dot32(branch_grad, own_out_w).astype(jnp.bfloat16)
    grad_heads = jnp.transpose(grad_heads.reshape(rows_here, ctx_size, share), (1, 0, 2))
    grad_heads = exchange(grad_heads, "ctx").reshape(-1, share)
    packed_grad, bias_line = run_backward(
        alive, packed, segment_row, line, grad_heads, attended_t, log_sum
    )
    own_grad = jnp.dot(buckets.T, bias_line[:pair_heads].T, precision=lax.Precision.HIGHEST)
    far = jnp.sum(bias_line[pair_heads : 3 * pair_heads], axis=1)
    half = NBUCK // 2
    own_grad = own_grad.at[half - 1].add(far[:pair_heads]).at[NBUCK - 1].add(far[pair_heads:])
    bias_acc = lax.dynamic_update_slice_in_dim(
        jnp.zeros(rel_bias.shape, jnp.float32), own_grad, ctx_index * pair_heads, 1
    )
    packed_grad = exchange(packed_grad.reshape(ctx_size, rows_here, 3 * share), "ctx")
    packed_grad = jnp.transpose(packed_grad, (1, 0, 2)).reshape(rows_here, 3 * head_cols)
    norm_one_grad = contract_cols(packed_grad, packed_w).astype(jnp.bfloat16)
    norm_one_grad = norm_one_grad.astype(jnp.float32) + swap_sides(norm_one_grad).astype(
        jnp.float32
    )
    spread_one = norm_one_grad * gain_one.astype(jnp.float32)
    input_grad = hidden_grad + scale_one * (
        spread_one - normal_one * jnp.mean(spread_one * normal_one, axis=1, keepdims=True)
    )
    first_gain = jnp.sum(norm_one_grad * normal_one, axis=0)[:, None]
    second_gain = jnp.sum(norm_grad * normal_two, axis=0)[:, None]
    router_part = jnp.dot(
        norm_two.astype(jnp.float32).T, logit_grad, precision=lax.Precision.HIGHEST
    )
    reduced = lax.psum_scatter(
        jnp.concatenate(
            [
                contract_rows(norm_one, packed_grad),
                contract_rows(branch_grad, attended_low),
                first_gain,
                second_gain,
                router_part,
            ],
            axis=1,
        ),
        ("shard", "ctx"),
        scatter_dimension=0,
        tiled=True,
    )
    grad_bias = lax.psum(bias_acc, ("shard", "ctx"))
    packed_rows = reduced[:, : 3 * head_cols].reshape(-1, ctx_size, 3, share)
    return (
        mixed,
        input_grad.astype(jnp.bfloat16),
        packed_rows[:, :, 0].reshape(-1, head_cols),
        packed_rows[:, :, 1].reshape(-1, head_cols),
        packed_rows[:, :, 2].reshape(-1, head_cols),
        reduced[:, 3 * head_cols : 4 * head_cols],
        grad_bias,
        reduced[:, 4 * head_cols],
        reduced[:, 4 * head_cols + 1],
        reduced[:, 4 * head_cols + 2 :],
        weight_grads[:, 0][None],
        weight_grads[:, 1][None],
        weight_grads[:, 2][None],
    )


def solution(mesh):
    placed = (
        P(("shard", "ctx"), None),
        P(("shard", "ctx"), None),
        P("shard", "ctx"),
        P("shard", None, None),
        P(("shard", "ctx"), None),
        P(("shard", "ctx"), "tensor"),
        P(("shard", "ctx"), "tensor"),
        P(("shard", "ctx"), "tensor"),
        P(("shard", "ctx"), "tensor"),
        P(None, "tensor"),
        P(("shard", "ctx")),
        P(("shard", "ctx")),
        P(("shard", "ctx"), None),
        P("shard", "ctx", "tensor"),
        P("shard", "ctx", "tensor"),
        P("shard", "ctx", "tensor"),
    )
    return jax.shard_map(
        local,
        mesh=mesh,
        in_specs=placed,
        out_specs=(
            P(("shard", "ctx"), None),
            P(("shard", "ctx"), None),
            P(("shard", "ctx"), "tensor"),
            P(("shard", "ctx"), "tensor"),
            P(("shard", "ctx"), "tensor"),
            P(("shard", "ctx"), "tensor"),
            P(None, "tensor"),
            P(("shard", "ctx")),
            P(("shard", "ctx")),
            P(("shard", "ctx"), None),
            P("shard", "ctx", "tensor"),
            P("shard", "ctx", "tensor"),
            P("shard", "ctx", "tensor"),
        ),
        check_vma=False,
    )
```

```python
import math
from functools import partial

import jax
import jax.numpy as jnp
from jax import lax
from jax.experimental import pallas as pl
from jax.experimental.pallas import tpu as pltpu
from jax.sharding import PartitionSpec as P

HEAD = 64
NBUCK = 32
TOP = 2
ATT_BLK = 512


FAR_STEPS = (12, 16, 23, 32, 46, 64, 91)


def bucket_ids(relative):
    distance = jnp.abs(relative)
    far = jnp.full(distance.shape, 8, jnp.int32)
    for bound in FAR_STEPS:
        far = far + (distance >= bound).astype(jnp.int32)
    near = jnp.where(distance < 8, distance, far)
    return near + jnp.where(relative > 0, NBUCK // 2, 0)


def contract_rows(left, right):
    return lax.dot_general(
        left, right, (((0,), (0,)), ((), ())), preferred_element_type=jnp.float32
    )


def contract_cols(left, right):
    return lax.dot_general(
        left, right, (((1,), (1,)), ((), ())), preferred_element_type=jnp.float32
    )


TILE = 256
BIG = 2.0**100
SPAN = 4 * TILE


def place_mask(segment_row):
    rows = lax.broadcasted_iota(jnp.int32, (128, segment_row.shape[1]), 0).astype(jnp.float32)
    apart = jnp.where(rows == segment_row, 0.0, -BIG)
    return jnp.where(rows < 8.0, apart, jnp.where(rows < 11.0, 1.0, 0.0))


def seat_rows(segment_row, extra):
    rows = lax.broadcasted_iota(jnp.int32, (128, segment_row.shape[1]), 0).astype(jnp.float32)
    own = jnp.where((rows == segment_row) & (rows < 8.0), 1.0, 0.0)
    if extra is None:
        return own.astype(jnp.bfloat16)
    high = extra.astype(jnp.bfloat16).astype(jnp.float32)
    rest = extra - high
    middle = rest.astype(jnp.bfloat16).astype(jnp.float32)
    low = rest - middle
    own = jnp.where(rows == 8.0, high, own)
    own = jnp.where(rows == 9.0, middle, own)
    return jnp.where(rows == 10.0, low, own).astype(jnp.bfloat16)


def fill_bias(line_ref, bias_ref):
    for head in range(2):
        line = line_ref[head : head + 1, :]
        turned = pltpu.roll(
            jnp.broadcast_to(line, (TILE, SPAN)), 0, axis=1, stride=1, stride_axis=0
        )
        bias_ref[head, 1] = turned[:, TILE : 2 * TILE]
        bias_ref[head, 2] = turned[:, :TILE]
        bias_ref[head, 3] = turned[:, 3 * TILE :]
        bias_ref[head, 0] = jnp.broadcast_to(line[:, 511:512], (TILE, TILE))
        bias_ref[head, 4] = jnp.broadcast_to(line[:, 513:514], (TILE, TILE))


def tile_at(index):
    return pl.ds(pl.multiple_of(index * TILE, TILE), TILE)


def dot32(left, right):
    return jnp.dot(left, right, preferred_element_type=jnp.float32)


def attention_forward(
    alive, packed, segment, line, out, out_t, log_sum, key_side, query_side, value_t, bias, top, acc
):
    length = packed.shape[0]
    tiles = length // TILE
    fill_bias(line, bias)

    def prepare(index, unused):
        spot = tile_at(index)
        seg = segment[0:1, spot]
        block = packed[spot, :].astype(jnp.float32)
        key_side[spot, :128] = packed[spot, 128:256]
        key_side[spot, 128:] = jnp.transpose(place_mask(seg)).astype(jnp.bfloat16)
        query_t = jnp.transpose(block[:, :128]) * 0.125
        seats = seat_rows(seg, None)
        half = lax.broadcasted_iota(jnp.int32, (128, TILE), 0) // HEAD
        values = jnp.transpose(block[:, 256:]).astype(jnp.bfloat16)
        ones = jnp.where(lax.broadcasted_iota(jnp.int32, (16, TILE), 0) == 0, 1.0, 0.0)
        for head in range(2):
            query_side[head, :128, spot] = jnp.where(half == head, query_t, 0.0).astype(
                jnp.bfloat16
            )
            query_side[head, 128:, spot] = seats
            value_t[head, :HEAD, spot] = values[HEAD * head : HEAD * (head + 1)]
            value_t[head, HEAD:, spot] = ones.astype(jnp.bfloat16)
        return unused

    lax.fori_loop(0, tiles, prepare, 0)

    def query_tile(query_index, unused):
        query_spot = tile_at(query_index)
        top[...] = jnp.full(top.shape, -3e38, jnp.float32)
        acc[...] = jnp.zeros(acc.shape, jnp.float32)

        def key_tile(key_index, carried):
            @pl.when(alive[query_index * tiles + key_index] == 1)
            def _():
                key_spot = tile_at(key_index)
                slot = jnp.clip(key_index - query_index, -2, 2) + 2
                keys = key_side[key_spot, :]
                for head in range(2):
                    scores = dot32(keys, query_side[head, :, query_spot]) + bias[head, slot]
                    before = top[head : head + 1, :]
                    now = jnp.maximum(before, jnp.max(scores, axis=0, keepdims=True))
                    weights = jnp.exp(scores - now).astype(jnp.bfloat16)
                    top[head : head + 1, :] = now
                    acc[head] = acc[head] * jnp.exp(before - now) + dot32(
                        value_t[head, :, key_spot], weights
                    )

            return carried

        lax.fori_loop(0, tiles, key_tile, 0)
        parts = []
        for head in range(2):
            total = acc[head, HEAD : HEAD + 1, :]
            part = acc[head, :HEAD, :] / total
            out_t[HEAD * head : HEAD * (head + 1), query_spot] = part
            log_sum[head : head + 1, query_spot] = top[head : head + 1, :] + jnp.log(total)
            parts.append(part)
        out[query_spot, :] = jnp.transpose(jnp.concatenate(parts, axis=0)).astype(jnp.bfloat16)
        return unused

    lax.fori_loop(0, tiles, query_tile, 0)


def attention_backward(
    alive,
    packed,
    segment,
    line,
    grads,
    out_t,
    log_sum,
    packed_grad,
    bias_grad,
    key_side,
    value_side,
    query_side,
    grad_side,
    key_t,
    query_pair,
    grad_pair,
    bias,
    bias_acc,
    query_acc,
    key_acc,
    value_acc,
):
    length = packed.shape[0]
    tiles = length // TILE
    fill_bias(line, bias)
    bias_acc[...] = jnp.zeros(bias_acc.shape, jnp.float32)

    def prepare(index, unused):
        spot = tile_at(index)
        seg = segment[0:1, spot]
        block = packed[spot, :].astype(jnp.float32)
        grad = grads[spot, :].astype(jnp.float32)
        seats = jnp.transpose(place_mask(seg)).astype(jnp.bfloat16)
        key_side[spot, :128] = packed[spot, 128:256]
        key_side[spot, 128:] = seats
        value_side[spot, :128] = packed[spot, 256:]
        value_side[spot, 128:] = seats
        key_t[:, spot] = jnp.transpose(block[:, 128:256]).astype(jnp.bfloat16)
        query_t = jnp.transpose(block[:, :128]) * 0.125
        grad_t = jnp.transpose(grad)
        half = lax.broadcasted_iota(jnp.int32, (128, TILE), 0) // HEAD
        side = lax.broadcasted_iota(jnp.int32, (TILE, 128), 1) // HEAD
        products = grad_t * out_t[:, spot]
        query_acc[:, spot] = jnp.zeros((128, TILE), jnp.float32)
        for head in range(2):
            query_side[head, :128, spot] = jnp.where(half == head, query_t, 0.0).astype(
                jnp.bfloat16
            )
            query_side[head, 128:, spot] = seat_rows(seg, -log_sum[head : head + 1, spot])
            delta = jnp.sum(products[HEAD * head : HEAD * (head + 1)], axis=0, keepdims=True)
            grad_side[head, :128, spot] = jnp.where(half == head, grad_t, 0.0).astype(jnp.bfloat16)
            grad_side[head, 128:, spot] = seat_rows(jnp.full_like(seg, -1.0), -delta)
            query_pair[index, TILE * head : TILE * (head + 1), :] = jnp.where(
                side == head, block[:, :128] * 0.125, 0.0
            ).astype(jnp.bfloat16)
            grad_pair[index, TILE * head : TILE * (head + 1), :] = jnp.where(
                side == head, grad, 0.0
            ).astype(jnp.bfloat16)
        return unused

    lax.fori_loop(0, tiles, prepare, 0)

    def key_tile(key_index, unused):
        key_spot = tile_at(key_index)
        key_acc[...] = jnp.zeros(key_acc.shape, jnp.float32)
        value_acc[...] = jnp.zeros(value_acc.shape, jnp.float32)

        def query_tile(query_index, carried):
            @pl.when(alive[query_index * tiles + key_index] == 1)
            def _():
                query_spot = tile_at(query_index)
                slot = jnp.clip(key_index - query_index, -2, 2) + 2
                keys = key_side[key_spot, :]
                values = value_side[key_spot, :]
                probs, score_grads = [], []
                for head in range(2):
                    scores = dot32(keys, query_side[head, :, query_spot]) + bias[head, slot]
                    prob = jnp.exp(scores)
                    score_grad = prob * dot32(values, grad_side[head, :, query_spot])
                    bias_acc[head, slot] += score_grad
                    score_grad = score_grad.astype(jnp.bfloat16)
                    probs.append(prob.astype(jnp.bfloat16))
                    score_grads.append(score_grad)
                    rows = slice(HEAD * head, HEAD * (head + 1))
                    query_acc[rows, query_spot] += dot32(key_t[rows, key_spot], score_grad)
                value_acc[...] += dot32(jnp.concatenate(probs, axis=1), grad_pair[query_index])
                key_acc[...] += dot32(jnp.concatenate(score_grads, axis=1), query_pair[query_index])

            return carried

        lax.fori_loop(0, tiles, query_tile, 0)
        packed_grad[key_spot, 128:256] = key_acc[...].astype(jnp.bfloat16)
        packed_grad[key_spot, 256:] = value_acc[...].astype(jnp.bfloat16)
        return unused

    lax.fori_loop(0, tiles, key_tile, 0)

    def finish(index, unused):
        spot = tile_at(index)
        packed_grad[spot, :128] = (jnp.transpose(query_acc[:, spot]) * 0.125).astype(jnp.bfloat16)
        return unused

    lax.fori_loop(0, tiles, finish, 0)
    rows = lax.broadcasted_iota(jnp.int32, (TILE, TILE), 0)
    columns = lax.broadcasted_iota(jnp.int32, (TILE, TILE), 1)
    flip = jnp.where(rows + columns == TILE - 1, 1.0, 0.0)
    bias_grad[...] = jnp.zeros(bias_grad.shape, jnp.float32)
    for head in range(2):
        spread = jnp.concatenate(
            [
                bias_acc[head, 2],
                bias_acc[head, 1],
                jnp.zeros((TILE, TILE), jnp.float32),
                bias_acc[head, 3],
            ],
            axis=1,
        )
        flipped = jnp.dot(
            flip, spread, precision=lax.Precision.HIGHEST, preferred_element_type=jnp.float32
        )
        turned = pltpu.roll(flipped, SPAN - TILE + 1, axis=1, stride=1, stride_axis=0)
        bias_grad[head : head + 1, :] = jnp.sum(turned, axis=0, keepdims=True)
        bias_grad[2 + head : 3 + head, :TILE] = jnp.sum(bias_acc[head, 0], axis=0, keepdims=True)
        bias_grad[4 + head : 5 + head, :TILE] = jnp.sum(bias_acc[head, 4], axis=0, keepdims=True)


def estimate(micros):
    return pl.CostEstimate(flops=int(micros * 1e9), bytes_accessed=0, transcendentals=0)


def in_vmem(count):
    return [pl.BlockSpec(memory_space=pltpu.VMEM)] * count


def run_forward(alive, packed, segment, line):
    length = packed.shape[0]
    return pl.pallas_call(
        attention_forward,
        out_shape=(
            jax.ShapeDtypeStruct((length, 128), jnp.bfloat16),
            jax.ShapeDtypeStruct((128, length), jnp.float32),
            jax.ShapeDtypeStruct((8, length), jnp.float32),
        ),
        in_specs=[pl.BlockSpec(memory_space=pltpu.SMEM)] + in_vmem(3),
        out_specs=tuple(in_vmem(3)),
        scratch_shapes=[
            pltpu.VMEM((length, 256), jnp.bfloat16),
            pltpu.VMEM((2, 256, length), jnp.bfloat16),
            pltpu.VMEM((2, HEAD + 16, length), jnp.bfloat16),
            pltpu.VMEM((2, 5, TILE, TILE), jnp.float32),
            pltpu.VMEM((8, TILE), jnp.float32),
            pltpu.VMEM((2, HEAD + 16, TILE), jnp.float32),
        ],
        compiler_params=pltpu.CompilerParams(vmem_limit_bytes=40 * 2**20),
        cost_estimate=estimate(20),
        name="attention_forward",
    )(alive, packed, segment, line)


def run_backward(alive, packed, segment, line, grads, out_t, log_sum):
    length = packed.shape[0]
    tiles = length // TILE
    return pl.pallas_call(
        attention_backward,
        out_shape=(
            jax.ShapeDtypeStruct((length, 384), jnp.bfloat16),
            jax.ShapeDtypeStruct((8, SPAN), jnp.float32),
        ),
        in_specs=[pl.BlockSpec(memory_space=pltpu.SMEM)] + in_vmem(6),
        out_specs=tuple(in_vmem(2)),
        scratch_shapes=[
            pltpu.VMEM((length, 256), jnp.bfloat16),
            pltpu.VMEM((length, 256), jnp.bfloat16),
            pltpu.VMEM((2, 256, length), jnp.bfloat16),
            pltpu.VMEM((2, 256, length), jnp.bfloat16),
            pltpu.VMEM((128, length), jnp.bfloat16),
            pltpu.VMEM((tiles, 2 * TILE, 128), jnp.bfloat16),
            pltpu.VMEM((tiles, 2 * TILE, 128), jnp.bfloat16),
            pltpu.VMEM((2, 5, TILE, TILE), jnp.float32),
            pltpu.VMEM((2, 5, TILE, TILE), jnp.float32),
            pltpu.VMEM((128, length), jnp.float32),
            pltpu.VMEM((TILE, 128), jnp.float32),
            pltpu.VMEM((TILE, 128), jnp.float32),
        ],
        compiler_params=pltpu.CompilerParams(vmem_limit_bytes=48 * 2**20),
        cost_estimate=estimate(26),
        name="attention_backward",
    )(alive, packed, segment, line, grads, out_t, log_sum)


def signed_span():
    places = jnp.arange(SPAN, dtype=jnp.int32)
    return jnp.where(places < SPAN // 2, -places, SPAN - places)


def span_buckets():
    return (bucket_ids(signed_span())[:, None] == jnp.arange(NBUCK)[None, :]).astype(jnp.float32)


def live_tiles(segments, live):
    tiles = segments.shape[0] // TILE
    grouped = segments.reshape(tiles, TILE)
    first, last = grouped[:, 0], grouped[:, -1]
    meets = (first[:, None] <= last[None, :]) & (first[None, :] <= last[:, None])
    spread = jnp.repeat(jnp.repeat(live, ATT_BLK // TILE, axis=0), ATT_BLK // TILE, axis=1)
    return (meets & (spread == 1)).astype(jnp.int32).reshape(-1)


MESH = pl.DeviceIdType.MESH


def gelu_parts(value):
    root = math.sqrt(2.0 / math.pi)
    square = value * value
    bend = jnp.tanh(root * value * (1.0 + 0.044715 * square))
    half = 0.5 * (1.0 + bend)
    slope = half + 0.5 * value * (1.0 - bend * bend) * (root * (1.0 + 0.134145 * square))
    return value * half, slope


def dot_last(left, right):
    return lax.dot_general(
        left, right, (((1,), (1,)), ((), ())), preferred_element_type=jnp.float32
    )


def expert_exchange(
    count,
    norm,
    gates,
    code_rows,
    code_cols,
    upstream,
    gate_hbm,
    up_hbm,
    down_hbm,
    row_grad,
    dot_rows,
    rows_hbm,
    slot_hbm,
    inner_hbm,
    gate_grad_hbm,
    up_grad_hbm,
    out_hbm,
    gate_w,
    up_w,
    down_w,
    rows,
    sent,
    gates_in,
    gates_out,
    slot_grad,
    inner,
    gate_grad,
    up_grad,
    outs,
    partial,
    peer_part,
    summed,
    back,
    dots_out,
    dots_in,
    final_out,
    final_in,
    final_dots,
    load_sem,
    store_sem,
    rows_send,
    rows_recv,
    pass_send,
    pass_recv,
    gates_send,
    gates_recv,
    part_send,
    part_recv,
    back_send,
    back_recv,
    dots_send,
    dots_recv,
    final_send,
    final_recv,
):
    own = lax.axis_index("shard")
    ctx = lax.axis_index("ctx")
    side = lax.axis_index("tensor")
    tokens, width = norm.shape
    room = upstream.shape[1]
    half = room // 2
    hidden = gate_w.shape[1]
    peer = (own, ctx, 1 - side)

    def source(step):
        flip = own // (count // 2)
        place = flip * (count - 1 - own) + (1 - flip) * own
        turn = step - 1
        turn = turn + (turn - place + count) // count
        other = flip * (count - 1 - turn) + (1 - flip) * turn
        first = 1 - (step + count - 1) // count
        return first * own + (1 - first) * other

    barrier = pltpu.get_barrier_semaphore()
    for step in range(1, count):
        pl.semaphore_signal(barrier, 1, device_id=(source(step), ctx, side), device_id_type=MESH)
    pl.semaphore_signal(barrier, 1, device_id=peer, device_id_type=MESH)
    loads = [
        pltpu.make_async_copy(source_ref, target, load_sem.at[number])
        for number, (source_ref, target) in enumerate(
            ((gate_hbm, gate_w), (up_hbm, up_w), (down_hbm, down_w))
        )
    ]
    for load in loads:
        load.start()
    pl.semaphore_wait(barrier, count)

    my_half = pl.ds(pl.multiple_of(side * half, half), half)
    peer_half = pl.ds(pl.multiple_of((1 - side) * half, half), half)

    def picked(expert, start, amount):
        slots = lax.broadcasted_iota(jnp.int32, (amount, tokens), 0) + expert * room + start
        slots = slots.astype(jnp.float32)
        hit = (code_rows[0:1, :] == slots) | (code_rows[1:2, :] == slots)
        return jnp.where(hit, 1.0, 0.0).astype(jnp.bfloat16)

    def slot_gates(expert):
        slots = lax.broadcasted_iota(jnp.int32, (tokens, room), 1) + expert * room
        slots = slots.astype(jnp.float32)
        held = jnp.where(code_cols[:, 0:1] == slots, gates[:, 0:1], 0.0)
        held = held + jnp.where(code_cols[:, 1:2] == slots, gates[:, 1:2], 0.0)
        return jnp.broadcast_to(jnp.sum(held, axis=0, keepdims=True), (8, room))

    def rows_copy(step):
        target = source(step)
        return pltpu.make_async_remote_copy(
            sent.at[step - 1],
            rows.at[own, my_half],
            rows_send.at[step - 1],
            rows_recv.at[own],
            device_id=(target, ctx, side),
            device_id_type=MESH,
        )

    def gates_copy(step):
        return pltpu.make_async_remote_copy(
            gates_out.at[step - 1],
            gates_in.at[own],
            gates_send.at[step - 1],
            gates_recv.at[own],
            device_id=(source(step), ctx, side),
            device_id_type=MESH,
        )

    def send_rows(step, unused):
        target = source(step)
        sent[step - 1] = dot32(picked(target, side * half, half), norm[...]).astype(jnp.bfloat16)
        rows_copy(step).start()
        gates_out[step - 1] = slot_gates(target)
        gates_copy(step).start()
        return unused

    lax.fori_loop(1, count, send_rows, 0)
    rows[own] = dot32(picked(own, 0, room), norm[...]).astype(jnp.bfloat16)
    gates_in[own] = slot_gates(own)
    for load in loads:
        load.wait()

    def landed(buffer, send, recv, origin):
        return pltpu.make_async_remote_copy(
            buffer, buffer, send, recv, device_id=peer, device_id_type=MESH
        )

    def pass_copy(origin):
        return pltpu.make_async_remote_copy(
            rows.at[origin, my_half],
            rows.at[origin, my_half],
            pass_send.at[origin],
            pass_recv.at[origin],
            device_id=peer,
            device_id_type=MESH,
        )

    def part_copy(step):
        return pltpu.make_async_remote_copy(
            partial.at[step, peer_half],
            peer_part.at[step],
            part_send.at[step],
            part_recv.at[step],
            device_id=peer,
            device_id_type=MESH,
        )

    def back_copy(step):
        return pltpu.make_async_remote_copy(
            summed.at[step],
            back.at[own],
            back_send.at[step],
            back_recv.at[own],
            device_id=(source(step), ctx, side),
            device_id_type=MESH,
        )

    def dots_copy(step):
        return pltpu.make_async_remote_copy(
            dots_out.at[step],
            dots_in.at[own],
            dots_send.at[step],
            dots_recv.at[own],
            device_id=(source(step), ctx, side),
            device_id_type=MESH,
        )

    def send_back(step):
        part_copy(step).wait_recv()
        summed[step] = (
            partial[step, my_half].astype(jnp.float32) + peer_part[step].astype(jnp.float32)
        ).astype(jnp.bfloat16)
        back_copy(step).start()

    cut = (hidden // 256 + 1) // 2 * 256
    pieces = (slice(0, cut), slice(cut, hidden))

    def run_chunk(step, unused):
        origin = source(step)

        @pl.when(step > 0)
        def _():
            landed(rows.at[origin, peer_half], pass_send.at[origin], pass_recv.at[origin], 0).wait_recv()
            landed(gates_in.at[origin], gates_send.at[0], gates_recv.at[origin], 0).wait_recv()

        gate_column = jnp.transpose(gates_in[origin])[:, 0:1]
        slot_grad[origin] = (upstream[origin].astype(jnp.float32) * gate_column).astype(
            jnp.bfloat16
        )

        def inside(piece):
            block = rows[origin]
            gate_pre = dot32(block, gate_w[:, piece])
            up_pre = dot32(block, up_w[:, piece])
            inner_grad = dot32(slot_grad[origin], down_w[:, piece])
            active, slope = gelu_parts(gate_pre)
            held = (active * up_pre).astype(jnp.bfloat16)
            inner[origin, :, piece] = held
            gate_grad[origin, :, piece] = (inner_grad * up_pre * slope).astype(jnp.bfloat16)
            up_grad[origin, :, piece] = (inner_grad * active).astype(jnp.bfloat16)
            return jnp.sum(active * up_pre * inner_grad, axis=1, keepdims=True)

        dots = inside(pieces[0])

        @pl.when(step < count - 1)
        def _():
            following = source(step + 1)
            landed(
                rows.at[following, my_half], rows_send.at[0], rows_recv.at[following], 0
            ).wait_recv()
            pass_copy(following).start()

        dots = dots + inside(pieces[1])
        dots_out[step] = jnp.transpose(jnp.broadcast_to(dots, (room, 128)))[0:8, :]

        @pl.when(step > 1)
        def _():
            send_back(step - 1)

        partial[step] = (
            dot_last(gate_grad[origin], gate_w[...]) + dot_last(up_grad[origin], up_w[...])
        ).astype(jnp.bfloat16)

        @pl.when(step > 0)
        def _():
            part_copy(step).start()
            dots_copy(step).start()

        return unused

    lax.fori_loop(0, count, run_chunk, 0)
    stores = [
        pltpu.make_async_copy(source_ref, target, store_sem.at[number])
        for number, (source_ref, target) in enumerate(
            (
                (rows, rows_hbm),
                (slot_grad, slot_hbm),
                (inner, inner_hbm),
                (gate_grad, gate_grad_hbm),
                (up_grad, up_grad_hbm),
            )
        )
    ]
    for store in stores:
        store.start()

    def run_out(step, unused):
        outs[step] = dot_last(inner[step], down_w[...]).astype(jnp.bfloat16)
        return unused

    lax.fori_loop(0, 1, run_out, 0)
    send_back(count - 1)
    lax.fori_loop(1, count, run_out, 0)
    out_store = pltpu.make_async_copy(outs, out_hbm, store_sem.at[5])
    out_store.start()

    def dots_landed(step, unused):
        origin = source(step)
        landed(dots_in.at[origin], dots_send.at[0], dots_recv.at[origin], 0).wait_recv()
        return unused

    def back_landed(step, unused):
        origin = source(step)
        landed(back.at[origin], back_send.at[0], back_recv.at[origin], 0).wait_recv()
        return unused

    lax.fori_loop(1, count, dots_landed, 0)
    dots_in[own] = dots_out[0]
    final_dots[0] = jnp.zeros((8, tokens), jnp.float32)
    for expert in range(count):
        column = jnp.transpose(dots_in[expert])[:, 0:1]
        slots = lax.broadcasted_iota(jnp.int32, (room, tokens), 0) + expert * room
        slots = slots.astype(jnp.float32)
        for choice in range(2):
            final_dots[0, choice : choice + 1, :] += jnp.sum(
                jnp.where(code_rows[choice : choice + 1, :] == slots, column, 0.0),
                axis=0,
                keepdims=True,
            )
    lax.fori_loop(1, count, back_landed, 0)
    blocks = final_out.shape[0]
    span = tokens // blocks

    def final_copy(block):
        return pltpu.make_async_remote_copy(
            final_out.at[block],
            final_in.at[block],
            final_send.at[block],
            final_recv.at[block],
            device_id=peer,
            device_id_type=MESH,
        )

    dots_final = pltpu.make_async_remote_copy(
        final_dots.at[0],
        final_dots.at[1],
        final_send.at[blocks],
        final_recv.at[blocks],
        device_id=peer,
        device_id_type=MESH,
    )
    dots_final.start()

    def combine(block, unused):
        spot = pl.ds(pl.multiple_of(block * span, span), span)

        def chosen(start, amount):
            slots = lax.broadcasted_iota(jnp.int32, (span, amount), 1) + start
            slots = slots.astype(jnp.float32)
            hit = (code_cols[spot, 0:1] == slots) | (code_cols[spot, 1:2] == slots)
            return jnp.where(hit, 1.0, 0.0).astype(jnp.bfloat16)

        total = dot32(chosen(own * room, room), partial[0])
        for step in range(1, count):
            origin = source(step)
            total = total + dot32(chosen(origin * room + side * half, half), back[origin])
        final_out[block] = total.astype(jnp.bfloat16)
        final_copy(block).start()
        return unused

    lax.fori_loop(0, blocks, combine, 0)

    def finish(block, unused):
        spot = pl.ds(pl.multiple_of(block * span, span), span)
        final_copy(block).wait_recv()
        row_grad[spot, :] = final_out[block].astype(jnp.float32) + final_in[block].astype(
            jnp.float32
        )
        return unused

    lax.fori_loop(0, blocks, finish, 0)
    dots_final.wait_recv()
    dot_rows[...] = final_dots[0] + final_dots[1]

    def drain(step, unused):
        rows_copy(step).wait_send()
        gates_copy(step).wait_send()
        pass_copy(source(step)).wait_send()
        part_copy(step).wait_send()
        back_copy(step).wait_send()
        dots_copy(step).wait_send()
        return unused

    lax.fori_loop(1, count, drain, 0)

    def drain_final(block, unused):
        final_copy(block).wait_send()
        return unused

    lax.fori_loop(0, blocks, drain_final, 0)
    dots_final.wait_send()
    for store in stores:
        store.wait()
    out_store.wait()


def run_experts(count, norm, gates, code_rows, code_cols, upstream, gate_w, up_w, down_w):
    tokens, width = norm.shape
    room = upstream.shape[1]
    half = room // 2
    hidden = gate_w.shape[1]
    blocks = 4
    low = jnp.bfloat16
    full = jnp.float32
    dma = pltpu.SemaphoreType.DMA
    return pl.pallas_call(
        partial(expert_exchange, count),
        out_shape=(
            jax.ShapeDtypeStruct((tokens, width), full),
            jax.ShapeDtypeStruct((8, tokens), full),
            jax.ShapeDtypeStruct((count, room, width), low),
            jax.ShapeDtypeStruct((count, room, width), low),
            jax.ShapeDtypeStruct((count, room, hidden), low),
            jax.ShapeDtypeStruct((count, room, hidden), low),
            jax.ShapeDtypeStruct((count, room, hidden), low),
            jax.ShapeDtypeStruct((count, room, width), low),
        ),
        in_specs=in_vmem(5) + [pl.BlockSpec(memory_space=pl.ANY)] * 3,
        out_specs=tuple(in_vmem(2) + [pl.BlockSpec(memory_space=pl.ANY)] * 6),
        scratch_shapes=[
            pltpu.VMEM((width, hidden), low),
            pltpu.VMEM((width, hidden), low),
            pltpu.VMEM((width, hidden), low),
            pltpu.VMEM((count, room, width), low),
            pltpu.VMEM((count - 1, half, width), low),
            pltpu.VMEM((count, 8, room), full),
            pltpu.VMEM((count - 1, 8, room), full),
            pltpu.VMEM((count, room, width), low),
            pltpu.VMEM((count, room, hidden), low),
            pltpu.VMEM((count, room, hidden), low),
            pltpu.VMEM((count, room, hidden), low),
            pltpu.VMEM((count, room, width), low),
            pltpu.VMEM((count, room, width), low),
            pltpu.VMEM((count, half, width), low),
            pltpu.VMEM((count, half, width), low),
            pltpu.VMEM((count, half, width), low),
            pltpu.VMEM((count, 8, room), full),
            pltpu.VMEM((count, 8, room), full),
            pltpu.VMEM((blocks, tokens // blocks, width), low),
            pltpu.VMEM((blocks, tokens // blocks, width), low),
            pltpu.VMEM((2, 8, tokens), full),
            dma((3,)),
            dma((6,)),
            dma((count,)),
            dma((count,)),
            dma((count,)),
            dma((count,)),
            dma((count,)),
            dma((count,)),
            dma((count,)),
            dma((count,)),
            dma((count,)),
            dma((count,)),
            dma((count,)),
            dma((count,)),
            dma((blocks + 1,)),
            dma((blocks + 1,)),
        ],
        compiler_params=pltpu.CompilerParams(
            collective_id=3, has_side_effects=True, vmem_limit_bytes=63 * 2**20
        ),
        cost_estimate=estimate(110),
        name="expert_exchange",
    )(norm, gates, code_rows, code_cols, upstream, gate_w, up_w, down_w)


LANES = 128


def places():
    own, ctx, side = lax.axis_index("shard"), lax.axis_index("ctx"), lax.axis_index("tensor")
    return own, ctx, side, ctx // 2, ctx % 2


def nearest(own, count, step):
    flip = own // (count // 2)
    place = flip * (count - 1 - own) + (1 - flip) * own
    turn = step - 1
    turn = turn + (turn - place + count) // count
    other = flip * (count - 1 - turn) + (1 - flip) * turn
    first = 1 - (step + count - 1) // count
    return first * own + (1 - first) * other


def across(chip, core, step):
    return (chip + 1 - step // 2) % 2 * 2 + (core + step + step // 2) % 2


def remote(source, target, send, recv, device):
    return pltpu.make_async_remote_copy(
        source, target, send, recv, device_id=device, device_id_type=MESH
    )


def greet(devices):
    barrier = pltpu.get_barrier_semaphore()
    for device in devices:
        pl.semaphore_signal(barrier, 1, device_id=device, device_id_type=MESH)
    pl.semaphore_wait(barrier, len(devices))


def gather_project(
    count,
    weight,
    tokens,
    segment,
    full,
    packed,
    norm,
    segments,
    outgoing,
    line_send,
    line_recv,
    chip_send,
    chip_recv,
    core_send,
    core_recv,
    packed_send,
    packed_recv,
    segment_send,
    segment_recv,
):
    own, ctx, side, chip, core = places()
    rows = weight.shape[0]
    share = packed.shape[2]
    ctx_size = packed.shape[0]
    chip_peer = (own, (1 - chip) * 2 + core, side)
    core_peer = (own, chip * 2 + 1 - core, side)
    greet(
        [(nearest(own, count, step), ctx, side) for step in range(1, count)]
        + [(own, across(chip, core, step), side) for step in range(3)]
    )

    def block(shard, place):
        return pl.ds(pl.multiple_of((shard * ctx_size + place) * rows, rows), rows)

    def to_line(step):
        device = (nearest(own, count, step), ctx, side)
        return remote(
            weight, full.at[block(own, ctx)], line_send.at[step], line_recv.at[own], device
        )

    def to_chip(shard, source):
        target = full.at[block(shard, ctx)]
        return remote(source, target, chip_send.at[shard], chip_recv.at[shard], chip_peer)

    def to_core(shard, place, source):
        index = shard * 2 + place // 2
        target = full.at[block(shard, place)]
        return remote(source, target, core_send.at[index], core_recv.at[index], core_peer)

    def to_segment(step):
        device = (own, across(chip, core, step), side)
        return remote(segment, segments.at[ctx], segment_send.at[step], segment_recv.at[ctx], device)

    for step in range(1, count):
        to_line(step).start()
    to_chip(own, weight).start()
    to_core(own, ctx, weight).start()
    for step in range(3):
        to_segment(step).start()
    full[block(own, ctx), :] = weight[...]
    segments[ctx] = segment[...]

    other_place = (1 - chip) * 2 + core

    def pass_line(step):
        shard = nearest(own, count, step)
        source = full.at[block(shard, ctx)]
        remote(source, source, line_send.at[0], line_recv.at[shard], core_peer).wait_recv()
        to_chip(shard, source).start()
        to_core(shard, ctx, source).start()

    def pass_chip(step):
        shard = nearest(own, count, step)
        source = full.at[block(shard, other_place)]
        remote(source, source, chip_send.at[0], chip_recv.at[shard], core_peer).wait_recv()
        to_core(shard, other_place, source).start()

    pass_chip(0)
    for step in range(1, count):
        pass_line(step)
        pass_chip(step)

    values = tokens[...].astype(jnp.float32)
    scale = lax.rsqrt(jnp.mean(values * values, axis=1, keepdims=True) + 1e-06)
    for shard in range(count):
        for place in range(2):
            spot = full.at[block(shard, place * 2 + 1 - core)]
            index = shard * 2 + place
            remote(spot, spot, core_send.at[0], core_recv.at[index], core_peer).wait_recv()
    gain = jnp.transpose(full[:, ctx_size * share :].astype(jnp.float32))[0:1, :]
    norm[...] = (values * scale * gain).astype(jnp.bfloat16)

    def project(place):
        spot = pl.ds(pl.multiple_of(place * share, LANES), share)
        return dot32(norm[...], full[:, spot]).astype(jnp.bfloat16)

    def to_packed(step):
        device = (own, across(chip, core, step), side)
        return remote(
            outgoing.at[step], packed.at[ctx], packed_send.at[step], packed_recv.at[ctx], device
        )

    for step in range(3):
        outgoing[step] = project(across(chip, core, step))
        to_packed(step).start()
    packed[ctx] = project(ctx)
    for step in range(3):
        place = across(chip, core, step)
        spot = packed.at[place]
        remote(spot, spot, packed_send.at[step], packed_recv.at[place], core_peer).wait_recv()
        spot = segments.at[place]
        remote(spot, spot, segment_send.at[step], segment_recv.at[place], core_peer).wait_recv()
    for step in range(3):
        to_packed(step).wait_send()
        to_segment(step).wait_send()
    for step in range(count):
        shard = nearest(own, count, step)
        if step:
            to_line(step).wait_send()
        to_chip(shard, weight).wait_send()
        to_core(shard, ctx, weight).wait_send()
        to_core(shard, other_place, weight).wait_send()


def run_gather(count, ctx_size, weight, tokens, segment):
    rows, columns = weight.shape
    here, width = tokens.shape
    share = (columns - LANES) // ctx_size
    dma = pltpu.SemaphoreType.DMA
    return pl.pallas_call(
        partial(gather_project, count),
        out_shape=(
            jax.ShapeDtypeStruct((rows * count * ctx_size, columns), jnp.bfloat16),
            jax.ShapeDtypeStruct((ctx_size, here, share), jnp.bfloat16),
            jax.ShapeDtypeStruct((here, width), jnp.bfloat16),
            jax.ShapeDtypeStruct((ctx_size, 8, here), jnp.float32),
        ),
        in_specs=in_vmem(3),
        out_specs=tuple(in_vmem(4)),
        scratch_shapes=[
            pltpu.VMEM((3, here, share), jnp.bfloat16),
            dma((count,)),
            dma((count,)),
            dma((count,)),
            dma((count,)),
            dma((2 * count,)),
            dma((2 * count,)),
            dma((3,)),
            dma((ctx_size,)),
            dma((3,)),
            dma((ctx_size,)),
        ],
        compiler_params=pltpu.CompilerParams(
            collective_id=1, has_side_effects=True, vmem_limit_bytes=48 * 2**20
        ),
        cost_estimate=estimate(45),
        name="gather_project",
    )(weight, tokens, segment)


def gradient_return(
    count,
    packed_grad,
    full,
    norm,
    tokens,
    bias_line,
    mixture,
    norm_grad,
    weight_grad,
    bias_grad,
    gain_grad,
    mixture_in,
    incoming,
    norm_t,
    outgoing,
    side_out,
    side_in,
    spread,
    core_in,
    chip_out,
    chip_in,
    line_out,
    line_in,
    bias_out,
    bias_in,
    spread_gain,
    grad_send,
    grad_recv,
    side_send,
    side_recv,
    core_send,
    core_recv,
    chip_send,
    chip_recv,
    line_send,
    line_recv,
    bias_send,
    bias_recv,
    mixture_sem,
):
    own, ctx, side, chip, core = places()
    ctx_size, here, share = packed_grad.shape
    width = norm.shape[1]
    halves = 2
    part = here // halves
    groups = ctx_size
    pair = (own, ctx, 1 - side)
    chip_peer = (own, (1 - chip) * 2 + core, side)
    core_peer = (own, chip * 2 + 1 - core, side)
    others = [
        (nearest(own, count, step), across(chip, core, turn), side)
        for step in range(count)
        for turn in range(4)
        if (step, turn) != (0, 3)
    ]
    greet(others + [pair])

    def to_owner(step, piece):
        place = across(chip, core, step)
        spot = pl.ds(piece * part, part)
        return remote(
            packed_grad.at[place, spot],
            incoming.at[ctx, spot],
            grad_send.at[step, piece],
            grad_recv.at[ctx, piece],
            (own, place, side),
        )

    for piece in range(halves):
        for step in range(3):
            to_owner(step, piece).start()
    incoming[ctx] = packed_grad[ctx]
    mixture_copy = remote(mixture, mixture_in, mixture_sem.at[0], mixture_sem.at[1], pair)
    mixture_copy.start()

    span = bias_line.shape[1]
    index = lax.broadcasted_iota(jnp.int32, (span, LANES), 0)
    relative = jnp.where(index < span // 2, -index, span - index)
    bucket = lax.broadcasted_iota(jnp.int32, (span, LANES), 1)
    onehot = jnp.where(bucket_ids(relative) == bucket, 1.0, 0.0)
    sums = jnp.dot(
        bias_line[...], onehot, precision=lax.Precision.HIGHEST, preferred_element_type=jnp.float32
    )
    far = jnp.sum(bias_line[...], axis=1, keepdims=True)
    lane = lax.broadcasted_iota(jnp.int32, (2, LANES), 1)
    total = sums[0:2] + jnp.where(lane == NBUCK // 2 - 1, far[2:4], 0.0)
    total = total + jnp.where(lane == NBUCK - 1, far[4:6], 0.0)
    bias_sum = jnp.concatenate([total, jnp.zeros((6, LANES), jnp.float32)], axis=0)

    def to_bias(number):
        return remote(
            bias_out.at[number],
            bias_in.at[own, ctx],
            bias_send.at[number],
            bias_recv.at[own, ctx],
            others[number],
        )

    norm_t[...] = jnp.transpose(norm[...].astype(jnp.float32)).astype(jnp.bfloat16)

    def to_side(piece):
        return remote(
            side_out.at[piece],
            side_in.at[piece],
            side_send.at[piece],
            side_recv.at[piece],
            pair,
        )

    values = tokens[...].astype(jnp.float32)
    normal = values * lax.rsqrt(jnp.mean(values * values, axis=1, keepdims=True) + 1e-06)
    for piece in range(halves):
        spot = pl.ds(piece * part, part)
        total = jnp.zeros((part, width), jnp.float32)
        for step in (3, 2, 0, 1):
            place = across(chip, core, step)
            if step != 3:
                target = incoming.at[place, spot]
                remote(
                    target, target, grad_send.at[0, 0], grad_recv.at[place, piece], pair
                ).wait_recv()
            columns = pl.ds(pl.multiple_of(place * share, LANES), share)
            total = total + dot_last(incoming[place, spot, :], full[:, columns])
        side_out[piece] = total.astype(jnp.bfloat16)
        to_side(piece).start()

    def to_core(group):
        return remote(
            outgoing.at[group, :, 1 - core],
            core_in.at[group],
            core_send.at[group],
            core_recv.at[group],
            core_peer,
        )

    def to_chip(group):
        return remote(
            chip_out.at[group],
            chip_in.at[group],
            chip_send.at[group],
            chip_recv.at[group],
            chip_peer,
        )

    def to_line(group, step):
        shard = nearest(own, count, step)
        return remote(
            line_out.at[group, shard],
            line_in.at[group, own],
            line_send.at[group, step],
            line_recv.at[group, own],
            (shard, ctx, side),
        )

    rows = norm_t.shape[0] // (count * ctx_size)

    def contract(group):
        found = dot32(norm_t[...], incoming[group])
        found = found.reshape(count * 2, 2, rows, share)
        outgoing[group] = found.astype(jnp.bfloat16)
        to_core(group).start()

    def over_chip(group):
        to_core(group).wait_recv()
        found = outgoing[group, :, core].astype(jnp.float32) + core_in[group].astype(jnp.float32)
        spread[group] = found.reshape(count, 2, rows, share)
        chip_out[group] = spread[group, :, 1 - chip].astype(jnp.bfloat16)
        to_chip(group).start()

    def over_line(group):
        to_chip(group).wait_recv()
        found = spread[group, :, chip] + chip_in[group].astype(jnp.float32)
        line_out[group] = found.astype(jnp.bfloat16)
        for step in range(1, count):
            to_line(group, step).start()

    def collect(group):
        total = line_out[group, own].astype(jnp.float32)
        for step in range(1, count):
            shard = nearest(own, count, step)
            spot = line_in.at[group, shard]
            remote(
                spot, spot, line_send.at[group, 0], line_recv.at[group, shard], pair
            ).wait_recv()
            total = total + spot[...].astype(jnp.float32)
        weight_grad[group] = total

    def finish_sides():
        gain = jnp.zeros((1, width), jnp.float32)
        for piece in range(halves):
            to_side(piece).wait_recv()
            total = side_out[piece].astype(jnp.float32) + side_in[piece].astype(jnp.float32)
            norm_grad[pl.ds(piece * part, part), :] = total
            gain = gain + jnp.sum(
                total * normal[piece * part : (piece + 1) * part], axis=0, keepdims=True
            )
        spread_gain[...] = jnp.broadcast_to(gain, (8, width))

        def message(shard, place):
            lanes = pl.ds(pl.multiple_of((shard * 2 + place // 2) * LANES, LANES), LANES)
            return jnp.concatenate([bias_sum, spread_gain[:, lanes]], axis=0)

        for number, (shard, place, _) in enumerate(others):
            bias_out[number] = message(shard, place)
            to_bias(number).start()
        bias_in[own, ctx] = message(own, ctx)

    for moment in range(groups + 3):
        if moment < groups:
            contract(moment)
        if 0 <= moment - 1 < groups:
            over_chip(moment - 1)
        if 0 <= moment - 2 < groups:
            over_line(moment - 2)
        if moment == groups:
            finish_sides()
        if 0 <= moment - 3 < groups:
            collect(moment - 3)

    for number, (shard, place, _) in enumerate(others):
        spot = bias_in.at[shard, place]
        remote(spot, spot, bias_send.at[0], bias_recv.at[shard, place], pair).wait_recv()
    for place in range(ctx_size):
        total = bias_in[0, place]
        for shard in range(1, count):
            total = total + bias_in[shard, place]
        bias_grad[place] = total[:8]
        gain_total = total[8:] if place == 0 else gain_total + total[8:]
    gain_grad[...] = gain_total

    mixture_copy.wait()
    for number in range(len(others)):
        to_bias(number).wait_send()
    for piece in range(halves):
        to_side(piece).wait_send()
        for step in range(3):
            to_owner(step, piece).wait_send()
    for group in range(groups):
        to_core(group).wait_send()
        to_chip(group).wait_send()
        for step in range(1, count):
            to_line(group, step).wait_send()


def run_return(count, packed_grad, full, norm, tokens, bias_line, mixture):
    ctx_size, here, share = packed_grad.shape
    width = norm.shape[1]
    rows = width // (count * ctx_size)
    low, wide = jnp.bfloat16, jnp.float32
    dma = pltpu.SemaphoreType.DMA
    columns = share
    return pl.pallas_call(
        partial(gradient_return, count),
        out_shape=(
            jax.ShapeDtypeStruct((here, width), wide),
            jax.ShapeDtypeStruct((ctx_size, rows, columns), wide),
            jax.ShapeDtypeStruct((ctx_size, 8, LANES), wide),
            jax.ShapeDtypeStruct((8, LANES), wide),
            jax.ShapeDtypeStruct((here, width), low),
        ),
        in_specs=in_vmem(6),
        out_specs=tuple(in_vmem(5)),
        scratch_shapes=[
            pltpu.VMEM((ctx_size, here, share), low),
            pltpu.VMEM((width, here), low),
            pltpu.VMEM((ctx_size, count * 2, 2, rows, columns), low),
            pltpu.VMEM((2, here // 2, width), low),
            pltpu.VMEM((2, here // 2, width), low),
            pltpu.VMEM((ctx_size, count, 2, rows, columns), wide),
            pltpu.VMEM((ctx_size, count * 2, rows, columns), low),
            pltpu.VMEM((ctx_size, count, rows, columns), low),
            pltpu.VMEM((ctx_size, count, rows, columns), low),
            pltpu.VMEM((ctx_size, count, rows, columns), low),
            pltpu.VMEM((ctx_size, count, rows, columns), low),
            pltpu.VMEM((15, 16, LANES), wide),
            pltpu.VMEM((count, ctx_size, 16, LANES), wide),
            pltpu.VMEM((8, width), wide),
            dma((3, 2)),
            dma((ctx_size, 2)),
            dma((2,)),
            dma((2,)),
            dma((ctx_size,)),
            dma((ctx_size,)),
            dma((ctx_size,)),
            dma((ctx_size,)),
            dma((ctx_size, count)),
            dma((ctx_size, count)),
            dma((15,)),
            dma((count, ctx_size)),
            dma((2,)),
        ],
        compiler_params=pltpu.CompilerParams(
            collective_id=2, has_side_effects=True, vmem_limit_bytes=60 * 2**20
        ),
        cost_estimate=estimate(45),
        name="gradient_return",
    )(packed_grad, full, norm, tokens, bias_line, mixture)


def swap_sides(member):
    return lax.ppermute(member, "tensor", [(0, 1), (1, 0)])


def exchange(member, axis):
    return lax.all_to_all(member, axis, split_axis=0, concat_axis=0, tiled=True)


def shifted(member, axis):
    size = lax.axis_size(axis)
    index = lax.axis_index(axis)

    def block(place):
        return lax.dynamic_index_in_dim(member, place, 0, False)

    parts = [block(index)]
    for shift in range(1, size):
        pairs = [(place, (place + shift) % size) for place in range(size)]
        parts.append(lax.ppermute(block((index + shift) % size), axis, pairs))
    return parts


def joined(parts, axis):
    size = len(parts)
    index = lax.axis_index(axis)
    result = jnp.zeros((size,) + parts[0].shape, parts[0].dtype)
    for shift in range(size):
        place = (index - shift + size) % size
        result = lax.dynamic_update_index_in_dim(result, parts[shift], place, 0)
    return result


def slot_codes(routes, experts, room):
    tokens = routes.shape[0]
    picks = routes[:, :, None] == jnp.arange(experts, dtype=jnp.int32)[None, None, :]
    named = jnp.sum(picks, axis=1).astype(jnp.bfloat16)
    index = jnp.arange(tokens, dtype=jnp.int32)
    before = (index[:, None] > index[None, :]).astype(jnp.bfloat16)
    rank = jnp.dot(before, named, preferred_element_type=jnp.float32)
    slots = rank + room * jnp.arange(experts, dtype=jnp.float32)[None, :]
    return picks, jnp.sum(jnp.where(picks, slots[:, None, :], 0.0), axis=2)


def experts_apart(norm_two, upstream, gates, codes, room, count, weights):
    tokens, width = norm_two.shape
    codes = codes.astype(jnp.int32).reshape(-1)
    shaped = (count, room, width)

    def sent(member):
        slots = jnp.zeros((count * room, width), jnp.bfloat16).at[codes].set(member)
        return exchange(slots.reshape(shaped), "shard").reshape(-1, width)

    slot_rows = sent(jnp.repeat(norm_two, TOP, axis=0))
    slot_grads = sent(
        (gates[:, :, None] * upstream[:, None, :]).reshape(-1, width).astype(jnp.bfloat16)
    )
    gate_mat, up_mat, down_mat = weights
    gate_pre = dot32(slot_rows, gate_mat)
    up_pre = dot32(slot_rows, up_mat)
    activated, slope = gelu_parts(gate_pre)
    inner = (activated * up_pre).astype(jnp.bfloat16)
    expert_out = contract_cols(inner, down_mat)
    inner_grad = dot32(slot_grads, down_mat)
    gate_grad = (inner_grad * up_pre * slope).astype(jnp.bfloat16)
    up_grad = (inner_grad * activated).astype(jnp.bfloat16)
    rows_grad = contract_cols(gate_grad, gate_mat) + contract_cols(up_grad, up_mat)

    def returned(member):
        member = lax.psum(member.astype(jnp.bfloat16), "tensor").reshape(shaped)
        member = exchange(member, "shard").reshape(-1, width)[codes]
        return member.astype(jnp.float32).reshape(tokens, TOP, width)

    per_choice = returned(expert_out)
    mixture = jnp.sum(gates[:, :, None] * per_choice, axis=1)
    dots = gates * jnp.sum(per_choice * upstream[:, None, :], axis=2)
    norm_grad = jnp.sum(returned(rows_grad), axis=1)
    return mixture, dots, norm_grad, slot_rows, slot_grads, inner, gate_grad, up_grad


def local_general(
    tokens_in,
    cotangent,
    segment_ids,
    live_blocks,
    routes,
    w_query,
    w_key,
    w_value,
    w_out,
    rel_bias,
    attn_gain,
    ffn_gain,
    router,
    w_gate,
    w_up,
    w_down,
):
    rows_here, width = tokens_in.shape
    ctx_size = lax.axis_size("ctx")
    side_count = lax.axis_size("tensor")
    ctx_index = lax.axis_index("ctx")
    side = lax.axis_index("tensor")
    head_cols = w_query.shape[1]
    share = head_cols // ctx_size
    experts = router.shape[1]
    room = max(2, 3 * rows_here // experts)

    picks, codes = slot_codes(routes, experts, room)

    def by_owner(member):
        return member.reshape(member.shape[0], ctx_size, share)

    packed_rows = jnp.stack([by_owner(w_query), by_owner(w_key), by_owner(w_value)], axis=2)
    gathered = lax.all_gather(
        jnp.concatenate(
            [
                packed_rows.reshape(w_query.shape[0], -1),
                attn_gain[:, None],
                ffn_gain[:, None],
                router,
            ],
            axis=1,
        ).astype(jnp.bfloat16),
        ("shard", "ctx"),
        axis=0,
        tiled=True,
    )
    packed_w = gathered[:, : 3 * head_cols]
    gain_one = gathered[:, 3 * head_cols]
    gain_two = gathered[:, 3 * head_cols + 1]
    router_w = gathered[:, 3 * head_cols + 2 :]
    out_w = lax.all_gather(w_out.astype(jnp.bfloat16), ("shard", "ctx", "tensor"), axis=0)
    out_w = out_w.reshape(-1, side_count, w_out.shape[0], head_cols)
    out_w = jnp.transpose(out_w, (0, 2, 1, 3)).reshape(width, side_count * head_cols)
    expert_weights = tuple(
        lax.all_gather(member.astype(jnp.bfloat16), "ctx", axis=1, tiled=True)[0]
        for member in (w_gate, w_up, w_down)
    )

    inputs = tokens_in.astype(jnp.float32)
    scale_one = lax.rsqrt(jnp.mean(inputs * inputs, axis=1, keepdims=True) + 1e-06)
    normal_one = inputs * scale_one
    norm_one = (normal_one * gain_one.astype(jnp.float32)).astype(jnp.bfloat16)
    packed = dot32(norm_one, packed_w).astype(jnp.bfloat16)
    packed = jnp.transpose(packed.reshape(rows_here, ctx_size, 3 * share), (1, 0, 2))
    packed = exchange(packed, "ctx").reshape(ctx_size * rows_here, 3 * share)
    segments = lax.all_gather(segment_ids.reshape(-1), "ctx", axis=0, tiled=True)
    alive = live_tiles(segments, live_blocks[0])
    segment_row = segments.astype(jnp.float32)[None]
    pair_heads = share // HEAD
    own_bias = lax.dynamic_slice_in_dim(rel_bias, ctx_index * pair_heads, pair_heads, 1)
    buckets = span_buckets()
    line = jnp.dot(own_bias.T, buckets.T, precision=lax.Precision.HIGHEST)
    attended, attended_t, log_sum = run_forward(alive, packed, segment_row, line)
    attended = attended.reshape(ctx_size, 1, rows_here, share)
    attended = jnp.broadcast_to(attended, (ctx_size, side_count, rows_here, share))
    attended = exchange(attended.reshape(-1, rows_here, share), ("ctx", "tensor"))
    attended = attended.reshape(ctx_size, side_count, rows_here, share)
    attended = jnp.transpose(attended, (2, 1, 0, 3))
    attended_low = lax.dynamic_index_in_dim(attended, side, 1, False).reshape(rows_here, head_cols)
    attended = attended.reshape(rows_here, side_count * head_cols)
    hidden_one = inputs + contract_cols(attended, out_w)
    scale_two = lax.rsqrt(jnp.mean(hidden_one * hidden_one, axis=1, keepdims=True) + 1e-06)
    normal_two = hidden_one * scale_two
    norm_two = (normal_two * gain_two.astype(jnp.float32)).astype(jnp.bfloat16)
    logits = dot32(norm_two, router_w)
    chosen = jnp.sum(jnp.where(picks, logits[:, None, :], 0.0), axis=2)
    gates = jax.nn.softmax(chosen, axis=1)
    upstream = cotangent.astype(jnp.float32)
    results = experts_apart(norm_two, upstream, gates, codes, room, experts, expert_weights)
    mixture, gate_dots, norm_grad, slot_rows, slot_grads, inner, gate_grad, up_grad = results
    weight_grads = lax.psum_scatter(
        jnp.stack(
            [
                contract_rows(slot_rows, gate_grad),
                contract_rows(slot_rows, up_grad),
                contract_rows(slot_grads, inner),
            ],
            axis=1,
        ).astype(jnp.bfloat16),
        "ctx",
        scatter_dimension=0,
        tiled=True,
    ).astype(jnp.float32)
    mixed = (hidden_one + mixture).astype(jnp.bfloat16)
    gate_shift = gate_dots - gates * jnp.sum(gate_dots, axis=1, keepdims=True)
    logit_grad = jnp.sum(jnp.where(picks, gate_shift[:, :, None], 0.0), axis=1)
    router_f = router_w.astype(jnp.float32)
    norm_grad = norm_grad + jnp.dot(logit_grad, router_f.T, precision=lax.Precision.HIGHEST)
    spread_two = norm_grad * gain_two.astype(jnp.float32)
    hidden_grad = upstream + scale_two * (
        spread_two - normal_two * jnp.mean(spread_two * normal_two, axis=1, keepdims=True)
    )
    branch_grad = hidden_grad.astype(jnp.bfloat16)
    own_out_w = lax.dynamic_slice_in_dim(out_w, side * head_cols, head_cols, 1)
    grad_heads = dot32(branch_grad, own_out_w).astype(jnp.bfloat16)
    grad_heads = jnp.transpose(grad_heads.reshape(rows_here, ctx_size, share), (1, 0, 2))
    grad_heads = exchange(grad_heads, "ctx").reshape(-1, share)
    packed_grad, bias_line = run_backward(
        alive, packed, segment_row, line, grad_heads, attended_t, log_sum
    )
    own_grad = jnp.dot(buckets.T, bias_line[:pair_heads].T, precision=lax.Precision.HIGHEST)
    far = jnp.sum(bias_line[pair_heads : 3 * pair_heads], axis=1)
    half = NBUCK // 2
    own_grad = own_grad.at[half - 1].add(far[:pair_heads]).at[NBUCK - 1].add(far[pair_heads:])
    bias_acc = lax.dynamic_update_slice_in_dim(
        jnp.zeros(rel_bias.shape, jnp.float32), own_grad, ctx_index * pair_heads, 1
    )
    packed_grad = exchange(packed_grad.reshape(ctx_size, rows_here, 3 * share), "ctx")
    packed_grad = jnp.transpose(packed_grad, (1, 0, 2)).reshape(rows_here, 3 * head_cols)
    norm_one_grad = contract_cols(packed_grad, packed_w).astype(jnp.bfloat16)
    norm_one_grad = norm_one_grad.astype(jnp.float32) + swap_sides(norm_one_grad).astype(
        jnp.float32
    )
    spread_one = norm_one_grad * gain_one.astype(jnp.float32)
    input_grad = hidden_grad + scale_one * (
        spread_one - normal_one * jnp.mean(spread_one * normal_one, axis=1, keepdims=True)
    )
    first_gain = jnp.sum(norm_one_grad * normal_one, axis=0)[:, None]
    second_gain = jnp.sum(norm_grad * normal_two, axis=0)[:, None]
    router_part = jnp.dot(
        norm_two.astype(jnp.float32).T, logit_grad, precision=lax.Precision.HIGHEST
    )
    reduced = lax.psum_scatter(
        jnp.concatenate(
            [
                contract_rows(norm_one, packed_grad),
                contract_rows(branch_grad, attended_low),
                first_gain,
                second_gain,
                router_part,
            ],
            axis=1,
        ),
        ("shard", "ctx"),
        scatter_dimension=0,
        tiled=True,
    )
    grad_bias = lax.psum(bias_acc, ("shard", "ctx"))
    packed_rows = reduced[:, : 3 * head_cols].reshape(-1, ctx_size, 3, share)
    return (
        mixed,
        input_grad.astype(jnp.bfloat16),
        packed_rows[:, :, 0].reshape(-1, head_cols),
        packed_rows[:, :, 1].reshape(-1, head_cols),
        packed_rows[:, :, 2].reshape(-1, head_cols),
        reduced[:, 3 * head_cols : 4 * head_cols],
        grad_bias,
        reduced[:, 4 * head_cols],
        reduced[:, 4 * head_cols + 1],
        reduced[:, 4 * head_cols + 2 :],
        weight_grads[:, 0][None],
        weight_grads[:, 1][None],
        weight_grads[:, 2][None],
    )


def local_fused(
    tokens_in,
    cotangent,
    segment_ids,
    live_blocks,
    routes,
    w_query,
    w_key,
    w_value,
    w_out,
    rel_bias,
    attn_gain,
    ffn_gain,
    router,
    w_gate,
    w_up,
    w_down,
):
    rows_here, width = tokens_in.shape
    count = lax.axis_size("shard")
    ctx_size = lax.axis_size("ctx")
    side_count = lax.axis_size("tensor")
    ctx_index = lax.axis_index("ctx")
    side = lax.axis_index("tensor")
    head_cols = w_query.shape[1]
    share = head_cols // ctx_size
    experts = router.shape[1]
    room = max(2, 3 * rows_here // experts)

    picks, codes = slot_codes(routes, experts, room)
    code_rows = jnp.pad(jnp.transpose(codes), ((0, 8 - TOP), (0, 0)), constant_values=-1.0)
    slots = jnp.arange(experts * room, dtype=jnp.int32).astype(jnp.float32)[:, None]
    chosen = (code_rows[0:1] == slots) | (code_rows[1:2] == slots)
    up_slots = dot32(chosen.astype(jnp.bfloat16), cotangent).astype(jnp.bfloat16)
    up_parts = shifted(up_slots.reshape(experts, room, width), "shard")

    def by_owner(member):
        return member.reshape(member.shape[0], ctx_size, share)

    packed_rows = jnp.stack([by_owner(w_query), by_owner(w_key), by_owner(w_value)], axis=2)
    rows = w_query.shape[0]
    weight = jnp.concatenate(
        [
            packed_rows.reshape(rows, -1),
            attn_gain[:, None],
            ffn_gain[:, None],
            router,
            jnp.zeros((rows, LANES - 2 - experts), jnp.float32),
        ],
        axis=1,
    ).astype(jnp.bfloat16)
    segment = jnp.broadcast_to(segment_ids.astype(jnp.float32), (8, rows_here))
    full, packed, norm_one, segments = run_gather(count, ctx_size, weight, tokens_in, segment)
    packed = packed.reshape(ctx_size * rows_here, 3 * share)
    gains = full[:, 3 * head_cols :].astype(jnp.float32)
    gain_one = gains[:, 0]
    gain_two = gains[:, 1]
    router_w = full[:, 3 * head_cols + 2 : 3 * head_cols + 2 + experts]
    out_w = lax.all_gather(w_out.astype(jnp.bfloat16), ("shard", "ctx", "tensor"), axis=0)
    out_w = out_w.reshape(-1, side_count, w_out.shape[0], head_cols)
    out_w = jnp.transpose(out_w, (0, 2, 1, 3)).reshape(width, side_count * head_cols)
    expert_weights = tuple(
        lax.all_gather(member.astype(jnp.bfloat16), "ctx", axis=1, tiled=True)[0]
        for member in (w_gate, w_up, w_down)
    )

    inputs = tokens_in.astype(jnp.float32)
    scale_one = lax.rsqrt(jnp.mean(inputs * inputs, axis=1, keepdims=True) + 1e-06)
    normal_one = inputs * scale_one
    segment_row = segments[:, 0].reshape(1, -1)
    alive = live_tiles(segment_row[0], live_blocks[0])
    pair_heads = share // HEAD
    own_bias = lax.dynamic_slice_in_dim(rel_bias, ctx_index * pair_heads, pair_heads, 1)
    line = jnp.dot(own_bias.T, span_buckets().T, precision=lax.Precision.HIGHEST)
    packed, up_parts[1], up_parts[2] = lax.optimization_barrier((packed, up_parts[1], up_parts[2]))
    attended, attended_t, log_sum = run_forward(alive, packed, segment_row, line)
    attended, up_parts[3] = lax.optimization_barrier((attended, up_parts[3]))
    attended = attended.reshape(ctx_size, 1, rows_here, share)
    attended = jnp.broadcast_to(attended, (ctx_size, side_count, rows_here, share))
    attended = exchange(attended.reshape(-1, rows_here, share), ("ctx", "tensor"))
    attended = attended.reshape(ctx_size, side_count, rows_here, share)
    attended = jnp.transpose(attended, (2, 1, 0, 3))
    attended_low = lax.dynamic_index_in_dim(attended, side, 1, False).reshape(rows_here, head_cols)
    attended = attended.reshape(rows_here, side_count * head_cols)
    hidden_one = inputs + contract_cols(attended, out_w)
    scale_two = lax.rsqrt(jnp.mean(hidden_one * hidden_one, axis=1, keepdims=True) + 1e-06)
    normal_two = hidden_one * scale_two
    norm_two = (normal_two * gain_two).astype(jnp.bfloat16)
    logits = dot32(norm_two, router_w)
    chosen = jnp.sum(jnp.where(picks, logits[:, None, :], 0.0), axis=2)
    gates = jax.nn.softmax(chosen, axis=1)
    upstream = cotangent.astype(jnp.float32)
    norm_grad, dots, slot_rows, slot_grads, inner, gate_grad, up_grad, outs = run_experts(
        count, norm_two, gates, code_rows, codes, joined(up_parts, "shard"), *expert_weights
    )
    half = room // 2
    theirs = swap_sides(lax.dynamic_slice_in_dim(outs, (1 - side) * half, half, 1))
    ours = lax.dynamic_slice_in_dim(outs, side * half, half, 1)

    def flat(member):
        return member.reshape(-1, member.shape[2])

    weight_grads = lax.psum_scatter(
        jnp.stack(
            [
                contract_rows(flat(slot_rows), flat(gate_grad)),
                contract_rows(flat(slot_rows), flat(up_grad)),
                contract_rows(flat(slot_grads), flat(inner)),
            ],
            axis=1,
        ).astype(jnp.bfloat16),
        "ctx",
        scatter_dimension=0,
        tiled=True,
    ).astype(jnp.float32)
    gate_dots = jnp.transpose(dots[:TOP])
    gate_shift = gate_dots - gates * jnp.sum(gate_dots, axis=1, keepdims=True)
    logit_grad = jnp.sum(jnp.where(picks, gate_shift[:, :, None], 0.0), axis=1)
    router_f = router_w.astype(jnp.float32)
    norm_grad = norm_grad + jnp.dot(logit_grad, router_f.T, precision=lax.Precision.HIGHEST)
    spread_two = norm_grad * gain_two
    hidden_grad = upstream + scale_two * (
        spread_two - normal_two * jnp.mean(spread_two * normal_two, axis=1, keepdims=True)
    )
    branch_grad = hidden_grad.astype(jnp.bfloat16)
    own_out_w = lax.dynamic_slice_in_dim(out_w, side * head_cols, head_cols, 1)
    grad_heads = dot32(branch_grad, own_out_w).astype(jnp.bfloat16)
    grad_heads = jnp.transpose(grad_heads.reshape(rows_here, ctx_size, share), (1, 0, 2))
    grad_heads = exchange(grad_heads, "ctx").reshape(-1, share)
    second_gain = jnp.sum(norm_grad * normal_two, axis=0)[:, None]
    router_part = jnp.dot(
        norm_two.astype(jnp.float32).T, logit_grad, precision=lax.Precision.HIGHEST
    )
    reduced = lax.psum_scatter(
        jnp.concatenate(
            [contract_rows(branch_grad, attended_low), second_gain, router_part], axis=1
        ),
        ("shard", "ctx"),
        scatter_dimension=0,
        tiled=True,
    )
    grad_heads, theirs = lax.optimization_barrier((grad_heads, theirs))
    ours = (ours.astype(jnp.float32) + theirs.astype(jnp.float32)).astype(jnp.bfloat16)
    ours = joined(shifted(ours, "shard"), "shard").reshape(-1, width)
    slots = jnp.arange(count * half, dtype=jnp.int32)
    slots = (slots // half * room + slots % half + side * half).astype(jnp.float32)
    mixing = sum(
        jnp.where(codes[:, k : k + 1] == slots[None, :], gates[:, k : k + 1], 0.0)
        for k in range(TOP)
    )
    mixture = dot32(mixing.astype(jnp.bfloat16), ours).astype(jnp.bfloat16)
    packed_grad, bias_line = run_backward(
        alive, packed, segment_row, line, grad_heads, attended_t, log_sum
    )
    packed_grad, mixture = lax.optimization_barrier((packed_grad, mixture))
    norm_one_grad, attention_grad, bias_grad, first_gain, peer_mixture = run_return(
        count,
        packed_grad.reshape(ctx_size, rows_here, 3 * share),
        full,
        norm_one,
        tokens_in,
        bias_line,
        mixture,
    )
    mixture = mixture.astype(jnp.float32) + peer_mixture.astype(jnp.float32)
    mixed = (hidden_one + mixture).astype(jnp.bfloat16)
    spread_one = norm_one_grad * gain_one
    input_grad = hidden_grad + scale_one * (
        spread_one - normal_one * jnp.mean(spread_one * normal_one, axis=1, keepdims=True)
    )
    attention_grad = attention_grad.reshape(ctx_size, rows, 3, share)

    def owned(number):
        return jnp.transpose(attention_grad[:, :, number], (1, 0, 2)).reshape(rows, head_cols)

    bias_grad = jnp.transpose(bias_grad[:, :pair_heads, :NBUCK], (2, 0, 1))
    return (
        mixed,
        input_grad.astype(jnp.bfloat16),
        owned(0),
        owned(1),
        owned(2),
        reduced[:, :head_cols],
        bias_grad.reshape(rel_bias.shape),
        lax.dynamic_slice_in_dim(first_gain[0], ctx_index % 2 * rows, rows, 0),
        reduced[:, head_cols],
        reduced[:, head_cols + 1 :],
        weight_grads[:, 0][None],
        weight_grads[:, 1][None],
        weight_grads[:, 2][None],
    )


def solution(mesh):
    placed = (
        P(("shard", "ctx"), None),
        P(("shard", "ctx"), None),
        P("shard", "ctx"),
        P("shard", None, None),
        P(("shard", "ctx"), None),
        P(("shard", "ctx"), "tensor"),
        P(("shard", "ctx"), "tensor"),
        P(("shard", "ctx"), "tensor"),
        P(("shard", "ctx"), "tensor"),
        P(None, "tensor"),
        P(("shard", "ctx")),
        P(("shard", "ctx")),
        P(("shard", "ctx"), None),
        P("shard", "ctx", "tensor"),
        P("shard", "ctx", "tensor"),
        P("shard", "ctx", "tensor"),
    )
    sizes = (mesh.shape["shard"], mesh.shape["ctx"], mesh.shape["tensor"])
    fused = sizes == (4, 4, 2)
    return jax.shard_map(
        local_fused if fused else local_general,
        mesh=mesh,
        in_specs=placed,
        out_specs=(
            P(("shard", "ctx"), None),
            P(("shard", "ctx"), None),
            P(("shard", "ctx"), "tensor"),
            P(("shard", "ctx"), "tensor"),
            P(("shard", "ctx"), "tensor"),
            P(("shard", "ctx"), "tensor"),
            P(None, "tensor"),
            P(("shard", "ctx")),
            P(("shard", "ctx")),
            P(("shard", "ctx"), None),
            P("shard", "ctx", "tensor"),
            P("shard", "ctx", "tensor"),
            P("shard", "ctx", "tensor"),
        ),
        check_vma=False,
    )
```

```python
import math
from functools import partial

import jax
import jax.numpy as jnp
from jax import lax
from jax.experimental import pallas as pl
from jax.experimental.pallas import tpu as pltpu
from jax.sharding import PartitionSpec as P

HEAD = 64
NBUCK = 32
TOP = 2
ATT_BLK = 512


FAR_STEPS = (12, 16, 23, 32, 46, 64, 91)


def bucket_ids(relative):
    distance = jnp.abs(relative)
    far = jnp.full(distance.shape, 8, jnp.int32)
    for bound in FAR_STEPS:
        far = far + (distance >= bound).astype(jnp.int32)
    near = jnp.where(distance < 8, distance, far)
    return near + jnp.where(relative > 0, NBUCK // 2, 0)


def contract_rows(left, right):
    return lax.dot_general(
        left, right, (((0,), (0,)), ((), ())), preferred_element_type=jnp.float32
    )


def contract_cols(left, right):
    return lax.dot_general(
        left, right, (((1,), (1,)), ((), ())), preferred_element_type=jnp.float32
    )


TILE = 256
BIG = 2.0**100
SPAN = 4 * TILE


def place_mask(segment_row):
    rows = lax.broadcasted_iota(jnp.int32, (128, segment_row.shape[1]), 0).astype(jnp.float32)
    apart = jnp.where(rows == segment_row, 0.0, -BIG)
    return jnp.where(rows < 8.0, apart, jnp.where(rows < 11.0, 1.0, 0.0))


def seat_rows(segment_row, extra):
    rows = lax.broadcasted_iota(jnp.int32, (128, segment_row.shape[1]), 0).astype(jnp.float32)
    own = jnp.where((rows == segment_row) & (rows < 8.0), 1.0, 0.0)
    if extra is None:
        return own.astype(jnp.bfloat16)
    high = extra.astype(jnp.bfloat16).astype(jnp.float32)
    rest = extra - high
    middle = rest.astype(jnp.bfloat16).astype(jnp.float32)
    low = rest - middle
    own = jnp.where(rows == 8.0, high, own)
    own = jnp.where(rows == 9.0, middle, own)
    return jnp.where(rows == 10.0, low, own).astype(jnp.bfloat16)


def fill_bias(line_ref, bias_ref):
    for head in range(2):
        line = line_ref[head : head + 1, :]
        turned = pltpu.roll(
            jnp.broadcast_to(line, (TILE, SPAN)), 0, axis=1, stride=1, stride_axis=0
        )
        bias_ref[head, 1] = turned[:, TILE : 2 * TILE]
        bias_ref[head, 2] = turned[:, :TILE]
        bias_ref[head, 3] = turned[:, 3 * TILE :]
        bias_ref[head, 0] = jnp.broadcast_to(line[:, 511:512], (TILE, TILE))
        bias_ref[head, 4] = jnp.broadcast_to(line[:, 513:514], (TILE, TILE))


def tile_at(index):
    return pl.ds(pl.multiple_of(index * TILE, TILE), TILE)


def dot32(left, right):
    return jnp.dot(left, right, preferred_element_type=jnp.float32)


def attention_forward(
    alive, packed, segment, line, out, out_t, log_sum, key_side, query_side, value_t, bias, top, acc
):
    length = packed.shape[0]
    tiles = length // TILE
    fill_bias(line, bias)

    def prepare(index, unused):
        spot = tile_at(index)
        seg = segment[0:1, spot]
        block = packed[spot, :].astype(jnp.float32)
        key_side[spot, :128] = packed[spot, 128:256]
        key_side[spot, 128:] = jnp.transpose(place_mask(seg)).astype(jnp.bfloat16)
        query_t = jnp.transpose(block[:, :128]) * 0.125
        seats = seat_rows(seg, None)
        half = lax.broadcasted_iota(jnp.int32, (128, TILE), 0) // HEAD
        values = jnp.transpose(block[:, 256:]).astype(jnp.bfloat16)
        ones = jnp.where(lax.broadcasted_iota(jnp.int32, (16, TILE), 0) == 0, 1.0, 0.0)
        for head in range(2):
            query_side[head, :128, spot] = jnp.where(half == head, query_t, 0.0).astype(
                jnp.bfloat16
            )
            query_side[head, 128:, spot] = seats
            value_t[head, :HEAD, spot] = values[HEAD * head : HEAD * (head + 1)]
            value_t[head, HEAD:, spot] = ones.astype(jnp.bfloat16)
        return unused

    lax.fori_loop(0, tiles, prepare, 0)

    def query_tile(query_index, unused):
        query_spot = tile_at(query_index)
        top[...] = jnp.full(top.shape, -3e38, jnp.float32)
        acc[...] = jnp.zeros(acc.shape, jnp.float32)

        def key_tile(key_index, carried):
            @pl.when(alive[query_index * tiles + key_index] == 1)
            def _():
                key_spot = tile_at(key_index)
                slot = jnp.clip(key_index - query_index, -2, 2) + 2
                keys = key_side[key_spot, :]
                for head in range(2):
                    scores = dot32(keys, query_side[head, :, query_spot]) + bias[head, slot]
                    before = top[head : head + 1, :]
                    now = jnp.maximum(before, jnp.max(scores, axis=0, keepdims=True))
                    weights = jnp.exp(scores - now).astype(jnp.bfloat16)
                    top[head : head + 1, :] = now
                    acc[head] = acc[head] * jnp.exp(before - now) + dot32(
                        value_t[head, :, key_spot], weights
                    )

            return carried

        lax.fori_loop(0, tiles, key_tile, 0)
        parts = []
        for head in range(2):
            total = acc[head, HEAD : HEAD + 1, :]
            part = acc[head, :HEAD, :] / total
            out_t[HEAD * head : HEAD * (head + 1), query_spot] = part
            log_sum[head : head + 1, query_spot] = top[head : head + 1, :] + jnp.log(total)
            parts.append(part)
        out[query_spot, :] = jnp.transpose(jnp.concatenate(parts, axis=0)).astype(jnp.bfloat16)
        return unused

    lax.fori_loop(0, tiles, query_tile, 0)


def attention_backward(
    alive,
    packed,
    segment,
    line,
    grads,
    out_t,
    log_sum,
    packed_grad,
    bias_grad,
    key_side,
    value_side,
    query_side,
    grad_side,
    key_t,
    query_pair,
    grad_pair,
    bias,
    bias_acc,
    query_acc,
    key_acc,
    value_acc,
):
    length = packed.shape[0]
    tiles = length // TILE
    fill_bias(line, bias)
    bias_acc[...] = jnp.zeros(bias_acc.shape, jnp.float32)

    def prepare(index, unused):
        spot = tile_at(index)
        seg = segment[0:1, spot]
        block = packed[spot, :].astype(jnp.float32)
        grad = grads[spot, :].astype(jnp.float32)
        seats = jnp.transpose(place_mask(seg)).astype(jnp.bfloat16)
        key_side[spot, :128] = packed[spot, 128:256]
        key_side[spot, 128:] = seats
        value_side[spot, :128] = packed[spot, 256:]
        value_side[spot, 128:] = seats
        key_t[:, spot] = jnp.transpose(block[:, 128:256]).astype(jnp.bfloat16)
        query_t = jnp.transpose(block[:, :128]) * 0.125
        grad_t = jnp.transpose(grad)
        half = lax.broadcasted_iota(jnp.int32, (128, TILE), 0) // HEAD
        side = lax.broadcasted_iota(jnp.int32, (TILE, 128), 1) // HEAD
        products = grad_t * out_t[:, spot]
        query_acc[:, spot] = jnp.zeros((128, TILE), jnp.float32)
        for head in range(2):
            query_side[head, :128, spot] = jnp.where(half == head, query_t, 0.0).astype(
                jnp.bfloat16
            )
            query_side[head, 128:, spot] = seat_rows(seg, -log_sum[head : head + 1, spot])
            delta = jnp.sum(products[HEAD * head : HEAD * (head + 1)], axis=0, keepdims=True)
            grad_side[head, :128, spot] = jnp.where(half == head, grad_t, 0.0).astype(jnp.bfloat16)
            grad_side[head, 128:, spot] = seat_rows(jnp.full_like(seg, -1.0), -delta)
            query_pair[index, TILE * head : TILE * (head + 1), :] = jnp.where(
                side == head, block[:, :128] * 0.125, 0.0
            ).astype(jnp.bfloat16)
            grad_pair[index, TILE * head : TILE * (head + 1), :] = jnp.where(
                side == head, grad, 0.0
            ).astype(jnp.bfloat16)
        return unused

    lax.fori_loop(0, tiles, prepare, 0)

    def key_tile(key_index, unused):
        key_spot = tile_at(key_index)
        key_acc[...] = jnp.zeros(key_acc.shape, jnp.float32)
        value_acc[...] = jnp.zeros(value_acc.shape, jnp.float32)

        def query_tile(query_index, carried):
            @pl.when(alive[query_index * tiles + key_index] == 1)
            def _():
                query_spot = tile_at(query_index)
                slot = jnp.clip(key_index - query_index, -2, 2) + 2
                keys = key_side[key_spot, :]
                values = value_side[key_spot, :]
                probs, score_grads = [], []
                for head in range(2):
                    scores = dot32(keys, query_side[head, :, query_spot]) + bias[head, slot]
                    prob = jnp.exp(scores)
                    score_grad = prob * dot32(values, grad_side[head, :, query_spot])
                    bias_acc[head, slot] += score_grad
                    score_grad = score_grad.astype(jnp.bfloat16)
                    probs.append(prob.astype(jnp.bfloat16))
                    score_grads.append(score_grad)
                    rows = slice(HEAD * head, HEAD * (head + 1))
                    query_acc[rows, query_spot] += dot32(key_t[rows, key_spot], score_grad)
                value_acc[...] += dot32(jnp.concatenate(probs, axis=1), grad_pair[query_index])
                key_acc[...] += dot32(jnp.concatenate(score_grads, axis=1), query_pair[query_index])

            return carried

        lax.fori_loop(0, tiles, query_tile, 0)
        packed_grad[key_spot, 128:256] = key_acc[...].astype(jnp.bfloat16)
        packed_grad[key_spot, 256:] = value_acc[...].astype(jnp.bfloat16)
        return unused

    lax.fori_loop(0, tiles, key_tile, 0)

    def finish(index, unused):
        spot = tile_at(index)
        packed_grad[spot, :128] = (jnp.transpose(query_acc[:, spot]) * 0.125).astype(jnp.bfloat16)
        return unused

    lax.fori_loop(0, tiles, finish, 0)
    rows = lax.broadcasted_iota(jnp.int32, (TILE, TILE), 0)
    columns = lax.broadcasted_iota(jnp.int32, (TILE, TILE), 1)
    flip = jnp.where(rows + columns == TILE - 1, 1.0, 0.0)
    bias_grad[...] = jnp.zeros(bias_grad.shape, jnp.float32)
    for head in range(2):
        spread = jnp.concatenate(
            [
                bias_acc[head, 2],
                bias_acc[head, 1],
                jnp.zeros((TILE, TILE), jnp.float32),
                bias_acc[head, 3],
            ],
            axis=1,
        )
        flipped = jnp.dot(
            flip, spread, precision=lax.Precision.HIGHEST, preferred_element_type=jnp.float32
        )
        turned = pltpu.roll(flipped, SPAN - TILE + 1, axis=1, stride=1, stride_axis=0)
        bias_grad[head : head + 1, :] = jnp.sum(turned, axis=0, keepdims=True)
        bias_grad[2 + head : 3 + head, :TILE] = jnp.sum(bias_acc[head, 0], axis=0, keepdims=True)
        bias_grad[4 + head : 5 + head, :TILE] = jnp.sum(bias_acc[head, 4], axis=0, keepdims=True)


def estimate(micros):
    return pl.CostEstimate(flops=int(micros * 1e9), bytes_accessed=0, transcendentals=0)


def in_vmem(count):
    return [pl.BlockSpec(memory_space=pltpu.VMEM)] * count


def run_forward(alive, packed, segment, line):
    length = packed.shape[0]
    return pl.pallas_call(
        attention_forward,
        out_shape=(
            jax.ShapeDtypeStruct((length, 128), jnp.bfloat16),
            jax.ShapeDtypeStruct((128, length), jnp.float32),
            jax.ShapeDtypeStruct((8, length), jnp.float32),
        ),
        in_specs=[pl.BlockSpec(memory_space=pltpu.SMEM)] + in_vmem(3),
        out_specs=tuple(in_vmem(3)),
        scratch_shapes=[
            pltpu.VMEM((length, 256), jnp.bfloat16),
            pltpu.VMEM((2, 256, length), jnp.bfloat16),
            pltpu.VMEM((2, HEAD + 16, length), jnp.bfloat16),
            pltpu.VMEM((2, 5, TILE, TILE), jnp.float32),
            pltpu.VMEM((8, TILE), jnp.float32),
            pltpu.VMEM((2, HEAD + 16, TILE), jnp.float32),
        ],
        compiler_params=pltpu.CompilerParams(vmem_limit_bytes=40 * 2**20),
        cost_estimate=estimate(20),
        name="attention_forward",
    )(alive, packed, segment, line)


def run_backward(alive, packed, segment, line, grads, out_t, log_sum):
    length = packed.shape[0]
    tiles = length // TILE
    return pl.pallas_call(
        attention_backward,
        out_shape=(
            jax.ShapeDtypeStruct((length, 384), jnp.bfloat16),
            jax.ShapeDtypeStruct((8, SPAN), jnp.float32),
        ),
        in_specs=[pl.BlockSpec(memory_space=pltpu.SMEM)] + in_vmem(6),
        out_specs=tuple(in_vmem(2)),
        scratch_shapes=[
            pltpu.VMEM((length, 256), jnp.bfloat16),
            pltpu.VMEM((length, 256), jnp.bfloat16),
            pltpu.VMEM((2, 256, length), jnp.bfloat16),
            pltpu.VMEM((2, 256, length), jnp.bfloat16),
            pltpu.VMEM((128, length), jnp.bfloat16),
            pltpu.VMEM((tiles, 2 * TILE, 128), jnp.bfloat16),
            pltpu.VMEM((tiles, 2 * TILE, 128), jnp.bfloat16),
            pltpu.VMEM((2, 5, TILE, TILE), jnp.float32),
            pltpu.VMEM((2, 5, TILE, TILE), jnp.float32),
            pltpu.VMEM((128, length), jnp.float32),
            pltpu.VMEM((TILE, 128), jnp.float32),
            pltpu.VMEM((TILE, 128), jnp.float32),
        ],
        compiler_params=pltpu.CompilerParams(vmem_limit_bytes=48 * 2**20),
        cost_estimate=estimate(26),
        name="attention_backward",
    )(alive, packed, segment, line, grads, out_t, log_sum)


def signed_span():
    places = jnp.arange(SPAN, dtype=jnp.int32)
    return jnp.where(places < SPAN // 2, -places, SPAN - places)


def span_buckets():
    return (bucket_ids(signed_span())[:, None] == jnp.arange(NBUCK)[None, :]).astype(jnp.float32)


def live_tiles(segments, live):
    tiles = segments.shape[0] // TILE
    grouped = segments.reshape(tiles, TILE)
    first, last = grouped[:, 0], grouped[:, -1]
    meets = (first[:, None] <= last[None, :]) & (first[None, :] <= last[:, None])
    spread = jnp.repeat(jnp.repeat(live, ATT_BLK // TILE, axis=0), ATT_BLK // TILE, axis=1)
    return (meets & (spread == 1)).astype(jnp.int32).reshape(-1)


MESH = pl.DeviceIdType.MESH


def gelu_parts(value):
    root = math.sqrt(2.0 / math.pi)
    square = value * value
    bend = jnp.tanh(root * value * (1.0 + 0.044715 * square))
    half = 0.5 * (1.0 + bend)
    slope = half + 0.5 * value * (1.0 - bend * bend) * (root * (1.0 + 0.134145 * square))
    return value * half, slope


def dot_last(left, right):
    return lax.dot_general(
        left, right, (((1,), (1,)), ((), ())), preferred_element_type=jnp.float32
    )


def expert_exchange(
    count,
    norm,
    gates,
    code_rows,
    code_cols,
    upstream,
    gate_own,
    gate_chip,
    gate_core,
    gate_far,
    up_own,
    up_chip,
    up_core,
    up_far,
    down_own,
    down_chip,
    down_core,
    down_far,
    row_grad,
    dot_rows,
    out_hbm,
    kept_hbm,
    given_hbm,
    gate_w,
    up_w,
    down_w,
    rows,
    sent,
    gates_in,
    gates_out,
    slot_grad,
    inner,
    gate_grad,
    up_grad,
    outs,
    partial,
    peer_part,
    summed,
    back,
    dots_out,
    dots_in,
    final_out,
    final_in,
    final_dots,
    core_in,
    load_sem,
    store_sem,
    rows_send,
    rows_recv,
    pass_send,
    pass_recv,
    gates_send,
    gates_recv,
    part_send,
    part_recv,
    back_send,
    back_recv,
    dots_send,
    dots_recv,
    final_send,
    final_recv,
    core_send,
    core_recv,
):
    own = lax.axis_index("shard")
    ctx = lax.axis_index("ctx")
    side = lax.axis_index("tensor")
    tokens, width = norm.shape
    room = upstream.shape[1]
    half = room // 2
    hidden = gate_w.shape[1]
    peer = (own, ctx, 1 - side)

    def source(step):
        flip = own // (count // 2)
        place = flip * (count - 1 - own) + (1 - flip) * own
        turn = step - 1
        turn = turn + (turn - place + count) // count
        other = flip * (count - 1 - turn) + (1 - flip) * turn
        first = 1 - (step + count - 1) // count
        return first * own + (1 - first) * other

    barrier = pltpu.get_barrier_semaphore()
    for step in range(1, count):
        pl.semaphore_signal(barrier, 1, device_id=(source(step), ctx, side), device_id_type=MESH)
    chip, core = ctx // 2, ctx % 2
    core_peer = (own, chip * 2 + 1 - core, side)
    for device in (peer, core_peer):
        pl.semaphore_signal(barrier, 1, device_id=device, device_id_type=MESH)
    deep = gate_own.shape[0]
    origins = (ctx, (1 - chip) * 2 + core, chip * 2 + 1 - core, (1 - chip) * 2 + 1 - core)
    pieces_of = (
        (gate_w, (gate_own, gate_chip, gate_core, gate_far)),
        (up_w, (up_own, up_chip, up_core, up_far)),
        (down_w, (down_own, down_chip, down_core, down_far)),
    )
    loads = []
    for number, (target, sources) in enumerate(pieces_of):
        for turn, source_ref in enumerate(sources):
            spot = pl.ds(pl.multiple_of(origins[turn] * deep, deep), deep)
            sem = load_sem.at[4 * number + turn]
            loads.append(pltpu.make_async_copy(source_ref, target.at[spot], sem))
    for load in loads:
        load.start()
    pl.semaphore_wait(barrier, count + 1)

    my_half = pl.ds(pl.multiple_of(side * half, half), half)
    peer_half = pl.ds(pl.multiple_of((1 - side) * half, half), half)

    def picked(expert, start, amount):
        slots = lax.broadcasted_iota(jnp.int32, (amount, tokens), 0) + expert * room + start
        slots = slots.astype(jnp.float32)
        hit = (code_rows[0:1, :] == slots) | (code_rows[1:2, :] == slots)
        return jnp.where(hit, 1.0, 0.0).astype(jnp.bfloat16)

    def slot_gates(expert):
        slots = lax.broadcasted_iota(jnp.int32, (tokens, room), 1) + expert * room
        slots = slots.astype(jnp.float32)
        held = jnp.where(code_cols[:, 0:1] == slots, gates[:, 0:1], 0.0)
        held = held + jnp.where(code_cols[:, 1:2] == slots, gates[:, 1:2], 0.0)
        return jnp.broadcast_to(jnp.sum(held, axis=0, keepdims=True), (8, room))

    def rows_copy(step):
        target = source(step)
        return pltpu.make_async_remote_copy(
            sent.at[step - 1],
            rows.at[own, my_half],
            rows_send.at[step - 1],
            rows_recv.at[own],
            device_id=(target, ctx, side),
            device_id_type=MESH,
        )

    def gates_copy(step):
        return pltpu.make_async_remote_copy(
            gates_out.at[step - 1],
            gates_in.at[own],
            gates_send.at[step - 1],
            gates_recv.at[own],
            device_id=(source(step), ctx, side),
            device_id_type=MESH,
        )

    def send_rows(step, unused):
        target = source(step)
        sent[step - 1] = dot32(picked(target, side * half, half), norm[...]).astype(jnp.bfloat16)
        rows_copy(step).start()
        gates_out[step - 1] = slot_gates(target)
        gates_copy(step).start()
        return unused

    lax.fori_loop(1, count, send_rows, 0)
    rows[own] = dot32(picked(own, 0, room), norm[...]).astype(jnp.bfloat16)
    gates_in[own] = slot_gates(own)
    for load in loads:
        load.wait()

    def landed(buffer, send, recv, origin):
        return pltpu.make_async_remote_copy(
            buffer, buffer, send, recv, device_id=peer, device_id_type=MESH
        )

    def pass_copy(origin):
        return pltpu.make_async_remote_copy(
            rows.at[origin, my_half],
            rows.at[origin, my_half],
            pass_send.at[origin],
            pass_recv.at[origin],
            device_id=peer,
            device_id_type=MESH,
        )

    def part_copy(step):
        return pltpu.make_async_remote_copy(
            partial.at[step, peer_half],
            peer_part.at[step],
            part_send.at[step],
            part_recv.at[step],
            device_id=peer,
            device_id_type=MESH,
        )

    def back_copy(step):
        return pltpu.make_async_remote_copy(
            summed.at[step],
            back.at[own],
            back_send.at[step],
            back_recv.at[own],
            device_id=(source(step), ctx, side),
            device_id_type=MESH,
        )

    def dots_copy(step):
        return pltpu.make_async_remote_copy(
            dots_out.at[step],
            dots_in.at[own],
            dots_send.at[step],
            dots_recv.at[own],
            device_id=(source(step), ctx, side),
            device_id_type=MESH,
        )

    def send_back(step):
        part_copy(step).wait_recv()
        summed[step] = (
            partial[step, my_half].astype(jnp.float32) + peer_part[step].astype(jnp.float32)
        ).astype(jnp.bfloat16)
        back_copy(step).start()

    cut = (hidden // 256 + 1) // 2 * 256
    pieces = (slice(0, cut), slice(cut, hidden))

    def run_chunk(step, unused):
        origin = source(step)

        @pl.when(step > 0)
        def _():
            landed(rows.at[origin, peer_half], pass_send.at[origin], pass_recv.at[origin], 0).wait_recv()
            landed(gates_in.at[origin], gates_send.at[0], gates_recv.at[origin], 0).wait_recv()

        gate_column = jnp.transpose(gates_in[origin])[:, 0:1]
        slot_grad[origin] = (upstream[origin].astype(jnp.float32) * gate_column).astype(
            jnp.bfloat16
        )

        def inside(piece):
            block = rows[origin]
            gate_pre = dot32(block, gate_w[:, piece])
            up_pre = dot32(block, up_w[:, piece])
            inner_grad = dot32(slot_grad[origin], down_w[:, piece])
            active, slope = gelu_parts(gate_pre)
            held = (active * up_pre).astype(jnp.bfloat16)
            inner[origin, :, piece] = held
            gate_grad[origin, :, piece] = (inner_grad * up_pre * slope).astype(jnp.bfloat16)
            up_grad[origin, :, piece] = (inner_grad * active).astype(jnp.bfloat16)
            return jnp.sum(active * up_pre * inner_grad, axis=1, keepdims=True)

        dots = inside(pieces[0])

        @pl.when(step < count - 1)
        def _():
            following = source(step + 1)
            landed(
                rows.at[following, my_half], rows_send.at[0], rows_recv.at[following], 0
            ).wait_recv()
            pass_copy(following).start()

        dots = dots + inside(pieces[1])
        dots_out[step] = jnp.transpose(jnp.broadcast_to(dots, (room, 128)))[0:8, :]

        @pl.when(step > 1)
        def _():
            send_back(step - 1)

        partial[step] = (
            dot_last(gate_grad[origin], gate_w[...]) + dot_last(up_grad[origin], up_w[...])
        ).astype(jnp.bfloat16)

        @pl.when(step > 0)
        def _():
            part_copy(step).start()
            dots_copy(step).start()

        return unused

    lax.fori_loop(0, count, run_chunk, 0)
    products = ((gate_w, rows, gate_grad), (up_w, rows, up_grad), (down_w, slot_grad, inner))

    def owner(turn):
        return turn % 2 * 2 + (core + 1 + turn // 2) % 2

    def to_core(number, turn):
        spot = pl.ds(pl.multiple_of(owner(turn) * deep, deep), deep)
        return pltpu.make_async_remote_copy(
            products[number][0].at[spot],
            core_in.at[number, turn],
            core_send.at[number, turn],
            core_recv.at[number, turn],
            device_id=core_peer,
            device_id_type=MESH,
        )

    def weigh(number):
        target, left, right = products[number]

        def block(turn, unused):
            spot = pl.ds(pl.multiple_of(owner(turn) * deep, deep), deep)
            lines = left[:, :, spot].reshape(count * room, deep)
            target[spot, :] = lax.dot_general(
                lines,
                right[...].reshape(count * room, hidden),
                (((0,), (0,)), ((), ())),
                preferred_element_type=jnp.float32,
            ).astype(jnp.bfloat16)

            @pl.when(turn < 2)
            def _():
                to_core(number, turn).start()

            return unused

        lax.fori_loop(0, 4, block, 0)

    def run_out(step, unused):
        outs[step] = dot_last(inner[step], down_w[...]).astype(jnp.bfloat16)
        return unused

    weigh(0)
    send_back(count - 1)
    lax.fori_loop(0, count, run_out, 0)
    out_store = pltpu.make_async_copy(outs, out_hbm, store_sem.at[0])
    out_store.start()
    weigh(1)

    def dots_landed(step, unused):
        origin = source(step)
        landed(dots_in.at[origin], dots_send.at[0], dots_recv.at[origin], 0).wait_recv()
        return unused

    def back_landed(step, unused):
        origin = source(step)
        landed(back.at[origin], back_send.at[0], back_recv.at[origin], 0).wait_recv()
        return unused

    lax.fori_loop(1, count, dots_landed, 0)
    dots_in[own] = dots_out[0]
    final_dots[0] = jnp.zeros((8, tokens), jnp.float32)
    for expert in range(count):
        column = jnp.transpose(dots_in[expert])[:, 0:1]
        slots = lax.broadcasted_iota(jnp.int32, (room, tokens), 0) + expert * room
        slots = slots.astype(jnp.float32)
        for choice in range(2):
            final_dots[0, choice : choice + 1, :] += jnp.sum(
                jnp.where(code_rows[choice : choice + 1, :] == slots, column, 0.0),
                axis=0,
                keepdims=True,
            )
    lax.fori_loop(1, count, back_landed, 0)
    blocks = final_out.shape[0]
    span = tokens // blocks

    def final_copy(block):
        return pltpu.make_async_remote_copy(
            final_out.at[block],
            final_in.at[block],
            final_send.at[block],
            final_recv.at[block],
            device_id=peer,
            device_id_type=MESH,
        )

    dots_final = pltpu.make_async_remote_copy(
        final_dots.at[0],
        final_dots.at[1],
        final_send.at[blocks],
        final_recv.at[blocks],
        device_id=peer,
        device_id_type=MESH,
    )
    dots_final.start()

    def combine(block, unused):
        spot = pl.ds(pl.multiple_of(block * span, span), span)

        def chosen(start, amount):
            slots = lax.broadcasted_iota(jnp.int32, (span, amount), 1) + start
            slots = slots.astype(jnp.float32)
            hit = (code_cols[spot, 0:1] == slots) | (code_cols[spot, 1:2] == slots)
            return jnp.where(hit, 1.0, 0.0).astype(jnp.bfloat16)

        total = dot32(chosen(own * room, room), partial[0])
        for step in range(1, count):
            origin = source(step)
            total = total + dot32(chosen(origin * room + side * half, half), back[origin])
        final_out[block] = total.astype(jnp.bfloat16)
        final_copy(block).start()
        return unused

    lax.fori_loop(0, blocks, combine, 0)

    weigh(2)

    def finish(block, unused):
        spot = pl.ds(pl.multiple_of(block * span, span), span)
        final_copy(block).wait_recv()
        row_grad[spot, :] = final_out[block].astype(jnp.float32) + final_in[block].astype(
            jnp.float32
        )
        return unused

    lax.fori_loop(0, blocks, finish, 0)
    dots_final.wait_recv()
    dot_rows[...] = final_dots[0] + final_dots[1]
    stores = []
    for number in range(3):
        for turn in range(2):
            spot = pl.ds(pl.multiple_of(owner(turn + 2) * deep, deep), deep)
            to_core(number, turn).wait_recv()
            core_in[number, turn] = (
                products[number][0][spot, :].astype(jnp.float32)
                + core_in[number, turn].astype(jnp.float32)
            ).astype(jnp.bfloat16)
        for place, target in enumerate((kept_hbm, given_hbm)):
            source_ref = core_in.at[number, chip * (1 - place) + (1 - chip) * place]
            sem = store_sem.at[1 + 2 * number + place]
            store = pltpu.make_async_copy(source_ref, target.at[number], sem)
            store.start()
            stores.append(store)

    def drain(step, unused):
        rows_copy(step).wait_send()
        gates_copy(step).wait_send()
        pass_copy(source(step)).wait_send()
        part_copy(step).wait_send()
        back_copy(step).wait_send()
        dots_copy(step).wait_send()
        return unused

    lax.fori_loop(1, count, drain, 0)

    def drain_final(block, unused):
        final_copy(block).wait_send()
        return unused

    lax.fori_loop(0, blocks, drain_final, 0)
    dots_final.wait_send()
    for number in range(3):
        for turn in range(2):
            to_core(number, turn).wait_send()
    for store in stores:
        store.wait()
    out_store.wait()


def run_experts(count, ctx_size, norm, gates, code_rows, code_cols, upstream, weights):
    tokens, width = norm.shape
    room = upstream.shape[1]
    half = room // 2
    hidden = weights[0].shape[1]
    blocks = 4
    low = jnp.bfloat16
    full = jnp.float32
    dma = pltpu.SemaphoreType.DMA
    return pl.pallas_call(
        partial(expert_exchange, count),
        out_shape=(
            jax.ShapeDtypeStruct((tokens, width), full),
            jax.ShapeDtypeStruct((8, tokens), full),
            jax.ShapeDtypeStruct((count, room, width), low),
            jax.ShapeDtypeStruct((3, width // ctx_size, hidden), low),
            jax.ShapeDtypeStruct((3, width // ctx_size, hidden), low),
        ),
        in_specs=in_vmem(5) + [pl.BlockSpec(memory_space=pl.ANY)] * 12,
        out_specs=tuple(in_vmem(2) + [pl.BlockSpec(memory_space=pl.ANY)] * 3),
        scratch_shapes=[
            pltpu.VMEM((width, hidden), low),
            pltpu.VMEM((width, hidden), low),
            pltpu.VMEM((width, hidden), low),
            pltpu.VMEM((count, room, width), low),
            pltpu.VMEM((count - 1, half, width), low),
            pltpu.VMEM((count, 8, room), full),
            pltpu.VMEM((count - 1, 8, room), full),
            pltpu.VMEM((count, room, width), low),
            pltpu.VMEM((count, room, hidden), low),
            pltpu.VMEM((count, room, hidden), low),
            pltpu.VMEM((count, room, hidden), low),
            pltpu.VMEM((count, room, width), low),
            pltpu.VMEM((count, room, width), low),
            pltpu.VMEM((count, half, width), low),
            pltpu.VMEM((count, half, width), low),
            pltpu.VMEM((count, half, width), low),
            pltpu.VMEM((count, 8, room), full),
            pltpu.VMEM((count, 8, room), full),
            pltpu.VMEM((blocks, tokens // blocks, width), low),
            pltpu.VMEM((blocks, tokens // blocks, width), low),
            pltpu.VMEM((2, 8, tokens), full),
            pltpu.VMEM((3, 2, width // ctx_size, hidden), low),
            dma((12,)),
            dma((7,)),
            dma((count,)),
            dma((count,)),
            dma((count,)),
            dma((count,)),
            dma((count,)),
            dma((count,)),
            dma((count,)),
            dma((count,)),
            dma((count,)),
            dma((count,)),
            dma((count,)),
            dma((count,)),
            dma((blocks + 1,)),
            dma((blocks + 1,)),
            dma((3, 2)),
            dma((3, 2)),
        ],
        cost_estimate=estimate(110),
        compiler_params=pltpu.CompilerParams(
            collective_id=3, has_side_effects=True, vmem_limit_bytes=63 * 2**20
        ),
        name="expert_exchange",
    )(norm, gates, code_rows, code_cols, upstream, *weights)


LANES = 128


def places():
    own, ctx, side = lax.axis_index("shard"), lax.axis_index("ctx"), lax.axis_index("tensor")
    return own, ctx, side, ctx // 2, ctx % 2


def nearest(own, count, step):
    flip = own // (count // 2)
    place = flip * (count - 1 - own) + (1 - flip) * own
    turn = step - 1
    turn = turn + (turn - place + count) // count
    other = flip * (count - 1 - turn) + (1 - flip) * turn
    first = 1 - (step + count - 1) // count
    return first * own + (1 - first) * other


def across(chip, core, step):
    return (chip + 1 - step // 2) % 2 * 2 + (core + step + step // 2) % 2


def remote(source, target, send, recv, device):
    return pltpu.make_async_remote_copy(
        source, target, send, recv, device_id=device, device_id_type=MESH
    )


def greet(devices):
    barrier = pltpu.get_barrier_semaphore()
    for device in devices:
        pl.semaphore_signal(barrier, 1, device_id=device, device_id_type=MESH)
    pl.semaphore_wait(barrier, len(devices))


def gather_project(
    count,
    weight,
    out_weight,
    tokens,
    segment,
    cotangent,
    code_rows,
    gate_hbm,
    up_hbm,
    down_hbm,
    full,
    packed,
    norm,
    segments,
    out_full,
    upstream,
    gate_low,
    up_low,
    down_low,
    gate_core,
    up_core,
    down_core,
    gate_chip,
    gate_far,
    outgoing,
    sent,
    experts_wide,
    line_send,
    line_recv,
    chip_send,
    chip_recv,
    core_send,
    core_recv,
    packed_send,
    packed_recv,
    segment_send,
    segment_recv,
    out_line_send,
    out_line_recv,
    out_chip_send,
    out_chip_recv,
    out_core_send,
    out_core_recv,
    out_pair_send,
    out_pair_recv,
    rows_send,
    rows_recv,
    pass_send,
    pass_recv,
    expert_send,
    expert_recv,
    load_sem,
):
    own, ctx, side, chip, core = places()
    rows = weight.shape[0]
    ctx_size, here, share = packed.shape
    room = upstream.shape[1]
    half = room // 2
    chip_peer = (own, (1 - chip) * 2 + core, side)
    core_peer = (own, chip * 2 + 1 - core, side)
    pair = (own, ctx, 1 - side)
    loads = [
        pltpu.make_async_copy(source, experts_wide.at[number], load_sem.at[number])
        for number, source in enumerate((gate_hbm, up_hbm, down_hbm))
    ]
    for load in loads:
        load.start()
    greet(
        [(nearest(own, count, step), ctx, side) for step in range(1, count)]
        + [(own, across(chip, core, step), side) for step in range(3)]
        + [pair]
    )

    def block(shard, place):
        return pl.ds(pl.multiple_of((shard * ctx_size + place) * rows, rows), rows)

    def along(origin, forward):
        turn = 2 * forward - 1
        target = own + turn
        there = (target + count) // count * (1 - target // count)
        return (target + count) % count, there

    def onward(origin):
        return 1 - (origin - own + count) // count

    def to_line(origin, forward, source, number):
        target, _ = along(origin, forward)
        spot = full.at[block(origin, ctx)]
        return remote(
            source, spot, line_send.at[number], line_recv.at[origin], (target, ctx, side)
        )

    def in_line(copy_of, origin, forward, source, number, act):
        _, there = along(origin, forward)

        @pl.when(there == 1)
        def _():
            act(copy_of(origin, forward, source, number))

    def to_chip(shard, source):
        target = full.at[block(shard, ctx)]
        return remote(source, target, chip_send.at[shard], chip_recv.at[shard], chip_peer)

    def to_core(shard, place, source):
        index = shard * 2 + place // 2
        target = full.at[block(shard, place)]
        return remote(source, target, core_send.at[index], core_recv.at[index], core_peer)

    def to_segment(step):
        device = (own, across(chip, core, step), side)
        return remote(segment, segments.at[ctx], segment_send.at[step], segment_recv.at[ctx], device)

    def out_to_line(origin, forward, source, number):
        target, _ = along(origin, forward)
        spot = out_full.at[side, block(origin, ctx)]
        return remote(
            source, spot, out_line_send.at[number], out_line_recv.at[origin], (target, ctx, side)
        )

    def start(copy):
        copy.start()

    def sent_off(copy):
        copy.wait_send()

    def out_to_chip(shard, source):
        target = out_full.at[side, block(shard, ctx)]
        return remote(source, target, out_chip_send.at[shard], out_chip_recv.at[shard], chip_peer)

    def out_to_core(which, shard, place, source):
        index = shard * 2 + place // 2
        target = out_full.at[which, block(shard, place)]
        return remote(
            source, target, out_core_send.at[which, index], out_core_recv.at[which, index], core_peer
        )

    def out_to_pair(shard, place, source):
        index = shard * 2 + place // 2
        target = out_full.at[side, block(shard, place)]
        return remote(source, target, out_pair_send.at[index], out_pair_recv.at[index], pair)

    for forward in range(2):
        in_line(to_line, own, forward, weight, forward, start)
    to_chip(own, weight).start()
    to_core(own, ctx, weight).start()
    for step in range(3):
        to_segment(step).start()
    for forward in range(2):
        in_line(out_to_line, own, forward, out_weight, forward, start)
    out_to_core(side, own, ctx, out_weight).start()
    out_to_pair(own, ctx, out_weight).start()
    full[block(own, ctx), :] = weight[...]
    out_full[side, block(own, ctx), :] = out_weight[...]
    segments[ctx] = segment[...]

    my_half = pl.ds(pl.multiple_of(side * half, half), half)
    peer_half = pl.ds(pl.multiple_of((1 - side) * half, half), half)

    def picked(expert, start, amount):
        slots = lax.broadcasted_iota(jnp.int32, (amount, here), 0) + expert * room + start
        slots = slots.astype(jnp.float32)
        hit = (code_rows[0:1, :] == slots) | (code_rows[1:2, :] == slots)
        rows_found = jnp.where(hit, 1.0, 0.0).astype(jnp.bfloat16)
        return dot32(rows_found, cotangent[...]).astype(jnp.bfloat16)

    def to_expert(step):
        return remote(
            sent.at[step - 1],
            upstream.at[own, my_half],
            rows_send.at[step - 1],
            rows_recv.at[own],
            (nearest(own, count, step), ctx, side),
        )

    def pass_rows(shard):
        spot = upstream.at[shard, my_half]
        return remote(spot, spot, pass_send.at[shard], pass_recv.at[shard], pair)

    lows = (gate_low, up_low, down_low)
    near = (gate_core, up_core, down_core)
    for number, load in enumerate(loads):
        load.wait()
        lows[number][...] = experts_wide[number].astype(jnp.bfloat16)
    for step in range(1, count):
        sent[step - 1] = picked(nearest(own, count, step), side * half, half)
    upstream[own] = picked(own, 0, room)

    def to_near(number):
        return remote(
            lows[number], near[number], expert_send.at[number], expert_recv.at[number], core_peer
        )

    gate_over = remote(gate_low, gate_chip, expert_send.at[3], expert_recv.at[3], chip_peer)
    gate_far_copy = remote(gate_chip, gate_far, expert_send.at[4], expert_recv.at[4], core_peer)

    other_place = (1 - chip) * 2 + core

    def pass_line(step):
        shard = nearest(own, count, step)
        source = full.at[block(shard, ctx)]
        remote(source, source, line_send.at[0], line_recv.at[shard], core_peer).wait_recv()
        in_line(to_line, shard, onward(shard), source, 1 + step, start)
        to_chip(shard, source).start()
        to_core(shard, ctx, source).start()

    def pass_chip(step):
        shard = nearest(own, count, step)
        source = full.at[block(shard, other_place)]
        remote(source, source, chip_send.at[0], chip_recv.at[shard], core_peer).wait_recv()
        to_core(shard, other_place, source).start()

    pass_chip(0)
    for step in range(1, count):
        pass_line(step)
        pass_chip(step)
    out_to_chip(own, out_weight).start()
    for step in range(1, count):
        shard = nearest(own, count, step)
        source = out_full.at[side, block(shard, ctx)]
        remote(source, source, line_send.at[0], out_line_recv.at[shard], core_peer).wait_recv()
        in_line(out_to_line, shard, onward(shard), source, 1 + step, start)
        out_to_chip(shard, source).start()
        out_to_core(side, shard, ctx, source).start()
        out_to_pair(shard, ctx, source).start()

    for step in range(1, count):
        to_expert(step).start()
    gate_over.start()
    values = tokens[...].astype(jnp.float32)
    scale = lax.rsqrt(jnp.mean(values * values, axis=1, keepdims=True) + 1e-06)
    for shard in range(count):
        for place in range(2):
            spot = full.at[block(shard, place * 2 + 1 - core)]
            index = shard * 2 + place
            remote(spot, spot, core_send.at[0], core_recv.at[index], core_peer).wait_recv()
    gain = jnp.transpose(full[:, ctx_size * share :].astype(jnp.float32))[0:1, :]
    norm[...] = (values * scale * gain).astype(jnp.bfloat16)

    def project(place):
        spot = pl.ds(pl.multiple_of(place * share, LANES), share)
        return dot32(norm[...], full[:, spot]).astype(jnp.bfloat16)

    def to_packed(step):
        device = (own, across(chip, core, step), side)
        return remote(
            outgoing.at[step], packed.at[ctx], packed_send.at[step], packed_recv.at[ctx], device
        )

    for step in range(3):
        outgoing[step] = project(across(chip, core, step))
        to_packed(step).start()
    packed[ctx] = project(ctx)
    for number in range(3):
        to_near(number).start()
    for step in range(count):
        shard = nearest(own, count, step)
        source = out_full.at[side, block(shard, other_place)]
        remote(source, source, line_send.at[0], out_chip_recv.at[shard], core_peer).wait_recv()
        out_to_core(side, shard, other_place, source).start()
        out_to_pair(shard, other_place, source).start()
    for step in range(1, count):
        shard = nearest(own, count, step)
        spot = upstream.at[shard, my_half]
        remote(spot, spot, rows_send.at[0], rows_recv.at[shard], pair).wait_recv()
        pass_rows(shard).start()
    gate_over.wait_recv()
    gate_far_copy.start()
    for step in range(count):
        shard = nearest(own, count, step)
        for place in (core, 2 + core):
            index = shard * 2 + place // 2
            source = out_full.at[1 - side, block(shard, place)]
            remote(source, source, line_send.at[0], out_pair_recv.at[index], pair).wait_recv()
            out_to_core(1 - side, shard, place, source).start()
    for step in range(3):
        place = across(chip, core, step)
        spot = packed.at[place]
        remote(spot, spot, packed_send.at[step], packed_recv.at[place], core_peer).wait_recv()
        spot = segments.at[place]
        remote(spot, spot, segment_send.at[step], segment_recv.at[place], core_peer).wait_recv()
    for which in (side, 1 - side):
        for shard in range(count):
            for place in range(2):
                spot = out_full.at[which, block(shard, place * 2 + 1 - core)]
                index = shard * 2 + place
                remote(
                    spot, spot, line_send.at[0], out_core_recv.at[which, index], core_peer
                ).wait_recv()
    for step in range(1, count):
        shard = nearest(own, count, step)
        spot = upstream.at[shard, peer_half]
        remote(spot, spot, pass_send.at[0], pass_recv.at[shard], pair).wait_recv()

    for step in range(3):
        to_packed(step).wait_send()
        to_segment(step).wait_send()
        to_near(step).wait()
    gate_over.wait_send()
    gate_far_copy.wait()
    for forward in range(2):
        in_line(to_line, own, forward, weight, forward, sent_off)
        in_line(out_to_line, own, forward, out_weight, forward, sent_off)
    for step in range(count):
        shard = nearest(own, count, step)
        if step:
            in_line(to_line, shard, onward(shard), weight, 1 + step, sent_off)
            in_line(out_to_line, shard, onward(shard), out_weight, 1 + step, sent_off)
            to_expert(step).wait_send()
            pass_rows(shard).wait_send()
        to_chip(shard, weight).wait_send()
        out_to_chip(shard, out_weight).wait_send()
        for place in (ctx, other_place):
            to_core(shard, place, weight).wait_send()
            out_to_pair(shard, place, out_weight).wait_send()
            out_to_core(side, shard, place, out_weight).wait_send()
            out_to_core(1 - side, shard, place, out_weight).wait_send()


def run_gather(count, ctx_size, room, weight, out_weight, tokens, segment, cotangent, code_rows, experts):
    rows, columns = weight.shape
    here, width = tokens.shape
    share = (columns - LANES) // ctx_size
    dma = pltpu.SemaphoreType.DMA
    low = jnp.bfloat16
    deep, hidden = experts[0].shape
    return pl.pallas_call(
        partial(gather_project, count),
        out_shape=(
            jax.ShapeDtypeStruct((rows * count * ctx_size, columns), low),
            jax.ShapeDtypeStruct((ctx_size, here, share), low),
            jax.ShapeDtypeStruct((here, width), low),
            jax.ShapeDtypeStruct((ctx_size, 8, here), jnp.float32),
            jax.ShapeDtypeStruct((2, rows * count * ctx_size, out_weight.shape[1]), low),
            jax.ShapeDtypeStruct((count, room, width), low),
            *[jax.ShapeDtypeStruct((deep, hidden), low)] * 8,
        ),
        in_specs=in_vmem(6) + [pl.BlockSpec(memory_space=pl.ANY)] * 3,
        out_specs=tuple(in_vmem(14)),
        scratch_shapes=[
            pltpu.VMEM((3, here, share), low),
            pltpu.VMEM((count - 1, room // 2, width), low),
            pltpu.VMEM((3, deep, hidden), jnp.float32),
            dma((count + 1,)),
            dma((count,)),
            dma((count,)),
            dma((count,)),
            dma((2 * count,)),
            dma((2 * count,)),
            dma((3,)),
            dma((ctx_size,)),
            dma((3,)),
            dma((ctx_size,)),
            dma((count + 1,)),
            dma((count,)),
            dma((count,)),
            dma((count,)),
            dma((2, 2 * count)),
            dma((2, 2 * count)),
            dma((2 * count,)),
            dma((2 * count,)),
            dma((count,)),
            dma((count,)),
            dma((count,)),
            dma((count,)),
            dma((5,)),
            dma((5,)),
            dma((3,)),
        ],
        compiler_params=pltpu.CompilerParams(
            collective_id=1, has_side_effects=True, vmem_limit_bytes=60 * 2**20
        ),
        cost_estimate=estimate(60),
        name="gather_project",
    )(weight, out_weight, tokens, segment, cotangent, code_rows, *experts)


def gradient_return(
    count,
    packed_grad,
    full,
    norm,
    tokens,
    bias_line,
    ours,
    theirs,
    gates,
    codes,
    branch_grad,
    attended,
    small,
    norm_grad,
    weight_grad,
    bias_grad,
    gain_grad,
    mixture,
    mixture_in,
    out_grad,
    incoming,
    norm_t,
    outgoing,
    side_out,
    side_in,
    spread,
    core_in,
    chip_out,
    chip_in,
    line_out,
    line_in,
    out_going,
    out_core_in,
    out_spread,
    out_chip_out,
    out_chip_in,
    out_line_out,
    out_line_in,
    bias_out,
    bias_in,
    spread_gain,
    mix_out,
    mix_in,
    grad_send,
    grad_recv,
    side_send,
    side_recv,
    core_send,
    core_recv,
    chip_send,
    chip_recv,
    line_send,
    line_recv,
    bias_send,
    bias_recv,
    mixture_sem,
    mix_send,
    mix_recv,
):
    own, ctx, side, chip, core = places()
    ctx_size, here, share = packed_grad.shape
    width = norm.shape[1]
    halves = 2
    part = here // halves
    groups = ctx_size
    pair = (own, ctx, 1 - side)
    chip_peer = (own, (1 - chip) * 2 + core, side)
    core_peer = (own, chip * 2 + 1 - core, side)
    others = [
        (nearest(own, count, step), across(chip, core, turn), side)
        for step in range(count)
        for turn in range(4)
        if (step, turn) != (0, 3)
    ]
    greet(others + [pair])

    def to_owner(step, piece):
        place = across(chip, core, step)
        spot = pl.ds(piece * part, part)
        return remote(
            packed_grad.at[place, spot],
            incoming.at[ctx, spot],
            grad_send.at[step, piece],
            grad_recv.at[ctx, piece],
            (own, place, side),
        )

    for piece in range(halves):
        for step in range(3):
            to_owner(step, piece).start()
    incoming[ctx] = packed_grad[ctx]

    def to_tokens(step):
        return remote(
            mix_out.at[step],
            mix_in.at[own],
            mix_send.at[step],
            mix_recv.at[own],
            (nearest(own, count, step), ctx, side),
        )

    for step in range(count):
        origin = nearest(own, count, step)
        found = ours[origin].astype(jnp.float32) + theirs[origin].astype(jnp.float32)
        if step:
            mix_out[step] = found.astype(jnp.bfloat16)
            to_tokens(step).start()
        else:
            mix_in[own] = found.astype(jnp.bfloat16)
    mixture_copy = remote(mixture, mixture_in, mixture_sem.at[0], mixture_sem.at[1], pair)

    def mix():
        half = mix_in.shape[1]
        total = jnp.zeros((here, width), jnp.float32)
        for step in range(count):
            origin = nearest(own, count, step)
            spot = mix_in.at[origin]
            if step:
                remote(spot, spot, mix_send.at[0], mix_recv.at[origin], pair).wait_recv()
            slots = lax.broadcasted_iota(jnp.int32, (here, half), 1)
            slots = (slots + (2 * origin + side) * half).astype(jnp.float32)
            mixing = jnp.where(codes[:, 0:1] == slots, gates[:, 0:1], 0.0)
            mixing = mixing + jnp.where(codes[:, 1:2] == slots, gates[:, 1:2], 0.0)
            total = total + dot32(mixing.astype(jnp.bfloat16), spot[...])
        mixture[...] = total.astype(jnp.bfloat16)
        mixture_copy.start()


    span = bias_line.shape[1]
    index = lax.broadcasted_iota(jnp.int32, (span, LANES), 0)
    relative = jnp.where(index < span // 2, -index, span - index)
    bucket = lax.broadcasted_iota(jnp.int32, (span, LANES), 1)
    onehot = jnp.where(bucket_ids(relative) == bucket, 1.0, 0.0)
    sums = jnp.dot(
        bias_line[...], onehot, precision=lax.Precision.HIGHEST, preferred_element_type=jnp.float32
    )
    far = jnp.sum(bias_line[...], axis=1, keepdims=True)
    lane = lax.broadcasted_iota(jnp.int32, (2, LANES), 1)
    total = sums[0:2] + jnp.where(lane == NBUCK // 2 - 1, far[2:4], 0.0)
    total = total + jnp.where(lane == NBUCK - 1, far[4:6], 0.0)
    bias_sum = jnp.concatenate([total, jnp.zeros((6, LANES), jnp.float32)], axis=0)

    def to_bias(number):
        return remote(
            bias_out.at[number],
            bias_in.at[own, ctx],
            bias_send.at[number],
            bias_recv.at[own, ctx],
            others[number],
        )

    stages = [
        (
            outgoing.at[group],
            core_in.at[group],
            spread.at[group],
            chip_out.at[group],
            chip_in.at[group],
            line_out.at[group],
            line_in.at[group],
            weight_grad.at[group],
        )
        for group in range(groups)
    ]
    stages.append(
        (
            out_going,
            out_core_in,
            out_spread,
            out_chip_out,
            out_chip_in,
            out_line_out,
            out_line_in,
            out_grad,
        )
    )
    rows = norm_t.shape[0] // (count * ctx_size)

    def to_core(group):
        source, target = stages[group][0].at[:, 1 - core], stages[group][1]
        return remote(source, target, core_send.at[group], core_recv.at[group], core_peer)

    def to_chip(group):
        source, target = stages[group][3], stages[group][4]
        return remote(source, target, chip_send.at[group], chip_recv.at[group], chip_peer)

    def to_line(group, step):
        shard = nearest(own, count, step)
        source, target = stages[group][5].at[shard], stages[group][6].at[own]
        send, recv = line_send.at[group, step], line_recv.at[group, own]
        return remote(source, target, send, recv, (shard, ctx, side))

    def contract(group):
        found = dot32(norm_t[...], incoming[group] if group < groups else attended[...])
        found = found.reshape(count * 2, 2, rows, found.shape[1])
        stages[group][0][...] = found.astype(jnp.bfloat16)
        to_core(group).start()

    def over_chip(group):
        to_core(group).wait_recv()
        source, arrived, summed, target = stages[group][:4]
        found = source[:, core].astype(jnp.float32) + arrived[...].astype(jnp.float32)
        summed[...] = found.reshape(count, 2, rows, found.shape[2])
        target[...] = summed[:, 1 - chip].astype(jnp.bfloat16)
        to_chip(group).start()

    def over_line(group):
        to_chip(group).wait_recv()
        found = stages[group][2][:, chip] + stages[group][4][...].astype(jnp.float32)
        stages[group][5][...] = found.astype(jnp.bfloat16)
        for step in range(1, count):
            to_line(group, step).start()

    def collect(group):
        total = stages[group][5][own].astype(jnp.float32)
        for step in range(1, count):
            shard = nearest(own, count, step)
            spot = stages[group][6].at[shard]
            remote(
                spot, spot, line_send.at[group, 0], line_recv.at[group, shard], pair
            ).wait_recv()
            total = total + spot[...].astype(jnp.float32)
        stages[group][7][...] = total

    norm_t[...] = jnp.transpose(branch_grad[...].astype(jnp.float32)).astype(jnp.bfloat16)
    contract(groups)
    norm_t[...] = jnp.transpose(norm[...].astype(jnp.float32)).astype(jnp.bfloat16)

    def to_side(piece):
        return remote(
            side_out.at[piece],
            side_in.at[piece],
            side_send.at[piece],
            side_recv.at[piece],
            pair,
        )

    values = tokens[...].astype(jnp.float32)
    normal = values * lax.rsqrt(jnp.mean(values * values, axis=1, keepdims=True) + 1e-06)
    for piece in range(halves):
        spot = pl.ds(piece * part, part)
        total = jnp.zeros((part, width), jnp.float32)
        for step in (3, 2, 0, 1):
            place = across(chip, core, step)
            if step != 3:
                target = incoming.at[place, spot]
                remote(
                    target, target, grad_send.at[0, 0], grad_recv.at[place, piece], pair
                ).wait_recv()
            columns = pl.ds(pl.multiple_of(place * share, LANES), share)
            total = total + dot_last(incoming[place, spot, :], full[:, columns])
        side_out[piece] = total.astype(jnp.bfloat16)
        to_side(piece).start()

    def finish_sides():
        gain = jnp.zeros((1, width), jnp.float32)
        for piece in range(halves):
            to_side(piece).wait_recv()
            total = side_out[piece].astype(jnp.float32) + side_in[piece].astype(jnp.float32)
            norm_grad[pl.ds(piece * part, part), :] = total
            gain = gain + jnp.sum(
                total * normal[piece * part : (piece + 1) * part], axis=0, keepdims=True
            )
        spread_gain[...] = small[...]
        spread_gain[0:1, :] = gain

        def message(shard, place):
            lanes = pl.ds(pl.multiple_of((shard * 2 + place // 2) * LANES, LANES), LANES)
            return jnp.concatenate([bias_sum, spread_gain[:, lanes]], axis=0)

        for number, (shard, place, _) in enumerate(others):
            bias_out[number] = message(shard, place)
            to_bias(number).start()
        bias_in[own, ctx] = message(own, ctx)

    over_chip(groups)
    for moment in range(groups + 3):
        if moment < groups:
            contract(moment)
        if moment == 0:
            over_line(groups)
        if 0 <= moment - 1 < groups:
            over_chip(moment - 1)
        if 0 <= moment - 2 < groups:
            over_line(moment - 2)
        if moment == 1:
            mix()
        if moment == groups:
            finish_sides()
            collect(groups)
        if 0 <= moment - 3 < groups:
            collect(moment - 3)

    for number, (shard, place, _) in enumerate(others):
        spot = bias_in.at[shard, place]
        remote(spot, spot, bias_send.at[0], bias_recv.at[shard, place], pair).wait_recv()
    for place in range(ctx_size):
        total = bias_in[0, place]
        for shard in range(1, count):
            total = total + bias_in[shard, place]
        bias_grad[place] = total[:8]
        gain_total = total[8:] if place == 0 else gain_total + total[8:]
    gain_grad[...] = gain_total

    mixture_copy.wait()
    for step in range(1, count):
        to_tokens(step).wait_send()
    for number in range(len(others)):
        to_bias(number).wait_send()
    for piece in range(halves):
        to_side(piece).wait_send()
        for step in range(3):
            to_owner(step, piece).wait_send()
    for group in range(groups + 1):
        to_core(group).wait_send()
        to_chip(group).wait_send()
        for step in range(1, count):
            to_line(group, step).wait_send()


def run_return(
    count,
    packed_grad,
    full,
    norm,
    tokens,
    bias_line,
    ours,
    theirs,
    gates,
    codes,
    branch_grad,
    attended,
    small,
):
    ctx_size, here, share = packed_grad.shape
    width = norm.shape[1]
    rows = width // (count * ctx_size)
    low, wide = jnp.bfloat16, jnp.float32
    dma = pltpu.SemaphoreType.DMA
    columns = share
    out_columns = attended.shape[1]
    return pl.pallas_call(
        partial(gradient_return, count),
        out_shape=(
            jax.ShapeDtypeStruct((here, width), wide),
            jax.ShapeDtypeStruct((ctx_size, rows, columns), wide),
            jax.ShapeDtypeStruct((ctx_size, 8, LANES), wide),
            jax.ShapeDtypeStruct((8, LANES), wide),
            jax.ShapeDtypeStruct((here, width), low),
            jax.ShapeDtypeStruct((here, width), low),
            jax.ShapeDtypeStruct((rows, out_columns), wide),
        ),
        in_specs=in_vmem(12),
        out_specs=tuple(in_vmem(7)),
        scratch_shapes=[
            pltpu.VMEM((ctx_size, here, share), low),
            pltpu.VMEM((width, here), low),
            pltpu.VMEM((ctx_size, count * 2, 2, rows, columns), low),
            pltpu.VMEM((2, here // 2, width), low),
            pltpu.VMEM((2, here // 2, width), low),
            pltpu.VMEM((ctx_size, count, 2, rows, columns), wide),
            pltpu.VMEM((ctx_size, count * 2, rows, columns), low),
            pltpu.VMEM((ctx_size, count, rows, columns), low),
            pltpu.VMEM((ctx_size, count, rows, columns), low),
            pltpu.VMEM((ctx_size, count, rows, columns), low),
            pltpu.VMEM((ctx_size, count, rows, columns), low),
            pltpu.VMEM((count * 2, 2, rows, out_columns), low),
            pltpu.VMEM((count * 2, rows, out_columns), low),
            pltpu.VMEM((count, 2, rows, out_columns), wide),
            pltpu.VMEM((count, rows, out_columns), low),
            pltpu.VMEM((count, rows, out_columns), low),
            pltpu.VMEM((count, rows, out_columns), low),
            pltpu.VMEM((count, rows, out_columns), low),
            pltpu.VMEM((15, 16, LANES), wide),
            pltpu.VMEM((count, ctx_size, 16, LANES), wide),
            pltpu.VMEM((8, width), wide),
            pltpu.VMEM(ours.shape, low),
            pltpu.VMEM(ours.shape, low),
            dma((3, 2)),
            dma((ctx_size, 2)),
            dma((2,)),
            dma((2,)),
            dma((ctx_size + 1,)),
            dma((ctx_size + 1,)),
            dma((ctx_size + 1,)),
            dma((ctx_size + 1,)),
            dma((ctx_size + 1, count)),
            dma((ctx_size + 1, count)),
            dma((15,)),
            dma((count, ctx_size)),
            dma((2,)),
            dma((count,)),
            dma((count,)),
        ],
        compiler_params=pltpu.CompilerParams(
            collective_id=2, has_side_effects=True, vmem_limit_bytes=60 * 2**20
        ),
        cost_estimate=estimate(45),
        name="gradient_return",
    )(
        packed_grad,
        full,
        norm,
        tokens,
        bias_line,
        ours,
        theirs,
        gates,
        codes,
        branch_grad,
        attended,
        small,
    )


def swap_sides(member):
    return lax.ppermute(member, "tensor", [(0, 1), (1, 0)])


def exchange(member, axis):
    return lax.all_to_all(member, axis, split_axis=0, concat_axis=0, tiled=True)


def slot_codes(routes, experts, room):
    tokens = routes.shape[0]
    picks = routes[:, :, None] == jnp.arange(experts, dtype=jnp.int32)[None, None, :]
    named = jnp.sum(picks, axis=1).astype(jnp.bfloat16)
    index = jnp.arange(tokens, dtype=jnp.int32)
    before = (index[:, None] > index[None, :]).astype(jnp.bfloat16)
    rank = jnp.dot(before, named, preferred_element_type=jnp.float32)
    slots = rank + room * jnp.arange(experts, dtype=jnp.float32)[None, :]
    return picks, jnp.sum(jnp.where(picks, slots[:, None, :], 0.0), axis=2)


def experts_apart(norm_two, upstream, gates, codes, room, count, weights):
    tokens, width = norm_two.shape
    codes = codes.astype(jnp.int32).reshape(-1)
    shaped = (count, room, width)

    def sent(member):
        slots = jnp.zeros((count * room, width), jnp.bfloat16).at[codes].set(member)
        return exchange(slots.reshape(shaped), "shard").reshape(-1, width)

    slot_rows = sent(jnp.repeat(norm_two, TOP, axis=0))
    slot_grads = sent(
        (gates[:, :, None] * upstream[:, None, :]).reshape(-1, width).astype(jnp.bfloat16)
    )
    gate_mat, up_mat, down_mat = weights
    gate_pre = dot32(slot_rows, gate_mat)
    up_pre = dot32(slot_rows, up_mat)
    activated, slope = gelu_parts(gate_pre)
    inner = (activated * up_pre).astype(jnp.bfloat16)
    expert_out = contract_cols(inner, down_mat)
    inner_grad = dot32(slot_grads, down_mat)
    gate_grad = (inner_grad * up_pre * slope).astype(jnp.bfloat16)
    up_grad = (inner_grad * activated).astype(jnp.bfloat16)
    rows_grad = contract_cols(gate_grad, gate_mat) + contract_cols(up_grad, up_mat)

    def returned(member):
        member = lax.psum(member.astype(jnp.bfloat16), "tensor").reshape(shaped)
        member = exchange(member, "shard").reshape(-1, width)[codes]
        return member.astype(jnp.float32).reshape(tokens, TOP, width)

    per_choice = returned(expert_out)
    mixture = jnp.sum(gates[:, :, None] * per_choice, axis=1)
    dots = gates * jnp.sum(per_choice * upstream[:, None, :], axis=2)
    norm_grad = jnp.sum(returned(rows_grad), axis=1)
    return mixture, dots, norm_grad, slot_rows, slot_grads, inner, gate_grad, up_grad


def local_general(
    tokens_in,
    cotangent,
    segment_ids,
    live_blocks,
    routes,
    w_query,
    w_key,
    w_value,
    w_out,
    rel_bias,
    attn_gain,
    ffn_gain,
    router,
    w_gate,
    w_up,
    w_down,
):
    rows_here, width = tokens_in.shape
    ctx_size = lax.axis_size("ctx")
    side_count = lax.axis_size("tensor")
    ctx_index = lax.axis_index("ctx")
    side = lax.axis_index("tensor")
    head_cols = w_query.shape[1]
    share = head_cols // ctx_size
    experts = router.shape[1]
    room = max(2, 3 * rows_here // experts)

    picks, codes = slot_codes(routes, experts, room)

    def by_owner(member):
        return member.reshape(member.shape[0], ctx_size, share)

    packed_rows = jnp.stack([by_owner(w_query), by_owner(w_key), by_owner(w_value)], axis=2)
    gathered = lax.all_gather(
        jnp.concatenate(
            [
                packed_rows.reshape(w_query.shape[0], -1),
                attn_gain[:, None],
                ffn_gain[:, None],
                router,
            ],
            axis=1,
        ).astype(jnp.bfloat16),
        ("shard", "ctx"),
        axis=0,
        tiled=True,
    )
    packed_w = gathered[:, : 3 * head_cols]
    gain_one = gathered[:, 3 * head_cols]
    gain_two = gathered[:, 3 * head_cols + 1]
    router_w = gathered[:, 3 * head_cols + 2 :]
    out_w = lax.all_gather(w_out.astype(jnp.bfloat16), ("shard", "ctx", "tensor"), axis=0)
    out_w = out_w.reshape(-1, side_count, w_out.shape[0], head_cols)
    out_w = jnp.transpose(out_w, (0, 2, 1, 3)).reshape(width, side_count * head_cols)
    expert_weights = tuple(
        lax.all_gather(member.astype(jnp.bfloat16), "ctx", axis=1, tiled=True)[0]
        for member in (w_gate, w_up, w_down)
    )

    inputs = tokens_in.astype(jnp.float32)
    scale_one = lax.rsqrt(jnp.mean(inputs * inputs, axis=1, keepdims=True) + 1e-06)
    normal_one = inputs * scale_one
    norm_one = (normal_one * gain_one.astype(jnp.float32)).astype(jnp.bfloat16)
    packed = dot32(norm_one, packed_w).astype(jnp.bfloat16)
    packed = jnp.transpose(packed.reshape(rows_here, ctx_size, 3 * share), (1, 0, 2))
    packed = exchange(packed, "ctx").reshape(ctx_size * rows_here, 3 * share)
    segments = lax.all_gather(segment_ids.reshape(-1), "ctx", axis=0, tiled=True)
    alive = live_tiles(segments, live_blocks[0])
    segment_row = segments.astype(jnp.float32)[None]
    pair_heads = share // HEAD
    own_bias = lax.dynamic_slice_in_dim(rel_bias, ctx_index * pair_heads, pair_heads, 1)
    buckets = span_buckets()
    line = jnp.dot(own_bias.T, buckets.T, precision=lax.Precision.HIGHEST)
    attended, attended_t, log_sum = run_forward(alive, packed, segment_row, line)
    attended = attended.reshape(ctx_size, 1, rows_here, share)
    attended = jnp.broadcast_to(attended, (ctx_size, side_count, rows_here, share))
    attended = exchange(attended.reshape(-1, rows_here, share), ("ctx", "tensor"))
    attended = attended.reshape(ctx_size, side_count, rows_here, share)
    attended = jnp.transpose(attended, (2, 1, 0, 3))
    attended_low = lax.dynamic_index_in_dim(attended, side, 1, False).reshape(rows_here, head_cols)
    attended = attended.reshape(rows_here, side_count * head_cols)
    hidden_one = inputs + contract_cols(attended, out_w)
    scale_two = lax.rsqrt(jnp.mean(hidden_one * hidden_one, axis=1, keepdims=True) + 1e-06)
    normal_two = hidden_one * scale_two
    norm_two = (normal_two * gain_two.astype(jnp.float32)).astype(jnp.bfloat16)
    logits = dot32(norm_two, router_w)
    chosen = jnp.sum(jnp.where(picks, logits[:, None, :], 0.0), axis=2)
    gates = jax.nn.softmax(chosen, axis=1)
    upstream = cotangent.astype(jnp.float32)
    results = experts_apart(norm_two, upstream, gates, codes, room, experts, expert_weights)
    mixture, gate_dots, norm_grad, slot_rows, slot_grads, inner, gate_grad, up_grad = results
    weight_grads = lax.psum_scatter(
        jnp.stack(
            [
                contract_rows(slot_rows, gate_grad),
                contract_rows(slot_rows, up_grad),
                contract_rows(slot_grads, inner),
            ],
            axis=1,
        ).astype(jnp.bfloat16),
        "ctx",
        scatter_dimension=0,
        tiled=True,
    ).astype(jnp.float32)
    mixed = (hidden_one + mixture).astype(jnp.bfloat16)
    gate_shift = gate_dots - gates * jnp.sum(gate_dots, axis=1, keepdims=True)
    logit_grad = jnp.sum(jnp.where(picks, gate_shift[:, :, None], 0.0), axis=1)
    router_f = router_w.astype(jnp.float32)
    norm_grad = norm_grad + jnp.dot(logit_grad, router_f.T, precision=lax.Precision.HIGHEST)
    spread_two = norm_grad * gain_two.astype(jnp.float32)
    hidden_grad = upstream + scale_two * (
        spread_two - normal_two * jnp.mean(spread_two * normal_two, axis=1, keepdims=True)
    )
    branch_grad = hidden_grad.astype(jnp.bfloat16)
    own_out_w = lax.dynamic_slice_in_dim(out_w, side * head_cols, head_cols, 1)
    grad_heads = dot32(branch_grad, own_out_w).astype(jnp.bfloat16)
    grad_heads = jnp.transpose(grad_heads.reshape(rows_here, ctx_size, share), (1, 0, 2))
    grad_heads = exchange(grad_heads, "ctx").reshape(-1, share)
    packed_grad, bias_line = run_backward(
        alive, packed, segment_row, line, grad_heads, attended_t, log_sum
    )
    own_grad = jnp.dot(buckets.T, bias_line[:pair_heads].T, precision=lax.Precision.HIGHEST)
    far = jnp.sum(bias_line[pair_heads : 3 * pair_heads], axis=1)
    half = NBUCK // 2
    own_grad = own_grad.at[half - 1].add(far[:pair_heads]).at[NBUCK - 1].add(far[pair_heads:])
    bias_acc = lax.dynamic_update_slice_in_dim(
        jnp.zeros(rel_bias.shape, jnp.float32), own_grad, ctx_index * pair_heads, 1
    )
    packed_grad = exchange(packed_grad.reshape(ctx_size, rows_here, 3 * share), "ctx")
    packed_grad = jnp.transpose(packed_grad, (1, 0, 2)).reshape(rows_here, 3 * head_cols)
    norm_one_grad = contract_cols(packed_grad, packed_w).astype(jnp.bfloat16)
    norm_one_grad = norm_one_grad.astype(jnp.float32) + swap_sides(norm_one_grad).astype(
        jnp.float32
    )
    spread_one = norm_one_grad * gain_one.astype(jnp.float32)
    input_grad = hidden_grad + scale_one * (
        spread_one - normal_one * jnp.mean(spread_one * normal_one, axis=1, keepdims=True)
    )
    first_gain = jnp.sum(norm_one_grad * normal_one, axis=0)[:, None]
    second_gain = jnp.sum(norm_grad * normal_two, axis=0)[:, None]
    router_part = jnp.dot(
        norm_two.astype(jnp.float32).T, logit_grad, precision=lax.Precision.HIGHEST
    )
    reduced = lax.psum_scatter(
        jnp.concatenate(
            [
                contract_rows(norm_one, packed_grad),
                contract_rows(branch_grad, attended_low),
                first_gain,
                second_gain,
                router_part,
            ],
            axis=1,
        ),
        ("shard", "ctx"),
        scatter_dimension=0,
        tiled=True,
    )
    grad_bias = lax.psum(bias_acc, ("shard", "ctx"))
    packed_rows = reduced[:, : 3 * head_cols].reshape(-1, ctx_size, 3, share)
    return (
        mixed,
        input_grad.astype(jnp.bfloat16),
        packed_rows[:, :, 0].reshape(-1, head_cols),
        packed_rows[:, :, 1].reshape(-1, head_cols),
        packed_rows[:, :, 2].reshape(-1, head_cols),
        reduced[:, 3 * head_cols : 4 * head_cols],
        grad_bias,
        reduced[:, 4 * head_cols],
        reduced[:, 4 * head_cols + 1],
        reduced[:, 4 * head_cols + 2 :],
        weight_grads[:, 0][None],
        weight_grads[:, 1][None],
        weight_grads[:, 2][None],
    )


def ppermute_ctx(member, flip):
    return lax.ppermute(member, "ctx", [(place, place ^ flip) for place in range(4)])


def local_fused(
    tokens_in,
    cotangent,
    segment_ids,
    live_blocks,
    routes,
    w_query,
    w_key,
    w_value,
    w_out,
    rel_bias,
    attn_gain,
    ffn_gain,
    router,
    w_gate,
    w_up,
    w_down,
):
    rows_here, width = tokens_in.shape
    count = lax.axis_size("shard")
    ctx_size = lax.axis_size("ctx")
    side_count = lax.axis_size("tensor")
    ctx_index = lax.axis_index("ctx")
    side = lax.axis_index("tensor")
    head_cols = w_query.shape[1]
    share = head_cols // ctx_size
    experts = router.shape[1]
    room = max(2, 3 * rows_here // experts)

    picks, codes = slot_codes(routes, experts, room)
    code_rows = jnp.pad(jnp.transpose(codes), ((0, 8 - TOP), (0, 0)), constant_values=-1.0)
    def by_owner(member):
        return member.reshape(member.shape[0], ctx_size, share)

    packed_rows = jnp.stack([by_owner(w_query), by_owner(w_key), by_owner(w_value)], axis=2)
    rows = w_query.shape[0]
    weight = jnp.concatenate(
        [
            packed_rows.reshape(rows, -1),
            attn_gain[:, None],
            ffn_gain[:, None],
            router,
            jnp.zeros((rows, LANES - 2 - experts), jnp.float32),
        ],
        axis=1,
    ).astype(jnp.bfloat16)
    segment = jnp.broadcast_to(segment_ids.astype(jnp.float32), (8, rows_here))
    full, packed, norm_one, segments, out_w, up_slots, *lows = run_gather(
        count,
        ctx_size,
        room,
        weight,
        w_out.astype(jnp.bfloat16),
        tokens_in,
        segment,
        cotangent,
        code_rows,
        (w_gate[0], w_up[0], w_down[0]),
    )
    packed = packed.reshape(ctx_size * rows_here, 3 * share)
    gains = full[:, 3 * head_cols :].astype(jnp.float32)
    gain_one = gains[:, 0]
    gain_two = gains[:, 1]
    router_w = full[:, 3 * head_cols + 2 : 3 * head_cols + 2 + experts]
    gate_low, up_low, down_low, gate_core, up_core, down_core, gate_chip, gate_far = lows
    up_chip, down_chip = ppermute_ctx(up_low, 2), ppermute_ctx(down_low, 2)

    inputs = tokens_in.astype(jnp.float32)
    scale_one = lax.rsqrt(jnp.mean(inputs * inputs, axis=1, keepdims=True) + 1e-06)
    normal_one = inputs * scale_one
    segment_row = segments[:, 0].reshape(1, -1)
    alive = live_tiles(segment_row[0], live_blocks[0])
    pair_heads = share // HEAD
    own_bias = lax.dynamic_slice_in_dim(rel_bias, ctx_index * pair_heads, pair_heads, 1)
    line = jnp.dot(own_bias.T, span_buckets().T, precision=lax.Precision.HIGHEST)
    attended, attended_t, log_sum = run_forward(alive, packed, segment_row, line)
    attended, up_chip = lax.optimization_barrier((attended, up_chip))
    expert_weights = [gate_low, gate_chip, gate_core, gate_far]
    expert_weights += [up_low, up_chip, up_core, ppermute_ctx(up_chip, 1)]
    expert_weights += [down_low, down_chip, down_core, ppermute_ctx(down_chip, 1)]
    attended = attended.reshape(ctx_size, 1, rows_here, share)
    attended = jnp.broadcast_to(attended, (ctx_size, side_count, rows_here, share))
    attended = exchange(attended.reshape(-1, rows_here, share), ("ctx", "tensor"))
    attended = attended.reshape(ctx_size, side_count, rows_here, share)
    attended = jnp.transpose(attended, (2, 1, 0, 3))
    attended_low = lax.dynamic_index_in_dim(attended, side, 1, False).reshape(rows_here, head_cols)
    branch = [
        contract_cols(attended[:, place].reshape(rows_here, head_cols), out_w[place])
        for place in range(side_count)
    ]
    hidden_one = inputs + (branch[0] + branch[1])
    scale_two = lax.rsqrt(jnp.mean(hidden_one * hidden_one, axis=1, keepdims=True) + 1e-06)
    normal_two = hidden_one * scale_two
    norm_two = (normal_two * gain_two).astype(jnp.bfloat16)
    logits = dot32(norm_two, router_w)
    chosen = jnp.sum(jnp.where(picks, logits[:, None, :], 0.0), axis=2)
    gates = jax.nn.softmax(chosen, axis=1)
    upstream = cotangent.astype(jnp.float32)
    norm_grad, dots, outs, kept, given = run_experts(
        count, ctx_size, norm_two, gates, code_rows, codes, up_slots, expert_weights
    )
    half = room // 2
    theirs = swap_sides(lax.dynamic_slice_in_dim(outs, (1 - side) * half, half, 1))
    ours = lax.dynamic_slice_in_dim(outs, side * half, half, 1)

    weight_grads = kept.astype(jnp.float32) + ppermute_ctx(given, 2).astype(jnp.float32)
    gate_dots = jnp.transpose(dots[:TOP])
    gate_shift = gate_dots - gates * jnp.sum(gate_dots, axis=1, keepdims=True)
    logit_grad = jnp.sum(jnp.where(picks, gate_shift[:, :, None], 0.0), axis=1)
    router_f = router_w.astype(jnp.float32)
    norm_grad = norm_grad + jnp.dot(logit_grad, router_f.T, precision=lax.Precision.HIGHEST)
    spread_two = norm_grad * gain_two
    hidden_grad = upstream + scale_two * (
        spread_two - normal_two * jnp.mean(spread_two * normal_two, axis=1, keepdims=True)
    )
    branch_grad = hidden_grad.astype(jnp.bfloat16)
    own_out_w = lax.dynamic_index_in_dim(out_w, side, 0, False)
    grad_heads = dot32(branch_grad, own_out_w).astype(jnp.bfloat16)
    grad_heads = jnp.transpose(grad_heads.reshape(rows_here, ctx_size, share), (1, 0, 2))
    grad_heads = exchange(grad_heads, "ctx").reshape(-1, share)
    second_gain = jnp.sum(norm_grad * normal_two, axis=0)[None]
    router_part = jnp.dot(
        logit_grad.T, norm_two.astype(jnp.float32), precision=lax.Precision.HIGHEST
    )
    small = jnp.concatenate(
        [jnp.zeros_like(second_gain), second_gain, router_part, jnp.zeros((6 - experts, width))]
    )
    packed_grad, bias_line = run_backward(
        alive, packed, segment_row, line, grad_heads, attended_t, log_sum
    )
    returned = run_return(
        count,
        packed_grad.reshape(ctx_size, rows_here, 3 * share),
        full,
        norm_one,
        tokens_in,
        bias_line,
        ours,
        theirs,
        gates,
        codes,
        branch_grad,
        attended_low,
        small,
    )
    norm_one_grad, attention_grad, bias_grad, gains_grad, mixture, peer_mixture, out_grad = returned
    mixture = mixture.astype(jnp.float32) + peer_mixture.astype(jnp.float32)
    mixed = (hidden_one + mixture).astype(jnp.bfloat16)
    spread_one = norm_one_grad * gain_one
    input_grad = hidden_grad + scale_one * (
        spread_one - normal_one * jnp.mean(spread_one * normal_one, axis=1, keepdims=True)
    )
    attention_grad = attention_grad.reshape(ctx_size, rows, 3, share)

    def owned(number):
        return jnp.transpose(attention_grad[:, :, number], (1, 0, 2)).reshape(rows, head_cols)

    gains_grad = lax.dynamic_slice_in_dim(gains_grad, ctx_index % 2 * rows, rows, 1)
    bias_grad = jnp.transpose(bias_grad[:, :pair_heads, :NBUCK], (2, 0, 1))
    return (
        mixed,
        input_grad.astype(jnp.bfloat16),
        owned(0),
        owned(1),
        owned(2),
        out_grad,
        bias_grad.reshape(rel_bias.shape),
        gains_grad[0],
        gains_grad[1],
        jnp.transpose(gains_grad[2 : 2 + experts]),
        weight_grads[0][None],
        weight_grads[1][None],
        weight_grads[2][None],
    )


def solution(mesh):
    placed = (
        P(("shard", "ctx"), None),
        P(("shard", "ctx"), None),
        P("shard", "ctx"),
        P("shard", None, None),
        P(("shard", "ctx"), None),
        P(("shard", "ctx"), "tensor"),
        P(("shard", "ctx"), "tensor"),
        P(("shard", "ctx"), "tensor"),
        P(("shard", "ctx"), "tensor"),
        P(None, "tensor"),
        P(("shard", "ctx")),
        P(("shard", "ctx")),
        P(("shard", "ctx"), None),
        P("shard", "ctx", "tensor"),
        P("shard", "ctx", "tensor"),
        P("shard", "ctx", "tensor"),
    )
    sizes = (mesh.shape["shard"], mesh.shape["ctx"], mesh.shape["tensor"])
    fused = sizes == (4, 4, 2)
    return jax.shard_map(
        local_fused if fused else local_general,
        mesh=mesh,
        in_specs=placed,
        out_specs=(
            P(("shard", "ctx"), None),
            P(("shard", "ctx"), None),
            P(("shard", "ctx"), "tensor"),
            P(("shard", "ctx"), "tensor"),
            P(("shard", "ctx"), "tensor"),
            P(("shard", "ctx"), "tensor"),
            P(None, "tensor"),
            P(("shard", "ctx")),
            P(("shard", "ctx")),
            P(("shard", "ctx"), None),
            P("shard", "ctx", "tensor"),
            P("shard", "ctx", "tensor"),
            P("shard", "ctx", "tensor"),
        ),
        check_vma=False,
    )
```

```python
import math
from functools import partial

import jax
import jax.numpy as jnp
from jax import lax
from jax.experimental import pallas as pl
from jax.experimental.pallas import tpu as pltpu
from jax.sharding import PartitionSpec as P

HEAD = 64
NBUCK = 32
TOP = 2
ATT_BLK = 512


FAR_STEPS = (12, 16, 23, 32, 46, 64, 91)


def bucket_ids(relative):
    distance = jnp.abs(relative)
    far = jnp.full(distance.shape, 8, jnp.int32)
    for bound in FAR_STEPS:
        far = far + (distance >= bound).astype(jnp.int32)
    near = jnp.where(distance < 8, distance, far)
    return near + jnp.where(relative > 0, NBUCK // 2, 0)


def contract_rows(left, right):
    return lax.dot_general(
        left, right, (((0,), (0,)), ((), ())), preferred_element_type=jnp.float32
    )


def contract_cols(left, right):
    return lax.dot_general(
        left, right, (((1,), (1,)), ((), ())), preferred_element_type=jnp.float32
    )


TILE = 256
BIG = 2.0**100
SPAN = 4 * TILE


def place_mask(segment_row):
    rows = lax.broadcasted_iota(jnp.int32, (128, segment_row.shape[1]), 0).astype(jnp.float32)
    apart = jnp.where(rows == segment_row, 0.0, -BIG)
    return jnp.where(rows < 8.0, apart, jnp.where(rows < 11.0, 1.0, 0.0))


def seat_rows(segment_row, extra):
    rows = lax.broadcasted_iota(jnp.int32, (128, segment_row.shape[1]), 0).astype(jnp.float32)
    own = jnp.where((rows == segment_row) & (rows < 8.0), 1.0, 0.0)
    if extra is None:
        return own.astype(jnp.bfloat16)
    high = extra.astype(jnp.bfloat16).astype(jnp.float32)
    rest = extra - high
    middle = rest.astype(jnp.bfloat16).astype(jnp.float32)
    low = rest - middle
    own = jnp.where(rows == 8.0, high, own)
    own = jnp.where(rows == 9.0, middle, own)
    return jnp.where(rows == 10.0, low, own).astype(jnp.bfloat16)


def fill_bias(line_ref, bias_ref):
    for head in range(2):
        line = line_ref[head : head + 1, :]
        turned = pltpu.roll(
            jnp.broadcast_to(line, (TILE, SPAN)), 0, axis=1, stride=1, stride_axis=0
        )
        bias_ref[head, 1] = turned[:, TILE : 2 * TILE]
        bias_ref[head, 2] = turned[:, :TILE]
        bias_ref[head, 3] = turned[:, 3 * TILE :]
        bias_ref[head, 0] = jnp.broadcast_to(line[:, 511:512], (TILE, TILE))
        bias_ref[head, 4] = jnp.broadcast_to(line[:, 513:514], (TILE, TILE))


def tile_at(index):
    return pl.ds(pl.multiple_of(index * TILE, TILE), TILE)


def dot32(left, right):
    return jnp.dot(left, right, preferred_element_type=jnp.float32)


def attention_forward(
    alive, packed, segment, line, out, out_t, log_sum, key_side, query_side, value_t, bias, top, acc
):
    length = packed.shape[0]
    tiles = length // TILE
    fill_bias(line, bias)

    def prepare(index, unused):
        spot = tile_at(index)
        seg = segment[0:1, spot]
        block = packed[spot, :].astype(jnp.float32)
        key_side[spot, :128] = packed[spot, 128:256]
        key_side[spot, 128:] = jnp.transpose(place_mask(seg)).astype(jnp.bfloat16)
        query_t = jnp.transpose(block[:, :128]) * 0.125
        seats = seat_rows(seg, None)
        half = lax.broadcasted_iota(jnp.int32, (128, TILE), 0) // HEAD
        values = jnp.transpose(block[:, 256:]).astype(jnp.bfloat16)
        ones = jnp.where(lax.broadcasted_iota(jnp.int32, (16, TILE), 0) == 0, 1.0, 0.0)
        for head in range(2):
            query_side[head, :128, spot] = jnp.where(half == head, query_t, 0.0).astype(
                jnp.bfloat16
            )
            query_side[head, 128:, spot] = seats
            value_t[head, :HEAD, spot] = values[HEAD * head : HEAD * (head + 1)]
            value_t[head, HEAD:, spot] = ones.astype(jnp.bfloat16)
        return unused

    lax.fori_loop(0, tiles, prepare, 0)

    def query_tile(query_index, unused):
        query_spot = tile_at(query_index)
        top[...] = jnp.full(top.shape, -3e38, jnp.float32)
        acc[...] = jnp.zeros(acc.shape, jnp.float32)

        def key_tile(key_index, carried):
            @pl.when(alive[query_index * tiles + key_index] == 1)
            def _():
                key_spot = tile_at(key_index)
                slot = jnp.clip(key_index - query_index, -2, 2) + 2
                keys = key_side[key_spot, :]
                for head in range(2):
                    scores = dot32(keys, query_side[head, :, query_spot]) + bias[head, slot]
                    before = top[head : head + 1, :]
                    now = jnp.maximum(before, jnp.max(scores, axis=0, keepdims=True))
                    weights = jnp.exp(scores - now).astype(jnp.bfloat16)
                    top[head : head + 1, :] = now
                    acc[head] = acc[head] * jnp.exp(before - now) + dot32(
                        value_t[head, :, key_spot], weights
                    )

            return carried

        lax.fori_loop(0, tiles, key_tile, 0)
        parts = []
        for head in range(2):
            total = acc[head, HEAD : HEAD + 1, :]
            part = acc[head, :HEAD, :] / total
            out_t[HEAD * head : HEAD * (head + 1), query_spot] = part
            log_sum[head : head + 1, query_spot] = top[head : head + 1, :] + jnp.log(total)
            parts.append(part)
        out[query_spot, :] = jnp.transpose(jnp.concatenate(parts, axis=0)).astype(jnp.bfloat16)
        return unused

    lax.fori_loop(0, tiles, query_tile, 0)


def attention_backward(
    alive,
    packed,
    segment,
    line,
    grads,
    out_t,
    log_sum,
    packed_grad,
    bias_grad,
    key_side,
    value_side,
    query_side,
    grad_side,
    key_t,
    query_pair,
    grad_pair,
    bias,
    bias_acc,
    query_acc,
    key_acc,
    value_acc,
):
    length = packed.shape[0]
    tiles = length // TILE
    fill_bias(line, bias)
    bias_acc[...] = jnp.zeros(bias_acc.shape, jnp.float32)

    def prepare(index, unused):
        spot = tile_at(index)
        seg = segment[0:1, spot]
        block = packed[spot, :].astype(jnp.float32)
        grad = grads[spot, :].astype(jnp.float32)
        seats = jnp.transpose(place_mask(seg)).astype(jnp.bfloat16)
        key_side[spot, :128] = packed[spot, 128:256]
        key_side[spot, 128:] = seats
        value_side[spot, :128] = packed[spot, 256:]
        value_side[spot, 128:] = seats
        key_t[:, spot] = jnp.transpose(block[:, 128:256]).astype(jnp.bfloat16)
        query_t = jnp.transpose(block[:, :128]) * 0.125
        grad_t = jnp.transpose(grad)
        half = lax.broadcasted_iota(jnp.int32, (128, TILE), 0) // HEAD
        side = lax.broadcasted_iota(jnp.int32, (TILE, 128), 1) // HEAD
        products = grad_t * out_t[:, spot]
        query_acc[:, spot] = jnp.zeros((128, TILE), jnp.float32)
        for head in range(2):
            query_side[head, :128, spot] = jnp.where(half == head, query_t, 0.0).astype(
                jnp.bfloat16
            )
            query_side[head, 128:, spot] = seat_rows(seg, -log_sum[head : head + 1, spot])
            delta = jnp.sum(products[HEAD * head : HEAD * (head + 1)], axis=0, keepdims=True)
            grad_side[head, :128, spot] = jnp.where(half == head, grad_t, 0.0).astype(jnp.bfloat16)
            grad_side[head, 128:, spot] = seat_rows(jnp.full_like(seg, -1.0), -delta)
            query_pair[index, TILE * head : TILE * (head + 1), :] = jnp.where(
                side == head, block[:, :128] * 0.125, 0.0
            ).astype(jnp.bfloat16)
            grad_pair[index, TILE * head : TILE * (head + 1), :] = jnp.where(
                side == head, grad, 0.0
            ).astype(jnp.bfloat16)
        return unused

    lax.fori_loop(0, tiles, prepare, 0)

    def key_tile(key_index, unused):
        key_spot = tile_at(key_index)
        key_acc[...] = jnp.zeros(key_acc.shape, jnp.float32)
        value_acc[...] = jnp.zeros(value_acc.shape, jnp.float32)

        def query_tile(query_index, carried):
            @pl.when(alive[query_index * tiles + key_index] == 1)
            def _():
                query_spot = tile_at(query_index)
                slot = jnp.clip(key_index - query_index, -2, 2) + 2
                keys = key_side[key_spot, :]
                values = value_side[key_spot, :]
                probs, score_grads = [], []
                for head in range(2):
                    scores = dot32(keys, query_side[head, :, query_spot]) + bias[head, slot]
                    prob = jnp.exp(scores)
                    score_grad = prob * dot32(values, grad_side[head, :, query_spot])
                    bias_acc[head, slot] += score_grad
                    score_grad = score_grad.astype(jnp.bfloat16)
                    probs.append(prob.astype(jnp.bfloat16))
                    score_grads.append(score_grad)
                    rows = slice(HEAD * head, HEAD * (head + 1))
                    query_acc[rows, query_spot] += dot32(key_t[rows, key_spot], score_grad)
                value_acc[...] += dot32(jnp.concatenate(probs, axis=1), grad_pair[query_index])
                key_acc[...] += dot32(jnp.concatenate(score_grads, axis=1), query_pair[query_index])

            return carried

        lax.fori_loop(0, tiles, query_tile, 0)
        packed_grad[key_spot, 128:256] = key_acc[...].astype(jnp.bfloat16)
        packed_grad[key_spot, 256:] = value_acc[...].astype(jnp.bfloat16)
        return unused

    lax.fori_loop(0, tiles, key_tile, 0)

    def finish(index, unused):
        spot = tile_at(index)
        packed_grad[spot, :128] = (jnp.transpose(query_acc[:, spot]) * 0.125).astype(jnp.bfloat16)
        return unused

    lax.fori_loop(0, tiles, finish, 0)
    rows = lax.broadcasted_iota(jnp.int32, (TILE, TILE), 0)
    columns = lax.broadcasted_iota(jnp.int32, (TILE, TILE), 1)
    flip = jnp.where(rows + columns == TILE - 1, 1.0, 0.0)
    bias_grad[...] = jnp.zeros(bias_grad.shape, jnp.float32)
    for head in range(2):
        spread = jnp.concatenate(
            [
                bias_acc[head, 2],
                bias_acc[head, 1],
                jnp.zeros((TILE, TILE), jnp.float32),
                bias_acc[head, 3],
            ],
            axis=1,
        )
        flipped = jnp.dot(
            flip, spread, precision=lax.Precision.HIGHEST, preferred_element_type=jnp.float32
        )
        turned = pltpu.roll(flipped, SPAN - TILE + 1, axis=1, stride=1, stride_axis=0)
        bias_grad[head : head + 1, :] = jnp.sum(turned, axis=0, keepdims=True)
        bias_grad[2 + head : 3 + head, :TILE] = jnp.sum(bias_acc[head, 0], axis=0, keepdims=True)
        bias_grad[4 + head : 5 + head, :TILE] = jnp.sum(bias_acc[head, 4], axis=0, keepdims=True)


def estimate(micros):
    return pl.CostEstimate(flops=int(micros * 1e9), bytes_accessed=0, transcendentals=0)


def in_vmem(count):
    return [pl.BlockSpec(memory_space=pltpu.VMEM)] * count


def run_forward(alive, packed, segment, line):
    length = packed.shape[0]
    return pl.pallas_call(
        attention_forward,
        out_shape=(
            jax.ShapeDtypeStruct((length, 128), jnp.bfloat16),
            jax.ShapeDtypeStruct((128, length), jnp.float32),
            jax.ShapeDtypeStruct((8, length), jnp.float32),
        ),
        in_specs=[pl.BlockSpec(memory_space=pltpu.SMEM)] + in_vmem(3),
        out_specs=tuple(in_vmem(3)),
        scratch_shapes=[
            pltpu.VMEM((length, 256), jnp.bfloat16),
            pltpu.VMEM((2, 256, length), jnp.bfloat16),
            pltpu.VMEM((2, HEAD + 16, length), jnp.bfloat16),
            pltpu.VMEM((2, 5, TILE, TILE), jnp.float32),
            pltpu.VMEM((8, TILE), jnp.float32),
            pltpu.VMEM((2, HEAD + 16, TILE), jnp.float32),
        ],
        compiler_params=pltpu.CompilerParams(vmem_limit_bytes=40 * 2**20),
        cost_estimate=estimate(20),
        name="attention_forward",
    )(alive, packed, segment, line)


def run_backward(alive, packed, segment, line, grads, out_t, log_sum):
    length = packed.shape[0]
    tiles = length // TILE
    return pl.pallas_call(
        attention_backward,
        out_shape=(
            jax.ShapeDtypeStruct((length, 384), jnp.bfloat16),
            jax.ShapeDtypeStruct((8, SPAN), jnp.float32),
        ),
        in_specs=[pl.BlockSpec(memory_space=pltpu.SMEM)] + in_vmem(6),
        out_specs=tuple(in_vmem(2)),
        scratch_shapes=[
            pltpu.VMEM((length, 256), jnp.bfloat16),
            pltpu.VMEM((length, 256), jnp.bfloat16),
            pltpu.VMEM((2, 256, length), jnp.bfloat16),
            pltpu.VMEM((2, 256, length), jnp.bfloat16),
            pltpu.VMEM((128, length), jnp.bfloat16),
            pltpu.VMEM((tiles, 2 * TILE, 128), jnp.bfloat16),
            pltpu.VMEM((tiles, 2 * TILE, 128), jnp.bfloat16),
            pltpu.VMEM((2, 5, TILE, TILE), jnp.float32),
            pltpu.VMEM((2, 5, TILE, TILE), jnp.float32),
            pltpu.VMEM((128, length), jnp.float32),
            pltpu.VMEM((TILE, 128), jnp.float32),
            pltpu.VMEM((TILE, 128), jnp.float32),
        ],
        compiler_params=pltpu.CompilerParams(vmem_limit_bytes=48 * 2**20),
        cost_estimate=estimate(26),
        name="attention_backward",
    )(alive, packed, segment, line, grads, out_t, log_sum)


def signed_span():
    places = jnp.arange(SPAN, dtype=jnp.int32)
    return jnp.where(places < SPAN // 2, -places, SPAN - places)


def span_buckets():
    return (bucket_ids(signed_span())[:, None] == jnp.arange(NBUCK)[None, :]).astype(jnp.float32)


def live_tiles(segments, live):
    tiles = segments.shape[0] // TILE
    grouped = segments.reshape(tiles, TILE)
    first, last = grouped[:, 0], grouped[:, -1]
    meets = (first[:, None] <= last[None, :]) & (first[None, :] <= last[:, None])
    spread = jnp.repeat(jnp.repeat(live, ATT_BLK // TILE, axis=0), ATT_BLK // TILE, axis=1)
    return (meets & (spread == 1)).astype(jnp.int32).reshape(-1)


MESH = pl.DeviceIdType.MESH
LANES = 128


def places():
    own, ctx, side = lax.axis_index("shard"), lax.axis_index("ctx"), lax.axis_index("tensor")
    return own, ctx, side, ctx // 2, ctx % 2


def nearest(own, count, step):
    flip = own // (count // 2)
    place = flip * (count - 1 - own) + (1 - flip) * own
    turn = step - 1
    turn = turn + (turn - place + count) // count
    other = flip * (count - 1 - turn) + (1 - flip) * turn
    first = 1 - (step + count - 1) // count
    return first * own + (1 - first) * other


def partner(own, turn):
    return (own // 2 + turn // 2) % 2 * 2 + (own + turn) % 2


def across(chip, core, step):
    return (chip + 1 - step // 2) % 2 * 2 + (core + step + step // 2) % 2


def remote(source, target, send, recv, device):
    return pltpu.make_async_remote_copy(
        source, target, send, recv, device_id=device, device_id_type=MESH
    )


def greet(devices):
    barrier = pltpu.get_barrier_semaphore()
    for device in devices:
        pl.semaphore_signal(barrier, 1, device_id=device, device_id_type=MESH)
    pl.semaphore_wait(barrier, len(devices))


def gelu_parts(value):
    root = math.sqrt(2.0 / math.pi)
    square = value * value
    bend = jnp.tanh(root * value * (1.0 + 0.044715 * square))
    half = 0.5 * (1.0 + bend)
    slope = half + 0.5 * value * (1.0 - bend * bend) * (root * (1.0 + 0.134145 * square))
    return value * half, slope


def dot_last(left, right):
    return lax.dot_general(
        left, right, (((1,), (1,)), ((), ())), preferred_element_type=jnp.float32
    )


def expert_exchange(
    count,
    norm,
    gates,
    code_rows,
    code_cols,
    upstream,
    gate_own,
    gate_chip,
    gate_core,
    gate_far,
    up_own,
    up_chip,
    up_core,
    up_far,
    down_own,
    down_chip,
    down_core,
    down_far,
    row_grad,
    dot_rows,
    own_hbm,
    mine_hbm,
    other_hbm,
    kept_hbm,
    gate_given,
    up_given,
    down_given,
    gate_w,
    up_w,
    down_w,
    rows,
    sent,
    gates_in,
    gates_out,
    slot_grad,
    inner,
    gate_grad,
    up_grad,
    outs,
    partial,
    peer_part,
    summed,
    back,
    dots_out,
    dots_in,
    final_out,
    final_in,
    final_dots,
    core_in,
    chip_in,
    load_sem,
    store_sem,
    rows_send,
    rows_recv,
    pass_send,
    pass_recv,
    gates_send,
    gates_recv,
    part_send,
    part_recv,
    back_send,
    back_recv,
    dots_send,
    dots_recv,
    final_send,
    final_recv,
    core_send,
    core_recv,
    chip_send,
    chip_recv,
):
    own = lax.axis_index("shard")
    ctx = lax.axis_index("ctx")
    side = lax.axis_index("tensor")
    tokens, width = norm.shape
    room = upstream.shape[1]
    half = room // 2
    hidden = gate_w.shape[1]
    peer = (own, ctx, 1 - side)

    def source(step):
        return partner(own, step)

    barrier = pltpu.get_barrier_semaphore()
    for step in range(1, count):
        pl.semaphore_signal(barrier, 1, device_id=(source(step), ctx, side), device_id_type=MESH)
    chip, core = ctx // 2, ctx % 2
    core_peer = (own, chip * 2 + 1 - core, side)
    chip_peer = (own, (1 - chip) * 2 + core, side)
    for device in (peer, core_peer, chip_peer):
        pl.semaphore_signal(barrier, 1, device_id=device, device_id_type=MESH)
    deep = gate_own.shape[0]
    origins = (ctx, (1 - chip) * 2 + core, chip * 2 + 1 - core, (1 - chip) * 2 + 1 - core)
    pieces_of = (
        (gate_w, (gate_own, gate_chip, gate_core, gate_far)),
        (up_w, (up_own, up_chip, up_core, up_far)),
        (down_w, (down_own, down_chip, down_core, down_far)),
    )
    loads = []
    for number, (target, sources) in enumerate(pieces_of):
        for turn, source_ref in enumerate(sources):
            spot = pl.ds(pl.multiple_of(origins[turn] * deep, deep), deep)
            sem = load_sem.at[4 * number + turn]
            loads.append(pltpu.make_async_copy(source_ref, target.at[spot], sem))
    for load in loads:
        load.start()
    pl.semaphore_wait(barrier, count + 2)

    my_half = pl.ds(pl.multiple_of(side * half, half), half)
    peer_half = pl.ds(pl.multiple_of((1 - side) * half, half), half)

    def picked(expert, start, amount):
        slots = lax.broadcasted_iota(jnp.int32, (amount, tokens), 0) + expert * room + start
        slots = slots.astype(jnp.float32)
        hit = (code_rows[0:1, :] == slots) | (code_rows[1:2, :] == slots)
        return jnp.where(hit, 1.0, 0.0).astype(jnp.bfloat16)

    def slot_gates(expert):
        slots = lax.broadcasted_iota(jnp.int32, (tokens, room), 1) + expert * room
        slots = slots.astype(jnp.float32)
        held = jnp.where(code_cols[:, 0:1] == slots, gates[:, 0:1], 0.0)
        held = held + jnp.where(code_cols[:, 1:2] == slots, gates[:, 1:2], 0.0)
        return jnp.broadcast_to(jnp.sum(held, axis=0, keepdims=True), (8, room))

    def rows_copy(step):
        target = source(step)
        return pltpu.make_async_remote_copy(
            sent.at[step - 1],
            rows.at[own, my_half],
            rows_send.at[step - 1],
            rows_recv.at[own],
            device_id=(target, ctx, side),
            device_id_type=MESH,
        )

    def gates_copy(step):
        return pltpu.make_async_remote_copy(
            gates_out.at[step - 1],
            gates_in.at[own],
            gates_send.at[step - 1],
            gates_recv.at[own],
            device_id=(source(step), ctx, side),
            device_id_type=MESH,
        )

    def send_rows(step, unused):
        target = source(step)
        sent[step - 1] = dot32(picked(target, side * half, half), norm[...]).astype(jnp.bfloat16)
        rows_copy(step).start()
        gates_out[step - 1] = slot_gates(target)
        gates_copy(step).start()
        return unused

    lax.fori_loop(1, count, send_rows, 0)
    rows[own] = dot32(picked(own, 0, room), norm[...]).astype(jnp.bfloat16)
    gates_in[own] = slot_gates(own)
    for load in loads:
        load.wait()

    def landed(buffer, send, recv, origin):
        return pltpu.make_async_remote_copy(
            buffer, buffer, send, recv, device_id=peer, device_id_type=MESH
        )

    def pass_copy(origin):
        return pltpu.make_async_remote_copy(
            rows.at[origin, my_half],
            rows.at[origin, my_half],
            pass_send.at[origin],
            pass_recv.at[origin],
            device_id=peer,
            device_id_type=MESH,
        )

    def part_copy(step):
        return pltpu.make_async_remote_copy(
            partial.at[step, peer_half],
            peer_part.at[step],
            part_send.at[step],
            part_recv.at[step],
            device_id=peer,
            device_id_type=MESH,
        )

    def back_copy(step):
        return pltpu.make_async_remote_copy(
            summed.at[step],
            back.at[own],
            back_send.at[step],
            back_recv.at[own],
            device_id=(source(step), ctx, side),
            device_id_type=MESH,
        )

    def dots_copy(step):
        return pltpu.make_async_remote_copy(
            dots_out.at[step],
            dots_in.at[own],
            dots_send.at[step],
            dots_recv.at[own],
            device_id=(source(step), ctx, side),
            device_id_type=MESH,
        )

    def send_back(step):
        part_copy(step).wait_recv()
        summed[step] = (
            partial[step, my_half].astype(jnp.float32) + peer_part[step].astype(jnp.float32)
        ).astype(jnp.bfloat16)
        back_copy(step).start()

    cut = (hidden // 256 + 1) // 2 * 256
    pieces = (slice(0, cut), slice(cut, hidden))

    def run_chunk(step, unused):
        origin = source(step)

        @pl.when(step > 0)
        def _():
            landed(rows.at[origin, peer_half], pass_send.at[origin], pass_recv.at[origin], 0).wait_recv()
            landed(gates_in.at[origin], gates_send.at[0], gates_recv.at[origin], 0).wait_recv()

        gate_column = jnp.transpose(gates_in[origin])[:, 0:1]
        slot_grad[origin] = (upstream[origin].astype(jnp.float32) * gate_column).astype(
            jnp.bfloat16
        )

        def inside(piece):
            block = rows[origin]
            gate_pre = dot32(block, gate_w[:, piece])
            up_pre = dot32(block, up_w[:, piece])
            inner_grad = dot32(slot_grad[origin], down_w[:, piece])
            active, slope = gelu_parts(gate_pre)
            held = (active * up_pre).astype(jnp.bfloat16)
            inner[origin, :, piece] = held
            gate_grad[origin, :, piece] = (inner_grad * up_pre * slope).astype(jnp.bfloat16)
            up_grad[origin, :, piece] = (inner_grad * active).astype(jnp.bfloat16)
            return jnp.sum(active * up_pre * inner_grad, axis=1, keepdims=True)

        dots = inside(pieces[0])

        @pl.when(step < count - 1)
        def _():
            following = source(step + 1)
            landed(
                rows.at[following, my_half], rows_send.at[0], rows_recv.at[following], 0
            ).wait_recv()
            pass_copy(following).start()

        dots = dots + inside(pieces[1])
        dots_out[step] = jnp.transpose(jnp.broadcast_to(dots, (room, 128)))[0:8, :]

        @pl.when(step > 1)
        def _():
            send_back(step - 1)

        partial[step] = (
            dot_last(gate_grad[origin], gate_w[...]) + dot_last(up_grad[origin], up_w[...])
        ).astype(jnp.bfloat16)

        @pl.when(step > 0)
        def _():
            part_copy(step).start()
            dots_copy(step).start()

        return unused

    lax.fori_loop(0, count, run_chunk, 0)
    products = ((gate_w, rows, gate_grad), (up_w, rows, up_grad), (down_w, slot_grad, inner))

    def owner(turn):
        return turn % 2 * 2 + (core + 1 + turn // 2) % 2

    def to_core(number, turn):
        spot = pl.ds(pl.multiple_of(owner(turn) * deep, deep), deep)
        return pltpu.make_async_remote_copy(
            products[number][0].at[spot],
            core_in.at[number, turn],
            core_send.at[number, turn],
            core_recv.at[number, turn],
            device_id=core_peer,
            device_id_type=MESH,
        )

    def weigh(number):
        target, left, right = products[number]

        def block(turn, unused):
            spot = pl.ds(pl.multiple_of(owner(turn) * deep, deep), deep)
            lines = left[:, :, spot].reshape(count * room, deep)
            target[spot, :] = lax.dot_general(
                lines,
                right[...].reshape(count * room, hidden),
                (((0,), (0,)), ((), ())),
                preferred_element_type=jnp.float32,
            ).astype(jnp.bfloat16)

            @pl.when(turn < 2)
            def _():
                to_core(number, turn).start()

            return unused

        lax.fori_loop(0, 4, block, 0)

    def run_out(step, unused):
        outs[step] = dot_last(inner[step], down_w[...]).astype(jnp.bfloat16)
        return unused

    def to_chip(number):
        return remote(
            core_in.at[number, 1 - chip],
            chip_in.at[0],
            chip_send.at[number],
            chip_recv.at[number],
            chip_peer,
        )

    def over_chip(number):
        for turn in range(2):
            spot = pl.ds(pl.multiple_of(owner(turn + 2) * deep, deep), deep)
            to_core(number, turn).wait_recv()
            core_in[number, turn] = (
                products[number][0][spot, :].astype(jnp.float32)
                + core_in[number, turn].astype(jnp.float32)
            ).astype(jnp.bfloat16)
        if number == 0:
            to_chip(number).start()

    weigh(0)
    send_back(count - 1)
    lax.fori_loop(0, count, run_out, 0)
    stores = [pltpu.make_async_copy(outs.at[own], own_hbm, store_sem.at[0])]
    for turn in range(1, count):
        origin = partner(own, turn)
        for place, (spot, target) in enumerate(((my_half, mine_hbm), (peer_half, other_hbm))):
            sem = store_sem.at[8 + 2 * turn + place]
            source_ref = outs.at[origin, spot]
            stores.append(pltpu.make_async_copy(source_ref, target.at[turn - 1], sem))
    for store in stores:
        store.start()
    weigh(1)
    over_chip(0)

    def dots_landed(step, unused):
        origin = source(step)
        landed(dots_in.at[origin], dots_send.at[0], dots_recv.at[origin], 0).wait_recv()
        return unused

    def back_landed(step, unused):
        origin = source(step)
        landed(back.at[origin], back_send.at[0], back_recv.at[origin], 0).wait_recv()
        return unused

    lax.fori_loop(1, count, dots_landed, 0)
    dots_in[own] = dots_out[0]
    final_dots[0] = jnp.zeros((8, tokens), jnp.float32)
    for expert in range(count):
        column = jnp.transpose(dots_in[expert])[:, 0:1]
        slots = lax.broadcasted_iota(jnp.int32, (room, tokens), 0) + expert * room
        slots = slots.astype(jnp.float32)
        for choice in range(2):
            final_dots[0, choice : choice + 1, :] += jnp.sum(
                jnp.where(code_rows[choice : choice + 1, :] == slots, column, 0.0),
                axis=0,
                keepdims=True,
            )
    lax.fori_loop(1, count, back_landed, 0)
    blocks = final_out.shape[0]
    span = tokens // blocks

    def final_copy(block):
        return pltpu.make_async_remote_copy(
            final_out.at[block],
            final_in.at[block],
            final_send.at[block],
            final_recv.at[block],
            device_id=peer,
            device_id_type=MESH,
        )

    dots_final = pltpu.make_async_remote_copy(
        final_dots.at[0],
        final_dots.at[1],
        final_send.at[blocks],
        final_recv.at[blocks],
        device_id=peer,
        device_id_type=MESH,
    )
    dots_final.start()

    def combine(block, unused):
        spot = pl.ds(pl.multiple_of(block * span, span), span)

        def chosen(start, amount):
            slots = lax.broadcasted_iota(jnp.int32, (span, amount), 1) + start
            slots = slots.astype(jnp.float32)
            hit = (code_cols[spot, 0:1] == slots) | (code_cols[spot, 1:2] == slots)
            return jnp.where(hit, 1.0, 0.0).astype(jnp.bfloat16)

        total = dot32(chosen(own * room, room), partial[0])
        for step in range(1, count):
            origin = source(step)
            total = total + dot32(chosen(origin * room + side * half, half), back[origin])
        final_out[block] = total.astype(jnp.bfloat16)
        final_copy(block).start()
        return unused

    lax.fori_loop(0, blocks, combine, 0)

    weigh(2)

    def finish(block, unused):
        spot = pl.ds(pl.multiple_of(block * span, span), span)
        final_copy(block).wait_recv()
        row_grad[spot, :] = final_out[block].astype(jnp.float32) + final_in[block].astype(
            jnp.float32
        )
        return unused

    lax.fori_loop(0, blocks, finish, 0)
    dots_final.wait_recv()
    dot_rows[...] = final_dots[0] + final_dots[1]
    to_chip(0).wait_recv()
    for number in range(3):
        if number:
            over_chip(number)
        given = core_in.at[number, 1 - chip] if number else chip_in.at[0]
        for place, source_ref in enumerate((core_in.at[number, chip], given)):
            target = (kept_hbm.at[number], (gate_given, up_given, down_given)[number])[place]
            sem = store_sem.at[4 + 2 * number + place]
            store = pltpu.make_async_copy(source_ref, target, sem)
            store.start()
            stores.append(store)

    def drain(step, unused):
        rows_copy(step).wait_send()
        gates_copy(step).wait_send()
        pass_copy(source(step)).wait_send()
        part_copy(step).wait_send()
        back_copy(step).wait_send()
        dots_copy(step).wait_send()
        return unused

    lax.fori_loop(1, count, drain, 0)

    def drain_final(block, unused):
        final_copy(block).wait_send()
        return unused

    lax.fori_loop(0, blocks, drain_final, 0)
    dots_final.wait_send()
    for number in range(3):
        for turn in range(2):
            to_core(number, turn).wait_send()
        if number == 0:
            to_chip(number).wait_send()
    for store in stores:
        store.wait()


def run_experts(count, ctx_size, norm, gates, code_rows, code_cols, upstream, weights):
    tokens, width = norm.shape
    room = upstream.shape[1]
    half = room // 2
    hidden = weights[0].shape[1]
    blocks = 4
    low = jnp.bfloat16
    full = jnp.float32
    dma = pltpu.SemaphoreType.DMA
    return pl.pallas_call(
        partial(expert_exchange, count),
        out_shape=(
            jax.ShapeDtypeStruct((tokens, width), full),
            jax.ShapeDtypeStruct((8, tokens), full),
            jax.ShapeDtypeStruct((room, width), low),
            jax.ShapeDtypeStruct((count - 1, half, width), low),
            jax.ShapeDtypeStruct((count - 1, half, width), low),
            jax.ShapeDtypeStruct((3, width // ctx_size, hidden), low),
            *[jax.ShapeDtypeStruct((width // ctx_size, hidden), low)] * 3,
        ),
        in_specs=in_vmem(5) + [pl.BlockSpec(memory_space=pl.ANY)] * 12,
        out_specs=tuple(in_vmem(2) + [pl.BlockSpec(memory_space=pl.ANY)] * 7),
        scratch_shapes=[
            pltpu.VMEM((width, hidden), low),
            pltpu.VMEM((width, hidden), low),
            pltpu.VMEM((width, hidden), low),
            pltpu.VMEM((count, room, width), low),
            pltpu.VMEM((count - 1, half, width), low),
            pltpu.VMEM((count, 8, room), full),
            pltpu.VMEM((count - 1, 8, room), full),
            pltpu.VMEM((count, room, width), low),
            pltpu.VMEM((count, room, hidden), low),
            pltpu.VMEM((count, room, hidden), low),
            pltpu.VMEM((count, room, hidden), low),
            pltpu.VMEM((count, room, width), low),
            pltpu.VMEM((count, room, width), low),
            pltpu.VMEM((count, half, width), low),
            pltpu.VMEM((count, half, width), low),
            pltpu.VMEM((count, half, width), low),
            pltpu.VMEM((count, 8, room), full),
            pltpu.VMEM((count, 8, room), full),
            pltpu.VMEM((blocks, tokens // blocks, width), low),
            pltpu.VMEM((blocks, tokens // blocks, width), low),
            pltpu.VMEM((2, 8, tokens), full),
            pltpu.VMEM((3, 2, width // ctx_size, hidden), low),
            pltpu.VMEM((1, width // ctx_size, hidden), low),
            dma((12,)),
            dma((16,)),
            dma((count,)),
            dma((count,)),
            dma((count,)),
            dma((count,)),
            dma((count,)),
            dma((count,)),
            dma((count,)),
            dma((count,)),
            dma((count,)),
            dma((count,)),
            dma((count,)),
            dma((count,)),
            dma((blocks + 1,)),
            dma((blocks + 1,)),
            dma((3, 2)),
            dma((3, 2)),
            dma((3,)),
            dma((3,)),
        ],
        cost_estimate=estimate(110),
        compiler_params=pltpu.CompilerParams(
            collective_id=3, has_side_effects=True, vmem_limit_bytes=67043328
        ),
        name="expert_exchange",
    )(norm, gates, code_rows, code_cols, upstream, *weights)


def gather_project(
    count,
    w_query,
    w_key,
    w_value,
    w_out,
    gains,
    router,
    tokens,
    segment_ids,
    cotangent,
    routes,
    gate_hbm,
    up_hbm,
    down_hbm,
    full_hbm,
    packed,
    norm_hbm,
    segments,
    out_hbm,
    upstream_hbm,
    gate_hbm_low,
    up_hbm_low,
    down_hbm_low,
    gate_core,
    up_core,
    down_core,
    gate_chip,
    gate_far,
    codes,
    code_rows,
    extras,
    full,
    norm,
    out_full,
    upstream,
    gate_low,
    up_low,
    down_low,
    weight,
    out_weight,
    segment,
    outgoing,
    sent,
    experts_wide,
    line_send,
    line_recv,
    chip_send,
    chip_recv,
    core_send,
    core_recv,
    packed_send,
    packed_recv,
    segment_send,
    segment_recv,
    out_line_send,
    out_line_recv,
    out_chip_send,
    out_chip_recv,
    out_core_send,
    out_core_recv,
    out_pair_send,
    out_pair_recv,
    rows_send,
    rows_recv,
    pass_send,
    pass_recv,
    expert_send,
    expert_recv,
    load_sem,
    store_sem,
):
    own, ctx, side, chip, core = places()
    rows = weight.shape[0]
    ctx_size, here, share = packed.shape
    room = upstream.shape[1]
    half = room // 2
    chip_peer = (own, (1 - chip) * 2 + core, side)
    core_peer = (own, chip * 2 + 1 - core, side)
    pair = (own, ctx, 1 - side)
    loads = [
        pltpu.make_async_copy(source, experts_wide.at[number], load_sem.at[number])
        for number, source in enumerate((gate_hbm, up_hbm, down_hbm))
    ]
    for load in loads:
        load.start()
    stores = []

    def store(source, target):
        copy = pltpu.make_async_copy(source, target, store_sem.at[len(stores)])
        copy.start()
        stores.append(copy)

    lane = lax.broadcasted_iota(jnp.int32, (rows, LANES), 1)
    column = jnp.transpose(jnp.concatenate([gains[...], jnp.zeros((6, rows))], axis=0))
    extra = jnp.where(lane == 0, column[:, 0:1], 0.0)
    extra = jnp.where(lane == 1, column[:, 1:2], extra)
    for expert in range(router.shape[1]):
        extra = jnp.where(lane == 2 + expert, router[:, expert : expert + 1], extra)
    for place in range(ctx_size):
        for number, member in enumerate((w_query, w_key, w_value)):
            target = slice(place * share + number * LANES, place * share + (number + 1) * LANES)
            found = member[:, place * LANES : (place + 1) * LANES]
            weight[:, target] = found.astype(jnp.bfloat16)
    weight[:, ctx_size * share :] = extra.astype(jnp.bfloat16)
    out_weight[...] = w_out[...].astype(jnp.bfloat16)
    segment[...] = jnp.broadcast_to(segment_ids[...].astype(jnp.float32), segment.shape)
    greet(
        [(nearest(own, count, step), ctx, side) for step in range(1, count)]
        + [(own, across(chip, core, step), side) for step in range(3)]
        + [pair]
    )

    def block(shard, place):
        return pl.ds(pl.multiple_of((shard * ctx_size + place) * rows, rows), rows)

    def along(origin, forward):
        turn = 2 * forward - 1
        target = own + turn
        there = (target + count) // count * (1 - target // count)
        return (target + count) % count, there

    def onward(origin):
        return 1 - (origin - own + count) // count

    def to_line(origin, forward, source, number):
        target, _ = along(origin, forward)
        spot = full.at[block(origin, ctx)]
        return remote(
            source, spot, line_send.at[number], line_recv.at[origin], (target, ctx, side)
        )

    def in_line(copy_of, origin, forward, source, number, act):
        _, there = along(origin, forward)

        @pl.when(there == 1)
        def _():
            act(copy_of(origin, forward, source, number))

    def to_chip(shard, source):
        target = full.at[block(shard, ctx)]
        return remote(source, target, chip_send.at[shard], chip_recv.at[shard], chip_peer)

    def to_core(shard, place, source):
        index = shard * 2 + place // 2
        target = full.at[block(shard, place)]
        return remote(source, target, core_send.at[index], core_recv.at[index], core_peer)

    def to_segment(step):
        device = (own, across(chip, core, step), side)
        return remote(segment, segments.at[ctx], segment_send.at[step], segment_recv.at[ctx], device)

    def out_to_line(origin, forward, source, number):
        target, _ = along(origin, forward)
        spot = out_full.at[side, block(origin, ctx)]
        return remote(
            source, spot, out_line_send.at[number], out_line_recv.at[origin], (target, ctx, side)
        )

    def start(copy):
        copy.start()

    def sent_off(copy):
        copy.wait_send()

    def out_to_chip(shard, source):
        target = out_full.at[side, block(shard, ctx)]
        return remote(source, target, out_chip_send.at[shard], out_chip_recv.at[shard], chip_peer)

    def out_to_core(which, shard, place, source):
        index = shard * 2 + place // 2
        target = out_full.at[which, block(shard, place)]
        return remote(
            source, target, out_core_send.at[which, index], out_core_recv.at[which, index], core_peer
        )

    def out_to_pair(shard, place, source):
        index = shard * 2 + place // 2
        target = out_full.at[side, block(shard, place)]
        return remote(source, target, out_pair_send.at[index], out_pair_recv.at[index], pair)

    for forward in range(2):
        in_line(to_line, own, forward, weight, forward, start)
    to_chip(own, weight).start()
    to_core(own, ctx, weight).start()
    for step in range(3):
        to_segment(step).start()
    for forward in range(2):
        in_line(out_to_line, own, forward, out_weight, forward, start)
    out_to_core(side, own, ctx, out_weight).start()
    out_to_pair(own, ctx, out_weight).start()
    full[block(own, ctx), :] = weight[...]
    out_full[side, block(own, ctx), :] = out_weight[...]
    segments[ctx] = segment[...]

    lane = lax.broadcasted_iota(jnp.int32, (here, LANES), 1).astype(jnp.float32)
    first = routes[:, 0:1].astype(jnp.float32)
    second = routes[:, 1:2].astype(jnp.float32)
    named = jnp.where((first == lane) | (second == lane), 1.0, 0.0).astype(jnp.bfloat16)
    later = lax.broadcasted_iota(jnp.int32, (here, here), 0)
    before = later > lax.broadcasted_iota(jnp.int32, (here, here), 1)
    slots = dot32(jnp.where(before, 1.0, 0.0).astype(jnp.bfloat16), named) + room * lane
    first = jnp.sum(jnp.where(first == lane, slots, 0.0), axis=1, keepdims=True)
    second = jnp.sum(jnp.where(second == lane, slots, 0.0), axis=1, keepdims=True)
    codes[:, 0:1] = first
    codes[:, 1:2] = second
    both = jnp.where(lane == 0.0, first, jnp.where(lane == 1.0, second, -1.0))
    code_rows[...] = jnp.transpose(both)[0:8]
    my_half = pl.ds(pl.multiple_of(side * half, half), half)
    peer_half = pl.ds(pl.multiple_of((1 - side) * half, half), half)

    def picked(expert, start, amount):
        slots = lax.broadcasted_iota(jnp.int32, (amount, here), 0) + expert * room + start
        slots = slots.astype(jnp.float32)
        hit = (code_rows[0:1, :] == slots) | (code_rows[1:2, :] == slots)
        rows_found = jnp.where(hit, 1.0, 0.0).astype(jnp.bfloat16)
        return dot32(rows_found, cotangent[...]).astype(jnp.bfloat16)

    def to_expert(step):
        return remote(
            sent.at[step - 1],
            upstream.at[own, my_half],
            rows_send.at[step - 1],
            rows_recv.at[own],
            (nearest(own, count, step), ctx, side),
        )

    def pass_rows(shard):
        spot, target = upstream.at[shard, my_half], upstream_hbm.at[shard, my_half]
        return remote(spot, target, pass_send.at[shard], pass_recv.at[shard], pair)

    lows = (gate_low, up_low, down_low)
    near = (gate_core, up_core, down_core)
    for number, load in enumerate(loads):
        load.wait()
        lows[number][...] = experts_wide[number].astype(jnp.bfloat16)
        store(lows[number], (gate_hbm_low, up_hbm_low, down_hbm_low)[number])
    for step in range(1, count):
        sent[step - 1] = picked(nearest(own, count, step), side * half, half)
    upstream[own] = picked(own, 0, room)
    store(upstream.at[own], upstream_hbm.at[own])

    def to_near(number):
        return remote(
            lows[number], near[number], expert_send.at[number], expert_recv.at[number], core_peer
        )

    gate_over = remote(gate_low, gate_chip, expert_send.at[3], expert_recv.at[3], chip_peer)
    gate_far_copy = remote(gate_chip, gate_far, expert_send.at[4], expert_recv.at[4], core_peer)

    other_place = (1 - chip) * 2 + core

    def pass_line(step):
        shard = nearest(own, count, step)
        source = full.at[block(shard, ctx)]
        remote(source, source, line_send.at[0], line_recv.at[shard], core_peer).wait_recv()
        in_line(to_line, shard, onward(shard), source, 1 + step, start)
        to_chip(shard, source).start()
        to_core(shard, ctx, source).start()

    def pass_chip(step):
        shard = nearest(own, count, step)
        source = full.at[block(shard, other_place)]
        remote(source, source, chip_send.at[0], chip_recv.at[shard], core_peer).wait_recv()
        to_core(shard, other_place, source).start()

    pass_chip(0)
    for step in range(1, count):
        pass_line(step)
        pass_chip(step)
    out_to_chip(own, out_weight).start()
    for step in range(1, count):
        shard = nearest(own, count, step)
        source = out_full.at[side, block(shard, ctx)]
        remote(source, source, line_send.at[0], out_line_recv.at[shard], core_peer).wait_recv()
        in_line(out_to_line, shard, onward(shard), source, 1 + step, start)
        out_to_chip(shard, source).start()
        out_to_core(side, shard, ctx, source).start()
        out_to_pair(shard, ctx, source).start()

    for step in range(1, count):
        to_expert(step).start()
    gate_over.start()
    values = tokens[...].astype(jnp.float32)
    scale = lax.rsqrt(jnp.mean(values * values, axis=1, keepdims=True) + 1e-06)
    for shard in range(count):
        for place in range(2):
            spot = full.at[block(shard, place * 2 + 1 - core)]
            index = shard * 2 + place
            remote(spot, spot, core_send.at[0], core_recv.at[index], core_peer).wait_recv()
    store(full, full_hbm)
    extras[...] = full[:, ctx_size * share :]
    gain = jnp.transpose(extras[...].astype(jnp.float32))[0:1, :]
    norm[...] = (values * scale * gain).astype(jnp.bfloat16)
    store(norm, norm_hbm)

    def project(place):
        spot = pl.ds(pl.multiple_of(place * share, LANES), share)
        return dot32(norm[...], full[:, spot]).astype(jnp.bfloat16)

    def to_packed(step):
        device = (own, across(chip, core, step), side)
        return remote(
            outgoing.at[step], packed.at[ctx], packed_send.at[step], packed_recv.at[ctx], device
        )

    for step in range(3):
        outgoing[step] = project(across(chip, core, step))
        to_packed(step).start()
    packed[ctx] = project(ctx)
    for number in range(3):
        to_near(number).start()
    for step in range(count):
        shard = nearest(own, count, step)
        source = out_full.at[side, block(shard, other_place)]
        remote(source, source, line_send.at[0], out_chip_recv.at[shard], core_peer).wait_recv()
        out_to_core(side, shard, other_place, source).start()
        out_to_pair(shard, other_place, source).start()
    for step in range(1, count):
        shard = nearest(own, count, step)
        spot = upstream.at[shard, my_half]
        remote(spot, spot, rows_send.at[0], rows_recv.at[shard], pair).wait_recv()
        pass_rows(shard).start()
        store(spot, upstream_hbm.at[shard, my_half])
    gate_over.wait_recv()
    gate_far_copy.start()
    for step in range(count):
        shard = nearest(own, count, step)
        for place in (core, 2 + core):
            index = shard * 2 + place // 2
            source = out_full.at[1 - side, block(shard, place)]
            remote(source, source, line_send.at[0], out_pair_recv.at[index], pair).wait_recv()
            out_to_core(1 - side, shard, place, source).start()
    for step in range(3):
        place = across(chip, core, step)
        spot = packed.at[place]
        remote(spot, spot, packed_send.at[step], packed_recv.at[place], core_peer).wait_recv()
        spot = segments.at[place]
        remote(spot, spot, segment_send.at[step], segment_recv.at[place], core_peer).wait_recv()
    for which in (side, 1 - side):
        for shard in range(count):
            for place in range(2):
                spot = out_full.at[which, block(shard, place * 2 + 1 - core)]
                index = shard * 2 + place
                remote(
                    spot, spot, line_send.at[0], out_core_recv.at[which, index], core_peer
                ).wait_recv()
        store(out_full.at[which], out_hbm.at[which])
    for step in range(1, count):
        shard = nearest(own, count, step)
        spot = upstream_hbm.at[shard, peer_half]
        remote(spot, spot, pass_send.at[0], pass_recv.at[shard], pair).wait_recv()

    for copy in stores:
        copy.wait()
    for step in range(3):
        to_packed(step).wait_send()
        to_segment(step).wait_send()
        to_near(step).wait()
    gate_over.wait_send()
    gate_far_copy.wait()
    for forward in range(2):
        in_line(to_line, own, forward, weight, forward, sent_off)
        in_line(out_to_line, own, forward, out_weight, forward, sent_off)
    for step in range(count):
        shard = nearest(own, count, step)
        if step:
            in_line(to_line, shard, onward(shard), weight, 1 + step, sent_off)
            in_line(out_to_line, shard, onward(shard), out_weight, 1 + step, sent_off)
            to_expert(step).wait_send()
            pass_rows(shard).wait_send()
        to_chip(shard, weight).wait_send()
        out_to_chip(shard, out_weight).wait_send()
        for place in (ctx, other_place):
            to_core(shard, place, weight).wait_send()
            out_to_pair(shard, place, out_weight).wait_send()
            out_to_core(side, shard, place, out_weight).wait_send()
            out_to_core(1 - side, shard, place, out_weight).wait_send()


def run_gather(count, ctx_size, room, members, experts):
    rows, head_columns = members[0].shape
    here, width = members[6].shape
    share = 3 * head_columns // ctx_size
    columns = ctx_size * share + LANES
    dma = pltpu.SemaphoreType.DMA
    low = jnp.bfloat16
    deep, hidden = experts[0].shape
    return pl.pallas_call(
        partial(gather_project, count),
        out_shape=(
            jax.ShapeDtypeStruct((rows * count * ctx_size, columns), low),
            jax.ShapeDtypeStruct((ctx_size, here, share), low),
            jax.ShapeDtypeStruct((here, width), low),
            jax.ShapeDtypeStruct((ctx_size, 8, here), jnp.float32),
            jax.ShapeDtypeStruct((2, rows * count * ctx_size, head_columns), low),
            jax.ShapeDtypeStruct((count, room, width), low),
            *[jax.ShapeDtypeStruct((deep, hidden), low)] * 8,
            jax.ShapeDtypeStruct((here, 2), jnp.float32),
            jax.ShapeDtypeStruct((8, here), jnp.float32),
            jax.ShapeDtypeStruct((rows * count * ctx_size, LANES), low),
        ),
        in_specs=in_vmem(10) + [pl.BlockSpec(memory_space=pl.ANY)] * 3,
        out_specs=tuple(
            pl.BlockSpec(memory_space=pltpu.VMEM if number in (1, 3, 14, 15, 16) else pl.ANY)
            for number in range(17)
        ),
        scratch_shapes=[
            pltpu.VMEM((rows * count * ctx_size, columns), low),
            pltpu.VMEM((here, width), low),
            pltpu.VMEM((2, rows * count * ctx_size, head_columns), low),
            pltpu.VMEM((count, room, width), low),
            pltpu.VMEM((deep, hidden), low),
            pltpu.VMEM((deep, hidden), low),
            pltpu.VMEM((deep, hidden), low),
            pltpu.VMEM((rows, columns), low),
            pltpu.VMEM((rows, head_columns), low),
            pltpu.VMEM((8, here), jnp.float32),
            pltpu.VMEM((3, here, share), low),
            pltpu.VMEM((count - 1, room // 2, width), low),
            pltpu.VMEM((3, deep, hidden), jnp.float32),
            dma((count + 1,)),
            dma((count,)),
            dma((count,)),
            dma((count,)),
            dma((2 * count,)),
            dma((2 * count,)),
            dma((3,)),
            dma((ctx_size,)),
            dma((3,)),
            dma((ctx_size,)),
            dma((count + 1,)),
            dma((count,)),
            dma((count,)),
            dma((count,)),
            dma((2, 2 * count)),
            dma((2, 2 * count)),
            dma((2 * count,)),
            dma((2 * count,)),
            dma((count,)),
            dma((count,)),
            dma((count,)),
            dma((count,)),
            dma((5,)),
            dma((5,)),
            dma((3,)),
            dma((12,)),
        ],
        compiler_params=pltpu.CompilerParams(
            collective_id=1, has_side_effects=True, vmem_limit_bytes=60 * 2**20
        ),
        cost_estimate=estimate(60),
        name="gather_project",
    )(*members, *experts)


def attend_out(
    attended,
    tokens,
    out_w,
    extras,
    routes,
    hidden_one,
    norm_two,
    gates,
    attended_low,
    gathered,
    send,
    recv,
):
    own, ctx, side, chip, core = places()
    here, width = tokens.shape
    heads = attended.shape[2]
    peers = [
        (across(chip, core, step), (side + other) % 2)
        for other in range(2)
        for step in range(4)
        if (other, step) != (0, 3)
    ]
    peers = peers[:2] + peers[3:5] + peers[2:3] + peers[5:]
    greet([(own, place, which) for place, which in peers])
    columns = pl.ds(pl.multiple_of(ctx * heads, heads), heads)

    def copy(number):
        place, which = peers[number]
        return remote(
            attended.at[place],
            gathered.at[side, :, columns],
            send.at[number],
            recv.at[side, ctx],
            (own, place, which),
        )

    for number in range(len(peers)):
        copy(number).start()
    gathered[side, :, columns] = attended[ctx]
    for place, which in peers:
        spot = gathered.at[which, :, pl.ds(pl.multiple_of(place * heads, heads), heads)]
        remote(
            spot, spot, send.at[0], recv.at[which, place], (own, place, which)
        ).wait_recv()
    attended_low[...] = gathered[side]
    hidden = tokens[...].astype(jnp.float32) + (
        dot_last(gathered[0], out_w[0]) + dot_last(gathered[1], out_w[1])
    )
    hidden_one[...] = hidden
    scale = lax.rsqrt(jnp.mean(hidden * hidden, axis=1, keepdims=True) + 1e-06)
    gain = jnp.transpose(extras[...].astype(jnp.float32))[1:2, :]
    norm = (hidden * scale * gain).astype(jnp.bfloat16)
    norm_two[...] = norm
    logits = dot32(norm, extras[...])
    lane = lax.broadcasted_iota(jnp.int32, (here, LANES), 1)
    first = jnp.sum(jnp.where(lane == routes[:, 0:1] + 2, logits, 0.0), axis=1, keepdims=True)
    second = jnp.sum(jnp.where(lane == routes[:, 1:2] + 2, logits, 0.0), axis=1, keepdims=True)
    highest = jnp.maximum(first, second)
    first, second = jnp.exp(first - highest), jnp.exp(second - highest)
    gates[:, 0:1] = first / (first + second)
    gates[:, 1:2] = second / (first + second)
    for number in range(len(peers)):
        copy(number).wait_send()


def run_attend_out(attended, tokens, out_w, extras, routes):
    here, width = tokens.shape
    heads = out_w.shape[2]
    low, wide = jnp.bfloat16, jnp.float32
    return pl.pallas_call(
        attend_out,
        out_shape=(
            jax.ShapeDtypeStruct((here, width), wide),
            jax.ShapeDtypeStruct((here, width), low),
            jax.ShapeDtypeStruct((here, 2), wide),
            jax.ShapeDtypeStruct((here, heads), low),
        ),
        in_specs=in_vmem(5),
        out_specs=tuple(in_vmem(4)),
        scratch_shapes=[
            pltpu.VMEM((2, here, heads), low),
            pltpu.SemaphoreType.DMA((7,)),
            pltpu.SemaphoreType.DMA((2, 4)),
        ],
        compiler_params=pltpu.CompilerParams(
            collective_id=4, has_side_effects=True, vmem_limit_bytes=40 * 2**20
        ),
        cost_estimate=estimate(25),
        name="attend_out",
    )(attended, tokens, out_w, extras, routes)


def attend_back(
    rows_grad,
    dot_rows,
    gates,
    routes,
    extras,
    hidden_one,
    cotangent,
    norm_two,
    out_w,
    hidden_grad,
    branch_grad,
    heads_grad,
    small,
    outgoing,
    send,
    recv,
):
    own, ctx, side, chip, core = places()
    here, width = hidden_one.shape
    heads = heads_grad.shape[2]
    greet([(own, across(chip, core, step), side) for step in range(3)])
    lane = lax.broadcasted_iota(jnp.int32, (here, LANES), 1)
    dots = jnp.transpose(dot_rows[...])
    total = dots[:, 0:1] + dots[:, 1:2]
    logit_grad = jnp.zeros((here, LANES), jnp.float32)
    for choice in range(TOP):
        shift = dots[:, choice : choice + 1] - gates[:, choice : choice + 1] * total
        logit_grad = jnp.where(lane == routes[:, choice : choice + 1] + 2, shift, logit_grad)
    extra = extras[...].astype(jnp.float32)
    norm_grad = rows_grad[...] + lax.dot_general(
        logit_grad,
        extra,
        (((1,), (1,)), ((), ())),
        precision=lax.Precision.HIGHEST,
        preferred_element_type=jnp.float32,
    )
    hidden = hidden_one[...]
    scale = lax.rsqrt(jnp.mean(hidden * hidden, axis=1, keepdims=True) + 1e-06)
    normal = hidden * scale
    spread = norm_grad * jnp.transpose(extra)[1:2, :]
    found = cotangent[...].astype(jnp.float32) + scale * (
        spread - normal * jnp.mean(spread * normal, axis=1, keepdims=True)
    )
    hidden_grad[...] = found
    branch_grad[...] = found.astype(jnp.bfloat16)

    def project(place):
        columns = pl.ds(pl.multiple_of(place * heads, heads), heads)
        return dot32(branch_grad[...], out_w[side, :, columns]).astype(jnp.bfloat16)

    def copy(step):
        place = across(chip, core, step)
        return remote(
            outgoing.at[step], heads_grad.at[ctx], send.at[step], recv.at[ctx], (own, place, side)
        )

    for step in range(3):
        outgoing[step] = project(across(chip, core, step))
        copy(step).start()
    heads_grad[ctx] = project(ctx)
    gain_row = jnp.sum(norm_grad * normal, axis=0, keepdims=True)
    routed = jnp.dot(
        jnp.transpose(logit_grad),
        norm_two[...].astype(jnp.float32),
        precision=lax.Precision.HIGHEST,
        preferred_element_type=jnp.float32,
    )
    line = lax.broadcasted_iota(jnp.int32, (8, width), 0)
    small[...] = jnp.where(line == 1, gain_row, routed[0:8])
    for step in range(3):
        place = across(chip, core, step)
        spot = heads_grad.at[place]
        remote(spot, spot, send.at[0], recv.at[place], (own, place, side)).wait_recv()
    for step in range(3):
        copy(step).wait_send()


def run_attend_back(
    rows_grad, dot_rows, gates, routes, extras, hidden_one, cotangent, norm_two, out_w
):
    here, width = hidden_one.shape
    low, wide = jnp.bfloat16, jnp.float32
    heads = out_w.shape[2] // 4
    return pl.pallas_call(
        attend_back,
        out_shape=(
            jax.ShapeDtypeStruct((here, width), wide),
            jax.ShapeDtypeStruct((here, width), low),
            jax.ShapeDtypeStruct((4, here, heads), low),
            jax.ShapeDtypeStruct((8, width), wide),
        ),
        in_specs=in_vmem(9),
        out_specs=tuple(in_vmem(4)),
        scratch_shapes=[
            pltpu.VMEM((3, here, heads), low),
            pltpu.SemaphoreType.DMA((3,)),
            pltpu.SemaphoreType.DMA((4,)),
        ],
        compiler_params=pltpu.CompilerParams(
            collective_id=5, has_side_effects=True, vmem_limit_bytes=48 * 2**20
        ),
        cost_estimate=estimate(20),
        name="attend_back",
    )(rows_grad, dot_rows, gates, routes, extras, hidden_one, cotangent, norm_two, out_w)


def gradient_return(
    count,
    packed_grad,
    full_hbm,
    norm,
    tokens,
    bias_line,
    own_hbm,
    mine,
    theirs,
    gates,
    codes,
    branch_grad,
    attended,
    small,
    one_hbm,
    grad_hbm,
    extras,
    mixed,
    input_grad,
    query_grad,
    key_grad,
    value_grad,
    bias_grad,
    gain_grad,
    out_grad,
    mixture,
    mixture_in,
    full,
    own_out,
    hidden_one,
    hidden_grad,
    mix_out,
    mix_in,
    incoming,
    norm_t,
    outgoing,
    side_out,
    side_in,
    spread,
    core_in,
    chip_out,
    chip_in,
    line_out,
    line_in,
    out_going,
    out_core_in,
    out_spread,
    out_chip_out,
    out_chip_in,
    out_line_out,
    out_line_in,
    bias_out,
    bias_in,
    spread_gain,
    grad_send,
    grad_recv,
    side_send,
    side_recv,
    core_send,
    core_recv,
    chip_send,
    chip_recv,
    line_send,
    line_recv,
    bias_send,
    bias_recv,
    mixture_sem,
    mix_send,
    mix_recv,
    load_sem,
):
    own, ctx, side, chip, core = places()
    ctx_size, here, share = packed_grad.shape
    width = norm.shape[1]
    halves = 2
    part = here // halves
    groups = ctx_size
    pair = (own, ctx, 1 - side)
    chip_peer = (own, (1 - chip) * 2 + core, side)
    core_peer = (own, chip * 2 + 1 - core, side)
    others = [
        (nearest(own, count, step), across(chip, core, turn), side)
        for step in range(count)
        for turn in range(4)
        if (step, turn) != (0, 3)
    ]
    pairs = ((full_hbm, full), (own_hbm, own_out), (grad_hbm, hidden_grad), (one_hbm, hidden_one))
    loads = [
        pltpu.make_async_copy(source, target, load_sem.at[number])
        for number, (source, target) in enumerate(pairs)
    ]
    for load in loads:
        load.start()
    greet(others + [pair])

    def to_owner(step, piece):
        place = across(chip, core, step)
        spot = pl.ds(piece * part, part)
        return remote(
            packed_grad.at[place, spot],
            incoming.at[ctx, spot],
            grad_send.at[step, piece],
            grad_recv.at[ctx, piece],
            (own, place, side),
        )

    for piece in range(halves):
        for step in range(3):
            to_owner(step, piece).start()
    incoming[ctx] = packed_grad[ctx]

    mixture_copy = remote(mixture, mixture_in, mixture_sem.at[0], mixture_sem.at[1], pair)

    def mixing(start, amount):
        slots = lax.broadcasted_iota(jnp.int32, (here, amount), 1) + start
        slots = slots.astype(jnp.float32)
        held = jnp.where(codes[:, 0:1] == slots, gates[:, 0:1], 0.0)
        held = held + jnp.where(codes[:, 1:2] == slots, gates[:, 1:2], 0.0)
        return held.astype(jnp.bfloat16)

    room, half = own_out.shape[0], mine.shape[1]

    def to_tokens(turn):
        return remote(
            mix_out.at[turn],
            mix_in.at[turn],
            mix_send.at[turn],
            mix_recv.at[turn],
            (partner(own, turn + 1), ctx, side),
        )

    for turn in range(count - 1):
        mix_out[turn] = (
            mine[turn].astype(jnp.float32) + theirs[turn].astype(jnp.float32)
        ).astype(jnp.bfloat16)
        to_tokens(turn).start()

    def mix():
        loads[1].wait()
        total = dot32(mixing(own * room, room), own_out[...])
        for turn in range(count - 1):
            to_tokens(turn).wait_recv()
            start = partner(own, turn + 1) * room + side * half
            total = total + dot32(mixing(start, half), mix_in[turn])
        mixture[...] = total.astype(jnp.bfloat16)
        mixture_copy.start()

    span = bias_line.shape[1]
    index = lax.broadcasted_iota(jnp.int32, (span, LANES), 0)
    relative = jnp.where(index < span // 2, -index, span - index)
    bucket = lax.broadcasted_iota(jnp.int32, (span, LANES), 1)
    onehot = jnp.where(bucket_ids(relative) == bucket, 1.0, 0.0)
    sums = jnp.dot(
        bias_line[...], onehot, precision=lax.Precision.HIGHEST, preferred_element_type=jnp.float32
    )
    far = jnp.sum(bias_line[...], axis=1, keepdims=True)
    lane = lax.broadcasted_iota(jnp.int32, (2, LANES), 1)
    total = sums[0:2] + jnp.where(lane == NBUCK // 2 - 1, far[2:4], 0.0)
    total = total + jnp.where(lane == NBUCK - 1, far[4:6], 0.0)
    bias_sum = jnp.concatenate([total, jnp.zeros((6, LANES), jnp.float32)], axis=0)

    def to_bias(number):
        return remote(
            bias_out.at[number],
            bias_in.at[own, ctx],
            bias_send.at[number],
            bias_recv.at[own, ctx],
            others[number],
        )

    stages = [
        (
            outgoing.at[group],
            core_in.at[group],
            spread.at[group],
            chip_out.at[group],
            chip_in.at[group],
            line_out.at[group],
            line_in.at[group],
            None,
        )
        for group in range(groups)
    ]
    stages.append(
        (
            out_going,
            out_core_in,
            out_spread,
            out_chip_out,
            out_chip_in,
            out_line_out,
            out_line_in,
            None,
        )
    )
    rows = norm_t.shape[0] // (count * ctx_size)

    def to_core(group):
        source, target = stages[group][0].at[:, 1 - core], stages[group][1]
        return remote(source, target, core_send.at[group], core_recv.at[group], core_peer)

    def to_chip(group):
        source, target = stages[group][3], stages[group][4]
        return remote(source, target, chip_send.at[group], chip_recv.at[group], chip_peer)

    def to_line(group, step):
        shard = nearest(own, count, step)
        source, target = stages[group][5].at[shard], stages[group][6].at[own]
        send, recv = line_send.at[group, step], line_recv.at[group, own]
        return remote(source, target, send, recv, (shard, ctx, side))

    def contract(group):
        found = dot32(norm_t[...], incoming[group] if group < groups else attended[...])
        found = found.reshape(count * 2, 2, rows, found.shape[1])
        stages[group][0][...] = found.astype(jnp.bfloat16)
        to_core(group).start()

    def over_chip(group):
        to_core(group).wait_recv()
        source, arrived, summed, target = stages[group][:4]
        found = source[:, core].astype(jnp.float32) + arrived[...].astype(jnp.float32)
        summed[...] = found.reshape(count, 2, rows, found.shape[2])
        target[...] = summed[:, 1 - chip].astype(jnp.bfloat16)
        to_chip(group).start()

    def over_line(group):
        to_chip(group).wait_recv()
        found = stages[group][2][:, chip] + stages[group][4][...].astype(jnp.float32)
        stages[group][5][...] = found.astype(jnp.bfloat16)
        for step in range(1, count):
            to_line(group, step).start()

    def collect(group):
        total = stages[group][5][own].astype(jnp.float32)
        for step in range(1, count):
            shard = nearest(own, count, step)
            spot = stages[group][6].at[shard]
            remote(
                spot, spot, line_send.at[group, 0], line_recv.at[group, shard], pair
            ).wait_recv()
            total = total + spot[...].astype(jnp.float32)
        if group == groups:
            out_grad[...] = total
        else:
            columns = slice(group * LANES, (group + 1) * LANES)
            for number, target in enumerate((query_grad, key_grad, value_grad)):
                target[:, columns] = total[:, number * LANES : (number + 1) * LANES]

    norm_t[...] = jnp.transpose(branch_grad[...].astype(jnp.float32)).astype(jnp.bfloat16)
    contract(groups)
    norm_t[...] = jnp.transpose(norm[...].astype(jnp.float32)).astype(jnp.bfloat16)

    def to_side(piece):
        return remote(
            side_out.at[piece],
            side_in.at[piece],
            side_send.at[piece],
            side_recv.at[piece],
            pair,
        )

    values = tokens[...].astype(jnp.float32)
    scale = lax.rsqrt(jnp.mean(values * values, axis=1, keepdims=True) + 1e-06)
    normal = values * scale
    first_gain = jnp.transpose(extras[...].astype(jnp.float32))[0:1, :]
    loads[0].wait()
    for piece in range(halves):
        spot = pl.ds(piece * part, part)
        total = jnp.zeros((part, width), jnp.float32)
        for step in (3, 2, 0, 1):
            place = across(chip, core, step)
            if step != 3:
                target = incoming.at[place, spot]
                remote(
                    target, target, grad_send.at[0, 0], grad_recv.at[place, piece], pair
                ).wait_recv()
            columns = pl.ds(pl.multiple_of(place * share, LANES), share)
            total = total + dot_last(incoming[place, spot, :], full[:, columns])
        side_out[piece] = total.astype(jnp.bfloat16)
        to_side(piece).start()

    def finish_sides():
        loads[2].wait()
        gain = jnp.zeros((1, width), jnp.float32)
        for piece in range(halves):
            to_side(piece).wait_recv()
            total = side_out[piece].astype(jnp.float32) + side_in[piece].astype(jnp.float32)
            lines = slice(piece * part, (piece + 1) * part)
            upright = normal[lines]
            gain = gain + jnp.sum(total * upright, axis=0, keepdims=True)
            total = total * first_gain
            total = total - upright * jnp.mean(total * upright, axis=1, keepdims=True)
            input_grad[lines, :] = (hidden_grad[lines, :] + scale[lines] * total).astype(
                jnp.bfloat16
            )
        spread_gain[...] = small[...]
        spread_gain[0:1, :] = gain

        def message(shard, place):
            lanes = pl.ds(pl.multiple_of((shard * 2 + place // 2) * LANES, LANES), LANES)
            return jnp.concatenate([bias_sum, spread_gain[:, lanes]], axis=0)

        for number, (shard, place, _) in enumerate(others):
            bias_out[number] = message(shard, place)
            to_bias(number).start()
        bias_in[own, ctx] = message(own, ctx)

    over_chip(groups)
    for moment in range(groups + 3):
        if moment < groups:
            contract(moment)
        if moment == 0:
            over_line(groups)
        if 0 <= moment - 1 < groups:
            over_chip(moment - 1)
        if 0 <= moment - 2 < groups:
            over_line(moment - 2)
        if moment == 2:
            mix()
        if moment == groups:
            finish_sides()
            collect(groups)
        if 0 <= moment - 3 < groups:
            collect(moment - 3)

    for number, (shard, place, _) in enumerate(others):
        spot = bias_in.at[shard, place]
        remote(spot, spot, bias_send.at[0], bias_recv.at[shard, place], pair).wait_recv()
    for place in range(ctx_size):
        total = bias_in[0, place]
        for shard in range(1, count):
            total = total + bias_in[shard, place]
        bias_grad[place] = total[:8]
        gain_total = total[8:] if place == 0 else gain_total + total[8:]
    gain_grad[...] = gain_total

    mixture_copy.wait()
    loads[3].wait()
    for turn in range(count - 1):
        to_tokens(turn).wait_send()
    mixed[...] = (
        hidden_one[...] + (mixture[...].astype(jnp.float32) + mixture_in[...].astype(jnp.float32))
    ).astype(jnp.bfloat16)
    for number in range(len(others)):
        to_bias(number).wait_send()
    for piece in range(halves):
        to_side(piece).wait_send()
        for step in range(3):
            to_owner(step, piece).wait_send()
    for group in range(groups + 1):
        to_core(group).wait_send()
        to_chip(group).wait_send()
        for step in range(1, count):
            to_line(group, step).wait_send()


def run_return(
    count,
    packed_grad,
    full,
    norm,
    tokens,
    bias_line,
    outs,
    gates,
    codes,
    branch_grad,
    attended,
    small,
    hidden_one,
    hidden_grad,
    extras,
):
    ctx_size, here, share = packed_grad.shape
    width = norm.shape[1]
    rows = width // (count * ctx_size)
    low, wide = jnp.bfloat16, jnp.float32
    dma = pltpu.SemaphoreType.DMA
    columns = share
    out_columns = attended.shape[1]
    return pl.pallas_call(
        partial(gradient_return, count),
        out_shape=(
            jax.ShapeDtypeStruct((here, width), low),
            jax.ShapeDtypeStruct((here, width), low),
            *[jax.ShapeDtypeStruct((rows, ctx_size * LANES), wide)] * 3,
            jax.ShapeDtypeStruct((ctx_size, 8, LANES), wide),
            jax.ShapeDtypeStruct((8, LANES), wide),
            jax.ShapeDtypeStruct((rows, out_columns), wide),
        ),
        in_specs=[
            pl.BlockSpec(memory_space=pl.ANY if number in (1, 5, 13, 14) else pltpu.VMEM)
            for number in range(16)
        ],
        out_specs=tuple(in_vmem(8)),
        scratch_shapes=[
            pltpu.VMEM((here, width), low),
            pltpu.VMEM((here, width), low),
            pltpu.VMEM(full.shape, low),
            pltpu.VMEM(outs[0].shape, low),
            pltpu.VMEM((here, width), wide),
            pltpu.VMEM((here, width), wide),
            pltpu.VMEM(outs[1].shape, low),
            pltpu.VMEM(outs[1].shape, low),
            pltpu.VMEM((ctx_size, here, share), low),
            pltpu.VMEM((width, here), low),
            pltpu.VMEM((ctx_size, count * 2, 2, rows, columns), low),
            pltpu.VMEM((2, here // 2, width), low),
            pltpu.VMEM((2, here // 2, width), low),
            pltpu.VMEM((ctx_size, count, 2, rows, columns), wide),
            pltpu.VMEM((ctx_size, count * 2, rows, columns), low),
            pltpu.VMEM((ctx_size, count, rows, columns), low),
            pltpu.VMEM((ctx_size, count, rows, columns), low),
            pltpu.VMEM((ctx_size, count, rows, columns), low),
            pltpu.VMEM((ctx_size, count, rows, columns), low),
            pltpu.VMEM((count * 2, 2, rows, out_columns), low),
            pltpu.VMEM((count * 2, rows, out_columns), low),
            pltpu.VMEM((count, 2, rows, out_columns), wide),
            pltpu.VMEM((count, rows, out_columns), low),
            pltpu.VMEM((count, rows, out_columns), low),
            pltpu.VMEM((count, rows, out_columns), low),
            pltpu.VMEM((count, rows, out_columns), low),
            pltpu.VMEM((15, 16, LANES), wide),
            pltpu.VMEM((count, ctx_size, 16, LANES), wide),
            pltpu.VMEM((8, width), wide),
            dma((3, 2)),
            dma((ctx_size, 2)),
            dma((2,)),
            dma((2,)),
            dma((ctx_size + 1,)),
            dma((ctx_size + 1,)),
            dma((ctx_size + 1,)),
            dma((ctx_size + 1,)),
            dma((ctx_size + 1, count)),
            dma((ctx_size + 1, count)),
            dma((15,)),
            dma((count, ctx_size)),
            dma((2,)),
            dma((3,)),
            dma((3,)),
            dma((4,)),
        ],
        compiler_params=pltpu.CompilerParams(
            collective_id=2, has_side_effects=True, vmem_limit_bytes=60 * 2**20
        ),
        cost_estimate=estimate(45),
        name="gradient_return",
    )(
        packed_grad,
        full,
        norm,
        tokens,
        bias_line,
        *outs,
        gates,
        codes,
        branch_grad,
        attended,
        small,
        hidden_one,
        hidden_grad,
        extras,
    )


def swap_sides(member):
    return lax.ppermute(member, "tensor", [(0, 1), (1, 0)])


def exchange(member, axis):
    return lax.all_to_all(member, axis, split_axis=0, concat_axis=0, tiled=True)


def slot_codes(routes, experts, room):
    tokens = routes.shape[0]
    picks = routes[:, :, None] == jnp.arange(experts, dtype=jnp.int32)[None, None, :]
    named = jnp.sum(picks, axis=1).astype(jnp.bfloat16)
    index = jnp.arange(tokens, dtype=jnp.int32)
    before = (index[:, None] > index[None, :]).astype(jnp.bfloat16)
    rank = jnp.dot(before, named, preferred_element_type=jnp.float32)
    slots = rank + room * jnp.arange(experts, dtype=jnp.float32)[None, :]
    return picks, jnp.sum(jnp.where(picks, slots[:, None, :], 0.0), axis=2)


def experts_apart(norm_two, upstream, gates, codes, room, count, weights):
    tokens, width = norm_two.shape
    codes = codes.astype(jnp.int32).reshape(-1)
    shaped = (count, room, width)

    def sent(member):
        slots = jnp.zeros((count * room, width), jnp.bfloat16).at[codes].set(member)
        return exchange(slots.reshape(shaped), "shard").reshape(-1, width)

    slot_rows = sent(jnp.repeat(norm_two, TOP, axis=0))
    slot_grads = sent(
        (gates[:, :, None] * upstream[:, None, :]).reshape(-1, width).astype(jnp.bfloat16)
    )
    gate_mat, up_mat, down_mat = weights
    gate_pre = dot32(slot_rows, gate_mat)
    up_pre = dot32(slot_rows, up_mat)
    activated, slope = gelu_parts(gate_pre)
    inner = (activated * up_pre).astype(jnp.bfloat16)
    expert_out = contract_cols(inner, down_mat)
    inner_grad = dot32(slot_grads, down_mat)
    gate_grad = (inner_grad * up_pre * slope).astype(jnp.bfloat16)
    up_grad = (inner_grad * activated).astype(jnp.bfloat16)
    rows_grad = contract_cols(gate_grad, gate_mat) + contract_cols(up_grad, up_mat)

    def returned(member):
        member = lax.psum(member.astype(jnp.bfloat16), "tensor").reshape(shaped)
        member = exchange(member, "shard").reshape(-1, width)[codes]
        return member.astype(jnp.float32).reshape(tokens, TOP, width)

    per_choice = returned(expert_out)
    mixture = jnp.sum(gates[:, :, None] * per_choice, axis=1)
    dots = gates * jnp.sum(per_choice * upstream[:, None, :], axis=2)
    norm_grad = jnp.sum(returned(rows_grad), axis=1)
    return mixture, dots, norm_grad, slot_rows, slot_grads, inner, gate_grad, up_grad


def local_general(
    tokens_in,
    cotangent,
    segment_ids,
    live_blocks,
    routes,
    w_query,
    w_key,
    w_value,
    w_out,
    rel_bias,
    attn_gain,
    ffn_gain,
    router,
    w_gate,
    w_up,
    w_down,
):
    rows_here, width = tokens_in.shape
    ctx_size = lax.axis_size("ctx")
    side_count = lax.axis_size("tensor")
    ctx_index = lax.axis_index("ctx")
    side = lax.axis_index("tensor")
    head_cols = w_query.shape[1]
    share = head_cols // ctx_size
    experts = router.shape[1]
    room = max(2, 3 * rows_here // experts)

    picks, codes = slot_codes(routes, experts, room)

    def by_owner(member):
        return member.reshape(member.shape[0], ctx_size, share)

    packed_rows = jnp.stack([by_owner(w_query), by_owner(w_key), by_owner(w_value)], axis=2)
    gathered = lax.all_gather(
        jnp.concatenate(
            [
                packed_rows.reshape(w_query.shape[0], -1),
                attn_gain[:, None],
                ffn_gain[:, None],
                router,
            ],
            axis=1,
        ).astype(jnp.bfloat16),
        ("shard", "ctx"),
        axis=0,
        tiled=True,
    )
    packed_w = gathered[:, : 3 * head_cols]
    gain_one = gathered[:, 3 * head_cols]
    gain_two = gathered[:, 3 * head_cols + 1]
    router_w = gathered[:, 3 * head_cols + 2 :]
    out_w = lax.all_gather(w_out.astype(jnp.bfloat16), ("shard", "ctx", "tensor"), axis=0)
    out_w = out_w.reshape(-1, side_count, w_out.shape[0], head_cols)
    out_w = jnp.transpose(out_w, (0, 2, 1, 3)).reshape(width, side_count * head_cols)
    expert_weights = tuple(
        lax.all_gather(member.astype(jnp.bfloat16), "ctx", axis=1, tiled=True)[0]
        for member in (w_gate, w_up, w_down)
    )

    inputs = tokens_in.astype(jnp.float32)
    scale_one = lax.rsqrt(jnp.mean(inputs * inputs, axis=1, keepdims=True) + 1e-06)
    normal_one = inputs * scale_one
    norm_one = (normal_one * gain_one.astype(jnp.float32)).astype(jnp.bfloat16)
    packed = dot32(norm_one, packed_w).astype(jnp.bfloat16)
    packed = jnp.transpose(packed.reshape(rows_here, ctx_size, 3 * share), (1, 0, 2))
    packed = exchange(packed, "ctx").reshape(ctx_size * rows_here, 3 * share)
    segments = lax.all_gather(segment_ids.reshape(-1), "ctx", axis=0, tiled=True)
    alive = live_tiles(segments, live_blocks[0])
    segment_row = segments.astype(jnp.float32)[None]
    pair_heads = share // HEAD
    own_bias = lax.dynamic_slice_in_dim(rel_bias, ctx_index * pair_heads, pair_heads, 1)
    buckets = span_buckets()
    line = jnp.dot(own_bias.T, buckets.T, precision=lax.Precision.HIGHEST)
    attended, attended_t, log_sum = run_forward(alive, packed, segment_row, line)
    attended = attended.reshape(ctx_size, 1, rows_here, share)
    attended = jnp.broadcast_to(attended, (ctx_size, side_count, rows_here, share))
    attended = exchange(attended.reshape(-1, rows_here, share), ("ctx", "tensor"))
    attended = attended.reshape(ctx_size, side_count, rows_here, share)
    attended = jnp.transpose(attended, (2, 1, 0, 3))
    attended_low = lax.dynamic_index_in_dim(attended, side, 1, False).reshape(rows_here, head_cols)
    attended = attended.reshape(rows_here, side_count * head_cols)
    hidden_one = inputs + contract_cols(attended, out_w)
    scale_two = lax.rsqrt(jnp.mean(hidden_one * hidden_one, axis=1, keepdims=True) + 1e-06)
    normal_two = hidden_one * scale_two
    norm_two = (normal_two * gain_two.astype(jnp.float32)).astype(jnp.bfloat16)
    logits = dot32(norm_two, router_w)
    chosen = jnp.sum(jnp.where(picks, logits[:, None, :], 0.0), axis=2)
    gates = jax.nn.softmax(chosen, axis=1)
    upstream = cotangent.astype(jnp.float32)
    results = experts_apart(norm_two, upstream, gates, codes, room, experts, expert_weights)
    mixture, gate_dots, norm_grad, slot_rows, slot_grads, inner, gate_grad, up_grad = results
    weight_grads = lax.psum_scatter(
        jnp.stack(
            [
                contract_rows(slot_rows, gate_grad),
                contract_rows(slot_rows, up_grad),
                contract_rows(slot_grads, inner),
            ],
            axis=1,
        ).astype(jnp.bfloat16),
        "ctx",
        scatter_dimension=0,
        tiled=True,
    ).astype(jnp.float32)
    mixed = (hidden_one + mixture).astype(jnp.bfloat16)
    gate_shift = gate_dots - gates * jnp.sum(gate_dots, axis=1, keepdims=True)
    logit_grad = jnp.sum(jnp.where(picks, gate_shift[:, :, None], 0.0), axis=1)
    router_f = router_w.astype(jnp.float32)
    norm_grad = norm_grad + jnp.dot(logit_grad, router_f.T, precision=lax.Precision.HIGHEST)
    spread_two = norm_grad * gain_two.astype(jnp.float32)
    hidden_grad = upstream + scale_two * (
        spread_two - normal_two * jnp.mean(spread_two * normal_two, axis=1, keepdims=True)
    )
    branch_grad = hidden_grad.astype(jnp.bfloat16)
    own_out_w = lax.dynamic_slice_in_dim(out_w, side * head_cols, head_cols, 1)
    grad_heads = dot32(branch_grad, own_out_w).astype(jnp.bfloat16)
    grad_heads = jnp.transpose(grad_heads.reshape(rows_here, ctx_size, share), (1, 0, 2))
    grad_heads = exchange(grad_heads, "ctx").reshape(-1, share)
    packed_grad, bias_line = run_backward(
        alive, packed, segment_row, line, grad_heads, attended_t, log_sum
    )
    own_grad = jnp.dot(buckets.T, bias_line[:pair_heads].T, precision=lax.Precision.HIGHEST)
    far = jnp.sum(bias_line[pair_heads : 3 * pair_heads], axis=1)
    half = NBUCK // 2
    own_grad = own_grad.at[half - 1].add(far[:pair_heads]).at[NBUCK - 1].add(far[pair_heads:])
    bias_acc = lax.dynamic_update_slice_in_dim(
        jnp.zeros(rel_bias.shape, jnp.float32), own_grad, ctx_index * pair_heads, 1
    )
    packed_grad = exchange(packed_grad.reshape(ctx_size, rows_here, 3 * share), "ctx")
    packed_grad = jnp.transpose(packed_grad, (1, 0, 2)).reshape(rows_here, 3 * head_cols)
    norm_one_grad = contract_cols(packed_grad, packed_w).astype(jnp.bfloat16)
    norm_one_grad = norm_one_grad.astype(jnp.float32) + swap_sides(norm_one_grad).astype(
        jnp.float32
    )
    spread_one = norm_one_grad * gain_one.astype(jnp.float32)
    input_grad = hidden_grad + scale_one * (
        spread_one - normal_one * jnp.mean(spread_one * normal_one, axis=1, keepdims=True)
    )
    first_gain = jnp.sum(norm_one_grad * normal_one, axis=0)[:, None]
    second_gain = jnp.sum(norm_grad * normal_two, axis=0)[:, None]
    router_part = jnp.dot(
        norm_two.astype(jnp.float32).T, logit_grad, precision=lax.Precision.HIGHEST
    )
    reduced = lax.psum_scatter(
        jnp.concatenate(
            [
                contract_rows(norm_one, packed_grad),
                contract_rows(branch_grad, attended_low),
                first_gain,
                second_gain,
                router_part,
            ],
            axis=1,
        ),
        ("shard", "ctx"),
        scatter_dimension=0,
        tiled=True,
    )
    grad_bias = lax.psum(bias_acc, ("shard", "ctx"))
    packed_rows = reduced[:, : 3 * head_cols].reshape(-1, ctx_size, 3, share)
    return (
        mixed,
        input_grad.astype(jnp.bfloat16),
        packed_rows[:, :, 0].reshape(-1, head_cols),
        packed_rows[:, :, 1].reshape(-1, head_cols),
        packed_rows[:, :, 2].reshape(-1, head_cols),
        reduced[:, 3 * head_cols : 4 * head_cols],
        grad_bias,
        reduced[:, 4 * head_cols],
        reduced[:, 4 * head_cols + 1],
        reduced[:, 4 * head_cols + 2 :],
        weight_grads[:, 0][None],
        weight_grads[:, 1][None],
        weight_grads[:, 2][None],
    )


def ppermute_ctx(member, flip):
    return lax.ppermute(member, "ctx", [(place, place ^ flip) for place in range(4)])


def local_fused(
    tokens_in,
    cotangent,
    segment_ids,
    live_blocks,
    routes,
    w_query,
    w_key,
    w_value,
    w_out,
    rel_bias,
    attn_gain,
    ffn_gain,
    router,
    w_gate,
    w_up,
    w_down,
):
    rows_here, width = tokens_in.shape
    count = lax.axis_size("shard")
    ctx_size = lax.axis_size("ctx")
    ctx_index = lax.axis_index("ctx")
    share = w_query.shape[1] // ctx_size
    rows = w_query.shape[0]
    experts = router.shape[1]
    room = max(2, 3 * rows_here // experts)
    members = (
        w_query,
        w_key,
        w_value,
        w_out,
        jnp.stack([attn_gain, ffn_gain]),
        router,
        tokens_in,
        segment_ids,
        cotangent,
        routes,
    )
    full, packed, norm_one, segments, out_w, up_slots, *lows = run_gather(
        count, ctx_size, room, members, (w_gate[0], w_up[0], w_down[0])
    )
    gate_low, up_low, down_low, gate_core, up_core, down_core, gate_chip, gate_far = lows[:8]
    codes, code_rows, extras = lows[8:]
    up_chip, down_chip = ppermute_ctx(up_low, 2), ppermute_ctx(down_low, 2)

    packed = packed.reshape(ctx_size * rows_here, 3 * share)
    segment_row = segments[:, 0].reshape(1, -1)
    alive = live_tiles(segment_row[0], live_blocks[0])
    pair_heads = share // HEAD
    own_bias = lax.dynamic_slice_in_dim(rel_bias, ctx_index * pair_heads, pair_heads, 1)
    line = jnp.dot(own_bias.T, span_buckets().T, precision=lax.Precision.HIGHEST)
    attended, attended_t, log_sum = run_forward(alive, packed, segment_row, line)
    attended, up_chip, down_chip = lax.optimization_barrier((attended, up_chip, down_chip))
    expert_weights = [gate_low, gate_chip, gate_core, gate_far]
    expert_weights += [up_low, up_chip, up_core, ppermute_ctx(up_chip, 1)]
    expert_weights += [down_low, down_chip, down_core, ppermute_ctx(down_chip, 1)]
    hidden_one, norm_two, gates, attended_low = run_attend_out(
        attended.reshape(ctx_size, rows_here, share), tokens_in, out_w, extras, routes
    )
    rows_grad, dots, own_out, mine, other, kept, *given = run_experts(
        count, ctx_size, norm_two, gates, code_rows, codes, up_slots, expert_weights
    )
    outs = [own_out, mine, swap_sides(other)]
    hidden_grad, branch_grad, heads_grad, small = run_attend_back(
        rows_grad, dots, gates, routes, extras, hidden_one, cotangent, norm_two, out_w
    )
    heads_grad, given[1], given[2] = lax.optimization_barrier((heads_grad, given[1], given[2]))
    given = [given[0], ppermute_ctx(given[1], 2), ppermute_ctx(given[2], 2)]
    weight_grads = [
        kept[number].astype(jnp.float32) + given[number].astype(jnp.float32) for number in range(3)
    ]
    packed_grad, bias_line = run_backward(
        alive, packed, segment_row, line, heads_grad.reshape(-1, share), attended_t, log_sum
    )
    returned = run_return(
        count,
        packed_grad.reshape(ctx_size, rows_here, 3 * share),
        full,
        norm_one,
        tokens_in,
        bias_line,
        outs,
        gates,
        codes,
        branch_grad,
        attended_low,
        small,
        hidden_one,
        hidden_grad,
        extras,
    )
    mixed, input_grad, query_grad, key_grad, value_grad, bias_grad, gains_grad, out_grad = returned
    gains_grad = lax.dynamic_slice_in_dim(gains_grad, ctx_index % 2 * rows, rows, 1)
    bias_grad = jnp.transpose(bias_grad[:, :pair_heads, :NBUCK], (2, 0, 1))
    return (
        mixed,
        input_grad,
        query_grad,
        key_grad,
        value_grad,
        out_grad,
        bias_grad.reshape(rel_bias.shape),
        gains_grad[0],
        gains_grad[1],
        jnp.transpose(gains_grad[2 : 2 + experts]),
        weight_grads[0][None],
        weight_grads[1][None],
        weight_grads[2][None],
    )


def solution(mesh):
    placed = (
        P(("shard", "ctx"), None),
        P(("shard", "ctx"), None),
        P("shard", "ctx"),
        P("shard", None, None),
        P(("shard", "ctx"), None),
        P(("shard", "ctx"), "tensor"),
        P(("shard", "ctx"), "tensor"),
        P(("shard", "ctx"), "tensor"),
        P(("shard", "ctx"), "tensor"),
        P(None, "tensor"),
        P(("shard", "ctx")),
        P(("shard", "ctx")),
        P(("shard", "ctx"), None),
        P("shard", "ctx", "tensor"),
        P("shard", "ctx", "tensor"),
        P("shard", "ctx", "tensor"),
    )
    sizes = (mesh.shape["shard"], mesh.shape["ctx"], mesh.shape["tensor"])
    fused = sizes == (4, 4, 2)
    return jax.shard_map(
        local_fused if fused else local_general,
        mesh=mesh,
        in_specs=placed,
        out_specs=(
            P(("shard", "ctx"), None),
            P(("shard", "ctx"), None),
            P(("shard", "ctx"), "tensor"),
            P(("shard", "ctx"), "tensor"),
            P(("shard", "ctx"), "tensor"),
            P(("shard", "ctx"), "tensor"),
            P(None, "tensor"),
            P(("shard", "ctx")),
            P(("shard", "ctx")),
            P(("shard", "ctx"), None),
            P("shard", "ctx", "tensor"),
            P("shard", "ctx", "tensor"),
            P("shard", "ctx", "tensor"),
        ),
        check_vma=False,
    )
```

```python
import math
from functools import partial

import jax
import jax.numpy as jnp
from jax import lax
from jax.experimental import pallas as pl
from jax.experimental.pallas import tpu as pltpu
from jax.sharding import PartitionSpec as P

HEAD = 64
NBUCK = 32
TOP = 2
ATT_BLK = 512


FAR_STEPS = (12, 16, 23, 32, 46, 64, 91)


def bucket_ids(relative):
    distance = jnp.abs(relative)
    far = jnp.full(distance.shape, 8, jnp.int32)
    for bound in FAR_STEPS:
        far = far + (distance >= bound).astype(jnp.int32)
    near = jnp.where(distance < 8, distance, far)
    return near + jnp.where(relative > 0, NBUCK // 2, 0)


def contract_rows(left, right):
    return lax.dot_general(
        left, right, (((0,), (0,)), ((), ())), preferred_element_type=jnp.float32
    )


def contract_cols(left, right):
    return lax.dot_general(
        left, right, (((1,), (1,)), ((), ())), preferred_element_type=jnp.float32
    )


TILE = 256
BIG = 2.0**100
SPAN = 4 * TILE


def place_mask(segment_row):
    rows = lax.broadcasted_iota(jnp.int32, (128, segment_row.shape[1]), 0).astype(jnp.float32)
    apart = jnp.where(rows == segment_row, 0.0, -BIG)
    return jnp.where(rows < 8.0, apart, jnp.where(rows < 11.0, 1.0, 0.0))


def seat_rows(segment_row, extra):
    rows = lax.broadcasted_iota(jnp.int32, (128, segment_row.shape[1]), 0).astype(jnp.float32)
    own = jnp.where((rows == segment_row) & (rows < 8.0), 1.0, 0.0)
    if extra is None:
        return own.astype(jnp.bfloat16)
    high = extra.astype(jnp.bfloat16).astype(jnp.float32)
    rest = extra - high
    middle = rest.astype(jnp.bfloat16).astype(jnp.float32)
    low = rest - middle
    own = jnp.where(rows == 8.0, high, own)
    own = jnp.where(rows == 9.0, middle, own)
    return jnp.where(rows == 10.0, low, own).astype(jnp.bfloat16)


def fill_bias(line_ref, bias_ref):
    for head in range(2):
        line = line_ref[head : head + 1, :]
        turned = pltpu.roll(
            jnp.broadcast_to(line, (TILE, SPAN)), 0, axis=1, stride=1, stride_axis=0
        )
        bias_ref[head, 1] = turned[:, TILE : 2 * TILE]
        bias_ref[head, 2] = turned[:, :TILE]
        bias_ref[head, 3] = turned[:, 3 * TILE :]
        bias_ref[head, 0] = jnp.broadcast_to(line[:, 511:512], (TILE, TILE))
        bias_ref[head, 4] = jnp.broadcast_to(line[:, 513:514], (TILE, TILE))


def tile_at(index):
    return pl.ds(pl.multiple_of(index * TILE, TILE), TILE)


def dot32(left, right):
    return jnp.dot(left, right, preferred_element_type=jnp.float32)


def attention_forward(
    alive, packed, segment, line, out, out_t, log_sum, key_side, query_side, value_t, bias, top, acc
):
    length = packed.shape[0]
    tiles = length // TILE
    fill_bias(line, bias)

    def prepare(index, unused):
        spot = tile_at(index)
        seg = segment[0:1, spot]
        block = packed[spot, :].astype(jnp.float32)
        key_side[spot, :128] = packed[spot, 128:256]
        key_side[spot, 128:] = jnp.transpose(place_mask(seg)).astype(jnp.bfloat16)
        query_t = jnp.transpose(block[:, :128]) * 0.125
        seats = seat_rows(seg, None)
        half = lax.broadcasted_iota(jnp.int32, (128, TILE), 0) // HEAD
        values = jnp.transpose(block[:, 256:]).astype(jnp.bfloat16)
        ones = jnp.where(lax.broadcasted_iota(jnp.int32, (16, TILE), 0) == 0, 1.0, 0.0)
        for head in range(2):
            query_side[head, :128, spot] = jnp.where(half == head, query_t, 0.0).astype(
                jnp.bfloat16
            )
            query_side[head, 128:, spot] = seats
            value_t[head, :HEAD, spot] = values[HEAD * head : HEAD * (head + 1)]
            value_t[head, HEAD:, spot] = ones.astype(jnp.bfloat16)
        return unused

    lax.fori_loop(0, tiles, prepare, 0)

    def query_tile(query_index, unused):
        query_spot = tile_at(query_index)
        top[...] = jnp.full(top.shape, -3e38, jnp.float32)
        acc[...] = jnp.zeros(acc.shape, jnp.float32)

        def key_tile(key_index, carried):
            @pl.when(alive[query_index * tiles + key_index] == 1)
            def _():
                key_spot = tile_at(key_index)
                slot = jnp.clip(key_index - query_index, -2, 2) + 2
                keys = key_side[key_spot, :]
                for head in range(2):
                    scores = dot32(keys, query_side[head, :, query_spot]) + bias[head, slot]
                    before = top[head : head + 1, :]
                    now = jnp.maximum(before, jnp.max(scores, axis=0, keepdims=True))
                    weights = jnp.exp(scores - now).astype(jnp.bfloat16)
                    top[head : head + 1, :] = now
                    acc[head] = acc[head] * jnp.exp(before - now) + dot32(
                        value_t[head, :, key_spot], weights
                    )

            return carried

        lax.fori_loop(0, tiles, key_tile, 0)
        parts = []
        for head in range(2):
            total = acc[head, HEAD : HEAD + 1, :]
            part = acc[head, :HEAD, :] / total
            out_t[HEAD * head : HEAD * (head + 1), query_spot] = part
            log_sum[head : head + 1, query_spot] = top[head : head + 1, :] + jnp.log(total)
            parts.append(part)
        out[query_spot, :] = jnp.transpose(jnp.concatenate(parts, axis=0)).astype(jnp.bfloat16)
        return unused

    lax.fori_loop(0, tiles, query_tile, 0)


def attention_backward(
    alive,
    packed,
    segment,
    line,
    grads,
    out_t,
    log_sum,
    packed_grad,
    bias_grad,
    key_side,
    value_side,
    query_side,
    grad_side,
    key_t,
    query_pair,
    grad_pair,
    bias,
    bias_acc,
    query_acc,
    key_acc,
    value_acc,
):
    length = packed.shape[0]
    tiles = length // TILE
    fill_bias(line, bias)
    bias_acc[...] = jnp.zeros(bias_acc.shape, jnp.float32)

    def prepare(index, unused):
        spot = tile_at(index)
        seg = segment[0:1, spot]
        block = packed[spot, :].astype(jnp.float32)
        grad = grads[spot, :].astype(jnp.float32)
        seats = jnp.transpose(place_mask(seg)).astype(jnp.bfloat16)
        key_side[spot, :128] = packed[spot, 128:256]
        key_side[spot, 128:] = seats
        value_side[spot, :128] = packed[spot, 256:]
        value_side[spot, 128:] = seats
        key_t[:, spot] = jnp.transpose(block[:, 128:256]).astype(jnp.bfloat16)
        query_t = jnp.transpose(block[:, :128]) * 0.125
        grad_t = jnp.transpose(grad)
        half = lax.broadcasted_iota(jnp.int32, (128, TILE), 0) // HEAD
        side = lax.broadcasted_iota(jnp.int32, (TILE, 128), 1) // HEAD
        products = grad_t * out_t[:, spot]
        query_acc[:, spot] = jnp.zeros((128, TILE), jnp.float32)
        for head in range(2):
            query_side[head, :128, spot] = jnp.where(half == head, query_t, 0.0).astype(
                jnp.bfloat16
            )
            query_side[head, 128:, spot] = seat_rows(seg, -log_sum[head : head + 1, spot])
            delta = jnp.sum(products[HEAD * head : HEAD * (head + 1)], axis=0, keepdims=True)
            grad_side[head, :128, spot] = jnp.where(half == head, grad_t, 0.0).astype(jnp.bfloat16)
            grad_side[head, 128:, spot] = seat_rows(jnp.full_like(seg, -1.0), -delta)
            query_pair[index, TILE * head : TILE * (head + 1), :] = jnp.where(
                side == head, block[:, :128] * 0.125, 0.0
            ).astype(jnp.bfloat16)
            grad_pair[index, TILE * head : TILE * (head + 1), :] = jnp.where(
                side == head, grad, 0.0
            ).astype(jnp.bfloat16)
        return unused

    lax.fori_loop(0, tiles, prepare, 0)

    def key_tile(key_index, unused):
        key_spot = tile_at(key_index)
        key_acc[...] = jnp.zeros(key_acc.shape, jnp.float32)
        value_acc[...] = jnp.zeros(value_acc.shape, jnp.float32)

        def query_tile(query_index, carried):
            @pl.when(alive[query_index * tiles + key_index] == 1)
            def _():
                query_spot = tile_at(query_index)
                slot = jnp.clip(key_index - query_index, -2, 2) + 2
                keys = key_side[key_spot, :]
                values = value_side[key_spot, :]
                probs, score_grads = [], []
                for head in range(2):
                    scores = dot32(keys, query_side[head, :, query_spot]) + bias[head, slot]
                    prob = jnp.exp(scores)
                    score_grad = prob * dot32(values, grad_side[head, :, query_spot])
                    bias_acc[head, slot] += score_grad
                    score_grad = score_grad.astype(jnp.bfloat16)
                    probs.append(prob.astype(jnp.bfloat16))
                    score_grads.append(score_grad)
                    rows = slice(HEAD * head, HEAD * (head + 1))
                    query_acc[rows, query_spot] += dot32(key_t[rows, key_spot], score_grad)
                value_acc[...] += dot32(jnp.concatenate(probs, axis=1), grad_pair[query_index])
                key_acc[...] += dot32(jnp.concatenate(score_grads, axis=1), query_pair[query_index])

            return carried

        lax.fori_loop(0, tiles, query_tile, 0)
        packed_grad[key_spot, 128:256] = key_acc[...].astype(jnp.bfloat16)
        packed_grad[key_spot, 256:] = value_acc[...].astype(jnp.bfloat16)
        return unused

    lax.fori_loop(0, tiles, key_tile, 0)

    def finish(index, unused):
        spot = tile_at(index)
        packed_grad[spot, :128] = (jnp.transpose(query_acc[:, spot]) * 0.125).astype(jnp.bfloat16)
        return unused

    lax.fori_loop(0, tiles, finish, 0)
    rows = lax.broadcasted_iota(jnp.int32, (TILE, TILE), 0)
    columns = lax.broadcasted_iota(jnp.int32, (TILE, TILE), 1)
    flip = jnp.where(rows + columns == TILE - 1, 1.0, 0.0)
    bias_grad[...] = jnp.zeros(bias_grad.shape, jnp.float32)
    for head in range(2):
        spread = jnp.concatenate(
            [
                bias_acc[head, 2],
                bias_acc[head, 1],
                jnp.zeros((TILE, TILE), jnp.float32),
                bias_acc[head, 3],
            ],
            axis=1,
        )
        flipped = jnp.dot(
            flip, spread, precision=lax.Precision.HIGHEST, preferred_element_type=jnp.float32
        )
        turned = pltpu.roll(flipped, SPAN - TILE + 1, axis=1, stride=1, stride_axis=0)
        bias_grad[head : head + 1, :] = jnp.sum(turned, axis=0, keepdims=True)
        bias_grad[2 + head : 3 + head, :TILE] = jnp.sum(bias_acc[head, 0], axis=0, keepdims=True)
        bias_grad[4 + head : 5 + head, :TILE] = jnp.sum(bias_acc[head, 4], axis=0, keepdims=True)


def in_hbm(count):
    return [pl.BlockSpec(memory_space=pl.ANY)] * count


def estimate(micros):
    return pl.CostEstimate(flops=int(micros * 1e9), bytes_accessed=0, transcendentals=0)


def in_vmem(count):
    return [pl.BlockSpec(memory_space=pltpu.VMEM)] * count


def run_forward(alive, packed, segment, line):
    length = packed.shape[0]
    return pl.pallas_call(
        attention_forward,
        out_shape=(
            jax.ShapeDtypeStruct((length, 128), jnp.bfloat16),
            jax.ShapeDtypeStruct((128, length), jnp.float32),
            jax.ShapeDtypeStruct((8, length), jnp.float32),
        ),
        in_specs=[pl.BlockSpec(memory_space=pltpu.SMEM)] + in_vmem(3),
        out_specs=tuple(in_vmem(3)),
        scratch_shapes=[
            pltpu.VMEM((length, 256), jnp.bfloat16),
            pltpu.VMEM((2, 256, length), jnp.bfloat16),
            pltpu.VMEM((2, HEAD + 16, length), jnp.bfloat16),
            pltpu.VMEM((2, 5, TILE, TILE), jnp.float32),
            pltpu.VMEM((8, TILE), jnp.float32),
            pltpu.VMEM((2, HEAD + 16, TILE), jnp.float32),
        ],
        compiler_params=pltpu.CompilerParams(vmem_limit_bytes=67043328),
        cost_estimate=estimate(20),
        name="attention_forward",
    )(alive, packed, segment, line)


def run_backward(alive, packed, segment, line, grads, out_t, log_sum):
    length = packed.shape[0]
    tiles = length // TILE
    return pl.pallas_call(
        attention_backward,
        out_shape=(
            jax.ShapeDtypeStruct((length, 384), jnp.bfloat16),
            jax.ShapeDtypeStruct((8, SPAN), jnp.float32),
        ),
        in_specs=[pl.BlockSpec(memory_space=pltpu.SMEM)] + in_vmem(6),
        out_specs=tuple(in_vmem(2)),
        scratch_shapes=[
            pltpu.VMEM((length, 256), jnp.bfloat16),
            pltpu.VMEM((length, 256), jnp.bfloat16),
            pltpu.VMEM((2, 256, length), jnp.bfloat16),
            pltpu.VMEM((2, 256, length), jnp.bfloat16),
            pltpu.VMEM((128, length), jnp.bfloat16),
            pltpu.VMEM((tiles, 2 * TILE, 128), jnp.bfloat16),
            pltpu.VMEM((tiles, 2 * TILE, 128), jnp.bfloat16),
            pltpu.VMEM((2, 5, TILE, TILE), jnp.float32),
            pltpu.VMEM((2, 5, TILE, TILE), jnp.float32),
            pltpu.VMEM((128, length), jnp.float32),
            pltpu.VMEM((TILE, 128), jnp.float32),
            pltpu.VMEM((TILE, 128), jnp.float32),
        ],
        compiler_params=pltpu.CompilerParams(vmem_limit_bytes=67043328),
        cost_estimate=estimate(4),
        name="attention_backward",
    )(alive, packed, segment, line, grads, out_t, log_sum)


def signed_span():
    places = jnp.arange(SPAN, dtype=jnp.int32)
    return jnp.where(places < SPAN // 2, -places, SPAN - places)


def span_buckets():
    return (bucket_ids(signed_span())[:, None] == jnp.arange(NBUCK)[None, :]).astype(jnp.float32)


def live_tiles(segments, live):
    tiles = segments.shape[0] // TILE
    grouped = segments.reshape(tiles, TILE)
    first, last = grouped[:, 0], grouped[:, -1]
    meets = (first[:, None] <= last[None, :]) & (first[None, :] <= last[:, None])
    spread = jnp.repeat(jnp.repeat(live, ATT_BLK // TILE, axis=0), ATT_BLK // TILE, axis=1)
    return (meets & (spread == 1)).astype(jnp.int32).reshape(-1)


MESH = pl.DeviceIdType.MESH
LANES = 128


def places():
    own, ctx, side = lax.axis_index("shard"), lax.axis_index("ctx"), lax.axis_index("tensor")
    return own, ctx, side, ctx // 2, ctx % 2


def nearest(own, count, step):
    flip = own // (count // 2)
    place = flip * (count - 1 - own) + (1 - flip) * own
    turn = step - 1
    turn = turn + (turn - place + count) // count
    other = flip * (count - 1 - turn) + (1 - flip) * turn
    first = 1 - (step + count - 1) // count
    return first * own + (1 - first) * other


def partner(own, turn):
    return (own // 2 + turn // 2) % 2 * 2 + (own + turn) % 2


def across(chip, core, step):
    return (chip + 1 - step // 2) % 2 * 2 + (core + step + step // 2) % 2


def remote(source, target, send, recv, device):
    return pltpu.make_async_remote_copy(
        source, target, send, recv, device_id=device, device_id_type=MESH
    )


def greet(devices):
    barrier = pltpu.get_barrier_semaphore()
    for device in devices:
        pl.semaphore_signal(barrier, 1, device_id=device, device_id_type=MESH)
    pl.semaphore_wait(barrier, len(devices))


def gelu_parts(value):
    root = math.sqrt(2.0 / math.pi)
    square = value * value
    bend = jnp.tanh(root * value * (1.0 + 0.044715 * square))
    half = 0.5 * (1.0 + bend)
    slope = half + 0.5 * value * (1.0 - bend * bend) * (root * (1.0 + 0.134145 * square))
    return value * half, slope


def dot_last(left, right):
    return lax.dot_general(
        left, right, (((1,), (1,)), ((), ())), preferred_element_type=jnp.float32
    )


def expert_exchange(
    count,
    norm,
    gates,
    code_rows,
    code_cols,
    upstream_hbm,
    gate_own,
    gate_chip,
    gate_core,
    gate_far,
    up_own,
    up_chip,
    up_core,
    up_far,
    down_own,
    down_chip,
    down_core,
    down_far,
    row_grad,
    dot_rows,
    own_hbm,
    out_first,
    out_one,
    out_near,
    out_two,
    out_three,
    out_last,
    kept_hbm,
    gate_given,
    pair_given,
    upstream,
    gate_w,
    up_w,
    down_w,
    rows,
    sent,
    gates_in,
    gates_out,
    slot_grad,
    inner,
    gate_grad,
    up_grad,
    outs,
    partial,
    peer_part,
    summed,
    back,
    dots_out,
    dots_in,
    final_out,
    final_in,
    final_dots,
    core_in,
    chip_in,
    load_sem,
    store_sem,
    rows_send,
    rows_recv,
    pass_send,
    pass_recv,
    gates_send,
    gates_recv,
    part_send,
    part_recv,
    back_send,
    back_recv,
    dots_send,
    dots_recv,
    final_send,
    final_recv,
    core_send,
    core_recv,
    chip_send,
    chip_recv,
):
    own = lax.axis_index("shard")
    ctx = lax.axis_index("ctx")
    side = lax.axis_index("tensor")
    tokens, width = norm.shape
    room = upstream.shape[1]
    half = room // 2
    hidden = gate_w.shape[1]
    peer = (own, ctx, 1 - side)

    def source(step):
        return partner(own, step)

    barrier = pltpu.get_barrier_semaphore()
    for step in range(1, count):
        pl.semaphore_signal(barrier, 1, device_id=(source(step), ctx, side), device_id_type=MESH)
    chip, core = ctx // 2, ctx % 2
    core_peer = (own, chip * 2 + 1 - core, side)
    chip_peer = (own, (1 - chip) * 2 + core, side)
    for device in (peer, core_peer, chip_peer):
        pl.semaphore_signal(barrier, 1, device_id=device, device_id_type=MESH)
    deep = gate_own.shape[0]
    origins = (ctx, (1 - chip) * 2 + core, chip * 2 + 1 - core, (1 - chip) * 2 + 1 - core)
    pieces_of = (
        (gate_w, (gate_own, gate_chip, gate_core, gate_far)),
        (up_w, (up_own, up_chip, up_core, up_far)),
        (down_w, (down_own, down_chip, down_core, down_far)),
    )
    loads = []
    for number, (target, sources) in enumerate(pieces_of):
        for turn, source_ref in enumerate(sources):
            spot = pl.ds(pl.multiple_of(origins[turn] * deep, deep), deep)
            sem = load_sem.at[4 * number + turn]
            loads.append(pltpu.make_async_copy(source_ref, target.at[spot], sem))
    loads.append(pltpu.make_async_copy(upstream_hbm, upstream, load_sem.at[12]))
    for load in loads:
        load.start()
    pl.semaphore_wait(barrier, count + 2)

    my_half = pl.ds(pl.multiple_of(side * half, half), half)
    peer_half = pl.ds(pl.multiple_of((1 - side) * half, half), half)

    def picked(expert, start, amount):
        slots = lax.broadcasted_iota(jnp.int32, (amount, tokens), 0) + expert * room + start
        slots = slots.astype(jnp.float32)
        hit = (code_rows[0:1, :] == slots) | (code_rows[1:2, :] == slots)
        return jnp.where(hit, 1.0, 0.0).astype(jnp.bfloat16)

    def slot_gates(expert):
        slots = lax.broadcasted_iota(jnp.int32, (tokens, room), 1) + expert * room
        slots = slots.astype(jnp.float32)
        held = jnp.where(code_cols[:, 0:1] == slots, gates[:, 0:1], 0.0)
        held = held + jnp.where(code_cols[:, 1:2] == slots, gates[:, 1:2], 0.0)
        return jnp.broadcast_to(jnp.sum(held, axis=0, keepdims=True), (8, room))

    def rows_copy(step):
        target = source(step)
        return pltpu.make_async_remote_copy(
            sent.at[step - 1],
            rows.at[own, my_half],
            rows_send.at[step - 1],
            rows_recv.at[own],
            device_id=(target, ctx, side),
            device_id_type=MESH,
        )

    def gates_copy(step):
        return pltpu.make_async_remote_copy(
            gates_out.at[step - 1],
            gates_in.at[own],
            gates_send.at[step - 1],
            gates_recv.at[own],
            device_id=(source(step), ctx, side),
            device_id_type=MESH,
        )

    def send_rows(step, unused):
        target = source(step)
        sent[step - 1] = dot32(picked(target, side * half, half), norm[...]).astype(jnp.bfloat16)
        rows_copy(step).start()
        gates_out[step - 1] = slot_gates(target)
        gates_copy(step).start()
        return unused

    lax.fori_loop(1, count, send_rows, 0)
    rows[own] = dot32(picked(own, 0, room), norm[...]).astype(jnp.bfloat16)
    gates_in[own] = slot_gates(own)
    for load in loads:
        load.wait()

    def landed(buffer, send, recv, origin):
        return pltpu.make_async_remote_copy(
            buffer, buffer, send, recv, device_id=peer, device_id_type=MESH
        )

    def pass_copy(origin):
        return pltpu.make_async_remote_copy(
            rows.at[origin, my_half],
            rows.at[origin, my_half],
            pass_send.at[origin],
            pass_recv.at[origin],
            device_id=peer,
            device_id_type=MESH,
        )

    def part_copy(step):
        return pltpu.make_async_remote_copy(
            partial.at[step, peer_half],
            peer_part.at[step],
            part_send.at[step],
            part_recv.at[step],
            device_id=peer,
            device_id_type=MESH,
        )

    def back_copy(step):
        return pltpu.make_async_remote_copy(
            summed.at[step],
            back.at[own],
            back_send.at[step],
            back_recv.at[own],
            device_id=(source(step), ctx, side),
            device_id_type=MESH,
        )

    def dots_copy(step):
        return pltpu.make_async_remote_copy(
            dots_out.at[step],
            dots_in.at[own],
            dots_send.at[step],
            dots_recv.at[own],
            device_id=(source(step), ctx, side),
            device_id_type=MESH,
        )

    def send_back(step):
        part_copy(step).wait_recv()
        summed[step] = (
            partial[step, my_half].astype(jnp.float32) + peer_part[step].astype(jnp.float32)
        ).astype(jnp.bfloat16)
        back_copy(step).start()

    cut = (hidden // 256 + 1) // 2 * 256
    pieces = (slice(0, cut), slice(cut, hidden))

    def run_chunk(step, unused):
        origin = source(step)

        @pl.when(step > 0)
        def _():
            landed(rows.at[origin, peer_half], pass_send.at[origin], pass_recv.at[origin], 0).wait_recv()
            landed(gates_in.at[origin], gates_send.at[0], gates_recv.at[origin], 0).wait_recv()

        gate_column = jnp.transpose(gates_in[origin])[:, 0:1]
        slot_grad[origin] = (upstream[origin].astype(jnp.float32) * gate_column).astype(
            jnp.bfloat16
        )

        def inside(piece):
            block = rows[origin]
            gate_pre = dot32(block, gate_w[:, piece])
            up_pre = dot32(block, up_w[:, piece])
            inner_grad = dot32(slot_grad[origin], down_w[:, piece])
            active, slope = gelu_parts(gate_pre)
            held = (active * up_pre).astype(jnp.bfloat16)
            inner[origin, :, piece] = held
            gate_grad[origin, :, piece] = (inner_grad * up_pre * slope).astype(jnp.bfloat16)
            up_grad[origin, :, piece] = (inner_grad * active).astype(jnp.bfloat16)
            return jnp.sum(active * up_pre * inner_grad, axis=1, keepdims=True)

        dots = inside(pieces[0])

        @pl.when(step < count - 1)
        def _():
            following = source(step + 1)
            landed(
                rows.at[following, my_half], rows_send.at[0], rows_recv.at[following], 0
            ).wait_recv()
            pass_copy(following).start()

        dots = dots + inside(pieces[1])
        dots_out[step] = jnp.transpose(jnp.broadcast_to(dots, (room, 128)))[0:8, :]

        @pl.when(step > 1)
        def _():
            send_back(step - 1)

        partial[step] = (
            dot_last(gate_grad[origin], gate_w[...]) + dot_last(up_grad[origin], up_w[...])
        ).astype(jnp.bfloat16)

        @pl.when(step > 0)
        def _():
            part_copy(step).start()
            dots_copy(step).start()

        return unused

    lax.fori_loop(0, count, run_chunk, 0)
    products = ((gate_w, rows, gate_grad), (up_w, rows, up_grad), (down_w, slot_grad, inner))

    def owner(turn):
        return turn % 2 * 2 + (core + 1 + turn // 2) % 2

    def to_core(number, turn):
        spot = pl.ds(pl.multiple_of(owner(turn) * deep, deep), deep)
        return pltpu.make_async_remote_copy(
            products[number][0].at[spot],
            core_in.at[number, turn],
            core_send.at[number, turn],
            core_recv.at[number, turn],
            device_id=core_peer,
            device_id_type=MESH,
        )

    def weigh(number):
        target, left, right = products[number]

        def block(turn, unused):
            spot = pl.ds(pl.multiple_of(owner(turn) * deep, deep), deep)
            lines = left[:, :, spot].reshape(count * room, deep)
            target[spot, :] = lax.dot_general(
                lines,
                right[...].reshape(count * room, hidden),
                (((0,), (0,)), ((), ())),
                preferred_element_type=jnp.float32,
            ).astype(jnp.bfloat16)

            @pl.when(turn < 2)
            def _():
                to_core(number, turn).start()

            return unused

        lax.fori_loop(0, 4, block, 0)

    def run_out(step, unused):
        outs[step] = dot_last(inner[step], down_w[...]).astype(jnp.bfloat16)
        return unused

    def to_chip(number):
        return remote(
            core_in.at[number, 1 - chip],
            chip_in.at[0],
            chip_send.at[number],
            chip_recv.at[number],
            chip_peer,
        )

    def over_chip(number):
        for turn in range(2):
            spot = pl.ds(pl.multiple_of(owner(turn + 2) * deep, deep), deep)
            to_core(number, turn).wait_recv()
            core_in[number, turn] = (
                products[number][0][spot, :].astype(jnp.float32)
                + core_in[number, turn].astype(jnp.float32)
            ).astype(jnp.bfloat16)
        if number == 0:
            to_chip(number).start()

    weigh(0)
    send_back(count - 1)
    lax.fori_loop(0, count, run_out, 0)
    moves = (
        (outs.at[own], own_hbm),
        (outs.at[partner(own, 1), pl.ds(0, half)], out_first),
        (outs.at[partner(own, 1), pl.ds(half, half)], out_one),
        (outs.at[partner(own, 2), pl.ds(0, half)], out_near),
        (outs.at[partner(own, 2), pl.ds(half, half)], out_two),
        (outs.at[partner(own, 3), pl.ds(0, half)], out_three),
        (outs.at[partner(own, 3), pl.ds(half, half)], out_last),
    )
    stores = []
    for number, (source_ref, target) in enumerate(moves):
        sem = store_sem.at[number if number == 0 else 10 + number]
        stores.append(pltpu.make_async_copy(source_ref, target, sem))
    for store in stores:
        store.start()
    weigh(1)
    over_chip(0)

    def dots_landed(step, unused):
        origin = source(step)
        landed(dots_in.at[origin], dots_send.at[0], dots_recv.at[origin], 0).wait_recv()
        return unused

    def back_landed(step, unused):
        origin = source(step)
        landed(back.at[origin], back_send.at[0], back_recv.at[origin], 0).wait_recv()
        return unused

    lax.fori_loop(1, count, dots_landed, 0)
    dots_in[own] = dots_out[0]
    final_dots[0] = jnp.zeros((8, tokens), jnp.float32)
    for expert in range(count):
        column = jnp.transpose(dots_in[expert])[:, 0:1]
        slots = lax.broadcasted_iota(jnp.int32, (room, tokens), 0) + expert * room
        slots = slots.astype(jnp.float32)
        for choice in range(2):
            final_dots[0, choice : choice + 1, :] += jnp.sum(
                jnp.where(code_rows[choice : choice + 1, :] == slots, column, 0.0),
                axis=0,
                keepdims=True,
            )
    lax.fori_loop(1, count, back_landed, 0)
    blocks = final_out.shape[0]
    span = tokens // blocks

    def final_copy(block):
        return pltpu.make_async_remote_copy(
            final_out.at[block],
            final_in.at[block],
            final_send.at[block],
            final_recv.at[block],
            device_id=peer,
            device_id_type=MESH,
        )

    dots_final = pltpu.make_async_remote_copy(
        final_dots.at[0],
        final_dots.at[1],
        final_send.at[blocks],
        final_recv.at[blocks],
        device_id=peer,
        device_id_type=MESH,
    )
    dots_final.start()

    def combine(block, unused):
        spot = pl.ds(pl.multiple_of(block * span, span), span)

        def chosen(start, amount):
            slots = lax.broadcasted_iota(jnp.int32, (span, amount), 1) + start
            slots = slots.astype(jnp.float32)
            hit = (code_cols[spot, 0:1] == slots) | (code_cols[spot, 1:2] == slots)
            return jnp.where(hit, 1.0, 0.0).astype(jnp.bfloat16)

        total = dot32(chosen(own * room, room), partial[0])
        for step in range(1, count):
            origin = source(step)
            total = total + dot32(chosen(origin * room + side * half, half), back[origin])
        final_out[block] = total.astype(jnp.bfloat16)
        final_copy(block).start()
        return unused

    lax.fori_loop(0, blocks, combine, 0)

    weigh(2)

    def finish(block, unused):
        spot = pl.ds(pl.multiple_of(block * span, span), span)
        final_copy(block).wait_recv()
        row_grad[spot, :] = final_out[block].astype(jnp.float32) + final_in[block].astype(
            jnp.float32
        )
        return unused

    lax.fori_loop(0, blocks, finish, 0)
    dots_final.wait_recv()
    dot_rows[...] = final_dots[0] + final_dots[1]
    to_chip(0).wait_recv()
    for number in range(3):
        if number:
            over_chip(number)
        given = core_in.at[number, 1 - chip] if number else chip_in.at[0]
        for place, source_ref in enumerate((core_in.at[number, chip], given)):
            target = (kept_hbm.at[number], pair_given.at[number - 1] if number else gate_given)[place]
            sem = store_sem.at[4 + 2 * number + place]
            store = pltpu.make_async_copy(source_ref, target, sem)
            store.start()
            stores.append(store)

    def drain(step, unused):
        rows_copy(step).wait_send()
        gates_copy(step).wait_send()
        pass_copy(source(step)).wait_send()
        part_copy(step).wait_send()
        back_copy(step).wait_send()
        dots_copy(step).wait_send()
        return unused

    lax.fori_loop(1, count, drain, 0)

    def drain_final(block, unused):
        final_copy(block).wait_send()
        return unused

    lax.fori_loop(0, blocks, drain_final, 0)
    dots_final.wait_send()
    for number in range(3):
        for turn in range(2):
            to_core(number, turn).wait_send()
        if number == 0:
            to_chip(number).wait_send()
    for store in stores:
        store.wait()


def run_experts(count, ctx_size, norm, gates, code_rows, code_cols, upstream, weights):
    tokens, width = norm.shape
    room = upstream.shape[1]
    half = room // 2
    hidden = weights[0].shape[1]
    blocks = 4
    low = jnp.bfloat16
    full = jnp.float32
    dma = pltpu.SemaphoreType.DMA
    return pl.pallas_call(
        partial(expert_exchange, count),
        out_shape=(
            jax.ShapeDtypeStruct((tokens, width), full),
            jax.ShapeDtypeStruct((8, tokens), full),
            jax.ShapeDtypeStruct((room, width), low),
            *[jax.ShapeDtypeStruct((half, width), low)] * 6,
            jax.ShapeDtypeStruct((3, width // ctx_size, hidden), low),
            jax.ShapeDtypeStruct((width // ctx_size, hidden), low),
            jax.ShapeDtypeStruct((2, width // ctx_size, hidden), low),
        ),
        in_specs=in_vmem(4) + [pl.BlockSpec(memory_space=pl.ANY)] * 13,
        out_specs=tuple(in_vmem(2) + [pl.BlockSpec(memory_space=pl.ANY)] * 10),
        scratch_shapes=[
            pltpu.VMEM(upstream.shape, low),
            pltpu.VMEM((width, hidden), low),
            pltpu.VMEM((width, hidden), low),
            pltpu.VMEM((width, hidden), low),
            pltpu.VMEM((count, room, width), low),
            pltpu.VMEM((count - 1, half, width), low),
            pltpu.VMEM((count, 8, room), full),
            pltpu.VMEM((count - 1, 8, room), full),
            pltpu.VMEM((count, room, width), low),
            pltpu.VMEM((count, room, hidden), low),
            pltpu.VMEM((count, room, hidden), low),
            pltpu.VMEM((count, room, hidden), low),
            pltpu.VMEM((count, room, width), low),
            pltpu.VMEM((count, room, width), low),
            pltpu.VMEM((count, half, width), low),
            pltpu.VMEM((count, half, width), low),
            pltpu.VMEM((count, half, width), low),
            pltpu.VMEM((count, 8, room), full),
            pltpu.VMEM((count, 8, room), full),
            pltpu.VMEM((blocks, tokens // blocks, width), low),
            pltpu.VMEM((blocks, tokens // blocks, width), low),
            pltpu.VMEM((2, 8, tokens), full),
            pltpu.VMEM((3, 2, width // ctx_size, hidden), low),
            pltpu.VMEM((1, width // ctx_size, hidden), low),
            dma((13,)),
            dma((18,)),
            dma((count,)),
            dma((count,)),
            dma((count,)),
            dma((count,)),
            dma((count,)),
            dma((count,)),
            dma((count,)),
            dma((count,)),
            dma((count,)),
            dma((count,)),
            dma((count,)),
            dma((count,)),
            dma((blocks + 1,)),
            dma((blocks + 1,)),
            dma((3, 2)),
            dma((3, 2)),
            dma((3,)),
            dma((3,)),
        ],
        cost_estimate=estimate(110),
        compiler_params=pltpu.CompilerParams(
            collective_id=3, has_side_effects=True, vmem_limit_bytes=67043328
        ),
        name="expert_exchange",
    )(norm, gates, code_rows, code_cols, upstream, *weights)


def begin(pairs, sems):
    copies = [
        pltpu.make_async_copy(source, target, sems.at[number])
        for number, (source, target) in enumerate(pairs)
    ]
    for copy in copies:
        copy.start()
    return copies


def gather_project(
    count,
    w_query,
    w_key,
    w_value,
    w_out,
    first_gain,
    second_gain,
    router,
    tokens,
    segment_ids,
    cotangent,
    routes,
    gate_hbm,
    up_hbm,
    down_hbm,
    full_hbm,
    packed,
    norm_hbm,
    segments,
    out_hbm,
    upstream_hbm,
    gate_hbm_low,
    up_hbm_low,
    down_hbm_low,
    gate_core,
    up_core,
    down_core,
    gate_chip,
    gate_far,
    codes,
    code_rows,
    extras,
    full,
    norm,
    out_full,
    upstream,
    gate_low,
    up_low,
    down_low,
    weight,
    out_weight,
    segment,
    outgoing,
    sent,
    experts_wide,
    line_send,
    line_recv,
    chip_send,
    chip_recv,
    core_send,
    core_recv,
    packed_send,
    packed_recv,
    segment_send,
    segment_recv,
    out_line_send,
    out_line_recv,
    out_chip_send,
    out_chip_recv,
    out_core_send,
    out_core_recv,
    out_pair_send,
    out_pair_recv,
    rows_send,
    rows_recv,
    pass_send,
    pass_recv,
    expert_send,
    expert_recv,
    load_sem,
    store_sem,
):
    own, ctx, side, chip, core = places()
    rows = weight.shape[0]
    ctx_size, here, share = packed.shape
    room = upstream.shape[1]
    half = room // 2
    chip_peer = (own, (1 - chip) * 2 + core, side)
    core_peer = (own, chip * 2 + 1 - core, side)
    pair = (own, ctx, 1 - side)
    loads = [
        pltpu.make_async_copy(source, experts_wide.at[number], load_sem.at[number])
        for number, source in enumerate((gate_hbm, up_hbm, down_hbm))
    ]
    for load in loads:
        load.start()
    stores = []

    def store(source, target):
        copy = pltpu.make_async_copy(source, target, store_sem.at[len(stores)])
        copy.start()
        stores.append(copy)

    experts = router.shape[0]
    extra = jnp.concatenate(
        [first_gain[...], second_gain[...], router[...], jnp.zeros((6 - experts, rows))], axis=0
    )
    weight[:, ctx_size * share :] = jnp.zeros((rows, LANES), jnp.bfloat16)
    extra_columns = slice(ctx_size * share, ctx_size * share + 8)
    weight[:, extra_columns] = jnp.transpose(extra).astype(jnp.bfloat16)
    for place in range(ctx_size):
        for number, member in enumerate((w_query, w_key, w_value)):
            target = slice(place * share + number * LANES, place * share + (number + 1) * LANES)
            found = member[:, place * LANES : (place + 1) * LANES]
            weight[:, target] = found.astype(jnp.bfloat16)
    out_weight[...] = w_out[...].astype(jnp.bfloat16)
    segment[...] = jnp.broadcast_to(segment_ids[...].astype(jnp.float32), segment.shape)
    greet(
        [(nearest(own, count, step), ctx, side) for step in range(1, count)]
        + [(own, across(chip, core, step), side) for step in range(3)]
        + [pair]
    )

    def block(shard, place):
        return pl.ds(pl.multiple_of((shard * ctx_size + place) * rows, rows), rows)

    def along(origin, forward):
        turn = 2 * forward - 1
        target = own + turn
        there = (target + count) // count * (1 - target // count)
        return (target + count) % count, there

    def onward(origin):
        return 1 - (origin - own + count) // count

    def to_line(origin, forward, source, number):
        target, _ = along(origin, forward)
        spot = full.at[block(origin, ctx)]
        return remote(
            source, spot, line_send.at[number], line_recv.at[origin], (target, ctx, side)
        )

    def in_line(copy_of, origin, forward, source, number, act):
        _, there = along(origin, forward)

        @pl.when(there == 1)
        def _():
            act(copy_of(origin, forward, source, number))

    def to_chip(shard, source):
        target = full.at[block(shard, ctx)]
        return remote(source, target, chip_send.at[shard], chip_recv.at[shard], chip_peer)

    def to_core(shard, place, source):
        index = shard * 2 + place // 2
        target = full.at[block(shard, place)]
        return remote(source, target, core_send.at[index], core_recv.at[index], core_peer)

    def to_segment(step):
        device = (own, across(chip, core, step), side)
        return remote(segment, segments.at[ctx], segment_send.at[step], segment_recv.at[ctx], device)

    def out_to_line(origin, forward, source, number):
        target, _ = along(origin, forward)
        spot = out_full.at[side, block(origin, ctx)]
        return remote(
            source, spot, out_line_send.at[number], out_line_recv.at[origin], (target, ctx, side)
        )

    def start(copy):
        copy.start()

    def sent_off(copy):
        copy.wait_send()

    def out_to_chip(shard, source):
        target = out_full.at[side, block(shard, ctx)]
        return remote(source, target, out_chip_send.at[shard], out_chip_recv.at[shard], chip_peer)

    def out_to_core(which, shard, place, source):
        index = shard * 2 + place // 2
        target = out_full.at[which, block(shard, place)]
        return remote(
            source, target, out_core_send.at[which, index], out_core_recv.at[which, index], core_peer
        )

    def out_to_pair(shard, place, source):
        index = shard * 2 + place // 2
        target = out_full.at[side, block(shard, place)]
        return remote(source, target, out_pair_send.at[index], out_pair_recv.at[index], pair)

    for forward in range(2):
        in_line(to_line, own, forward, weight, forward, start)
    to_chip(own, weight).start()
    to_core(own, ctx, weight).start()
    for step in range(3):
        to_segment(step).start()
    for forward in range(2):
        in_line(out_to_line, own, forward, out_weight, forward, start)
    out_to_core(side, own, ctx, out_weight).start()
    out_to_pair(own, ctx, out_weight).start()
    full[block(own, ctx), :] = weight[...]
    out_full[side, block(own, ctx), :] = out_weight[...]
    segments[ctx] = segment[...]

    lane = lax.broadcasted_iota(jnp.int32, (here, LANES), 1).astype(jnp.float32)
    named = jnp.concatenate([routes[...].astype(jnp.float32), jnp.zeros((6, here))], axis=0)
    columns = jnp.transpose(named)
    first, second = columns[:, 0:1], columns[:, 1:2]
    codes[:, 2:3] = first
    codes[:, 3:4] = second
    named = jnp.where((first == lane) | (second == lane), 1.0, 0.0).astype(jnp.bfloat16)
    later = lax.broadcasted_iota(jnp.int32, (here, here), 0)
    before = later > lax.broadcasted_iota(jnp.int32, (here, here), 1)
    slots = dot32(jnp.where(before, 1.0, 0.0).astype(jnp.bfloat16), named) + room * lane
    first = jnp.sum(jnp.where(first == lane, slots, 0.0), axis=1, keepdims=True)
    second = jnp.sum(jnp.where(second == lane, slots, 0.0), axis=1, keepdims=True)
    codes[:, 0:1] = first
    codes[:, 1:2] = second
    both = jnp.where(lane == 0.0, first, jnp.where(lane == 1.0, second, -1.0))
    code_rows[...] = jnp.transpose(both)[0:8]
    my_half = pl.ds(pl.multiple_of(side * half, half), half)
    peer_half = pl.ds(pl.multiple_of((1 - side) * half, half), half)

    def picked(expert, start, amount):
        slots = lax.broadcasted_iota(jnp.int32, (amount, here), 0) + expert * room + start
        slots = slots.astype(jnp.float32)
        hit = (code_rows[0:1, :] == slots) | (code_rows[1:2, :] == slots)
        rows_found = jnp.where(hit, 1.0, 0.0).astype(jnp.bfloat16)
        return dot32(rows_found, cotangent[...]).astype(jnp.bfloat16)

    def to_expert(step):
        return remote(
            sent.at[step - 1],
            upstream.at[own, my_half],
            rows_send.at[step - 1],
            rows_recv.at[own],
            (nearest(own, count, step), ctx, side),
        )

    def pass_rows(shard):
        spot, target = upstream.at[shard, my_half], upstream_hbm.at[shard, my_half]
        return remote(spot, target, pass_send.at[shard], pass_recv.at[shard], pair)

    lows = (gate_low, up_low, down_low)
    near = (gate_core, up_core, down_core)
    for number, load in enumerate(loads):
        load.wait()
        lows[number][...] = experts_wide[number].astype(jnp.bfloat16)
        store(lows[number], (gate_hbm_low, up_hbm_low, down_hbm_low)[number])
    for step in range(1, count):
        sent[step - 1] = picked(nearest(own, count, step), side * half, half)
    upstream[own] = picked(own, 0, room)
    store(upstream.at[own], upstream_hbm.at[own])

    def to_near(number):
        return remote(
            lows[number], near[number], expert_send.at[number], expert_recv.at[number], core_peer
        )

    gate_over = remote(gate_low, gate_chip, expert_send.at[3], expert_recv.at[3], chip_peer)
    gate_far_copy = remote(gate_chip, gate_far, expert_send.at[4], expert_recv.at[4], core_peer)

    other_place = (1 - chip) * 2 + core

    def pass_line(step):
        shard = nearest(own, count, step)
        source = full.at[block(shard, ctx)]
        remote(source, source, line_send.at[0], line_recv.at[shard], core_peer).wait_recv()
        in_line(to_line, shard, onward(shard), source, 1 + step, start)
        to_chip(shard, source).start()
        to_core(shard, ctx, source).start()

    def pass_chip(step):
        shard = nearest(own, count, step)
        source = full.at[block(shard, other_place)]
        remote(source, source, chip_send.at[0], chip_recv.at[shard], core_peer).wait_recv()
        to_core(shard, other_place, source).start()

    pass_chip(0)
    for step in range(1, count):
        pass_line(step)
        pass_chip(step)
    out_to_chip(own, out_weight).start()
    for step in range(1, count):
        shard = nearest(own, count, step)
        source = out_full.at[side, block(shard, ctx)]
        remote(source, source, line_send.at[0], out_line_recv.at[shard], core_peer).wait_recv()
        in_line(out_to_line, shard, onward(shard), source, 1 + step, start)
        out_to_chip(shard, source).start()
        out_to_core(side, shard, ctx, source).start()
        out_to_pair(shard, ctx, source).start()

    for step in range(1, count):
        to_expert(step).start()
    gate_over.start()
    values = tokens[...].astype(jnp.float32)
    scale = lax.rsqrt(jnp.mean(values * values, axis=1, keepdims=True) + 1e-06)
    for shard in range(count):
        for place in range(2):
            spot = full.at[block(shard, place * 2 + 1 - core)]
            index = shard * 2 + place
            remote(spot, spot, core_send.at[0], core_recv.at[index], core_peer).wait_recv()
    store(full, full_hbm)
    extras[...] = full[:, ctx_size * share :]
    gain = jnp.transpose(extras[...].astype(jnp.float32))[0:1, :]
    norm[...] = (values * scale * gain).astype(jnp.bfloat16)
    store(norm, norm_hbm)

    def project(place):
        spot = pl.ds(pl.multiple_of(place * share, LANES), share)
        return dot32(norm[...], full[:, spot]).astype(jnp.bfloat16)

    def to_packed(step):
        device = (own, across(chip, core, step), side)
        return remote(
            outgoing.at[step], packed.at[ctx], packed_send.at[step], packed_recv.at[ctx], device
        )

    for step in range(3):
        outgoing[step] = project(across(chip, core, step))
        to_packed(step).start()
    packed[ctx] = project(ctx)
    for number in range(3):
        to_near(number).start()
    for step in range(count):
        shard = nearest(own, count, step)
        source = out_full.at[side, block(shard, other_place)]
        remote(source, source, line_send.at[0], out_chip_recv.at[shard], core_peer).wait_recv()
        out_to_core(side, shard, other_place, source).start()
        out_to_pair(shard, other_place, source).start()
    for step in range(1, count):
        shard = nearest(own, count, step)
        spot = upstream.at[shard, my_half]
        remote(spot, spot, rows_send.at[0], rows_recv.at[shard], pair).wait_recv()
        pass_rows(shard).start()
        store(spot, upstream_hbm.at[shard, my_half])
    gate_over.wait_recv()
    gate_far_copy.start()
    for step in range(count):
        shard = nearest(own, count, step)
        for place in (core, 2 + core):
            index = shard * 2 + place // 2
            source = out_full.at[1 - side, block(shard, place)]
            remote(source, source, line_send.at[0], out_pair_recv.at[index], pair).wait_recv()
            out_to_core(1 - side, shard, place, source).start()
    for step in range(3):
        place = across(chip, core, step)
        spot = packed.at[place]
        remote(spot, spot, packed_send.at[step], packed_recv.at[place], core_peer).wait_recv()
        spot = segments.at[place]
        remote(spot, spot, segment_send.at[step], segment_recv.at[place], core_peer).wait_recv()
    for which in (side, 1 - side):
        for shard in range(count):
            for place in range(2):
                spot = out_full.at[which, block(shard, place * 2 + 1 - core)]
                index = shard * 2 + place
                remote(
                    spot, spot, line_send.at[0], out_core_recv.at[which, index], core_peer
                ).wait_recv()
        store(out_full.at[which], out_hbm.at[which])
    for step in range(1, count):
        shard = nearest(own, count, step)
        spot = upstream_hbm.at[shard, peer_half]
        remote(spot, spot, pass_send.at[0], pass_recv.at[shard], pair).wait_recv()

    for copy in stores:
        copy.wait()
    for step in range(3):
        to_packed(step).wait_send()
        to_segment(step).wait_send()
        to_near(step).wait()
    gate_over.wait_send()
    gate_far_copy.wait()
    for forward in range(2):
        in_line(to_line, own, forward, weight, forward, sent_off)
        in_line(out_to_line, own, forward, out_weight, forward, sent_off)
    for step in range(count):
        shard = nearest(own, count, step)
        if step:
            in_line(to_line, shard, onward(shard), weight, 1 + step, sent_off)
            in_line(out_to_line, shard, onward(shard), out_weight, 1 + step, sent_off)
            to_expert(step).wait_send()
            pass_rows(shard).wait_send()
        to_chip(shard, weight).wait_send()
        out_to_chip(shard, out_weight).wait_send()
        for place in (ctx, other_place):
            to_core(shard, place, weight).wait_send()
            out_to_pair(shard, place, out_weight).wait_send()
            out_to_core(side, shard, place, out_weight).wait_send()
            out_to_core(1 - side, shard, place, out_weight).wait_send()


def run_gather(count, ctx_size, room, members, experts):
    rows, head_columns = members[0].shape
    here, width = members[7].shape
    share = 3 * head_columns // ctx_size
    columns = ctx_size * share + LANES
    dma = pltpu.SemaphoreType.DMA
    low = jnp.bfloat16
    deep, hidden = experts[0].shape
    return pl.pallas_call(
        partial(gather_project, count),
        out_shape=(
            jax.ShapeDtypeStruct((rows * count * ctx_size, columns), low),
            jax.ShapeDtypeStruct((ctx_size, here, share), low),
            jax.ShapeDtypeStruct((here, width), low),
            jax.ShapeDtypeStruct((ctx_size, 8, here), jnp.float32),
            jax.ShapeDtypeStruct((2, rows * count * ctx_size, head_columns), low),
            jax.ShapeDtypeStruct((count, room, width), low),
            *[jax.ShapeDtypeStruct((deep, hidden), low)] * 8,
            jax.ShapeDtypeStruct((here, 4), jnp.float32),
            jax.ShapeDtypeStruct((8, here), jnp.float32),
            jax.ShapeDtypeStruct((rows * count * ctx_size, LANES), low),
        ),
        in_specs=in_vmem(11) + [pl.BlockSpec(memory_space=pl.ANY)] * 3,
        out_specs=tuple(
            pl.BlockSpec(memory_space=pltpu.VMEM if number in (1, 3, 14, 15, 16) else pl.ANY)
            for number in range(17)
        ),
        scratch_shapes=[
            pltpu.VMEM((rows * count * ctx_size, columns), low),
            pltpu.VMEM((here, width), low),
            pltpu.VMEM((2, rows * count * ctx_size, head_columns), low),
            pltpu.VMEM((count, room, width), low),
            pltpu.VMEM((deep, hidden), low),
            pltpu.VMEM((deep, hidden), low),
            pltpu.VMEM((deep, hidden), low),
            pltpu.VMEM((rows, columns), low),
            pltpu.VMEM((rows, head_columns), low),
            pltpu.VMEM((8, here), jnp.float32),
            pltpu.VMEM((3, here, share), low),
            pltpu.VMEM((count - 1, room // 2, width), low),
            pltpu.VMEM((3, deep, hidden), jnp.float32),
            dma((count + 1,)),
            dma((count,)),
            dma((count,)),
            dma((count,)),
            dma((2 * count,)),
            dma((2 * count,)),
            dma((3,)),
            dma((ctx_size,)),
            dma((3,)),
            dma((ctx_size,)),
            dma((count + 1,)),
            dma((count,)),
            dma((count,)),
            dma((count,)),
            dma((2, 2 * count)),
            dma((2, 2 * count)),
            dma((2 * count,)),
            dma((2 * count,)),
            dma((count,)),
            dma((count,)),
            dma((count,)),
            dma((count,)),
            dma((5,)),
            dma((5,)),
            dma((3,)),
            dma((12,)),
        ],
        compiler_params=pltpu.CompilerParams(
            collective_id=1, has_side_effects=True, vmem_limit_bytes=67043328
        ),
        cost_estimate=estimate(60),
        name="gather_project",
    )(*members, *experts)


def attend_out(
    attended,
    tokens_hbm,
    out_hbm,
    extras_hbm,
    codes,
    hidden_hbm,
    norm_hbm,
    gates,
    low_hbm,
    gathered,
    tokens,
    out_w,
    extras,
    hidden_one,
    norm_two,
    send,
    recv,
    load_sem,
    store_sem,
):
    own, ctx, side, chip, core = places()
    here, width = tokens.shape
    heads = attended.shape[2]
    peers = [
        (across(chip, core, step), (side + other) % 2)
        for other in range(2)
        for step in range(4)
        if (other, step) != (0, 3)
    ]
    peers = peers[:2] + peers[3:5] + peers[2:3] + peers[5:]
    columns = pl.ds(pl.multiple_of(ctx * heads, heads), heads)
    loads = begin(
        (
            (attended.at[ctx], gathered.at[side, :, columns]),
            (tokens_hbm, tokens),
            (out_hbm, out_w),
            (extras_hbm, extras),
        ),
        load_sem,
    )
    greet([(own, place, which) for place, which in peers])

    def copy(number):
        place, which = peers[number]
        return remote(
            attended.at[place],
            gathered.at[side, :, columns],
            send.at[number],
            recv.at[side, ctx],
            (own, place, which),
        )

    for number in range(len(peers)):
        copy(number).start()
    for load in loads:
        load.wait()
    for place, which in peers:
        spot = gathered.at[which, :, pl.ds(pl.multiple_of(place * heads, heads), heads)]
        remote(
            spot, spot, send.at[0], recv.at[which, place], (own, place, which)
        ).wait_recv()
    stores = begin(((gathered.at[side], low_hbm),), store_sem)
    hidden = tokens[...].astype(jnp.float32) + (
        dot_last(gathered[0], out_w[0]) + dot_last(gathered[1], out_w[1])
    )
    hidden_one[...] = hidden
    stores += begin(((hidden_one, hidden_hbm),), store_sem.at[pl.ds(1, 1)])
    scale = lax.rsqrt(jnp.mean(hidden * hidden, axis=1, keepdims=True) + 1e-06)
    gain = jnp.transpose(extras[...].astype(jnp.float32))[1:2, :]
    norm = (hidden * scale * gain).astype(jnp.bfloat16)
    norm_two[...] = norm
    stores += begin(((norm_two, norm_hbm),), store_sem.at[pl.ds(2, 1)])
    logits = dot32(norm, extras[...])
    lane = lax.broadcasted_iota(jnp.int32, (here, LANES), 1).astype(jnp.float32)
    first = jnp.sum(jnp.where(lane == codes[:, 2:3] + 2.0, logits, 0.0), axis=1, keepdims=True)
    second = jnp.sum(jnp.where(lane == codes[:, 3:4] + 2.0, logits, 0.0), axis=1, keepdims=True)
    highest = jnp.maximum(first, second)
    first, second = jnp.exp(first - highest), jnp.exp(second - highest)
    gates[:, 0:1] = first / (first + second)
    gates[:, 1:2] = second / (first + second)
    for number in range(len(peers)):
        copy(number).wait_send()
    for store in stores:
        store.wait()


def run_attend_out(attended, tokens, out_w, extras, codes):
    here, width = tokens.shape
    heads = out_w.shape[2]
    low, wide = jnp.bfloat16, jnp.float32
    return pl.pallas_call(
        attend_out,
        out_shape=(
            jax.ShapeDtypeStruct((here, width), wide),
            jax.ShapeDtypeStruct((here, width), low),
            jax.ShapeDtypeStruct((here, 2), wide),
            jax.ShapeDtypeStruct((here, heads), low),
        ),
        in_specs=in_hbm(4) + in_vmem(1),
        out_specs=tuple(in_hbm(2) + in_vmem(1) + in_hbm(1)),
        scratch_shapes=[
            pltpu.VMEM((2, here, heads), low),
            pltpu.VMEM(tokens.shape, low),
            pltpu.VMEM(out_w.shape, low),
            pltpu.VMEM(extras.shape, low),
            pltpu.VMEM((here, width), wide),
            pltpu.VMEM((here, width), low),
            pltpu.SemaphoreType.DMA((7,)),
            pltpu.SemaphoreType.DMA((2, 4)),
            pltpu.SemaphoreType.DMA((4,)),
            pltpu.SemaphoreType.DMA((3,)),
        ],
        compiler_params=pltpu.CompilerParams(
            collective_id=4, has_side_effects=True, vmem_limit_bytes=67043328
        ),
        cost_estimate=estimate(25),
        name="attend_out",
    )(attended, tokens, out_w, extras, codes)


def attend_back(
    rows_hbm,
    dot_rows,
    gates,
    codes,
    extras_hbm,
    one_hbm,
    cotangent_hbm,
    norm_hbm,
    out_hbm,
    hidden_hbm,
    branch_hbm,
    heads_grad,
    small,
    rows_grad,
    extras,
    hidden_one,
    cotangent,
    norm_two,
    out_w,
    hidden_grad,
    branch_grad,
    outgoing,
    send,
    recv,
    load_sem,
    store_sem,
):
    own, ctx, side, chip, core = places()
    here, width = hidden_one.shape
    heads = heads_grad.shape[2]
    loads = begin(
        (
            (rows_hbm, rows_grad),
            (extras_hbm, extras),
            (one_hbm, hidden_one),
            (cotangent_hbm, cotangent),
            (out_hbm.at[side], out_w),
            (norm_hbm, norm_two),
        ),
        load_sem,
    )
    greet([(own, across(chip, core, step), side) for step in range(3)])
    lane = lax.broadcasted_iota(jnp.int32, (here, LANES), 1).astype(jnp.float32)
    dots = jnp.transpose(dot_rows[...])
    total = dots[:, 0:1] + dots[:, 1:2]
    logit_grad = jnp.zeros((here, LANES), jnp.float32)
    for choice in range(TOP):
        shift = dots[:, choice : choice + 1] - gates[:, choice : choice + 1] * total
        logit_grad = jnp.where(lane == codes[:, 2 + choice : 3 + choice] + 2.0, shift, logit_grad)
    for load in loads:
        load.wait()
    extra = extras[...].astype(jnp.float32)
    norm_grad = rows_grad[...] + lax.dot_general(
        logit_grad,
        extra,
        (((1,), (1,)), ((), ())),
        precision=lax.Precision.HIGHEST,
        preferred_element_type=jnp.float32,
    )
    hidden = hidden_one[...]
    scale = lax.rsqrt(jnp.mean(hidden * hidden, axis=1, keepdims=True) + 1e-06)
    normal = hidden * scale
    spread = norm_grad * jnp.transpose(extra)[1:2, :]
    found = cotangent[...].astype(jnp.float32) + scale * (
        spread - normal * jnp.mean(spread * normal, axis=1, keepdims=True)
    )
    hidden_grad[...] = found
    branch_grad[...] = found.astype(jnp.bfloat16)
    stores = begin(((hidden_grad, hidden_hbm), (branch_grad, branch_hbm)), store_sem)

    def project(place):
        columns = pl.ds(pl.multiple_of(place * heads, heads), heads)
        return dot32(branch_grad[...], out_w[:, columns]).astype(jnp.bfloat16)

    def copy(step):
        place = across(chip, core, step)
        return remote(
            outgoing.at[step], heads_grad.at[ctx], send.at[step], recv.at[ctx], (own, place, side)
        )

    for step in range(3):
        outgoing[step] = project(across(chip, core, step))
        copy(step).start()
    outgoing[3] = project(ctx)
    stores += begin(((outgoing.at[3], heads_grad.at[ctx]),), store_sem.at[pl.ds(2, 1)])
    gain_row = jnp.sum(norm_grad * normal, axis=0, keepdims=True)
    routed = jnp.dot(
        jnp.transpose(logit_grad),
        norm_two[...].astype(jnp.float32),
        precision=lax.Precision.HIGHEST,
        preferred_element_type=jnp.float32,
    )
    line = lax.broadcasted_iota(jnp.int32, (8, width), 0)
    small[...] = jnp.where(line == 1, gain_row, routed[0:8])
    for step in range(3):
        place = across(chip, core, step)
        spot = heads_grad.at[place]
        remote(spot, spot, send.at[0], recv.at[place], (own, place, side)).wait_recv()
    for step in range(3):
        copy(step).wait_send()
    for store in stores:
        store.wait()


def run_attend_back(
    rows_grad, dot_rows, gates, codes, extras, hidden_one, cotangent, norm_two, out_w
):
    here, width = hidden_one.shape
    low, wide = jnp.bfloat16, jnp.float32
    heads = out_w.shape[2] // 4
    return pl.pallas_call(
        attend_back,
        out_shape=(
            jax.ShapeDtypeStruct((here, width), wide),
            jax.ShapeDtypeStruct((here, width), low),
            jax.ShapeDtypeStruct((4, here, heads), low),
            jax.ShapeDtypeStruct((8, width), wide),
        ),
        in_specs=in_hbm(1) + in_vmem(3) + in_hbm(5),
        out_specs=tuple(in_hbm(3) + in_vmem(1)),
        scratch_shapes=[
            pltpu.VMEM((here, width), wide),
            pltpu.VMEM(extras.shape, low),
            pltpu.VMEM((here, width), wide),
            pltpu.VMEM((here, width), low),
            pltpu.VMEM((here, width), low),
            pltpu.VMEM(out_w.shape[1:], low),
            pltpu.VMEM((here, width), wide),
            pltpu.VMEM((here, width), low),
            pltpu.VMEM((4, here, heads), low),
            pltpu.SemaphoreType.DMA((3,)),
            pltpu.SemaphoreType.DMA((4,)),
            pltpu.SemaphoreType.DMA((6,)),
            pltpu.SemaphoreType.DMA((3,)),
        ],
        compiler_params=pltpu.CompilerParams(
            collective_id=5, has_side_effects=True, vmem_limit_bytes=67043328
        ),
        cost_estimate=estimate(4),
        name="attend_back",
    )(rows_grad, dot_rows, gates, codes, extras, hidden_one, cotangent, norm_two, out_w)


def gradient_return(
    count,
    packed_grad,
    full_hbm,
    norm,
    tokens,
    bias_line,
    own_hbm,
    first_hbm,
    one_out_hbm,
    near_out_hbm,
    two_out_hbm,
    three_out_hbm,
    last_hbm,
    gates,
    codes,
    branch_grad,
    attended,
    small,
    one_hbm,
    grad_hbm,
    extras,
    mixed,
    input_grad,
    query_grad,
    key_grad,
    value_grad,
    bias_grad,
    gain_grad,
    out_grad,
    mixture,
    mixture_in,
    full,
    outs,
    hidden_one,
    hidden_grad,
    incoming,
    norm_t,
    outgoing,
    side_out,
    side_in,
    spread,
    core_in,
    chip_out,
    chip_in,
    line_out,
    line_in,
    out_going,
    out_core_in,
    out_spread,
    out_chip_out,
    out_chip_in,
    out_line_out,
    out_line_in,
    bias_out,
    bias_in,
    spread_gain,
    grad_send,
    grad_recv,
    side_send,
    side_recv,
    core_send,
    core_recv,
    chip_send,
    chip_recv,
    line_send,
    line_recv,
    bias_send,
    bias_recv,
    mixture_sem,
    mix_sem,
    load_sem,
):
    own, ctx, side, chip, core = places()
    ctx_size, here, share = packed_grad.shape
    width = norm.shape[1]
    halves = 2
    part = here // halves
    groups = ctx_size
    pair = (own, ctx, 1 - side)
    chip_peer = (own, (1 - chip) * 2 + core, side)
    core_peer = (own, chip * 2 + 1 - core, side)
    others = [
        (nearest(own, count, step), across(chip, core, turn), side)
        for step in range(count)
        for turn in range(4)
        if (step, turn) != (0, 3)
    ]
    room, half = outs.shape[1], last_hbm.shape[0]
    pairs = (
        (full_hbm, full),
        (own_hbm, outs.at[0]),
        (grad_hbm, hidden_grad),
        (one_hbm, hidden_one),
        (first_hbm, outs.at[1, pl.ds(0, half)]),
        (one_out_hbm, outs.at[1, pl.ds(half, half)]),
        (near_out_hbm, outs.at[2, pl.ds(0, half)]),
        (two_out_hbm, outs.at[2, pl.ds(half, half)]),
        (three_out_hbm, outs.at[3, pl.ds(0, half)]),
    )
    loads = [
        pltpu.make_async_copy(source, target, load_sem.at[number])
        for number, (source, target) in enumerate(pairs)
    ]
    for load in loads:
        load.start()
    greet(others + [pair])

    def to_owner(step, piece):
        place = across(chip, core, step)
        spot = pl.ds(piece * part, part)
        return remote(
            packed_grad.at[place, spot],
            incoming.at[ctx, spot],
            grad_send.at[step, piece],
            grad_recv.at[ctx, piece],
            (own, place, side),
        )

    for piece in range(halves):
        for step in range(3):
            to_owner(step, piece).start()
    incoming[ctx] = packed_grad[ctx]

    mixture_copy = remote(mixture, mixture_in, mixture_sem.at[0], mixture_sem.at[1], pair)

    def mixing(start, amount):
        slots = lax.broadcasted_iota(jnp.int32, (here, amount), 1) + start
        slots = slots.astype(jnp.float32)
        held = jnp.where(codes[:, 0:1] == slots, gates[:, 0:1], 0.0)
        held = held + jnp.where(codes[:, 1:2] == slots, gates[:, 1:2], 0.0)
        return held.astype(jnp.bfloat16)

    last_copy = remote(
        last_hbm,
        outs.at[3, pl.ds(half, half)],
        mix_sem.at[0],
        mix_sem.at[1],
        (partner(own, 3), ctx, side),
    )
    last_copy.start()

    def mix():
        for number in (1, 4, 5, 6, 7, 8):
            loads[number].wait()
        last_copy.wait_recv()
        total = jnp.zeros((here, width), jnp.float32)
        for turn in range(count):
            total = total + dot32(mixing(partner(own, turn) * room, room), outs[turn])
        mixture[...] = total.astype(jnp.bfloat16)
        mixture_copy.start()

    span = bias_line.shape[1]
    index = lax.broadcasted_iota(jnp.int32, (span, LANES), 0)
    relative = jnp.where(index < span // 2, -index, span - index)
    bucket = lax.broadcasted_iota(jnp.int32, (span, LANES), 1)
    onehot = jnp.where(bucket_ids(relative) == bucket, 1.0, 0.0)
    sums = jnp.dot(
        bias_line[...], onehot, precision=lax.Precision.HIGHEST, preferred_element_type=jnp.float32
    )
    far = jnp.sum(bias_line[...], axis=1, keepdims=True)
    lane = lax.broadcasted_iota(jnp.int32, (2, LANES), 1)
    total = sums[0:2] + jnp.where(lane == NBUCK // 2 - 1, far[2:4], 0.0)
    total = total + jnp.where(lane == NBUCK - 1, far[4:6], 0.0)
    bias_sum = jnp.concatenate([total, jnp.zeros((6, LANES), jnp.float32)], axis=0)

    def to_bias(number):
        return remote(
            bias_out.at[number],
            bias_in.at[own, ctx],
            bias_send.at[number],
            bias_recv.at[own, ctx],
            others[number],
        )

    stages = [
        (
            outgoing.at[group],
            core_in.at[group],
            spread.at[group],
            chip_out.at[group],
            chip_in.at[group],
            line_out.at[group],
            line_in.at[group],
            None,
        )
        for group in range(groups)
    ]
    stages.append(
        (
            out_going,
            out_core_in,
            out_spread,
            out_chip_out,
            out_chip_in,
            out_line_out,
            out_line_in,
            None,
        )
    )
    rows = norm_t.shape[0] // (count * ctx_size)

    def to_core(group):
        source, target = stages[group][0].at[:, 1 - core], stages[group][1]
        return remote(source, target, core_send.at[group], core_recv.at[group], core_peer)

    def to_chip(group):
        source, target = stages[group][3], stages[group][4]
        return remote(source, target, chip_send.at[group], chip_recv.at[group], chip_peer)

    def to_line(group, step):
        shard = nearest(own, count, step)
        source, target = stages[group][5].at[shard], stages[group][6].at[own]
        send, recv = line_send.at[group, step], line_recv.at[group, own]
        return remote(source, target, send, recv, (shard, ctx, side))

    def contract(group):
        found = dot32(norm_t[...], incoming[group] if group < groups else attended[...])
        found = found.reshape(count * 2, 2, rows, found.shape[1])
        stages[group][0][...] = found.astype(jnp.bfloat16)
        to_core(group).start()

    def over_chip(group):
        to_core(group).wait_recv()
        source, arrived, summed, target = stages[group][:4]
        found = source[:, core].astype(jnp.float32) + arrived[...].astype(jnp.float32)
        summed[...] = found.reshape(count, 2, rows, found.shape[2])
        target[...] = summed[:, 1 - chip].astype(jnp.bfloat16)
        to_chip(group).start()

    def over_line(group):
        to_chip(group).wait_recv()
        found = stages[group][2][:, chip] + stages[group][4][...].astype(jnp.float32)
        stages[group][5][...] = found.astype(jnp.bfloat16)
        for step in range(1, count):
            to_line(group, step).start()

    def collect(group):
        total = stages[group][5][own].astype(jnp.float32)
        for step in range(1, count):
            shard = nearest(own, count, step)
            spot = stages[group][6].at[shard]
            remote(
                spot, spot, line_send.at[group, 0], line_recv.at[group, shard], pair
            ).wait_recv()
            total = total + spot[...].astype(jnp.float32)
        if group == groups:
            out_grad[...] = total
        else:
            columns = slice(group * LANES, (group + 1) * LANES)
            for number, target in enumerate((query_grad, key_grad, value_grad)):
                target[:, columns] = total[:, number * LANES : (number + 1) * LANES]

    norm_t[...] = jnp.transpose(branch_grad[...].astype(jnp.float32)).astype(jnp.bfloat16)
    contract(groups)
    norm_t[...] = jnp.transpose(norm[...].astype(jnp.float32)).astype(jnp.bfloat16)
    over_chip(groups)

    def to_side(piece):
        return remote(
            side_out.at[piece],
            side_in.at[piece],
            side_send.at[piece],
            side_recv.at[piece],
            pair,
        )

    values = tokens[...].astype(jnp.float32)
    scale = lax.rsqrt(jnp.mean(values * values, axis=1, keepdims=True) + 1e-06)
    normal = values * scale
    first_gain = jnp.transpose(extras[...].astype(jnp.float32))[0:1, :]
    loads[0].wait()

    def landed(piece):
        for step in range(3):
            place = across(chip, core, step)
            target = incoming.at[place, pl.ds(piece * part, part)]
            remote(
                target, target, grad_send.at[0, 0], grad_recv.at[place, piece], pair
            ).wait_recv()

    def send_side(piece):
        spot = pl.ds(piece * part, part)
        total = jnp.zeros((part, width), jnp.float32)
        for place in range(ctx_size):
            columns = slice(place * share, (place + 1) * share)
            total = total + dot_last(incoming[place, spot, :], full[:, columns])
        side_out[piece] = total.astype(jnp.bfloat16)
        to_side(piece).start()

    def finish_sides():
        loads[2].wait()
        gain = jnp.zeros((1, width), jnp.float32)
        for piece in range(halves):
            to_side(piece).wait_recv()
            total = side_out[piece].astype(jnp.float32) + side_in[piece].astype(jnp.float32)
            lines = slice(piece * part, (piece + 1) * part)
            upright = normal[lines]
            gain = gain + jnp.sum(total * upright, axis=0, keepdims=True)
            total = total * first_gain
            total = total - upright * jnp.mean(total * upright, axis=1, keepdims=True)
            input_grad[lines, :] = (hidden_grad[lines, :] + scale[lines] * total).astype(
                jnp.bfloat16
            )
        spread_gain[...] = small[...]
        spread_gain[0:1, :] = gain

        def message(shard, place):
            lanes = pl.ds(pl.multiple_of((shard * 2 + place // 2) * LANES, LANES), LANES)
            return jnp.concatenate([bias_sum, spread_gain[:, lanes]], axis=0)

        for number, (shard, place, _) in enumerate(others):
            bias_out[number] = message(shard, place)
            to_bias(number).start()
        bias_in[own, ctx] = message(own, ctx)

    landed(0)
    send_side(0)
    landed(1)
    contract(0)
    send_side(1)
    over_chip(0)
    contract(1)
    contract(2)
    over_chip(1)
    mix()
    contract(3)
    over_chip(2)
    over_line(groups)
    over_chip(3)
    over_line(0)
    over_line(1)
    over_line(2)
    over_line(3)
    finish_sides()
    for group in (groups, 0, 1, 2, 3):
        collect(group)

    for number, (shard, place, _) in enumerate(others):
        spot = bias_in.at[shard, place]
        remote(spot, spot, bias_send.at[0], bias_recv.at[shard, place], pair).wait_recv()
    for place in range(ctx_size):
        total = bias_in[0, place]
        for shard in range(1, count):
            total = total + bias_in[shard, place]
        bias_grad[place] = total[:8]
        gain_total = total[8:] if place == 0 else gain_total + total[8:]
    gain_grad[...] = gain_total

    mixture_copy.wait()
    loads[3].wait()
    last_copy.wait_send()
    mixed[...] = (
        hidden_one[...] + (mixture[...].astype(jnp.float32) + mixture_in[...].astype(jnp.float32))
    ).astype(jnp.bfloat16)
    for number in range(len(others)):
        to_bias(number).wait_send()
    for piece in range(halves):
        to_side(piece).wait_send()
        for step in range(3):
            to_owner(step, piece).wait_send()
    for group in range(groups + 1):
        to_core(group).wait_send()
        to_chip(group).wait_send()
        for step in range(1, count):
            to_line(group, step).wait_send()


def run_return(
    count,
    packed_grad,
    full,
    norm,
    tokens,
    bias_line,
    outs,
    gates,
    codes,
    branch_grad,
    attended,
    small,
    hidden_one,
    hidden_grad,
    extras,
):
    ctx_size, here, share = packed_grad.shape
    width = norm.shape[1]
    rows = width // (count * ctx_size)
    low, wide = jnp.bfloat16, jnp.float32
    dma = pltpu.SemaphoreType.DMA
    columns = share
    out_columns = attended.shape[1]
    return pl.pallas_call(
        partial(gradient_return, count),
        out_shape=(
            jax.ShapeDtypeStruct((here, width), low),
            jax.ShapeDtypeStruct((here, width), low),
            *[jax.ShapeDtypeStruct((rows, ctx_size * LANES), wide)] * 3,
            jax.ShapeDtypeStruct((ctx_size, 8, LANES), wide),
            jax.ShapeDtypeStruct((8, LANES), wide),
            jax.ShapeDtypeStruct((rows, out_columns), wide),
        ),
        in_specs=[
            pl.BlockSpec(memory_space=pl.ANY if number in (1, 5, 6, 7, 8, 9, 10, 11, 17, 18) else pltpu.VMEM)
            for number in range(20)
        ],
        out_specs=tuple(in_vmem(8)),
        scratch_shapes=[
            pltpu.VMEM((here, width), low),
            pltpu.VMEM((here, width), low),
            pltpu.VMEM(full.shape, low),
            pltpu.VMEM((count,) + outs[0].shape, low),
            pltpu.VMEM((here, width), wide),
            pltpu.VMEM((here, width), wide),
            pltpu.VMEM((ctx_size, here, share), low),
            pltpu.VMEM((width, here), low),
            pltpu.VMEM((ctx_size, count * 2, 2, rows, columns), low),
            pltpu.VMEM((2, here // 2, width), low),
            pltpu.VMEM((2, here // 2, width), low),
            pltpu.VMEM((ctx_size, count, 2, rows, columns), wide),
            pltpu.VMEM((ctx_size, count * 2, rows, columns), low),
            pltpu.VMEM((ctx_size, count, rows, columns), low),
            pltpu.VMEM((ctx_size, count, rows, columns), low),
            pltpu.VMEM((ctx_size, count, rows, columns), low),
            pltpu.VMEM((ctx_size, count, rows, columns), low),
            pltpu.VMEM((count * 2, 2, rows, out_columns), low),
            pltpu.VMEM((count * 2, rows, out_columns), low),
            pltpu.VMEM((count, 2, rows, out_columns), wide),
            pltpu.VMEM((count, rows, out_columns), low),
            pltpu.VMEM((count, rows, out_columns), low),
            pltpu.VMEM((count, rows, out_columns), low),
            pltpu.VMEM((count, rows, out_columns), low),
            pltpu.VMEM((15, 16, LANES), wide),
            pltpu.VMEM((count, ctx_size, 16, LANES), wide),
            pltpu.VMEM((8, width), wide),
            dma((3, 2)),
            dma((ctx_size, 2)),
            dma((2,)),
            dma((2,)),
            dma((ctx_size + 1,)),
            dma((ctx_size + 1,)),
            dma((ctx_size + 1,)),
            dma((ctx_size + 1,)),
            dma((ctx_size + 1, count)),
            dma((ctx_size + 1, count)),
            dma((15,)),
            dma((count, ctx_size)),
            dma((2,)),
            dma((2,)),
            dma((9,)),
        ],
        compiler_params=pltpu.CompilerParams(
            collective_id=2, has_side_effects=True, vmem_limit_bytes=67043328
        ),
        cost_estimate=estimate(45),
        name="gradient_return",
    )(
        packed_grad,
        full,
        norm,
        tokens,
        bias_line,
        *outs,
        gates,
        codes,
        branch_grad,
        attended,
        small,
        hidden_one,
        hidden_grad,
        extras,
    )


def swap_sides(member):
    return lax.ppermute(member, "tensor", [(0, 1), (1, 0)])


def exchange(member, axis):
    return lax.all_to_all(member, axis, split_axis=0, concat_axis=0, tiled=True)


def slot_codes(routes, experts, room):
    tokens = routes.shape[0]
    picks = routes[:, :, None] == jnp.arange(experts, dtype=jnp.int32)[None, None, :]
    named = jnp.sum(picks, axis=1).astype(jnp.bfloat16)
    index = jnp.arange(tokens, dtype=jnp.int32)
    before = (index[:, None] > index[None, :]).astype(jnp.bfloat16)
    rank = jnp.dot(before, named, preferred_element_type=jnp.float32)
    slots = rank + room * jnp.arange(experts, dtype=jnp.float32)[None, :]
    return picks, jnp.sum(jnp.where(picks, slots[:, None, :], 0.0), axis=2)


def experts_apart(norm_two, upstream, gates, codes, room, count, weights):
    tokens, width = norm_two.shape
    codes = codes.astype(jnp.int32).reshape(-1)
    shaped = (count, room, width)

    def sent(member):
        slots = jnp.zeros((count * room, width), jnp.bfloat16).at[codes].set(member)
        return exchange(slots.reshape(shaped), "shard").reshape(-1, width)

    slot_rows = sent(jnp.repeat(norm_two, TOP, axis=0))
    slot_grads = sent(
        (gates[:, :, None] * upstream[:, None, :]).reshape(-1, width).astype(jnp.bfloat16)
    )
    gate_mat, up_mat, down_mat = weights
    gate_pre = dot32(slot_rows, gate_mat)
    up_pre = dot32(slot_rows, up_mat)
    activated, slope = gelu_parts(gate_pre)
    inner = (activated * up_pre).astype(jnp.bfloat16)
    expert_out = contract_cols(inner, down_mat)
    inner_grad = dot32(slot_grads, down_mat)
    gate_grad = (inner_grad * up_pre * slope).astype(jnp.bfloat16)
    up_grad = (inner_grad * activated).astype(jnp.bfloat16)
    rows_grad = contract_cols(gate_grad, gate_mat) + contract_cols(up_grad, up_mat)

    def returned(member):
        member = lax.psum(member.astype(jnp.bfloat16), "tensor").reshape(shaped)
        member = exchange(member, "shard").reshape(-1, width)[codes]
        return member.astype(jnp.float32).reshape(tokens, TOP, width)

    per_choice = returned(expert_out)
    mixture = jnp.sum(gates[:, :, None] * per_choice, axis=1)
    dots = gates * jnp.sum(per_choice * upstream[:, None, :], axis=2)
    norm_grad = jnp.sum(returned(rows_grad), axis=1)
    return mixture, dots, norm_grad, slot_rows, slot_grads, inner, gate_grad, up_grad


def local_general(
    tokens_in,
    cotangent,
    segment_ids,
    live_blocks,
    routes,
    w_query,
    w_key,
    w_value,
    w_out,
    rel_bias,
    attn_gain,
    ffn_gain,
    router,
    w_gate,
    w_up,
    w_down,
):
    rows_here, width = tokens_in.shape
    ctx_size = lax.axis_size("ctx")
    side_count = lax.axis_size("tensor")
    ctx_index = lax.axis_index("ctx")
    side = lax.axis_index("tensor")
    head_cols = w_query.shape[1]
    share = head_cols // ctx_size
    experts = router.shape[1]
    room = max(2, 3 * rows_here // experts)

    picks, codes = slot_codes(routes, experts, room)

    def by_owner(member):
        return member.reshape(member.shape[0], ctx_size, share)

    packed_rows = jnp.stack([by_owner(w_query), by_owner(w_key), by_owner(w_value)], axis=2)
    gathered = lax.all_gather(
        jnp.concatenate(
            [
                packed_rows.reshape(w_query.shape[0], -1),
                attn_gain[:, None],
                ffn_gain[:, None],
                router,
            ],
            axis=1,
        ).astype(jnp.bfloat16),
        ("shard", "ctx"),
        axis=0,
        tiled=True,
    )
    packed_w = gathered[:, : 3 * head_cols]
    gain_one = gathered[:, 3 * head_cols]
    gain_two = gathered[:, 3 * head_cols + 1]
    router_w = gathered[:, 3 * head_cols + 2 :]
    out_w = lax.all_gather(w_out.astype(jnp.bfloat16), ("shard", "ctx", "tensor"), axis=0)
    out_w = out_w.reshape(-1, side_count, w_out.shape[0], head_cols)
    out_w = jnp.transpose(out_w, (0, 2, 1, 3)).reshape(width, side_count * head_cols)
    expert_weights = tuple(
        lax.all_gather(member.astype(jnp.bfloat16), "ctx", axis=1, tiled=True)[0]
        for member in (w_gate, w_up, w_down)
    )

    inputs = tokens_in.astype(jnp.float32)
    scale_one = lax.rsqrt(jnp.mean(inputs * inputs, axis=1, keepdims=True) + 1e-06)
    normal_one = inputs * scale_one
    norm_one = (normal_one * gain_one.astype(jnp.float32)).astype(jnp.bfloat16)
    packed = dot32(norm_one, packed_w).astype(jnp.bfloat16)
    packed = jnp.transpose(packed.reshape(rows_here, ctx_size, 3 * share), (1, 0, 2))
    packed = exchange(packed, "ctx").reshape(ctx_size * rows_here, 3 * share)
    segments = lax.all_gather(segment_ids.reshape(-1), "ctx", axis=0, tiled=True)
    alive = live_tiles(segments, live_blocks[0])
    segment_row = segments.astype(jnp.float32)[None]
    pair_heads = share // HEAD
    own_bias = lax.dynamic_slice_in_dim(rel_bias, ctx_index * pair_heads, pair_heads, 1)
    buckets = span_buckets()
    line = jnp.dot(own_bias.T, buckets.T, precision=lax.Precision.HIGHEST)
    attended, attended_t, log_sum = run_forward(alive, packed, segment_row, line)
    attended = attended.reshape(ctx_size, 1, rows_here, share)
    attended = jnp.broadcast_to(attended, (ctx_size, side_count, rows_here, share))
    attended = exchange(attended.reshape(-1, rows_here, share), ("ctx", "tensor"))
    attended = attended.reshape(ctx_size, side_count, rows_here, share)
    attended = jnp.transpose(attended, (2, 1, 0, 3))
    attended_low = lax.dynamic_index_in_dim(attended, side, 1, False).reshape(rows_here, head_cols)
    attended = attended.reshape(rows_here, side_count * head_cols)
    hidden_one = inputs + contract_cols(attended, out_w)
    scale_two = lax.rsqrt(jnp.mean(hidden_one * hidden_one, axis=1, keepdims=True) + 1e-06)
    normal_two = hidden_one * scale_two
    norm_two = (normal_two * gain_two.astype(jnp.float32)).astype(jnp.bfloat16)
    logits = dot32(norm_two, router_w)
    chosen = jnp.sum(jnp.where(picks, logits[:, None, :], 0.0), axis=2)
    gates = jax.nn.softmax(chosen, axis=1)
    upstream = cotangent.astype(jnp.float32)
    results = experts_apart(norm_two, upstream, gates, codes, room, experts, expert_weights)
    mixture, gate_dots, norm_grad, slot_rows, slot_grads, inner, gate_grad, up_grad = results
    weight_grads = lax.psum_scatter(
        jnp.stack(
            [
                contract_rows(slot_rows, gate_grad),
                contract_rows(slot_rows, up_grad),
                contract_rows(slot_grads, inner),
            ],
            axis=1,
        ).astype(jnp.bfloat16),
        "ctx",
        scatter_dimension=0,
        tiled=True,
    ).astype(jnp.float32)
    mixed = (hidden_one + mixture).astype(jnp.bfloat16)
    gate_shift = gate_dots - gates * jnp.sum(gate_dots, axis=1, keepdims=True)
    logit_grad = jnp.sum(jnp.where(picks, gate_shift[:, :, None], 0.0), axis=1)
    router_f = router_w.astype(jnp.float32)
    norm_grad = norm_grad + jnp.dot(logit_grad, router_f.T, precision=lax.Precision.HIGHEST)
    spread_two = norm_grad * gain_two.astype(jnp.float32)
    hidden_grad = upstream + scale_two * (
        spread_two - normal_two * jnp.mean(spread_two * normal_two, axis=1, keepdims=True)
    )
    branch_grad = hidden_grad.astype(jnp.bfloat16)
    own_out_w = lax.dynamic_slice_in_dim(out_w, side * head_cols, head_cols, 1)
    grad_heads = dot32(branch_grad, own_out_w).astype(jnp.bfloat16)
    grad_heads = jnp.transpose(grad_heads.reshape(rows_here, ctx_size, share), (1, 0, 2))
    grad_heads = exchange(grad_heads, "ctx").reshape(-1, share)
    packed_grad, bias_line = run_backward(
        alive, packed, segment_row, line, grad_heads, attended_t, log_sum
    )
    own_grad = jnp.dot(buckets.T, bias_line[:pair_heads].T, precision=lax.Precision.HIGHEST)
    far = jnp.sum(bias_line[pair_heads : 3 * pair_heads], axis=1)
    half = NBUCK // 2
    own_grad = own_grad.at[half - 1].add(far[:pair_heads]).at[NBUCK - 1].add(far[pair_heads:])
    bias_acc = lax.dynamic_update_slice_in_dim(
        jnp.zeros(rel_bias.shape, jnp.float32), own_grad, ctx_index * pair_heads, 1
    )
    packed_grad = exchange(packed_grad.reshape(ctx_size, rows_here, 3 * share), "ctx")
    packed_grad = jnp.transpose(packed_grad, (1, 0, 2)).reshape(rows_here, 3 * head_cols)
    norm_one_grad = contract_cols(packed_grad, packed_w).astype(jnp.bfloat16)
    norm_one_grad = norm_one_grad.astype(jnp.float32) + swap_sides(norm_one_grad).astype(
        jnp.float32
    )
    spread_one = norm_one_grad * gain_one.astype(jnp.float32)
    input_grad = hidden_grad + scale_one * (
        spread_one - normal_one * jnp.mean(spread_one * normal_one, axis=1, keepdims=True)
    )
    first_gain = jnp.sum(norm_one_grad * normal_one, axis=0)[:, None]
    second_gain = jnp.sum(norm_grad * normal_two, axis=0)[:, None]
    router_part = jnp.dot(
        norm_two.astype(jnp.float32).T, logit_grad, precision=lax.Precision.HIGHEST
    )
    reduced = lax.psum_scatter(
        jnp.concatenate(
            [
                contract_rows(norm_one, packed_grad),
                contract_rows(branch_grad, attended_low),
                first_gain,
                second_gain,
                router_part,
            ],
            axis=1,
        ),
        ("shard", "ctx"),
        scatter_dimension=0,
        tiled=True,
    )
    grad_bias = lax.psum(bias_acc, ("shard", "ctx"))
    packed_rows = reduced[:, : 3 * head_cols].reshape(-1, ctx_size, 3, share)
    return (
        mixed,
        input_grad.astype(jnp.bfloat16),
        packed_rows[:, :, 0].reshape(-1, head_cols),
        packed_rows[:, :, 1].reshape(-1, head_cols),
        packed_rows[:, :, 2].reshape(-1, head_cols),
        reduced[:, 3 * head_cols : 4 * head_cols],
        grad_bias,
        reduced[:, 4 * head_cols],
        reduced[:, 4 * head_cols + 1],
        reduced[:, 4 * head_cols + 2 :],
        weight_grads[:, 0][None],
        weight_grads[:, 1][None],
        weight_grads[:, 2][None],
    )


def ppermute_ctx(member, flip):
    return lax.ppermute(member, "ctx", [(place, place ^ flip) for place in range(4)])


def local_fused(
    tokens_in,
    cotangent,
    segment_ids,
    live_blocks,
    routes,
    w_query,
    w_key,
    w_value,
    w_out,
    rel_bias,
    attn_gain,
    ffn_gain,
    router,
    w_gate,
    w_up,
    w_down,
):
    rows_here, width = tokens_in.shape
    count = lax.axis_size("shard")
    ctx_size = lax.axis_size("ctx")
    ctx_index = lax.axis_index("ctx")
    share = w_query.shape[1] // ctx_size
    rows = w_query.shape[0]
    experts = router.shape[1]
    room = max(2, 3 * rows_here // experts)
    members = (
        w_query,
        w_key,
        w_value,
        w_out,
        attn_gain[None],
        ffn_gain[None],
        router.T,
        tokens_in,
        segment_ids,
        cotangent,
        routes.T,
    )
    full, packed, norm_one, segments, out_w, up_slots, *lows = run_gather(
        count, ctx_size, room, members, (w_gate[0], w_up[0], w_down[0])
    )
    gate_low, up_low, down_low, gate_core, up_core, down_core, gate_chip, gate_far = lows[:8]
    codes, code_rows, extras = lows[8:]
    up_chip, down_chip = ppermute_ctx(up_low, 2), ppermute_ctx(down_low, 2)

    packed = packed.reshape(ctx_size * rows_here, 3 * share)
    segment_row = segments[:, 0].reshape(1, -1)
    alive = live_tiles(segment_row[0], live_blocks[0])
    pair_heads = share // HEAD
    own_bias = lax.dynamic_slice_in_dim(rel_bias, ctx_index * pair_heads, pair_heads, 1)
    line = jnp.dot(own_bias.T, span_buckets().T, precision=lax.Precision.HIGHEST)
    attended, attended_t, log_sum = run_forward(alive, packed, segment_row, line)
    attended, up_chip, down_chip = lax.optimization_barrier((attended, up_chip, down_chip))
    expert_weights = [gate_low, gate_chip, gate_core, gate_far]
    expert_weights += [up_low, up_chip, up_core, ppermute_ctx(up_chip, 1)]
    expert_weights += [down_low, down_chip, down_core, ppermute_ctx(down_chip, 1)]
    hidden_one, norm_two, gates, attended_low = run_attend_out(
        attended.reshape(ctx_size, rows_here, share), tokens_in, out_w, extras, codes
    )
    rows_grad, dots, own_out, *outs, last_out, kept, gate_given, pair_given = run_experts(
        count, ctx_size, norm_two, gates, code_rows, codes, up_slots, expert_weights
    )
    for number, turn in enumerate((1, 1, 2, 2, 3)):
        pairs = [(place, place ^ turn) for place in range(count)]
        outs[number] = lax.ppermute(outs[number], "shard", pairs)
    hidden_grad, branch_grad, heads_grad, small = run_attend_back(
        rows_grad, dots, gates, codes, extras, hidden_one, cotangent, norm_two, out_w
    )
    heads_grad, pair_given, outs[0] = lax.optimization_barrier((heads_grad, pair_given, outs[0]))
    pair_given = ppermute_ctx(pair_given, 2)
    outs = [own_out, *outs, last_out]
    given = [gate_given, pair_given[0], pair_given[1]]
    weight_grads = [
        kept[number].astype(jnp.float32) + given[number].astype(jnp.float32) for number in range(3)
    ]
    packed_grad, bias_line = run_backward(
        alive, packed, segment_row, line, heads_grad.reshape(-1, share), attended_t, log_sum
    )
    returned = run_return(
        count,
        packed_grad.reshape(ctx_size, rows_here, 3 * share),
        full,
        norm_one,
        tokens_in,
        bias_line,
        outs,
        gates,
        codes,
        branch_grad,
        attended_low,
        small,
        hidden_one,
        hidden_grad,
        extras,
    )
    mixed, input_grad, query_grad, key_grad, value_grad, bias_grad, gains_grad, out_grad = returned
    gains_grad = lax.dynamic_slice_in_dim(gains_grad, ctx_index % 2 * rows, rows, 1)
    bias_grad = jnp.transpose(bias_grad[:, :pair_heads, :NBUCK], (2, 0, 1))
    return (
        mixed,
        input_grad,
        query_grad,
        key_grad,
        value_grad,
        out_grad,
        bias_grad.reshape(rel_bias.shape),
        gains_grad[0],
        gains_grad[1],
        jnp.transpose(gains_grad[2 : 2 + experts]),
        weight_grads[0][None],
        weight_grads[1][None],
        weight_grads[2][None],
    )


def solution(mesh):
    placed = (
        P(("shard", "ctx"), None),
        P(("shard", "ctx"), None),
        P("shard", "ctx"),
        P("shard", None, None),
        P(("shard", "ctx"), None),
        P(("shard", "ctx"), "tensor"),
        P(("shard", "ctx"), "tensor"),
        P(("shard", "ctx"), "tensor"),
        P(("shard", "ctx"), "tensor"),
        P(None, "tensor"),
        P(("shard", "ctx")),
        P(("shard", "ctx")),
        P(("shard", "ctx"), None),
        P("shard", "ctx", "tensor"),
        P("shard", "ctx", "tensor"),
        P("shard", "ctx", "tensor"),
    )
    sizes = (mesh.shape["shard"], mesh.shape["ctx"], mesh.shape["tensor"])
    fused = sizes == (4, 4, 2)
    return jax.shard_map(
        local_fused if fused else local_general,
        mesh=mesh,
        in_specs=placed,
        out_specs=(
            P(("shard", "ctx"), None),
            P(("shard", "ctx"), None),
            P(("shard", "ctx"), "tensor"),
            P(("shard", "ctx"), "tensor"),
            P(("shard", "ctx"), "tensor"),
            P(("shard", "ctx"), "tensor"),
            P(None, "tensor"),
            P(("shard", "ctx")),
            P(("shard", "ctx")),
            P(("shard", "ctx"), None),
            P("shard", "ctx", "tensor"),
            P("shard", "ctx", "tensor"),
            P("shard", "ctx", "tensor"),
        ),
        check_vma=False,
    )
```

```python
import math
from functools import partial

import jax
import jax.numpy as jnp
from jax import lax
from jax.experimental import pallas as pl
from jax.experimental.pallas import tpu as pltpu
from jax.sharding import PartitionSpec as P

HEAD = 64
NBUCK = 32
TOP = 2
ATT_BLK = 512


FAR_STEPS = (12, 16, 23, 32, 46, 64, 91)


def bucket_ids(relative):
    distance = jnp.abs(relative)
    far = jnp.full(distance.shape, 8, jnp.int32)
    for bound in FAR_STEPS:
        far = far + (distance >= bound).astype(jnp.int32)
    near = jnp.where(distance < 8, distance, far)
    return near + jnp.where(relative > 0, NBUCK // 2, 0)


def contract_rows(left, right):
    return lax.dot_general(
        left, right, (((0,), (0,)), ((), ())), preferred_element_type=jnp.float32
    )


def contract_cols(left, right):
    return lax.dot_general(
        left, right, (((1,), (1,)), ((), ())), preferred_element_type=jnp.float32
    )


TILE = 256
BIG = 2.0**100
SPAN = 4 * TILE


def place_mask(segment_row):
    rows = lax.broadcasted_iota(jnp.int32, (128, segment_row.shape[1]), 0).astype(jnp.float32)
    apart = jnp.where(rows == segment_row, 0.0, -BIG)
    return jnp.where(rows < 8.0, apart, jnp.where(rows < 11.0, 1.0, 0.0))


def seat_rows(segment_row, extra):
    rows = lax.broadcasted_iota(jnp.int32, (128, segment_row.shape[1]), 0).astype(jnp.float32)
    own = jnp.where((rows == segment_row) & (rows < 8.0), 1.0, 0.0)
    if extra is None:
        return own.astype(jnp.bfloat16)
    high = extra.astype(jnp.bfloat16).astype(jnp.float32)
    rest = extra - high
    middle = rest.astype(jnp.bfloat16).astype(jnp.float32)
    low = rest - middle
    own = jnp.where(rows == 8.0, high, own)
    own = jnp.where(rows == 9.0, middle, own)
    return jnp.where(rows == 10.0, low, own).astype(jnp.bfloat16)


def fill_bias(line_ref, bias_ref):
    for head in range(2):
        line = line_ref[head : head + 1, :]
        turned = pltpu.roll(
            jnp.broadcast_to(line, (TILE, SPAN)), 0, axis=1, stride=1, stride_axis=0
        )
        bias_ref[head, 1] = turned[:, TILE : 2 * TILE]
        bias_ref[head, 2] = turned[:, :TILE]
        bias_ref[head, 3] = turned[:, 3 * TILE :]
        bias_ref[head, 0] = jnp.broadcast_to(line[:, 511:512], (TILE, TILE))
        bias_ref[head, 4] = jnp.broadcast_to(line[:, 513:514], (TILE, TILE))


def tile_at(index):
    return pl.ds(pl.multiple_of(index * TILE, TILE), TILE)


def dot32(left, right):
    return jnp.dot(left, right, preferred_element_type=jnp.float32)


def attention_forward(
    alive, packed, segment, line, out, out_t, log_sum, key_side, query_side, value_t, bias, top, acc
):
    length = packed.shape[0]
    tiles = length // TILE
    fill_bias(line, bias)

    def prepare(index, unused):
        spot = tile_at(index)
        seg = segment[0:1, spot]
        block = packed[spot, :].astype(jnp.float32)
        key_side[spot, :128] = packed[spot, 128:256]
        key_side[spot, 128:] = jnp.transpose(place_mask(seg)).astype(jnp.bfloat16)
        query_t = jnp.transpose(block[:, :128]) * 0.125
        seats = seat_rows(seg, None)
        half = lax.broadcasted_iota(jnp.int32, (128, TILE), 0) // HEAD
        values = jnp.transpose(block[:, 256:]).astype(jnp.bfloat16)
        ones = jnp.where(lax.broadcasted_iota(jnp.int32, (16, TILE), 0) == 0, 1.0, 0.0)
        for head in range(2):
            query_side[head, :128, spot] = jnp.where(half == head, query_t, 0.0).astype(
                jnp.bfloat16
            )
            query_side[head, 128:, spot] = seats
            value_t[head, :HEAD, spot] = values[HEAD * head : HEAD * (head + 1)]
            value_t[head, HEAD:, spot] = ones.astype(jnp.bfloat16)
        return unused

    lax.fori_loop(0, tiles, prepare, 0)

    def query_tile(query_index, unused):
        query_spot = tile_at(query_index)
        top[...] = jnp.full(top.shape, -3e38, jnp.float32)
        acc[...] = jnp.zeros(acc.shape, jnp.float32)

        def key_tile(key_index, carried):
            @pl.when(alive[query_index * tiles + key_index] == 1)
            def _():
                key_spot = tile_at(key_index)
                slot = jnp.clip(key_index - query_index, -2, 2) + 2
                keys = key_side[key_spot, :]
                for head in range(2):
                    scores = dot32(keys, query_side[head, :, query_spot]) + bias[head, slot]
                    before = top[head : head + 1, :]
                    now = jnp.maximum(before, jnp.max(scores, axis=0, keepdims=True))
                    weights = jnp.exp(scores - now).astype(jnp.bfloat16)
                    top[head : head + 1, :] = now
                    acc[head] = acc[head] * jnp.exp(before - now) + dot32(
                        value_t[head, :, key_spot], weights
                    )

            return carried

        lax.fori_loop(0, tiles, key_tile, 0)
        parts = []
        for head in range(2):
            total = acc[head, HEAD : HEAD + 1, :]
            part = acc[head, :HEAD, :] / total
            out_t[HEAD * head : HEAD * (head + 1), query_spot] = part
            log_sum[head : head + 1, query_spot] = top[head : head + 1, :] + jnp.log(total)
            parts.append(part)
        out[query_spot, :] = jnp.transpose(jnp.concatenate(parts, axis=0)).astype(jnp.bfloat16)
        return unused

    lax.fori_loop(0, tiles, query_tile, 0)


def attention_backward(
    alive,
    packed,
    segment,
    line,
    grads,
    out_t,
    log_sum,
    packed_grad,
    bias_grad,
    key_side,
    value_side,
    query_side,
    grad_side,
    key_t,
    query_pair,
    grad_pair,
    bias,
    bias_acc,
    query_acc,
    key_acc,
    value_acc,
):
    length = packed.shape[0]
    tiles = length // TILE
    fill_bias(line, bias)
    bias_acc[...] = jnp.zeros(bias_acc.shape, jnp.float32)

    def prepare(index, unused):
        spot = tile_at(index)
        seg = segment[0:1, spot]
        block = packed[spot, :].astype(jnp.float32)
        grad = grads[spot, :].astype(jnp.float32)
        seats = jnp.transpose(place_mask(seg)).astype(jnp.bfloat16)
        key_side[spot, :128] = packed[spot, 128:256]
        key_side[spot, 128:] = seats
        value_side[spot, :128] = packed[spot, 256:]
        value_side[spot, 128:] = seats
        key_t[:, spot] = jnp.transpose(block[:, 128:256]).astype(jnp.bfloat16)
        query_t = jnp.transpose(block[:, :128]) * 0.125
        grad_t = jnp.transpose(grad)
        half = lax.broadcasted_iota(jnp.int32, (128, TILE), 0) // HEAD
        side = lax.broadcasted_iota(jnp.int32, (TILE, 128), 1) // HEAD
        products = grad_t * out_t[:, spot]
        query_acc[:, spot] = jnp.zeros((128, TILE), jnp.float32)
        for head in range(2):
            query_side[head, :128, spot] = jnp.where(half == head, query_t, 0.0).astype(
                jnp.bfloat16
            )
            query_side[head, 128:, spot] = seat_rows(seg, -log_sum[head : head + 1, spot])
            delta = jnp.sum(products[HEAD * head : HEAD * (head + 1)], axis=0, keepdims=True)
            grad_side[head, :128, spot] = jnp.where(half == head, grad_t, 0.0).astype(jnp.bfloat16)
            grad_side[head, 128:, spot] = seat_rows(jnp.full_like(seg, -1.0), -delta)
            query_pair[index, TILE * head : TILE * (head + 1), :] = jnp.where(
                side == head, block[:, :128] * 0.125, 0.0
            ).astype(jnp.bfloat16)
            grad_pair[index, TILE * head : TILE * (head + 1), :] = jnp.where(
                side == head, grad, 0.0
            ).astype(jnp.bfloat16)
        return unused

    lax.fori_loop(0, tiles, prepare, 0)

    def key_tile(key_index, unused):
        key_spot = tile_at(key_index)
        key_acc[...] = jnp.zeros(key_acc.shape, jnp.float32)
        value_acc[...] = jnp.zeros(value_acc.shape, jnp.float32)

        def query_tile(query_index, carried):
            @pl.when(alive[query_index * tiles + key_index] == 1)
            def _():
                query_spot = tile_at(query_index)
                slot = jnp.clip(key_index - query_index, -2, 2) + 2
                keys = key_side[key_spot, :]
                values = value_side[key_spot, :]
                probs, score_grads = [], []
                for head in range(2):
                    scores = dot32(keys, query_side[head, :, query_spot]) + bias[head, slot]
                    prob = jnp.exp(scores)
                    score_grad = prob * dot32(values, grad_side[head, :, query_spot])
                    bias_acc[head, slot] += score_grad
                    score_grad = score_grad.astype(jnp.bfloat16)
                    probs.append(prob.astype(jnp.bfloat16))
                    score_grads.append(score_grad)
                    rows = slice(HEAD * head, HEAD * (head + 1))
                    query_acc[rows, query_spot] += dot32(key_t[rows, key_spot], score_grad)
                value_acc[...] += dot32(jnp.concatenate(probs, axis=1), grad_pair[query_index])
                key_acc[...] += dot32(jnp.concatenate(score_grads, axis=1), query_pair[query_index])

            return carried

        lax.fori_loop(0, tiles, query_tile, 0)
        packed_grad[key_spot, 128:256] = key_acc[...].astype(jnp.bfloat16)
        packed_grad[key_spot, 256:] = value_acc[...].astype(jnp.bfloat16)
        return unused

    lax.fori_loop(0, tiles, key_tile, 0)

    def finish(index, unused):
        spot = tile_at(index)
        packed_grad[spot, :128] = (jnp.transpose(query_acc[:, spot]) * 0.125).astype(jnp.bfloat16)
        return unused

    lax.fori_loop(0, tiles, finish, 0)
    rows = lax.broadcasted_iota(jnp.int32, (TILE, TILE), 0)
    columns = lax.broadcasted_iota(jnp.int32, (TILE, TILE), 1)
    flip = jnp.where(rows + columns == TILE - 1, 1.0, 0.0)
    bias_grad[...] = jnp.zeros(bias_grad.shape, jnp.float32)
    for head in range(2):
        spread = jnp.concatenate(
            [
                bias_acc[head, 2],
                bias_acc[head, 1],
                jnp.zeros((TILE, TILE), jnp.float32),
                bias_acc[head, 3],
            ],
            axis=1,
        )
        flipped = jnp.dot(
            flip, spread, precision=lax.Precision.HIGHEST, preferred_element_type=jnp.float32
        )
        turned = pltpu.roll(flipped, SPAN - TILE + 1, axis=1, stride=1, stride_axis=0)
        bias_grad[head : head + 1, :] = jnp.sum(turned, axis=0, keepdims=True)
        bias_grad[2 + head : 3 + head, :TILE] = jnp.sum(bias_acc[head, 0], axis=0, keepdims=True)
        bias_grad[4 + head : 5 + head, :TILE] = jnp.sum(bias_acc[head, 4], axis=0, keepdims=True)


def in_hbm(count):
    return [pl.BlockSpec(memory_space=pl.ANY)] * count


def estimate(micros):
    return pl.CostEstimate(flops=int(micros * 1e9), bytes_accessed=0, transcendentals=0)


def in_vmem(count):
    return [pl.BlockSpec(memory_space=pltpu.VMEM)] * count


def run_forward(alive, packed, segment, line):
    length = packed.shape[0]
    return pl.pallas_call(
        attention_forward,
        out_shape=(
            jax.ShapeDtypeStruct((length, 128), jnp.bfloat16),
            jax.ShapeDtypeStruct((128, length), jnp.float32),
            jax.ShapeDtypeStruct((8, length), jnp.float32),
        ),
        in_specs=[pl.BlockSpec(memory_space=pltpu.SMEM)] + in_vmem(3),
        out_specs=tuple(in_vmem(3)),
        scratch_shapes=[
            pltpu.VMEM((length, 256), jnp.bfloat16),
            pltpu.VMEM((2, 256, length), jnp.bfloat16),
            pltpu.VMEM((2, HEAD + 16, length), jnp.bfloat16),
            pltpu.VMEM((2, 5, TILE, TILE), jnp.float32),
            pltpu.VMEM((8, TILE), jnp.float32),
            pltpu.VMEM((2, HEAD + 16, TILE), jnp.float32),
        ],
        compiler_params=pltpu.CompilerParams(vmem_limit_bytes=67043328),
        cost_estimate=estimate(20),
        name="attention_forward",
    )(alive, packed, segment, line)


def run_backward(alive, packed, segment, line, grads, out_t, log_sum):
    length = packed.shape[0]
    tiles = length // TILE
    return pl.pallas_call(
        attention_backward,
        out_shape=(
            jax.ShapeDtypeStruct((length, 384), jnp.bfloat16),
            jax.ShapeDtypeStruct((8, SPAN), jnp.float32),
        ),
        in_specs=[pl.BlockSpec(memory_space=pltpu.SMEM)] + in_vmem(6),
        out_specs=tuple(in_vmem(2)),
        scratch_shapes=[
            pltpu.VMEM((length, 256), jnp.bfloat16),
            pltpu.VMEM((length, 256), jnp.bfloat16),
            pltpu.VMEM((2, 256, length), jnp.bfloat16),
            pltpu.VMEM((2, 256, length), jnp.bfloat16),
            pltpu.VMEM((128, length), jnp.bfloat16),
            pltpu.VMEM((tiles, 2 * TILE, 128), jnp.bfloat16),
            pltpu.VMEM((tiles, 2 * TILE, 128), jnp.bfloat16),
            pltpu.VMEM((2, 5, TILE, TILE), jnp.float32),
            pltpu.VMEM((2, 5, TILE, TILE), jnp.float32),
            pltpu.VMEM((128, length), jnp.float32),
            pltpu.VMEM((TILE, 128), jnp.float32),
            pltpu.VMEM((TILE, 128), jnp.float32),
        ],
        compiler_params=pltpu.CompilerParams(vmem_limit_bytes=67043328),
        cost_estimate=estimate(4),
        name="attention_backward",
    )(alive, packed, segment, line, grads, out_t, log_sum)


def signed_span():
    places = jnp.arange(SPAN, dtype=jnp.int32)
    return jnp.where(places < SPAN // 2, -places, SPAN - places)


def span_buckets():
    return (bucket_ids(signed_span())[:, None] == jnp.arange(NBUCK)[None, :]).astype(jnp.float32)


def live_tiles(segments, live):
    tiles = segments.shape[0] // TILE
    grouped = segments.reshape(tiles, TILE)
    first, last = grouped[:, 0], grouped[:, -1]
    meets = (first[:, None] <= last[None, :]) & (first[None, :] <= last[:, None])
    spread = jnp.repeat(jnp.repeat(live, ATT_BLK // TILE, axis=0), ATT_BLK // TILE, axis=1)
    return (meets & (spread == 1)).astype(jnp.int32).reshape(-1)


MESH = pl.DeviceIdType.MESH
LANES = 128
CUTS = 2
HALVES = 4


def places():
    own, ctx, side = lax.axis_index("shard"), lax.axis_index("ctx"), lax.axis_index("tensor")
    return own, ctx, side, ctx // 2, ctx % 2


def nearest(own, count, step):
    flip = own // (count // 2)
    place = flip * (count - 1 - own) + (1 - flip) * own
    turn = step - 1
    turn = turn + (turn - place + count) // count
    other = flip * (count - 1 - turn) + (1 - flip) * turn
    first = 1 - (step + count - 1) // count
    return first * own + (1 - first) * other


def partner(own, turn):
    return (own // 2 + turn // 2) % 2 * 2 + (own + turn) % 2


def across(chip, core, step):
    return (chip + 1 - step // 2) % 2 * 2 + (core + step + step // 2) % 2


def remote(source, target, send, recv, device):
    return pltpu.make_async_remote_copy(
        source, target, send, recv, device_id=device, device_id_type=MESH
    )


def greet(devices):
    barrier = pltpu.get_barrier_semaphore()
    for device in devices:
        pl.semaphore_signal(barrier, 1, device_id=device, device_id_type=MESH)
    pl.semaphore_wait(barrier, len(devices))


def gelu_parts(value):
    root = math.sqrt(2.0 / math.pi)
    square = value * value
    bend = jnp.tanh(root * value * (1.0 + 0.044715 * square))
    half = 0.5 * (1.0 + bend)
    slope = half + 0.5 * value * (1.0 - bend * bend) * (root * (1.0 + 0.134145 * square))
    return value * half, slope


def dot_last(left, right):
    return lax.dot_general(
        left, right, (((1,), (1,)), ((), ())), preferred_element_type=jnp.float32
    )


def expert_exchange(
    count,
    norm,
    gates,
    code_rows,
    code_cols,
    upstream_hbm,
    gate_own,
    gate_chip,
    gate_core,
    gate_far,
    up_own,
    up_chip,
    up_core,
    up_far,
    down_own,
    down_chip,
    down_core,
    down_far,
    row_grad,
    dot_rows,
    own_hbm,
    out_first,
    out_one,
    out_near,
    out_two,
    out_three,
    out_last,
    kept_hbm,
    gate_given,
    pair_given,
    upstream,
    gate_w,
    up_w,
    down_w,
    rows,
    sent,
    gates_in,
    gates_out,
    slot_grad,
    inner,
    gate_grad,
    up_grad,
    outs,
    partial,
    peer_part,
    summed,
    back,
    dots_out,
    dots_in,
    final_out,
    final_in,
    final_dots,
    core_in,
    chip_in,
    load_sem,
    store_sem,
    rows_send,
    rows_recv,
    pass_send,
    pass_recv,
    gates_send,
    gates_recv,
    part_send,
    part_recv,
    back_send,
    back_recv,
    dots_send,
    dots_recv,
    final_send,
    final_recv,
    core_send,
    core_recv,
    chip_send,
    chip_recv,
):
    own = lax.axis_index("shard")
    ctx = lax.axis_index("ctx")
    side = lax.axis_index("tensor")
    tokens, width = norm.shape
    room = upstream.shape[1]
    half = room // 2
    hidden = gate_w.shape[1]
    peer = (own, ctx, 1 - side)

    def source(step):
        return partner(own, step)

    barrier = pltpu.get_barrier_semaphore()
    for step in range(1, count):
        pl.semaphore_signal(barrier, 1, device_id=(source(step), ctx, side), device_id_type=MESH)
    chip, core = ctx // 2, ctx % 2
    core_peer = (own, chip * 2 + 1 - core, side)
    chip_peer = (own, (1 - chip) * 2 + core, side)
    for device in (peer, core_peer, chip_peer):
        pl.semaphore_signal(barrier, 1, device_id=device, device_id_type=MESH)
    deep = gate_own.shape[0]
    origins = (ctx, (1 - chip) * 2 + core, chip * 2 + 1 - core, (1 - chip) * 2 + 1 - core)
    pieces_of = (
        (gate_w, (gate_own, gate_chip, gate_core, gate_far)),
        (up_w, (up_own, up_chip, up_core, up_far)),
        (down_w, (down_own, down_chip, down_core, down_far)),
    )
    loads = []
    for number, (target, sources) in enumerate(pieces_of):
        for turn, source_ref in enumerate(sources):
            spot = pl.ds(pl.multiple_of(origins[turn] * deep, deep), deep)
            sem = load_sem.at[4 * number + turn]
            loads.append(pltpu.make_async_copy(source_ref, target.at[spot], sem))
    loads.append(pltpu.make_async_copy(upstream_hbm, upstream, load_sem.at[12]))
    for load in loads:
        load.start()
    pl.semaphore_wait(barrier, count + 2)

    my_half = pl.ds(pl.multiple_of(side * half, half), half)
    peer_half = pl.ds(pl.multiple_of((1 - side) * half, half), half)
    cut = half // CUTS

    def lines(which, piece):
        return pl.ds(pl.multiple_of(which * half + piece * cut, cut), cut)


    def picked(expert, start, amount):
        slots = lax.broadcasted_iota(jnp.int32, (amount, tokens), 0) + expert * room + start
        slots = slots.astype(jnp.float32)
        hit = (code_rows[0:1, :] == slots) | (code_rows[1:2, :] == slots)
        return jnp.where(hit, 1.0, 0.0).astype(jnp.bfloat16)

    def slot_gates(expert):
        slots = lax.broadcasted_iota(jnp.int32, (tokens, room), 1) + expert * room
        slots = slots.astype(jnp.float32)
        held = jnp.where(code_cols[:, 0:1] == slots, gates[:, 0:1], 0.0)
        held = held + jnp.where(code_cols[:, 1:2] == slots, gates[:, 1:2], 0.0)
        return jnp.broadcast_to(jnp.sum(held, axis=0, keepdims=True), (8, room))

    def rows_copy(step, piece):
        target = source(step)
        return pltpu.make_async_remote_copy(
            sent.at[step - 1, lines(0, piece)],
            rows.at[own, lines(side, piece)],
            rows_send.at[step - 1, piece],
            rows_recv.at[own, piece],
            device_id=(target, ctx, side),
            device_id_type=MESH,
        )

    def gates_copy(step):
        return pltpu.make_async_remote_copy(
            gates_out.at[step - 1],
            gates_in.at[own],
            gates_send.at[step - 1],
            gates_recv.at[own],
            device_id=(source(step), ctx, side),
            device_id_type=MESH,
        )

    def send_rows(step, unused):
        target = source(step)
        sent[step - 1] = dot32(picked(target, side * half, half), norm[...]).astype(jnp.bfloat16)
        for piece in range(CUTS):
            rows_copy(step, piece).start()
        gates_out[step - 1] = slot_gates(target)
        gates_copy(step).start()
        return unused

    lax.fori_loop(1, count, send_rows, 0)
    rows[own] = dot32(picked(own, 0, room), norm[...]).astype(jnp.bfloat16)
    gates_in[own] = slot_gates(own)
    for load in loads:
        load.wait()

    def landed(buffer, send, recv, origin):
        return pltpu.make_async_remote_copy(
            buffer, buffer, send, recv, device_id=peer, device_id_type=MESH
        )

    def pass_copy(origin, piece):
        spot = rows.at[origin, lines(side, piece)]
        return remote(spot, spot, pass_send.at[origin, piece], pass_recv.at[origin, piece], peer)

    def part_copy(step, piece):
        return remote(
            partial.at[step, lines(1 - side, piece)],
            peer_part.at[step, lines(0, piece)],
            part_send.at[step, piece],
            part_recv.at[step, piece],
            peer,
        )

    def back_copy(step, piece):
        return remote(
            summed.at[step, lines(0, piece)],
            back.at[own, lines(0, piece)],
            back_send.at[step, piece],
            back_recv.at[own, piece],
            (source(step), ctx, side),
        )

    def dots_copy(step):
        return pltpu.make_async_remote_copy(
            dots_out.at[step],
            dots_in.at[own],
            dots_send.at[step],
            dots_recv.at[own],
            device_id=(source(step), ctx, side),
            device_id_type=MESH,
        )

    def send_back(step):
        for piece in range(CUTS):
            part_copy(step, piece).wait_recv()
            summed[step, lines(0, piece), :] = (
                partial[step, lines(side, piece), :].astype(jnp.float32)
                + peer_part[step, lines(0, piece), :].astype(jnp.float32)
            ).astype(jnp.bfloat16)
            back_copy(step, piece).start()

    edge = (hidden // 256 + 1) // 2 * 256
    pieces = (slice(0, edge), slice(edge, hidden))

    def run_chunk(step, unused):
        origin = source(step)

        @pl.when(step > 0)
        def _():
            for piece in range(CUTS):
                spot = rows.at[origin, lines(1 - side, piece)]
                landed(spot, pass_send.at[0, 0], pass_recv.at[origin, piece], 0).wait_recv()
            landed(gates_in.at[origin], gates_send.at[0], gates_recv.at[origin], 0).wait_recv()

        gate_column = jnp.transpose(gates_in[origin])[:, 0:1]
        slot_grad[origin] = (upstream[origin].astype(jnp.float32) * gate_column).astype(
            jnp.bfloat16
        )

        def inside(piece):
            block = rows[origin]
            gate_pre = dot32(block, gate_w[:, piece])
            up_pre = dot32(block, up_w[:, piece])
            inner_grad = dot32(slot_grad[origin], down_w[:, piece])
            active, slope = gelu_parts(gate_pre)
            held = (active * up_pre).astype(jnp.bfloat16)
            inner[origin, :, piece] = held
            gate_grad[origin, :, piece] = (inner_grad * up_pre * slope).astype(jnp.bfloat16)
            up_grad[origin, :, piece] = (inner_grad * active).astype(jnp.bfloat16)
            return jnp.sum(active * up_pre * inner_grad, axis=1, keepdims=True)

        dots = inside(pieces[0])

        @pl.when(step < count - 1)
        def _():
            following = source(step + 1)
            for piece in range(CUTS):
                spot = rows.at[following, lines(side, piece)]
                landed(spot, rows_send.at[0, 0], rows_recv.at[following, piece], 0).wait_recv()
                pass_copy(following, piece).start()

        dots = dots + inside(pieces[1])
        dots_out[step] = jnp.transpose(jnp.broadcast_to(dots, (room, 128)))[0:8, :]

        @pl.when(step > 1)
        def _():
            send_back(step - 1)

        for spot in (peer_half, my_half):
            found = dot_last(gate_grad[origin, spot, :], gate_w[...])
            found = found + dot_last(up_grad[origin, spot, :], up_w[...])
            partial[step, spot, :] = found.astype(jnp.bfloat16)
            if spot is peer_half:

                @pl.when(step > 0)
                def _():
                    for piece in range(CUTS):
                        part_copy(step, piece).start()
                    dots_copy(step).start()

        return unused

    lax.fori_loop(0, count, run_chunk, 0)
    products = ((gate_w, rows, gate_grad), (up_w, rows, up_grad), (down_w, slot_grad, inner))

    def owner(turn):
        return turn % 2 * 2 + (core + 1 + turn // 2) % 2

    def to_core(number, turn):
        spot = pl.ds(pl.multiple_of(owner(turn) * deep, deep), deep)
        return pltpu.make_async_remote_copy(
            products[number][0].at[spot],
            core_in.at[number, turn],
            core_send.at[number, turn],
            core_recv.at[number, turn],
            device_id=core_peer,
            device_id_type=MESH,
        )

    def weigh(number):
        target, left, right = products[number]

        def block(turn, unused):
            spot = pl.ds(pl.multiple_of(owner(turn) * deep, deep), deep)
            lines = left[:, :, spot].reshape(count * room, deep)
            target[spot, :] = lax.dot_general(
                lines,
                right[...].reshape(count * room, hidden),
                (((0,), (0,)), ((), ())),
                preferred_element_type=jnp.float32,
            ).astype(jnp.bfloat16)

            @pl.when(turn < 2)
            def _():
                to_core(number, turn).start()

            return unused

        lax.fori_loop(0, 4, block, 0)

    def run_out(step, unused):
        outs[step] = dot_last(inner[step], down_w[...]).astype(jnp.bfloat16)
        return unused

    def to_chip(number):
        return remote(
            core_in.at[number, 1 - chip],
            chip_in.at[0],
            chip_send.at[number],
            chip_recv.at[number],
            chip_peer,
        )

    def over_chip(number):
        for turn in range(2):
            spot = pl.ds(pl.multiple_of(owner(turn + 2) * deep, deep), deep)
            to_core(number, turn).wait_recv()
            core_in[number, turn] = (
                products[number][0][spot, :].astype(jnp.float32)
                + core_in[number, turn].astype(jnp.float32)
            ).astype(jnp.bfloat16)
        if number == 0:
            to_chip(number).start()

    weigh(0)
    send_back(count - 1)
    lax.fori_loop(0, count, run_out, 0)
    moves = (
        (outs.at[own], own_hbm),
        (outs.at[partner(own, 1), pl.ds(0, half)], out_first),
        (outs.at[partner(own, 1), pl.ds(half, half)], out_one),
        (outs.at[partner(own, 2), pl.ds(0, half)], out_near),
        (outs.at[partner(own, 2), pl.ds(half, half)], out_two),
        (outs.at[partner(own, 3), pl.ds(0, half)], out_three),
        (outs.at[partner(own, 3), pl.ds(half, half)], out_last),
    )
    stores = []
    for number, (source_ref, target) in enumerate(moves):
        sem = store_sem.at[number if number == 0 else 10 + number]
        stores.append(pltpu.make_async_copy(source_ref, target, sem))
    for store in stores:
        store.start()
    weigh(1)
    over_chip(0)

    def dots_landed(step, unused):
        origin = source(step)
        landed(dots_in.at[origin], dots_send.at[0], dots_recv.at[origin], 0).wait_recv()
        return unused

    def back_landed(step, unused):
        origin = source(step)
        for piece in range(CUTS):
            spot = back.at[origin, lines(0, piece)]
            landed(spot, back_send.at[0, 0], back_recv.at[origin, piece], 0).wait_recv()
        return unused

    lax.fori_loop(1, count, dots_landed, 0)
    dots_in[own] = dots_out[0]
    final_dots[0] = jnp.zeros((8, tokens), jnp.float32)
    for expert in range(count):
        column = jnp.transpose(dots_in[expert])[:, 0:1]
        slots = lax.broadcasted_iota(jnp.int32, (room, tokens), 0) + expert * room
        slots = slots.astype(jnp.float32)
        for choice in range(2):
            final_dots[0, choice : choice + 1, :] += jnp.sum(
                jnp.where(code_rows[choice : choice + 1, :] == slots, column, 0.0),
                axis=0,
                keepdims=True,
            )
    lax.fori_loop(1, count, back_landed, 0)
    blocks = final_out.shape[0]
    span = tokens // blocks

    def final_copy(block):
        return pltpu.make_async_remote_copy(
            final_out.at[block],
            final_in.at[block],
            final_send.at[block],
            final_recv.at[block],
            device_id=peer,
            device_id_type=MESH,
        )

    dots_final = pltpu.make_async_remote_copy(
        final_dots.at[0],
        final_dots.at[1],
        final_send.at[blocks],
        final_recv.at[blocks],
        device_id=peer,
        device_id_type=MESH,
    )
    dots_final.start()

    def combine(block, unused):
        spot = pl.ds(pl.multiple_of(block * span, span), span)

        def chosen(start, amount):
            slots = lax.broadcasted_iota(jnp.int32, (span, amount), 1) + start
            slots = slots.astype(jnp.float32)
            hit = (code_cols[spot, 0:1] == slots) | (code_cols[spot, 1:2] == slots)
            return jnp.where(hit, 1.0, 0.0).astype(jnp.bfloat16)

        total = dot32(chosen(own * room, room), partial[0])
        for step in range(1, count):
            origin = source(step)
            total = total + dot32(chosen(origin * room + side * half, half), back[origin])
        final_out[block] = total.astype(jnp.bfloat16)
        final_copy(block).start()
        return unused

    lax.fori_loop(0, blocks, combine, 0)

    weigh(2)

    def finish(block, unused):
        spot = pl.ds(pl.multiple_of(block * span, span), span)
        final_copy(block).wait_recv()
        row_grad[spot, :] = final_out[block].astype(jnp.float32) + final_in[block].astype(
            jnp.float32
        )
        return unused

    lax.fori_loop(0, blocks, finish, 0)
    dots_final.wait_recv()
    dot_rows[...] = final_dots[0] + final_dots[1]
    to_chip(0).wait_recv()
    for number in range(3):
        if number:
            over_chip(number)
        given = core_in.at[number, 1 - chip] if number else chip_in.at[0]
        for place, source_ref in enumerate((core_in.at[number, chip], given)):
            target = (kept_hbm.at[number], pair_given.at[number - 1] if number else gate_given)[place]
            sem = store_sem.at[4 + 2 * number + place]
            store = pltpu.make_async_copy(source_ref, target, sem)
            store.start()
            stores.append(store)

    def drain(step, unused):
        for piece in range(CUTS):
            rows_copy(step, piece).wait_send()
            pass_copy(source(step), piece).wait_send()
            part_copy(step, piece).wait_send()
            back_copy(step, piece).wait_send()
        gates_copy(step).wait_send()
        dots_copy(step).wait_send()
        return unused

    lax.fori_loop(1, count, drain, 0)

    def drain_final(block, unused):
        final_copy(block).wait_send()
        return unused

    lax.fori_loop(0, blocks, drain_final, 0)
    dots_final.wait_send()
    for number in range(3):
        for turn in range(2):
            to_core(number, turn).wait_send()
        if number == 0:
            to_chip(number).wait_send()
    for store in stores:
        store.wait()


def run_experts(count, ctx_size, norm, gates, code_rows, code_cols, upstream, weights):
    tokens, width = norm.shape
    room = upstream.shape[1]
    half = room // 2
    hidden = weights[0].shape[1]
    blocks = 4
    low = jnp.bfloat16
    full = jnp.float32
    dma = pltpu.SemaphoreType.DMA
    return pl.pallas_call(
        partial(expert_exchange, count),
        out_shape=(
            jax.ShapeDtypeStruct((tokens, width), full),
            jax.ShapeDtypeStruct((8, tokens), full),
            jax.ShapeDtypeStruct((room, width), low),
            *[jax.ShapeDtypeStruct((half, width), low)] * 6,
            jax.ShapeDtypeStruct((3, width // ctx_size, hidden), low),
            jax.ShapeDtypeStruct((width // ctx_size, hidden), low),
            jax.ShapeDtypeStruct((2, width // ctx_size, hidden), low),
        ),
        in_specs=in_vmem(4) + [pl.BlockSpec(memory_space=pl.ANY)] * 13,
        out_specs=tuple(in_vmem(2) + [pl.BlockSpec(memory_space=pl.ANY)] * 10),
        scratch_shapes=[
            pltpu.VMEM(upstream.shape, low),
            pltpu.VMEM((width, hidden), low),
            pltpu.VMEM((width, hidden), low),
            pltpu.VMEM((width, hidden), low),
            pltpu.VMEM((count, room, width), low),
            pltpu.VMEM((count - 1, half, width), low),
            pltpu.VMEM((count, 8, room), full),
            pltpu.VMEM((count - 1, 8, room), full),
            pltpu.VMEM((count, room, width), low),
            pltpu.VMEM((count, room, hidden), low),
            pltpu.VMEM((count, room, hidden), low),
            pltpu.VMEM((count, room, hidden), low),
            pltpu.VMEM((count, room, width), low),
            pltpu.VMEM((count, room, width), low),
            pltpu.VMEM((count, half, width), low),
            pltpu.VMEM((count, half, width), low),
            pltpu.VMEM((count, half, width), low),
            pltpu.VMEM((count, 8, room), full),
            pltpu.VMEM((count, 8, room), full),
            pltpu.VMEM((blocks, tokens // blocks, width), low),
            pltpu.VMEM((blocks, tokens // blocks, width), low),
            pltpu.VMEM((2, 8, tokens), full),
            pltpu.VMEM((3, 2, width // ctx_size, hidden), low),
            pltpu.VMEM((1, width // ctx_size, hidden), low),
            dma((13,)),
            dma((18,)),
            dma((count, CUTS)),
            dma((count, CUTS)),
            dma((count, CUTS)),
            dma((count, CUTS)),
            dma((count,)),
            dma((count,)),
            dma((count, CUTS)),
            dma((count, CUTS)),
            dma((count, CUTS)),
            dma((count, CUTS)),
            dma((count,)),
            dma((count,)),
            dma((blocks + 1,)),
            dma((blocks + 1,)),
            dma((3, 2)),
            dma((3, 2)),
            dma((3,)),
            dma((3,)),
        ],
        cost_estimate=estimate(110),
        compiler_params=pltpu.CompilerParams(
            collective_id=3, has_side_effects=True, vmem_limit_bytes=67043328
        ),
        name="expert_exchange",
    )(norm, gates, code_rows, code_cols, upstream, *weights)


def begin(pairs, sems):
    copies = [
        pltpu.make_async_copy(source, target, sems.at[number])
        for number, (source, target) in enumerate(pairs)
    ]
    for copy in copies:
        copy.start()
    return copies


def gather_project(
    count,
    w_query,
    w_key,
    w_value,
    w_out,
    first_gain,
    second_gain,
    router,
    tokens,
    segment_ids,
    cotangent,
    routes,
    gate_hbm,
    up_hbm,
    down_hbm,
    full_hbm,
    packed,
    norm_hbm,
    segments,
    out_hbm,
    upstream_hbm,
    gate_hbm_low,
    up_hbm_low,
    down_hbm_low,
    gate_core,
    up_core,
    down_core,
    gate_chip,
    gate_far,
    codes,
    code_rows,
    extras,
    full,
    norm,
    out_full,
    upstream,
    gate_low,
    up_low,
    down_low,
    weight,
    out_weight,
    segment,
    outgoing,
    sent,
    experts_wide,
    line_send,
    line_recv,
    chip_send,
    chip_recv,
    core_send,
    core_recv,
    packed_send,
    packed_recv,
    segment_send,
    segment_recv,
    out_line_send,
    out_line_recv,
    out_chip_send,
    out_chip_recv,
    out_core_send,
    out_core_recv,
    out_pair_send,
    out_pair_recv,
    rows_send,
    rows_recv,
    pass_send,
    pass_recv,
    expert_send,
    expert_recv,
    load_sem,
    store_sem,
):
    own, ctx, side, chip, core = places()
    rows = weight.shape[0]
    ctx_size, here, share = packed.shape
    room = upstream.shape[1]
    half = room // 2
    chip_peer = (own, (1 - chip) * 2 + core, side)
    core_peer = (own, chip * 2 + 1 - core, side)
    pair = (own, ctx, 1 - side)
    loads = [
        pltpu.make_async_copy(source, experts_wide.at[number], load_sem.at[number])
        for number, source in enumerate((gate_hbm, up_hbm, down_hbm))
    ]
    for load in loads:
        load.start()
    stores = []

    def store(source, target):
        copy = pltpu.make_async_copy(source, target, store_sem.at[len(stores)])
        copy.start()
        stores.append(copy)

    experts = router.shape[0]
    extra = jnp.concatenate(
        [first_gain[...], second_gain[...], router[...], jnp.zeros((6 - experts, rows))], axis=0
    )
    weight[:, ctx_size * share :] = jnp.zeros((rows, LANES), jnp.bfloat16)
    extra_columns = slice(ctx_size * share, ctx_size * share + 8)
    weight[:, extra_columns] = jnp.transpose(extra).astype(jnp.bfloat16)
    for place in range(ctx_size):
        for number, member in enumerate((w_query, w_key, w_value)):
            target = slice(place * share + number * LANES, place * share + (number + 1) * LANES)
            found = member[:, place * LANES : (place + 1) * LANES]
            weight[:, target] = found.astype(jnp.bfloat16)
    out_weight[...] = w_out[...].astype(jnp.bfloat16)
    segment[...] = jnp.broadcast_to(segment_ids[...].astype(jnp.float32), segment.shape)
    greet(
        [(nearest(own, count, step), ctx, side) for step in range(1, count)]
        + [(own, across(chip, core, step), side) for step in range(3)]
        + [pair]
    )

    def block(shard, place):
        return pl.ds(pl.multiple_of((shard * ctx_size + place) * rows, rows), rows)

    def along(origin, forward):
        turn = 2 * forward - 1
        target = own + turn
        there = (target + count) // count * (1 - target // count)
        return (target + count) % count, there

    def onward(origin):
        return 1 - (origin - own + count) // count

    def to_line(origin, forward, source, number):
        target, _ = along(origin, forward)
        spot = full.at[block(origin, ctx)]
        return remote(
            source, spot, line_send.at[number], line_recv.at[origin], (target, ctx, side)
        )

    def in_line(copy_of, origin, forward, source, number, act):
        _, there = along(origin, forward)

        @pl.when(there == 1)
        def _():
            act(copy_of(origin, forward, source, number))

    def to_chip(shard, source):
        target = full.at[block(shard, ctx)]
        return remote(source, target, chip_send.at[shard], chip_recv.at[shard], chip_peer)

    def to_core(shard, place, source):
        index = shard * 2 + place // 2
        target = full.at[block(shard, place)]
        return remote(source, target, core_send.at[index], core_recv.at[index], core_peer)

    def to_segment(step):
        device = (own, across(chip, core, step), side)
        return remote(segment, segments.at[ctx], segment_send.at[step], segment_recv.at[ctx], device)

    def out_to_line(origin, forward, source, number):
        target, _ = along(origin, forward)
        spot = out_full.at[side, block(origin, ctx)]
        return remote(
            source, spot, out_line_send.at[number], out_line_recv.at[origin], (target, ctx, side)
        )

    def start(copy):
        copy.start()

    def sent_off(copy):
        copy.wait_send()

    def out_to_chip(shard, source):
        target = out_full.at[side, block(shard, ctx)]
        return remote(source, target, out_chip_send.at[shard], out_chip_recv.at[shard], chip_peer)

    def out_to_core(which, shard, place, source):
        index = shard * 2 + place // 2
        target = out_full.at[which, block(shard, place)]
        return remote(
            source, target, out_core_send.at[which, index], out_core_recv.at[which, index], core_peer
        )

    def out_to_pair(shard, place, source):
        index = shard * 2 + place // 2
        target = out_full.at[side, block(shard, place)]
        return remote(source, target, out_pair_send.at[index], out_pair_recv.at[index], pair)

    for forward in range(2):
        in_line(to_line, own, forward, weight, forward, start)
    to_chip(own, weight).start()
    to_core(own, ctx, weight).start()
    for step in range(3):
        to_segment(step).start()
    for forward in range(2):
        in_line(out_to_line, own, forward, out_weight, forward, start)
    out_to_core(side, own, ctx, out_weight).start()
    out_to_pair(own, ctx, out_weight).start()
    full[block(own, ctx), :] = weight[...]
    out_full[side, block(own, ctx), :] = out_weight[...]
    segments[ctx] = segment[...]

    lane = lax.broadcasted_iota(jnp.int32, (here, LANES), 1).astype(jnp.float32)
    named = jnp.concatenate([routes[...].astype(jnp.float32), jnp.zeros((6, here))], axis=0)
    columns = jnp.transpose(named)
    first, second = columns[:, 0:1], columns[:, 1:2]
    codes[:, 2:3] = first
    codes[:, 3:4] = second
    named = jnp.where((first == lane) | (second == lane), 1.0, 0.0).astype(jnp.bfloat16)
    later = lax.broadcasted_iota(jnp.int32, (here, here), 0)
    before = later > lax.broadcasted_iota(jnp.int32, (here, here), 1)
    slots = dot32(jnp.where(before, 1.0, 0.0).astype(jnp.bfloat16), named) + room * lane
    first = jnp.sum(jnp.where(first == lane, slots, 0.0), axis=1, keepdims=True)
    second = jnp.sum(jnp.where(second == lane, slots, 0.0), axis=1, keepdims=True)
    codes[:, 0:1] = first
    codes[:, 1:2] = second
    both = jnp.where(lane == 0.0, first, jnp.where(lane == 1.0, second, -1.0))
    code_rows[...] = jnp.transpose(both)[0:8]
    my_half = pl.ds(pl.multiple_of(side * half, half), half)
    peer_half = pl.ds(pl.multiple_of((1 - side) * half, half), half)

    def picked(expert, start, amount):
        slots = lax.broadcasted_iota(jnp.int32, (amount, here), 0) + expert * room + start
        slots = slots.astype(jnp.float32)
        hit = (code_rows[0:1, :] == slots) | (code_rows[1:2, :] == slots)
        rows_found = jnp.where(hit, 1.0, 0.0).astype(jnp.bfloat16)
        return dot32(rows_found, cotangent[...]).astype(jnp.bfloat16)

    cut = half // CUTS

    def lines(which, piece):
        return pl.ds(pl.multiple_of(which * half + piece * cut, cut), cut)

    def to_expert(step, piece):
        return remote(
            sent.at[step - 1, lines(0, piece)],
            upstream.at[own, lines(side, piece)],
            rows_send.at[step - 1, piece],
            rows_recv.at[own, piece],
            (nearest(own, count, step), ctx, side),
        )

    def pass_rows(shard, piece):
        spot = lines(side, piece)
        source, target = upstream.at[shard, spot], upstream_hbm.at[shard, spot]
        return remote(source, target, pass_send.at[shard, piece], pass_recv.at[shard, piece], pair)

    lows = (gate_low, up_low, down_low)
    near = (gate_core, up_core, down_core)
    for number, load in enumerate(loads):
        load.wait()
        lows[number][...] = experts_wide[number].astype(jnp.bfloat16)
        store(lows[number], (gate_hbm_low, up_hbm_low, down_hbm_low)[number])
    for step in range(1, count):
        sent[step - 1] = picked(nearest(own, count, step), side * half, half)
    upstream[own] = picked(own, 0, room)
    store(upstream.at[own], upstream_hbm.at[own])

    def to_near(number):
        return remote(
            lows[number], near[number], expert_send.at[number], expert_recv.at[number], core_peer
        )

    gate_over = remote(gate_low, gate_chip, expert_send.at[3], expert_recv.at[3], chip_peer)
    gate_far_copy = remote(gate_chip, gate_far, expert_send.at[4], expert_recv.at[4], core_peer)

    other_place = (1 - chip) * 2 + core

    def pass_line(step):
        shard = nearest(own, count, step)
        source = full.at[block(shard, ctx)]
        remote(source, source, line_send.at[0], line_recv.at[shard], core_peer).wait_recv()
        in_line(to_line, shard, onward(shard), source, 1 + step, start)
        to_chip(shard, source).start()
        to_core(shard, ctx, source).start()

    def pass_chip(step):
        shard = nearest(own, count, step)
        source = full.at[block(shard, other_place)]
        remote(source, source, chip_send.at[0], chip_recv.at[shard], core_peer).wait_recv()
        to_core(shard, other_place, source).start()

    pass_chip(0)
    for step in range(1, count):
        pass_line(step)
        pass_chip(step)
    out_to_chip(own, out_weight).start()
    for step in range(1, count):
        shard = nearest(own, count, step)
        source = out_full.at[side, block(shard, ctx)]
        remote(source, source, line_send.at[0], out_line_recv.at[shard], core_peer).wait_recv()
        in_line(out_to_line, shard, onward(shard), source, 1 + step, start)
        out_to_chip(shard, source).start()
        out_to_core(side, shard, ctx, source).start()
        out_to_pair(shard, ctx, source).start()

    for step in range(1, count):
        for piece in range(CUTS):
            to_expert(step, piece).start()
    gate_over.start()
    values = tokens[...].astype(jnp.float32)
    scale = lax.rsqrt(jnp.mean(values * values, axis=1, keepdims=True) + 1e-06)
    for shard in range(count):
        for place in range(2):
            spot = full.at[block(shard, place * 2 + 1 - core)]
            index = shard * 2 + place
            remote(spot, spot, core_send.at[0], core_recv.at[index], core_peer).wait_recv()
    store(full, full_hbm)
    extras[...] = full[:, ctx_size * share :]
    gain = jnp.transpose(extras[...].astype(jnp.float32))[0:1, :]
    norm[...] = (values * scale * gain).astype(jnp.bfloat16)
    store(norm, norm_hbm)

    def project(place):
        spot = pl.ds(pl.multiple_of(place * share, LANES), share)
        return dot32(norm[...], full[:, spot]).astype(jnp.bfloat16)

    def to_packed(step):
        device = (own, across(chip, core, step), side)
        return remote(
            outgoing.at[step], packed.at[ctx], packed_send.at[step], packed_recv.at[ctx], device
        )

    for step in range(3):
        outgoing[step] = project(across(chip, core, step))
        to_packed(step).start()
    packed[ctx] = project(ctx)
    for number in range(3):
        to_near(number).start()
    for step in range(count):
        shard = nearest(own, count, step)
        source = out_full.at[side, block(shard, other_place)]
        remote(source, source, line_send.at[0], out_chip_recv.at[shard], core_peer).wait_recv()
        out_to_core(side, shard, other_place, source).start()
        out_to_pair(shard, other_place, source).start()
    for step in range(1, count):
        shard = nearest(own, count, step)
        for piece in range(CUTS):
            spot = upstream.at[shard, lines(side, piece)]
            remote(spot, spot, line_send.at[0], rows_recv.at[shard, piece], pair).wait_recv()
            pass_rows(shard, piece).start()
        store(upstream.at[shard, my_half], upstream_hbm.at[shard, my_half])
    gate_over.wait_recv()
    gate_far_copy.start()
    for step in range(count):
        shard = nearest(own, count, step)
        for place in (core, 2 + core):
            index = shard * 2 + place // 2
            source = out_full.at[1 - side, block(shard, place)]
            remote(source, source, line_send.at[0], out_pair_recv.at[index], pair).wait_recv()
            out_to_core(1 - side, shard, place, source).start()
    for step in range(3):
        place = across(chip, core, step)
        spot = packed.at[place]
        remote(spot, spot, packed_send.at[step], packed_recv.at[place], core_peer).wait_recv()
        spot = segments.at[place]
        remote(spot, spot, segment_send.at[step], segment_recv.at[place], core_peer).wait_recv()
    for which in (side, 1 - side):
        for shard in range(count):
            for place in range(2):
                spot = out_full.at[which, block(shard, place * 2 + 1 - core)]
                index = shard * 2 + place
                remote(
                    spot, spot, line_send.at[0], out_core_recv.at[which, index], core_peer
                ).wait_recv()
        store(out_full.at[which], out_hbm.at[which])
    for step in range(1, count):
        shard = nearest(own, count, step)
        for piece in range(CUTS):
            spot = upstream_hbm.at[shard, lines(1 - side, piece)]
            remote(spot, spot, line_send.at[0], pass_recv.at[shard, piece], pair).wait_recv()

    for copy in stores:
        copy.wait()
    for step in range(3):
        to_packed(step).wait_send()
        to_segment(step).wait_send()
        to_near(step).wait()
    gate_over.wait_send()
    gate_far_copy.wait()
    for forward in range(2):
        in_line(to_line, own, forward, weight, forward, sent_off)
        in_line(out_to_line, own, forward, out_weight, forward, sent_off)
    for step in range(count):
        shard = nearest(own, count, step)
        if step:
            in_line(to_line, shard, onward(shard), weight, 1 + step, sent_off)
            in_line(out_to_line, shard, onward(shard), out_weight, 1 + step, sent_off)
            for piece in range(CUTS):
                to_expert(step, piece).wait_send()
                pass_rows(shard, piece).wait_send()
        to_chip(shard, weight).wait_send()
        out_to_chip(shard, out_weight).wait_send()
        for place in (ctx, other_place):
            to_core(shard, place, weight).wait_send()
            out_to_pair(shard, place, out_weight).wait_send()
            out_to_core(side, shard, place, out_weight).wait_send()
            out_to_core(1 - side, shard, place, out_weight).wait_send()


def run_gather(count, ctx_size, room, members, experts):
    rows, head_columns = members[0].shape
    here, width = members[7].shape
    share = 3 * head_columns // ctx_size
    columns = ctx_size * share + LANES
    dma = pltpu.SemaphoreType.DMA
    low = jnp.bfloat16
    deep, hidden = experts[0].shape
    return pl.pallas_call(
        partial(gather_project, count),
        out_shape=(
            jax.ShapeDtypeStruct((rows * count * ctx_size, columns), low),
            jax.ShapeDtypeStruct((ctx_size, here, share), low),
            jax.ShapeDtypeStruct((here, width), low),
            jax.ShapeDtypeStruct((ctx_size, 8, here), jnp.float32),
            jax.ShapeDtypeStruct((2, rows * count * ctx_size, head_columns), low),
            jax.ShapeDtypeStruct((count, room, width), low),
            *[jax.ShapeDtypeStruct((deep, hidden), low)] * 8,
            jax.ShapeDtypeStruct((here, 4), jnp.float32),
            jax.ShapeDtypeStruct((8, here), jnp.float32),
            jax.ShapeDtypeStruct((rows * count * ctx_size, LANES), low),
        ),
        in_specs=in_vmem(11) + [pl.BlockSpec(memory_space=pl.ANY)] * 3,
        out_specs=tuple(
            pl.BlockSpec(memory_space=pltpu.VMEM if number in (1, 3, 14, 15, 16) else pl.ANY)
            for number in range(17)
        ),
        scratch_shapes=[
            pltpu.VMEM((rows * count * ctx_size, columns), low),
            pltpu.VMEM((here, width), low),
            pltpu.VMEM((2, rows * count * ctx_size, head_columns), low),
            pltpu.VMEM((count, room, width), low),
            pltpu.VMEM((deep, hidden), low),
            pltpu.VMEM((deep, hidden), low),
            pltpu.VMEM((deep, hidden), low),
            pltpu.VMEM((rows, columns), low),
            pltpu.VMEM((rows, head_columns), low),
            pltpu.VMEM((8, here), jnp.float32),
            pltpu.VMEM((3, here, share), low),
            pltpu.VMEM((count - 1, room // 2, width), low),
            pltpu.VMEM((3, deep, hidden), jnp.float32),
            dma((count + 1,)),
            dma((count,)),
            dma((count,)),
            dma((count,)),
            dma((2 * count,)),
            dma((2 * count,)),
            dma((3,)),
            dma((ctx_size,)),
            dma((3,)),
            dma((ctx_size,)),
            dma((count + 1,)),
            dma((count,)),
            dma((count,)),
            dma((count,)),
            dma((2, 2 * count)),
            dma((2, 2 * count)),
            dma((2 * count,)),
            dma((2 * count,)),
            dma((count, CUTS)),
            dma((count, CUTS)),
            dma((count, CUTS)),
            dma((count, CUTS)),
            dma((5,)),
            dma((5,)),
            dma((3,)),
            dma((12,)),
        ],
        compiler_params=pltpu.CompilerParams(
            collective_id=1, has_side_effects=True, vmem_limit_bytes=67043328
        ),
        cost_estimate=estimate(60),
        name="gather_project",
    )(*members, *experts)


def attend_out(
    attended,
    tokens_hbm,
    out_hbm,
    extras_hbm,
    codes,
    hidden_hbm,
    norm_hbm,
    gates,
    low_hbm,
    gathered,
    tokens,
    out_w,
    extras,
    hidden_one,
    norm_two,
    send,
    recv,
    load_sem,
    store_sem,
):
    own, ctx, side, chip, core = places()
    here, width = tokens.shape
    heads = attended.shape[2]
    peers = [
        (across(chip, core, step), (side + other) % 2)
        for other in range(2)
        for step in range(4)
        if (other, step) != (0, 3)
    ]
    peers = peers[:2] + peers[3:5] + peers[2:3] + peers[5:]
    columns = pl.ds(pl.multiple_of(ctx * heads, heads), heads)
    loads = begin(
        (
            (attended.at[ctx], gathered.at[side, :, columns]),
            (tokens_hbm, tokens),
            (out_hbm, out_w),
            (extras_hbm, extras),
        ),
        load_sem,
    )
    greet([(own, place, which) for place, which in peers])

    def copy(number):
        place, which = peers[number]
        return remote(
            attended.at[place],
            gathered.at[side, :, columns],
            send.at[number],
            recv.at[side, ctx],
            (own, place, which),
        )

    for number in range(len(peers)):
        copy(number).start()
    for load in loads:
        load.wait()
    for place, which in peers:
        spot = gathered.at[which, :, pl.ds(pl.multiple_of(place * heads, heads), heads)]
        remote(
            spot, spot, send.at[0], recv.at[which, place], (own, place, which)
        ).wait_recv()
    stores = begin(((gathered.at[side], low_hbm),), store_sem)
    hidden = tokens[...].astype(jnp.float32) + (
        dot_last(gathered[0], out_w[0]) + dot_last(gathered[1], out_w[1])
    )
    hidden_one[...] = hidden
    stores += begin(((hidden_one, hidden_hbm),), store_sem.at[pl.ds(1, 1)])
    scale = lax.rsqrt(jnp.mean(hidden * hidden, axis=1, keepdims=True) + 1e-06)
    gain = jnp.transpose(extras[...].astype(jnp.float32))[1:2, :]
    norm = (hidden * scale * gain).astype(jnp.bfloat16)
    norm_two[...] = norm
    stores += begin(((norm_two, norm_hbm),), store_sem.at[pl.ds(2, 1)])
    logits = dot32(norm, extras[...])
    lane = lax.broadcasted_iota(jnp.int32, (here, LANES), 1).astype(jnp.float32)
    first = jnp.sum(jnp.where(lane == codes[:, 2:3] + 2.0, logits, 0.0), axis=1, keepdims=True)
    second = jnp.sum(jnp.where(lane == codes[:, 3:4] + 2.0, logits, 0.0), axis=1, keepdims=True)
    highest = jnp.maximum(first, second)
    first, second = jnp.exp(first - highest), jnp.exp(second - highest)
    gates[:, 0:1] = first / (first + second)
    gates[:, 1:2] = second / (first + second)
    for number in range(len(peers)):
        copy(number).wait_send()
    for store in stores:
        store.wait()


def run_attend_out(attended, tokens, out_w, extras, codes):
    here, width = tokens.shape
    heads = out_w.shape[2]
    low, wide = jnp.bfloat16, jnp.float32
    return pl.pallas_call(
        attend_out,
        out_shape=(
            jax.ShapeDtypeStruct((here, width), wide),
            jax.ShapeDtypeStruct((here, width), low),
            jax.ShapeDtypeStruct((here, 2), wide),
            jax.ShapeDtypeStruct((here, heads), low),
        ),
        in_specs=in_hbm(4) + in_vmem(1),
        out_specs=tuple(in_hbm(2) + in_vmem(1) + in_hbm(1)),
        scratch_shapes=[
            pltpu.VMEM((2, here, heads), low),
            pltpu.VMEM(tokens.shape, low),
            pltpu.VMEM(out_w.shape, low),
            pltpu.VMEM(extras.shape, low),
            pltpu.VMEM((here, width), wide),
            pltpu.VMEM((here, width), low),
            pltpu.SemaphoreType.DMA((7,)),
            pltpu.SemaphoreType.DMA((2, 4)),
            pltpu.SemaphoreType.DMA((4,)),
            pltpu.SemaphoreType.DMA((3,)),
        ],
        compiler_params=pltpu.CompilerParams(
            collective_id=4, has_side_effects=True, vmem_limit_bytes=67043328
        ),
        cost_estimate=estimate(25),
        name="attend_out",
    )(attended, tokens, out_w, extras, codes)


def attend_back(
    rows_hbm,
    dot_rows,
    gates,
    codes,
    extras_hbm,
    one_hbm,
    cotangent_hbm,
    norm_hbm,
    out_hbm,
    hidden_hbm,
    branch_hbm,
    heads_grad,
    small,
    rows_grad,
    extras,
    hidden_one,
    cotangent,
    norm_two,
    out_w,
    hidden_grad,
    branch_grad,
    outgoing,
    send,
    recv,
    load_sem,
    store_sem,
):
    own, ctx, side, chip, core = places()
    here, width = hidden_one.shape
    heads = heads_grad.shape[2]
    loads = begin(
        (
            (rows_hbm, rows_grad),
            (extras_hbm, extras),
            (one_hbm, hidden_one),
            (cotangent_hbm, cotangent),
            (out_hbm.at[side], out_w),
            (norm_hbm, norm_two),
        ),
        load_sem,
    )
    greet([(own, across(chip, core, step), side) for step in range(3)])
    lane = lax.broadcasted_iota(jnp.int32, (here, LANES), 1).astype(jnp.float32)
    dots = jnp.transpose(dot_rows[...])
    total = dots[:, 0:1] + dots[:, 1:2]
    logit_grad = jnp.zeros((here, LANES), jnp.float32)
    for choice in range(TOP):
        shift = dots[:, choice : choice + 1] - gates[:, choice : choice + 1] * total
        logit_grad = jnp.where(lane == codes[:, 2 + choice : 3 + choice] + 2.0, shift, logit_grad)
    for load in loads:
        load.wait()
    extra = extras[...].astype(jnp.float32)
    norm_grad = rows_grad[...] + lax.dot_general(
        logit_grad,
        extra,
        (((1,), (1,)), ((), ())),
        precision=lax.Precision.HIGHEST,
        preferred_element_type=jnp.float32,
    )
    hidden = hidden_one[...]
    scale = lax.rsqrt(jnp.mean(hidden * hidden, axis=1, keepdims=True) + 1e-06)
    normal = hidden * scale
    spread = norm_grad * jnp.transpose(extra)[1:2, :]
    found = cotangent[...].astype(jnp.float32) + scale * (
        spread - normal * jnp.mean(spread * normal, axis=1, keepdims=True)
    )
    hidden_grad[...] = found
    branch_grad[...] = found.astype(jnp.bfloat16)
    stores = begin(((hidden_grad, hidden_hbm), (branch_grad, branch_hbm)), store_sem)

    def project(place):
        columns = pl.ds(pl.multiple_of(place * heads, heads), heads)
        return dot32(branch_grad[...], out_w[:, columns]).astype(jnp.bfloat16)

    def copy(step):
        place = across(chip, core, step)
        return remote(
            outgoing.at[step], heads_grad.at[ctx], send.at[step], recv.at[ctx], (own, place, side)
        )

    for step in range(3):
        outgoing[step] = project(across(chip, core, step))
        copy(step).start()
    outgoing[3] = project(ctx)
    stores += begin(((outgoing.at[3], heads_grad.at[ctx]),), store_sem.at[pl.ds(2, 1)])
    gain_row = jnp.sum(norm_grad * normal, axis=0, keepdims=True)
    routed = jnp.dot(
        jnp.transpose(logit_grad),
        norm_two[...].astype(jnp.float32),
        precision=lax.Precision.HIGHEST,
        preferred_element_type=jnp.float32,
    )
    line = lax.broadcasted_iota(jnp.int32, (8, width), 0)
    small[...] = jnp.where(line == 1, gain_row, routed[0:8])
    for step in range(3):
        place = across(chip, core, step)
        spot = heads_grad.at[place]
        remote(spot, spot, send.at[0], recv.at[place], (own, place, side)).wait_recv()
    for step in range(3):
        copy(step).wait_send()
    for store in stores:
        store.wait()


def run_attend_back(
    rows_grad, dot_rows, gates, codes, extras, hidden_one, cotangent, norm_two, out_w
):
    here, width = hidden_one.shape
    low, wide = jnp.bfloat16, jnp.float32
    heads = out_w.shape[2] // 4
    return pl.pallas_call(
        attend_back,
        out_shape=(
            jax.ShapeDtypeStruct((here, width), wide),
            jax.ShapeDtypeStruct((here, width), low),
            jax.ShapeDtypeStruct((4, here, heads), low),
            jax.ShapeDtypeStruct((8, width), wide),
        ),
        in_specs=in_hbm(1) + in_vmem(3) + in_hbm(5),
        out_specs=tuple(in_hbm(3) + in_vmem(1)),
        scratch_shapes=[
            pltpu.VMEM((here, width), wide),
            pltpu.VMEM(extras.shape, low),
            pltpu.VMEM((here, width), wide),
            pltpu.VMEM((here, width), low),
            pltpu.VMEM((here, width), low),
            pltpu.VMEM(out_w.shape[1:], low),
            pltpu.VMEM((here, width), wide),
            pltpu.VMEM((here, width), low),
            pltpu.VMEM((4, here, heads), low),
            pltpu.SemaphoreType.DMA((3,)),
            pltpu.SemaphoreType.DMA((4,)),
            pltpu.SemaphoreType.DMA((6,)),
            pltpu.SemaphoreType.DMA((3,)),
        ],
        compiler_params=pltpu.CompilerParams(
            collective_id=5, has_side_effects=True, vmem_limit_bytes=67043328
        ),
        cost_estimate=estimate(4),
        name="attend_back",
    )(rows_grad, dot_rows, gates, codes, extras, hidden_one, cotangent, norm_two, out_w)


def gradient_return(
    count,
    packed_grad,
    full_hbm,
    norm,
    tokens,
    bias_line,
    own_hbm,
    first_hbm,
    one_out_hbm,
    near_out_hbm,
    two_out_hbm,
    three_out_hbm,
    last_hbm,
    gates,
    codes,
    branch_grad,
    attended,
    small,
    one_hbm,
    grad_hbm,
    extras,
    mixed,
    input_grad,
    query_grad,
    key_grad,
    value_grad,
    bias_grad,
    gain_grad,
    out_grad,
    mixture,
    mixture_in,
    full,
    outs,
    hidden_one,
    hidden_grad,
    incoming,
    norm_t,
    outgoing,
    side_out,
    side_in,
    spread,
    core_in,
    chip_out,
    chip_in,
    line_out,
    line_in,
    out_going,
    out_core_in,
    out_spread,
    out_chip_out,
    out_chip_in,
    out_line_out,
    out_line_in,
    bias_out,
    bias_in,
    spread_gain,
    grad_send,
    grad_recv,
    side_send,
    side_recv,
    core_send,
    core_recv,
    chip_send,
    chip_recv,
    line_send,
    line_recv,
    bias_send,
    bias_recv,
    mixture_sem,
    mix_sem,
    load_sem,
):
    own, ctx, side, chip, core = places()
    ctx_size, here, share = packed_grad.shape
    width = norm.shape[1]
    halves = HALVES
    part = here // halves
    groups = ctx_size
    pair = (own, ctx, 1 - side)
    chip_peer = (own, (1 - chip) * 2 + core, side)
    core_peer = (own, chip * 2 + 1 - core, side)
    others = [
        (nearest(own, count, step), across(chip, core, turn), side)
        for step in range(count)
        for turn in range(4)
        if (step, turn) != (0, 3)
    ]
    room, half = outs.shape[1], last_hbm.shape[0]
    pairs = (
        (full_hbm, full),
        (own_hbm, outs.at[0]),
        (grad_hbm, hidden_grad),
        (one_hbm, hidden_one),
        (first_hbm, outs.at[1, pl.ds(0, half)]),
        (one_out_hbm, outs.at[1, pl.ds(half, half)]),
        (near_out_hbm, outs.at[2, pl.ds(0, half)]),
        (two_out_hbm, outs.at[2, pl.ds(half, half)]),
        (three_out_hbm, outs.at[3, pl.ds(0, half)]),
    )
    loads = [
        pltpu.make_async_copy(source, target, load_sem.at[number])
        for number, (source, target) in enumerate(pairs)
    ]
    for load in loads:
        load.start()
    greet(others + [pair])

    def to_owner(step, piece):
        place = across(chip, core, step)
        spot = pl.ds(piece * part, part)
        return remote(
            packed_grad.at[place, spot],
            incoming.at[ctx, spot],
            grad_send.at[step, piece],
            grad_recv.at[ctx, piece],
            (own, place, side),
        )

    for piece in range(halves):
        for step in range(3):
            to_owner(step, piece).start()
    incoming[ctx] = packed_grad[ctx]

    mixture_copy = remote(mixture, mixture_in, mixture_sem.at[0], mixture_sem.at[1], pair)

    def mixing(start, amount):
        slots = lax.broadcasted_iota(jnp.int32, (here, amount), 1) + start
        slots = slots.astype(jnp.float32)
        held = jnp.where(codes[:, 0:1] == slots, gates[:, 0:1], 0.0)
        held = held + jnp.where(codes[:, 1:2] == slots, gates[:, 1:2], 0.0)
        return held.astype(jnp.bfloat16)

    last_copy = remote(
        last_hbm,
        outs.at[3, pl.ds(half, half)],
        mix_sem.at[0],
        mix_sem.at[1],
        (partner(own, 3), ctx, side),
    )
    last_copy.start()

    def mix():
        for number in (1, 4, 5, 6, 7, 8):
            loads[number].wait()
        last_copy.wait_recv()
        total = jnp.zeros((here, width), jnp.float32)
        for turn in range(count):
            total = total + dot32(mixing(partner(own, turn) * room, room), outs[turn])
        mixture[...] = total.astype(jnp.bfloat16)
        mixture_copy.start()

    span = bias_line.shape[1]
    index = lax.broadcasted_iota(jnp.int32, (span, LANES), 0)
    relative = jnp.where(index < span // 2, -index, span - index)
    bucket = lax.broadcasted_iota(jnp.int32, (span, LANES), 1)
    onehot = jnp.where(bucket_ids(relative) == bucket, 1.0, 0.0)
    sums = jnp.dot(
        bias_line[...], onehot, precision=lax.Precision.HIGHEST, preferred_element_type=jnp.float32
    )
    far = jnp.sum(bias_line[...], axis=1, keepdims=True)
    lane = lax.broadcasted_iota(jnp.int32, (2, LANES), 1)
    total = sums[0:2] + jnp.where(lane == NBUCK // 2 - 1, far[2:4], 0.0)
    total = total + jnp.where(lane == NBUCK - 1, far[4:6], 0.0)
    bias_sum = jnp.concatenate([total, jnp.zeros((6, LANES), jnp.float32)], axis=0)

    def to_bias(number):
        return remote(
            bias_out.at[number],
            bias_in.at[own, ctx],
            bias_send.at[number],
            bias_recv.at[own, ctx],
            others[number],
        )

    stages = [
        (
            outgoing.at[group],
            core_in.at[group],
            spread.at[group],
            chip_out.at[group],
            chip_in.at[group],
            line_out.at[group],
            line_in.at[group],
            None,
        )
        for group in range(groups)
    ]
    stages.append(
        (
            out_going,
            out_core_in,
            out_spread,
            out_chip_out,
            out_chip_in,
            out_line_out,
            out_line_in,
            None,
        )
    )
    rows = norm_t.shape[0] // (count * ctx_size)

    def to_core(group):
        source, target = stages[group][0].at[:, 1 - core], stages[group][1]
        return remote(source, target, core_send.at[group], core_recv.at[group], core_peer)

    def to_chip(group):
        source, target = stages[group][3], stages[group][4]
        return remote(source, target, chip_send.at[group], chip_recv.at[group], chip_peer)

    def to_line(group, step):
        shard = nearest(own, count, step)
        source, target = stages[group][5].at[shard], stages[group][6].at[own]
        send, recv = line_send.at[group, step], line_recv.at[group, own]
        return remote(source, target, send, recv, (shard, ctx, side))

    def contract(group):
        found = dot32(norm_t[...], incoming[group] if group < groups else attended[...])
        found = found.reshape(count * 2, 2, rows, found.shape[1])
        stages[group][0][...] = found.astype(jnp.bfloat16)
        to_core(group).start()

    def over_chip(group):
        to_core(group).wait_recv()
        source, arrived, summed, target = stages[group][:4]
        found = source[:, core].astype(jnp.float32) + arrived[...].astype(jnp.float32)
        summed[...] = found.reshape(count, 2, rows, found.shape[2])
        target[...] = summed[:, 1 - chip].astype(jnp.bfloat16)
        to_chip(group).start()

    def over_line(group):
        to_chip(group).wait_recv()
        found = stages[group][2][:, chip] + stages[group][4][...].astype(jnp.float32)
        stages[group][5][...] = found.astype(jnp.bfloat16)
        for step in range(1, count):
            to_line(group, step).start()

    def collect(group):
        total = stages[group][5][own].astype(jnp.float32)
        for step in range(1, count):
            shard = nearest(own, count, step)
            spot = stages[group][6].at[shard]
            remote(
                spot, spot, line_send.at[group, 0], line_recv.at[group, shard], pair
            ).wait_recv()
            total = total + spot[...].astype(jnp.float32)
        if group == groups:
            out_grad[...] = total
        else:
            columns = slice(group * LANES, (group + 1) * LANES)
            for number, target in enumerate((query_grad, key_grad, value_grad)):
                target[:, columns] = total[:, number * LANES : (number + 1) * LANES]

    norm_t[...] = jnp.transpose(branch_grad[...].astype(jnp.float32)).astype(jnp.bfloat16)
    contract(groups)
    norm_t[...] = jnp.transpose(norm[...].astype(jnp.float32)).astype(jnp.bfloat16)
    over_chip(groups)

    def to_side(piece):
        return remote(
            side_out.at[piece],
            side_in.at[piece],
            side_send.at[piece],
            side_recv.at[piece],
            pair,
        )

    values = tokens[...].astype(jnp.float32)
    scale = lax.rsqrt(jnp.mean(values * values, axis=1, keepdims=True) + 1e-06)
    normal = values * scale
    first_gain = jnp.transpose(extras[...].astype(jnp.float32))[0:1, :]
    loads[0].wait()

    def landed(piece):
        for step in range(3):
            place = across(chip, core, step)
            target = incoming.at[place, pl.ds(piece * part, part)]
            remote(
                target, target, grad_send.at[0, 0], grad_recv.at[place, piece], pair
            ).wait_recv()

    def send_side(piece):
        spot = pl.ds(piece * part, part)
        total = jnp.zeros((part, width), jnp.float32)
        for place in range(ctx_size):
            columns = slice(place * share, (place + 1) * share)
            total = total + dot_last(incoming[place, spot, :], full[:, columns])
        side_out[piece] = total.astype(jnp.bfloat16)
        to_side(piece).start()

    def finish_sides():
        loads[2].wait()
        gain = jnp.zeros((1, width), jnp.float32)
        for piece in range(halves):
            to_side(piece).wait_recv()
            total = side_out[piece].astype(jnp.float32) + side_in[piece].astype(jnp.float32)
            lines = slice(piece * part, (piece + 1) * part)
            upright = normal[lines]
            gain = gain + jnp.sum(total * upright, axis=0, keepdims=True)
            total = total * first_gain
            total = total - upright * jnp.mean(total * upright, axis=1, keepdims=True)
            input_grad[lines, :] = (hidden_grad[lines, :] + scale[lines] * total).astype(
                jnp.bfloat16
            )
        spread_gain[...] = small[...]
        spread_gain[0:1, :] = gain

        def message(shard, place):
            lanes = pl.ds(pl.multiple_of((shard * 2 + place // 2) * LANES, LANES), LANES)
            return jnp.concatenate([bias_sum, spread_gain[:, lanes]], axis=0)

        for number, (shard, place, _) in enumerate(others):
            bias_out[number] = message(shard, place)
            to_bias(number).start()
        bias_in[own, ctx] = message(own, ctx)

    for piece in range(halves - 1):
        landed(piece)
        send_side(piece)
    landed(halves - 1)
    contract(0)
    send_side(halves - 1)
    over_chip(0)
    contract(1)
    contract(2)
    over_chip(1)
    mix()
    contract(3)
    over_chip(2)
    over_line(groups)
    over_chip(3)
    over_line(0)
    over_line(1)
    over_line(2)
    over_line(3)
    finish_sides()
    for group in (groups, 0, 1, 2, 3):
        collect(group)

    for number, (shard, place, _) in enumerate(others):
        spot = bias_in.at[shard, place]
        remote(spot, spot, bias_send.at[0], bias_recv.at[shard, place], pair).wait_recv()
    for place in range(ctx_size):
        total = bias_in[0, place]
        for shard in range(1, count):
            total = total + bias_in[shard, place]
        bias_grad[place] = total[:8]
        gain_total = total[8:] if place == 0 else gain_total + total[8:]
    gain_grad[...] = gain_total

    mixture_copy.wait()
    loads[3].wait()
    last_copy.wait_send()
    mixed[...] = (
        hidden_one[...] + (mixture[...].astype(jnp.float32) + mixture_in[...].astype(jnp.float32))
    ).astype(jnp.bfloat16)
    for number in range(len(others)):
        to_bias(number).wait_send()
    for piece in range(halves):
        to_side(piece).wait_send()
        for step in range(3):
            to_owner(step, piece).wait_send()
    for group in range(groups + 1):
        to_core(group).wait_send()
        to_chip(group).wait_send()
        for step in range(1, count):
            to_line(group, step).wait_send()


def run_return(
    count,
    packed_grad,
    full,
    norm,
    tokens,
    bias_line,
    outs,
    gates,
    codes,
    branch_grad,
    attended,
    small,
    hidden_one,
    hidden_grad,
    extras,
):
    ctx_size, here, share = packed_grad.shape
    width = norm.shape[1]
    rows = width // (count * ctx_size)
    low, wide = jnp.bfloat16, jnp.float32
    dma = pltpu.SemaphoreType.DMA
    columns = share
    out_columns = attended.shape[1]
    return pl.pallas_call(
        partial(gradient_return, count),
        out_shape=(
            jax.ShapeDtypeStruct((here, width), low),
            jax.ShapeDtypeStruct((here, width), low),
            *[jax.ShapeDtypeStruct((rows, ctx_size * LANES), wide)] * 3,
            jax.ShapeDtypeStruct((ctx_size, 8, LANES), wide),
            jax.ShapeDtypeStruct((8, LANES), wide),
            jax.ShapeDtypeStruct((rows, out_columns), wide),
        ),
        in_specs=[
            pl.BlockSpec(memory_space=pl.ANY if number in (1, 5, 6, 7, 8, 9, 10, 11, 17, 18) else pltpu.VMEM)
            for number in range(20)
        ],
        out_specs=tuple(in_vmem(8)),
        scratch_shapes=[
            pltpu.VMEM((here, width), low),
            pltpu.VMEM((here, width), low),
            pltpu.VMEM(full.shape, low),
            pltpu.VMEM((count,) + outs[0].shape, low),
            pltpu.VMEM((here, width), wide),
            pltpu.VMEM((here, width), wide),
            pltpu.VMEM((ctx_size, here, share), low),
            pltpu.VMEM((width, here), low),
            pltpu.VMEM((ctx_size, count * 2, 2, rows, columns), low),
            pltpu.VMEM((HALVES, here // HALVES, width), low),
            pltpu.VMEM((HALVES, here // HALVES, width), low),
            pltpu.VMEM((ctx_size, count, 2, rows, columns), wide),
            pltpu.VMEM((ctx_size, count * 2, rows, columns), low),
            pltpu.VMEM((ctx_size, count, rows, columns), low),
            pltpu.VMEM((ctx_size, count, rows, columns), low),
            pltpu.VMEM((ctx_size, count, rows, columns), low),
            pltpu.VMEM((ctx_size, count, rows, columns), low),
            pltpu.VMEM((count * 2, 2, rows, out_columns), low),
            pltpu.VMEM((count * 2, rows, out_columns), low),
            pltpu.VMEM((count, 2, rows, out_columns), wide),
            pltpu.VMEM((count, rows, out_columns), low),
            pltpu.VMEM((count, rows, out_columns), low),
            pltpu.VMEM((count, rows, out_columns), low),
            pltpu.VMEM((count, rows, out_columns), low),
            pltpu.VMEM((15, 16, LANES), wide),
            pltpu.VMEM((count, ctx_size, 16, LANES), wide),
            pltpu.VMEM((8, width), wide),
            dma((3, HALVES)),
            dma((ctx_size, HALVES)),
            dma((HALVES,)),
            dma((HALVES,)),
            dma((ctx_size + 1,)),
            dma((ctx_size + 1,)),
            dma((ctx_size + 1,)),
            dma((ctx_size + 1,)),
            dma((ctx_size + 1, count)),
            dma((ctx_size + 1, count)),
            dma((15,)),
            dma((count, ctx_size)),
            dma((2,)),
            dma((2,)),
            dma((9,)),
        ],
        compiler_params=pltpu.CompilerParams(
            collective_id=2, has_side_effects=True, vmem_limit_bytes=67043328
        ),
        cost_estimate=estimate(45),
        name="gradient_return",
    )(
        packed_grad,
        full,
        norm,
        tokens,
        bias_line,
        *outs,
        gates,
        codes,
        branch_grad,
        attended,
        small,
        hidden_one,
        hidden_grad,
        extras,
    )


def swap_sides(member):
    return lax.ppermute(member, "tensor", [(0, 1), (1, 0)])


def exchange(member, axis):
    return lax.all_to_all(member, axis, split_axis=0, concat_axis=0, tiled=True)


def slot_codes(routes, experts, room):
    tokens = routes.shape[0]
    picks = routes[:, :, None] == jnp.arange(experts, dtype=jnp.int32)[None, None, :]
    named = jnp.sum(picks, axis=1).astype(jnp.bfloat16)
    index = jnp.arange(tokens, dtype=jnp.int32)
    before = (index[:, None] > index[None, :]).astype(jnp.bfloat16)
    rank = jnp.dot(before, named, preferred_element_type=jnp.float32)
    slots = rank + room * jnp.arange(experts, dtype=jnp.float32)[None, :]
    return picks, jnp.sum(jnp.where(picks, slots[:, None, :], 0.0), axis=2)


def experts_apart(norm_two, upstream, gates, codes, room, count, weights):
    tokens, width = norm_two.shape
    codes = codes.astype(jnp.int32).reshape(-1)
    shaped = (count, room, width)

    def sent(member):
        slots = jnp.zeros((count * room, width), jnp.bfloat16).at[codes].set(member)
        return exchange(slots.reshape(shaped), "shard").reshape(-1, width)

    slot_rows = sent(jnp.repeat(norm_two, TOP, axis=0))
    slot_grads = sent(
        (gates[:, :, None] * upstream[:, None, :]).reshape(-1, width).astype(jnp.bfloat16)
    )
    gate_mat, up_mat, down_mat = weights
    gate_pre = dot32(slot_rows, gate_mat)
    up_pre = dot32(slot_rows, up_mat)
    activated, slope = gelu_parts(gate_pre)
    inner = (activated * up_pre).astype(jnp.bfloat16)
    expert_out = contract_cols(inner, down_mat)
    inner_grad = dot32(slot_grads, down_mat)
    gate_grad = (inner_grad * up_pre * slope).astype(jnp.bfloat16)
    up_grad = (inner_grad * activated).astype(jnp.bfloat16)
    rows_grad = contract_cols(gate_grad, gate_mat) + contract_cols(up_grad, up_mat)

    def returned(member):
        member = lax.psum(member.astype(jnp.bfloat16), "tensor").reshape(shaped)
        member = exchange(member, "shard").reshape(-1, width)[codes]
        return member.astype(jnp.float32).reshape(tokens, TOP, width)

    per_choice = returned(expert_out)
    mixture = jnp.sum(gates[:, :, None] * per_choice, axis=1)
    dots = gates * jnp.sum(per_choice * upstream[:, None, :], axis=2)
    norm_grad = jnp.sum(returned(rows_grad), axis=1)
    return mixture, dots, norm_grad, slot_rows, slot_grads, inner, gate_grad, up_grad


def local_general(
    tokens_in,
    cotangent,
    segment_ids,
    live_blocks,
    routes,
    w_query,
    w_key,
    w_value,
    w_out,
    rel_bias,
    attn_gain,
    ffn_gain,
    router,
    w_gate,
    w_up,
    w_down,
):
    rows_here, width = tokens_in.shape
    ctx_size = lax.axis_size("ctx")
    side_count = lax.axis_size("tensor")
    ctx_index = lax.axis_index("ctx")
    side = lax.axis_index("tensor")
    head_cols = w_query.shape[1]
    share = head_cols // ctx_size
    experts = router.shape[1]
    room = max(2, 3 * rows_here // experts)

    picks, codes = slot_codes(routes, experts, room)

    def by_owner(member):
        return member.reshape(member.shape[0], ctx_size, share)

    packed_rows = jnp.stack([by_owner(w_query), by_owner(w_key), by_owner(w_value)], axis=2)
    gathered = lax.all_gather(
        jnp.concatenate(
            [
                packed_rows.reshape(w_query.shape[0], -1),
                attn_gain[:, None],
                ffn_gain[:, None],
                router,
            ],
            axis=1,
        ).astype(jnp.bfloat16),
        ("shard", "ctx"),
        axis=0,
        tiled=True,
    )
    packed_w = gathered[:, : 3 * head_cols]
    gain_one = gathered[:, 3 * head_cols]
    gain_two = gathered[:, 3 * head_cols + 1]
    router_w = gathered[:, 3 * head_cols + 2 :]
    out_w = lax.all_gather(w_out.astype(jnp.bfloat16), ("shard", "ctx", "tensor"), axis=0)
    out_w = out_w.reshape(-1, side_count, w_out.shape[0], head_cols)
    out_w = jnp.transpose(out_w, (0, 2, 1, 3)).reshape(width, side_count * head_cols)
    expert_weights = tuple(
        lax.all_gather(member.astype(jnp.bfloat16), "ctx", axis=1, tiled=True)[0]
        for member in (w_gate, w_up, w_down)
    )

    inputs = tokens_in.astype(jnp.float32)
    scale_one = lax.rsqrt(jnp.mean(inputs * inputs, axis=1, keepdims=True) + 1e-06)
    normal_one = inputs * scale_one
    norm_one = (normal_one * gain_one.astype(jnp.float32)).astype(jnp.bfloat16)
    packed = dot32(norm_one, packed_w).astype(jnp.bfloat16)
    packed = jnp.transpose(packed.reshape(rows_here, ctx_size, 3 * share), (1, 0, 2))
    packed = exchange(packed, "ctx").reshape(ctx_size * rows_here, 3 * share)
    segments = lax.all_gather(segment_ids.reshape(-1), "ctx", axis=0, tiled=True)
    alive = live_tiles(segments, live_blocks[0])
    segment_row = segments.astype(jnp.float32)[None]
    pair_heads = share // HEAD
    own_bias = lax.dynamic_slice_in_dim(rel_bias, ctx_index * pair_heads, pair_heads, 1)
    buckets = span_buckets()
    line = jnp.dot(own_bias.T, buckets.T, precision=lax.Precision.HIGHEST)
    attended, attended_t, log_sum = run_forward(alive, packed, segment_row, line)
    attended = attended.reshape(ctx_size, 1, rows_here, share)
    attended = jnp.broadcast_to(attended, (ctx_size, side_count, rows_here, share))
    attended = exchange(attended.reshape(-1, rows_here, share), ("ctx", "tensor"))
    attended = attended.reshape(ctx_size, side_count, rows_here, share)
    attended = jnp.transpose(attended, (2, 1, 0, 3))
    attended_low = lax.dynamic_index_in_dim(attended, side, 1, False).reshape(rows_here, head_cols)
    attended = attended.reshape(rows_here, side_count * head_cols)
    hidden_one = inputs + contract_cols(attended, out_w)
    scale_two = lax.rsqrt(jnp.mean(hidden_one * hidden_one, axis=1, keepdims=True) + 1e-06)
    normal_two = hidden_one * scale_two
    norm_two = (normal_two * gain_two.astype(jnp.float32)).astype(jnp.bfloat16)
    logits = dot32(norm_two, router_w)
    chosen = jnp.sum(jnp.where(picks, logits[:, None, :], 0.0), axis=2)
    gates = jax.nn.softmax(chosen, axis=1)
    upstream = cotangent.astype(jnp.float32)
    results = experts_apart(norm_two, upstream, gates, codes, room, experts, expert_weights)
    mixture, gate_dots, norm_grad, slot_rows, slot_grads, inner, gate_grad, up_grad = results
    weight_grads = lax.psum_scatter(
        jnp.stack(
            [
                contract_rows(slot_rows, gate_grad),
                contract_rows(slot_rows, up_grad),
                contract_rows(slot_grads, inner),
            ],
            axis=1,
        ).astype(jnp.bfloat16),
        "ctx",
        scatter_dimension=0,
        tiled=True,
    ).astype(jnp.float32)
    mixed = (hidden_one + mixture).astype(jnp.bfloat16)
    gate_shift = gate_dots - gates * jnp.sum(gate_dots, axis=1, keepdims=True)
    logit_grad = jnp.sum(jnp.where(picks, gate_shift[:, :, None], 0.0), axis=1)
    router_f = router_w.astype(jnp.float32)
    norm_grad = norm_grad + jnp.dot(logit_grad, router_f.T, precision=lax.Precision.HIGHEST)
    spread_two = norm_grad * gain_two.astype(jnp.float32)
    hidden_grad = upstream + scale_two * (
        spread_two - normal_two * jnp.mean(spread_two * normal_two, axis=1, keepdims=True)
    )
    branch_grad = hidden_grad.astype(jnp.bfloat16)
    own_out_w = lax.dynamic_slice_in_dim(out_w, side * head_cols, head_cols, 1)
    grad_heads = dot32(branch_grad, own_out_w).astype(jnp.bfloat16)
    grad_heads = jnp.transpose(grad_heads.reshape(rows_here, ctx_size, share), (1, 0, 2))
    grad_heads = exchange(grad_heads, "ctx").reshape(-1, share)
    packed_grad, bias_line = run_backward(
        alive, packed, segment_row, line, grad_heads, attended_t, log_sum
    )
    own_grad = jnp.dot(buckets.T, bias_line[:pair_heads].T, precision=lax.Precision.HIGHEST)
    far = jnp.sum(bias_line[pair_heads : 3 * pair_heads], axis=1)
    half = NBUCK // 2
    own_grad = own_grad.at[half - 1].add(far[:pair_heads]).at[NBUCK - 1].add(far[pair_heads:])
    bias_acc = lax.dynamic_update_slice_in_dim(
        jnp.zeros(rel_bias.shape, jnp.float32), own_grad, ctx_index * pair_heads, 1
    )
    packed_grad = exchange(packed_grad.reshape(ctx_size, rows_here, 3 * share), "ctx")
    packed_grad = jnp.transpose(packed_grad, (1, 0, 2)).reshape(rows_here, 3 * head_cols)
    norm_one_grad = contract_cols(packed_grad, packed_w).astype(jnp.bfloat16)
    norm_one_grad = norm_one_grad.astype(jnp.float32) + swap_sides(norm_one_grad).astype(
        jnp.float32
    )
    spread_one = norm_one_grad * gain_one.astype(jnp.float32)
    input_grad = hidden_grad + scale_one * (
        spread_one - normal_one * jnp.mean(spread_one * normal_one, axis=1, keepdims=True)
    )
    first_gain = jnp.sum(norm_one_grad * normal_one, axis=0)[:, None]
    second_gain = jnp.sum(norm_grad * normal_two, axis=0)[:, None]
    router_part = jnp.dot(
        norm_two.astype(jnp.float32).T, logit_grad, precision=lax.Precision.HIGHEST
    )
    reduced = lax.psum_scatter(
        jnp.concatenate(
            [
                contract_rows(norm_one, packed_grad),
                contract_rows(branch_grad, attended_low),
                first_gain,
                second_gain,
                router_part,
            ],
            axis=1,
        ),
        ("shard", "ctx"),
        scatter_dimension=0,
        tiled=True,
    )
    grad_bias = lax.psum(bias_acc, ("shard", "ctx"))
    packed_rows = reduced[:, : 3 * head_cols].reshape(-1, ctx_size, 3, share)
    return (
        mixed,
        input_grad.astype(jnp.bfloat16),
        packed_rows[:, :, 0].reshape(-1, head_cols),
        packed_rows[:, :, 1].reshape(-1, head_cols),
        packed_rows[:, :, 2].reshape(-1, head_cols),
        reduced[:, 3 * head_cols : 4 * head_cols],
        grad_bias,
        reduced[:, 4 * head_cols],
        reduced[:, 4 * head_cols + 1],
        reduced[:, 4 * head_cols + 2 :],
        weight_grads[:, 0][None],
        weight_grads[:, 1][None],
        weight_grads[:, 2][None],
    )


def ppermute_ctx(member, flip):
    return lax.ppermute(member, "ctx", [(place, place ^ flip) for place in range(4)])


def local_fused(
    tokens_in,
    cotangent,
    segment_ids,
    live_blocks,
    routes,
    w_query,
    w_key,
    w_value,
    w_out,
    rel_bias,
    attn_gain,
    ffn_gain,
    router,
    w_gate,
    w_up,
    w_down,
):
    rows_here, width = tokens_in.shape
    count = lax.axis_size("shard")
    ctx_size = lax.axis_size("ctx")
    ctx_index = lax.axis_index("ctx")
    share = w_query.shape[1] // ctx_size
    rows = w_query.shape[0]
    experts = router.shape[1]
    room = max(2, 3 * rows_here // experts)
    members = (
        w_query,
        w_key,
        w_value,
        w_out,
        attn_gain[None],
        ffn_gain[None],
        router.T,
        tokens_in,
        segment_ids,
        cotangent,
        routes.T,
    )
    full, packed, norm_one, segments, out_w, up_slots, *lows = run_gather(
        count, ctx_size, room, members, (w_gate[0], w_up[0], w_down[0])
    )
    gate_low, up_low, down_low, gate_core, up_core, down_core, gate_chip, gate_far = lows[:8]
    codes, code_rows, extras = lows[8:]
    up_chip, down_chip = ppermute_ctx(up_low, 2), ppermute_ctx(down_low, 2)

    packed = packed.reshape(ctx_size * rows_here, 3 * share)
    segment_row = segments[:, 0].reshape(1, -1)
    alive = live_tiles(segment_row[0], live_blocks[0])
    pair_heads = share // HEAD
    own_bias = lax.dynamic_slice_in_dim(rel_bias, ctx_index * pair_heads, pair_heads, 1)
    line = jnp.dot(own_bias.T, span_buckets().T, precision=lax.Precision.HIGHEST)
    attended, attended_t, log_sum = run_forward(alive, packed, segment_row, line)
    attended, up_chip, down_chip = lax.optimization_barrier((attended, up_chip, down_chip))
    expert_weights = [gate_low, gate_chip, gate_core, gate_far]
    expert_weights += [up_low, up_chip, up_core, ppermute_ctx(up_chip, 1)]
    expert_weights += [down_low, down_chip, down_core, ppermute_ctx(down_chip, 1)]
    hidden_one, norm_two, gates, attended_low = run_attend_out(
        attended.reshape(ctx_size, rows_here, share), tokens_in, out_w, extras, codes
    )
    rows_grad, dots, own_out, *outs, last_out, kept, gate_given, pair_given = run_experts(
        count, ctx_size, norm_two, gates, code_rows, codes, up_slots, expert_weights
    )
    for number, turn in enumerate((1, 1, 2, 2, 3)):
        pairs = [(place, place ^ turn) for place in range(count)]
        outs[number] = lax.ppermute(outs[number], "shard", pairs)
    hidden_grad, branch_grad, heads_grad, small = run_attend_back(
        rows_grad, dots, gates, codes, extras, hidden_one, cotangent, norm_two, out_w
    )
    heads_grad, pair_given, outs[0] = lax.optimization_barrier((heads_grad, pair_given, outs[0]))
    pair_given = ppermute_ctx(pair_given, 2)
    outs = [own_out, *outs, last_out]
    given = [gate_given, pair_given[0], pair_given[1]]
    weight_grads = [
        kept[number].astype(jnp.float32) + given[number].astype(jnp.float32) for number in range(3)
    ]
    packed_grad, bias_line = run_backward(
        alive, packed, segment_row, line, heads_grad.reshape(-1, share), attended_t, log_sum
    )
    returned = run_return(
        count,
        packed_grad.reshape(ctx_size, rows_here, 3 * share),
        full,
        norm_one,
        tokens_in,
        bias_line,
        outs,
        gates,
        codes,
        branch_grad,
        attended_low,
        small,
        hidden_one,
        hidden_grad,
        extras,
    )
    mixed, input_grad, query_grad, key_grad, value_grad, bias_grad, gains_grad, out_grad = returned
    gains_grad = lax.dynamic_slice_in_dim(gains_grad, ctx_index % 2 * rows, rows, 1)
    bias_grad = jnp.transpose(bias_grad[:, :pair_heads, :NBUCK], (2, 0, 1))
    return (
        mixed,
        input_grad,
        query_grad,
        key_grad,
        value_grad,
        out_grad,
        bias_grad.reshape(rel_bias.shape),
        gains_grad[0],
        gains_grad[1],
        jnp.transpose(gains_grad[2 : 2 + experts]),
        weight_grads[0][None],
        weight_grads[1][None],
        weight_grads[2][None],
    )


def solution(mesh):
    placed = (
        P(("shard", "ctx"), None),
        P(("shard", "ctx"), None),
        P("shard", "ctx"),
        P("shard", None, None),
        P(("shard", "ctx"), None),
        P(("shard", "ctx"), "tensor"),
        P(("shard", "ctx"), "tensor"),
        P(("shard", "ctx"), "tensor"),
        P(("shard", "ctx"), "tensor"),
        P(None, "tensor"),
        P(("shard", "ctx")),
        P(("shard", "ctx")),
        P(("shard", "ctx"), None),
        P("shard", "ctx", "tensor"),
        P("shard", "ctx", "tensor"),
        P("shard", "ctx", "tensor"),
    )
    sizes = (mesh.shape["shard"], mesh.shape["ctx"], mesh.shape["tensor"])
    fused = sizes == (4, 4, 2)
    return jax.shard_map(
        local_fused if fused else local_general,
        mesh=mesh,
        in_specs=placed,
        out_specs=(
            P(("shard", "ctx"), None),
            P(("shard", "ctx"), None),
            P(("shard", "ctx"), "tensor"),
            P(("shard", "ctx"), "tensor"),
            P(("shard", "ctx"), "tensor"),
            P(("shard", "ctx"), "tensor"),
            P(None, "tensor"),
            P(("shard", "ctx")),
            P(("shard", "ctx")),
            P(("shard", "ctx"), None),
            P("shard", "ctx", "tensor"),
            P("shard", "ctx", "tensor"),
            P("shard", "ctx", "tensor"),
        ),
        check_vma=False,
    )
```

```python
import math
from functools import partial

import jax
import jax.numpy as jnp
from jax import lax
from jax.experimental import pallas as pl
from jax.experimental.pallas import tpu as pltpu
from jax.sharding import PartitionSpec as P

HEAD = 64
NBUCK = 32
TOP = 2
ATT_BLK = 512


FAR_STEPS = (12, 16, 23, 32, 46, 64, 91)


def bucket_ids(relative):
    distance = jnp.abs(relative)
    far = jnp.full(distance.shape, 8, jnp.int32)
    for bound in FAR_STEPS:
        far = far + (distance >= bound).astype(jnp.int32)
    near = jnp.where(distance < 8, distance, far)
    return near + jnp.where(relative > 0, NBUCK // 2, 0)


def contract_rows(left, right):
    return lax.dot_general(
        left, right, (((0,), (0,)), ((), ())), preferred_element_type=jnp.float32
    )


def contract_cols(left, right):
    return lax.dot_general(
        left, right, (((1,), (1,)), ((), ())), preferred_element_type=jnp.float32
    )


TILE = 256
BIG = 2.0**100
SPAN = 4 * TILE


def place_mask(segment_row):
    rows = lax.broadcasted_iota(jnp.int32, (128, segment_row.shape[1]), 0).astype(jnp.float32)
    apart = jnp.where(rows == segment_row, 0.0, -BIG)
    return jnp.where(rows < 8.0, apart, jnp.where(rows < 11.0, 1.0, 0.0))


def seat_rows(segment_row, extra):
    rows = lax.broadcasted_iota(jnp.int32, (128, segment_row.shape[1]), 0).astype(jnp.float32)
    own = jnp.where((rows == segment_row) & (rows < 8.0), 1.0, 0.0)
    if extra is None:
        return own.astype(jnp.bfloat16)
    high = extra.astype(jnp.bfloat16).astype(jnp.float32)
    rest = extra - high
    middle = rest.astype(jnp.bfloat16).astype(jnp.float32)
    low = rest - middle
    own = jnp.where(rows == 8.0, high, own)
    own = jnp.where(rows == 9.0, middle, own)
    return jnp.where(rows == 10.0, low, own).astype(jnp.bfloat16)


def fill_bias(line_ref, bias_ref):
    for head in range(2):
        line = line_ref[head : head + 1, :]
        turned = pltpu.roll(
            jnp.broadcast_to(line, (TILE, SPAN)), 0, axis=1, stride=1, stride_axis=0
        )
        bias_ref[head, 1] = turned[:, TILE : 2 * TILE]
        bias_ref[head, 2] = turned[:, :TILE]
        bias_ref[head, 3] = turned[:, 3 * TILE :]
        bias_ref[head, 0] = jnp.broadcast_to(line[:, 511:512], (TILE, TILE))
        bias_ref[head, 4] = jnp.broadcast_to(line[:, 513:514], (TILE, TILE))


def tile_at(index):
    return pl.ds(pl.multiple_of(index * TILE, TILE), TILE)


def dot32(left, right):
    return jnp.dot(left, right, preferred_element_type=jnp.float32)


def attention_forward(
    alive, packed, segment, line, out, out_t, log_sum, key_side, query_side, value_t, bias, top, acc
):
    length = packed.shape[0]
    tiles = length // TILE
    fill_bias(line, bias)

    def prepare(index, unused):
        spot = tile_at(index)
        seg = segment[0:1, spot]
        block = packed[spot, :].astype(jnp.float32)
        key_side[spot, :128] = packed[spot, 128:256]
        key_side[spot, 128:] = jnp.transpose(place_mask(seg)).astype(jnp.bfloat16)
        query_t = jnp.transpose(block[:, :128]) * 0.125
        seats = seat_rows(seg, None)
        half = lax.broadcasted_iota(jnp.int32, (128, TILE), 0) // HEAD
        values = jnp.transpose(block[:, 256:]).astype(jnp.bfloat16)
        ones = jnp.where(lax.broadcasted_iota(jnp.int32, (16, TILE), 0) == 0, 1.0, 0.0)
        for head in range(2):
            query_side[head, :128, spot] = jnp.where(half == head, query_t, 0.0).astype(
                jnp.bfloat16
            )
            query_side[head, 128:, spot] = seats
            value_t[head, :HEAD, spot] = values[HEAD * head : HEAD * (head + 1)]
            value_t[head, HEAD:, spot] = ones.astype(jnp.bfloat16)
        return unused

    lax.fori_loop(0, tiles, prepare, 0)

    def query_tile(query_index, unused):
        query_spot = tile_at(query_index)
        top[...] = jnp.full(top.shape, -3e38, jnp.float32)
        acc[...] = jnp.zeros(acc.shape, jnp.float32)

        def key_tile(key_index, carried):
            @pl.when(alive[query_index * tiles + key_index] == 1)
            def _():
                key_spot = tile_at(key_index)
                slot = jnp.clip(key_index - query_index, -2, 2) + 2
                keys = key_side[key_spot, :]
                for head in range(2):
                    scores = dot32(keys, query_side[head, :, query_spot]) + bias[head, slot]
                    before = top[head : head + 1, :]
                    now = jnp.maximum(before, jnp.max(scores, axis=0, keepdims=True))
                    weights = jnp.exp(scores - now).astype(jnp.bfloat16)
                    top[head : head + 1, :] = now
                    acc[head] = acc[head] * jnp.exp(before - now) + dot32(
                        value_t[head, :, key_spot], weights
                    )

            return carried

        lax.fori_loop(0, tiles, key_tile, 0)
        parts = []
        for head in range(2):
            total = acc[head, HEAD : HEAD + 1, :]
            part = acc[head, :HEAD, :] / total
            out_t[HEAD * head : HEAD * (head + 1), query_spot] = part
            log_sum[head : head + 1, query_spot] = top[head : head + 1, :] + jnp.log(total)
            parts.append(part)
        out[query_spot, :] = jnp.transpose(jnp.concatenate(parts, axis=0)).astype(jnp.bfloat16)
        return unused

    lax.fori_loop(0, tiles, query_tile, 0)


def attention_backward(
    alive,
    packed,
    segment,
    line,
    grads,
    out_t,
    log_sum,
    packed_grad,
    bias_grad,
    key_side,
    value_side,
    query_side,
    grad_side,
    key_t,
    query_pair,
    grad_pair,
    bias,
    bias_acc,
    query_acc,
    key_acc,
    value_acc,
):
    length = packed.shape[0]
    tiles = length // TILE
    fill_bias(line, bias)
    bias_acc[...] = jnp.zeros(bias_acc.shape, jnp.float32)

    def prepare(index, unused):
        spot = tile_at(index)
        seg = segment[0:1, spot]
        block = packed[spot, :].astype(jnp.float32)
        grad = grads[spot, :].astype(jnp.float32)
        seats = jnp.transpose(place_mask(seg)).astype(jnp.bfloat16)
        key_side[spot, :128] = packed[spot, 128:256]
        key_side[spot, 128:] = seats
        value_side[spot, :128] = packed[spot, 256:]
        value_side[spot, 128:] = seats
        key_t[:, spot] = jnp.transpose(block[:, 128:256]).astype(jnp.bfloat16)
        query_t = jnp.transpose(block[:, :128]) * 0.125
        grad_t = jnp.transpose(grad)
        half = lax.broadcasted_iota(jnp.int32, (128, TILE), 0) // HEAD
        side = lax.broadcasted_iota(jnp.int32, (TILE, 128), 1) // HEAD
        products = grad_t * out_t[:, spot]
        query_acc[:, spot] = jnp.zeros((128, TILE), jnp.float32)
        for head in range(2):
            query_side[head, :128, spot] = jnp.where(half == head, query_t, 0.0).astype(
                jnp.bfloat16
            )
            query_side[head, 128:, spot] = seat_rows(seg, -log_sum[head : head + 1, spot])
            delta = jnp.sum(products[HEAD * head : HEAD * (head + 1)], axis=0, keepdims=True)
            grad_side[head, :128, spot] = jnp.where(half == head, grad_t, 0.0).astype(jnp.bfloat16)
            grad_side[head, 128:, spot] = seat_rows(jnp.full_like(seg, -1.0), -delta)
            query_pair[index, TILE * head : TILE * (head + 1), :] = jnp.where(
                side == head, block[:, :128] * 0.125, 0.0
            ).astype(jnp.bfloat16)
            grad_pair[index, TILE * head : TILE * (head + 1), :] = jnp.where(
                side == head, grad, 0.0
            ).astype(jnp.bfloat16)
        return unused

    lax.fori_loop(0, tiles, prepare, 0)

    def key_tile(key_index, unused):
        key_spot = tile_at(key_index)
        key_acc[...] = jnp.zeros(key_acc.shape, jnp.float32)
        value_acc[...] = jnp.zeros(value_acc.shape, jnp.float32)

        def query_tile(query_index, carried):
            @pl.when(alive[query_index * tiles + key_index] == 1)
            def _():
                query_spot = tile_at(query_index)
                slot = jnp.clip(key_index - query_index, -2, 2) + 2
                keys = key_side[key_spot, :]
                values = value_side[key_spot, :]
                probs, score_grads = [], []
                for head in range(2):
                    scores = dot32(keys, query_side[head, :, query_spot]) + bias[head, slot]
                    prob = jnp.exp(scores)
                    score_grad = prob * dot32(values, grad_side[head, :, query_spot])
                    bias_acc[head, slot] += score_grad
                    score_grad = score_grad.astype(jnp.bfloat16)
                    probs.append(prob.astype(jnp.bfloat16))
                    score_grads.append(score_grad)
                    rows = slice(HEAD * head, HEAD * (head + 1))
                    query_acc[rows, query_spot] += dot32(key_t[rows, key_spot], score_grad)
                value_acc[...] += dot32(jnp.concatenate(probs, axis=1), grad_pair[query_index])
                key_acc[...] += dot32(jnp.concatenate(score_grads, axis=1), query_pair[query_index])

            return carried

        lax.fori_loop(0, tiles, query_tile, 0)
        packed_grad[key_spot, 128:256] = key_acc[...].astype(jnp.bfloat16)
        packed_grad[key_spot, 256:] = value_acc[...].astype(jnp.bfloat16)
        return unused

    lax.fori_loop(0, tiles, key_tile, 0)

    def finish(index, unused):
        spot = tile_at(index)
        packed_grad[spot, :128] = (jnp.transpose(query_acc[:, spot]) * 0.125).astype(jnp.bfloat16)
        return unused

    lax.fori_loop(0, tiles, finish, 0)
    rows = lax.broadcasted_iota(jnp.int32, (TILE, TILE), 0)
    columns = lax.broadcasted_iota(jnp.int32, (TILE, TILE), 1)
    flip = jnp.where(rows + columns == TILE - 1, 1.0, 0.0)
    bias_grad[...] = jnp.zeros(bias_grad.shape, jnp.float32)
    for head in range(2):
        spread = jnp.concatenate(
            [
                bias_acc[head, 2],
                bias_acc[head, 1],
                jnp.zeros((TILE, TILE), jnp.float32),
                bias_acc[head, 3],
            ],
            axis=1,
        )
        flipped = jnp.dot(
            flip, spread, precision=lax.Precision.HIGHEST, preferred_element_type=jnp.float32
        )
        turned = pltpu.roll(flipped, SPAN - TILE + 1, axis=1, stride=1, stride_axis=0)
        bias_grad[head : head + 1, :] = jnp.sum(turned, axis=0, keepdims=True)
        bias_grad[2 + head : 3 + head, :TILE] = jnp.sum(bias_acc[head, 0], axis=0, keepdims=True)
        bias_grad[4 + head : 5 + head, :TILE] = jnp.sum(bias_acc[head, 4], axis=0, keepdims=True)


def in_hbm(count):
    return [pl.BlockSpec(memory_space=pl.ANY)] * count


def estimate(micros):
    return pl.CostEstimate(flops=int(micros * 1e9), bytes_accessed=0, transcendentals=0)


def in_vmem(count):
    return [pl.BlockSpec(memory_space=pltpu.VMEM)] * count


def run_forward(alive, packed, segment, line):
    length = packed.shape[0]
    return pl.pallas_call(
        attention_forward,
        out_shape=(
            jax.ShapeDtypeStruct((length, 128), jnp.bfloat16),
            jax.ShapeDtypeStruct((128, length), jnp.float32),
            jax.ShapeDtypeStruct((8, length), jnp.float32),
        ),
        in_specs=[pl.BlockSpec(memory_space=pltpu.SMEM)] + in_vmem(3),
        out_specs=tuple(in_vmem(3)),
        scratch_shapes=[
            pltpu.VMEM((length, 256), jnp.bfloat16),
            pltpu.VMEM((2, 256, length), jnp.bfloat16),
            pltpu.VMEM((2, HEAD + 16, length), jnp.bfloat16),
            pltpu.VMEM((2, 5, TILE, TILE), jnp.float32),
            pltpu.VMEM((8, TILE), jnp.float32),
            pltpu.VMEM((2, HEAD + 16, TILE), jnp.float32),
        ],
        compiler_params=pltpu.CompilerParams(vmem_limit_bytes=67043328),
        cost_estimate=estimate(20),
        name="attention_forward",
    )(alive, packed, segment, line)


def run_backward(alive, packed, segment, line, grads, out_t, log_sum):
    length = packed.shape[0]
    tiles = length // TILE
    return pl.pallas_call(
        attention_backward,
        out_shape=(
            jax.ShapeDtypeStruct((length, 384), jnp.bfloat16),
            jax.ShapeDtypeStruct((8, SPAN), jnp.float32),
        ),
        in_specs=[pl.BlockSpec(memory_space=pltpu.SMEM)] + in_vmem(6),
        out_specs=tuple(in_vmem(2)),
        scratch_shapes=[
            pltpu.VMEM((length, 256), jnp.bfloat16),
            pltpu.VMEM((length, 256), jnp.bfloat16),
            pltpu.VMEM((2, 256, length), jnp.bfloat16),
            pltpu.VMEM((2, 256, length), jnp.bfloat16),
            pltpu.VMEM((128, length), jnp.bfloat16),
            pltpu.VMEM((tiles, 2 * TILE, 128), jnp.bfloat16),
            pltpu.VMEM((tiles, 2 * TILE, 128), jnp.bfloat16),
            pltpu.VMEM((2, 5, TILE, TILE), jnp.float32),
            pltpu.VMEM((2, 5, TILE, TILE), jnp.float32),
            pltpu.VMEM((128, length), jnp.float32),
            pltpu.VMEM((TILE, 128), jnp.float32),
            pltpu.VMEM((TILE, 128), jnp.float32),
        ],
        compiler_params=pltpu.CompilerParams(vmem_limit_bytes=67043328),
        cost_estimate=estimate(4),
        name="attention_backward",
    )(alive, packed, segment, line, grads, out_t, log_sum)


def signed_span():
    places = jnp.arange(SPAN, dtype=jnp.int32)
    return jnp.where(places < SPAN // 2, -places, SPAN - places)


def span_buckets():
    return (bucket_ids(signed_span())[:, None] == jnp.arange(NBUCK)[None, :]).astype(jnp.float32)


def live_tiles(segments, live):
    tiles = segments.shape[0] // TILE
    grouped = segments.reshape(tiles, TILE)
    first, last = grouped[:, 0], grouped[:, -1]
    meets = (first[:, None] <= last[None, :]) & (first[None, :] <= last[:, None])
    spread = jnp.repeat(jnp.repeat(live, ATT_BLK // TILE, axis=0), ATT_BLK // TILE, axis=1)
    return (meets & (spread == 1)).astype(jnp.int32).reshape(-1)


MESH = pl.DeviceIdType.MESH
LANES = 128
CUTS = 2
HALVES = 4


def places():
    own, ctx, side = lax.axis_index("shard"), lax.axis_index("ctx"), lax.axis_index("tensor")
    return own, ctx, side, ctx // 2, ctx % 2


def nearest(own, count, step):
    flip = own // (count // 2)
    place = flip * (count - 1 - own) + (1 - flip) * own
    turn = step - 1
    turn = turn + (turn - place + count) // count
    other = flip * (count - 1 - turn) + (1 - flip) * turn
    first = 1 - (step + count - 1) // count
    return first * own + (1 - first) * other


def partner(own, turn):
    return (own // 2 + turn // 2) % 2 * 2 + (own + turn) % 2


def across(chip, core, step):
    return (chip + 1 - step // 2) % 2 * 2 + (core + step + step // 2) % 2


def remote(source, target, send, recv, device):
    return pltpu.make_async_remote_copy(
        source, target, send, recv, device_id=device, device_id_type=MESH
    )


def greet(devices):
    barrier = pltpu.get_barrier_semaphore()
    for device in devices:
        pl.semaphore_signal(barrier, 1, device_id=device, device_id_type=MESH)
    pl.semaphore_wait(barrier, len(devices))


def gelu_parts(value):
    root = math.sqrt(2.0 / math.pi)
    square = value * value
    bend = jnp.tanh(root * value * (1.0 + 0.044715 * square))
    half = 0.5 * (1.0 + bend)
    slope = half + 0.5 * value * (1.0 - bend * bend) * (root * (1.0 + 0.134145 * square))
    return value * half, slope


def dot_last(left, right):
    return lax.dot_general(
        left, right, (((1,), (1,)), ((), ())), preferred_element_type=jnp.float32
    )


def expert_exchange(
    count,
    norm,
    gates,
    code_rows,
    code_cols,
    upstream_hbm,
    gate_own,
    gate_chip,
    gate_core,
    gate_far,
    up_own,
    up_chip,
    up_core,
    up_far,
    down_own,
    down_chip,
    down_core,
    down_far,
    row_grad,
    dot_rows,
    own_hbm,
    out_first,
    out_one,
    out_near,
    out_two,
    out_three,
    out_last,
    kept_hbm,
    gate_given,
    pair_given,
    upstream,
    gate_w,
    up_w,
    down_w,
    rows,
    sent,
    gates_in,
    gates_out,
    slot_grad,
    inner,
    gate_grad,
    up_grad,
    outs,
    partial,
    peer_part,
    summed,
    back,
    dots_out,
    dots_in,
    final_out,
    final_in,
    final_dots,
    core_in,
    chip_in,
    load_sem,
    store_sem,
    rows_send,
    rows_recv,
    pass_send,
    pass_recv,
    gates_send,
    gates_recv,
    part_send,
    part_recv,
    back_send,
    back_recv,
    dots_send,
    dots_recv,
    final_send,
    final_recv,
    core_send,
    core_recv,
    chip_send,
    chip_recv,
):
    own = lax.axis_index("shard")
    ctx = lax.axis_index("ctx")
    side = lax.axis_index("tensor")
    tokens, width = norm.shape
    room = upstream.shape[1]
    half = room // 2
    hidden = gate_w.shape[1]
    peer = (own, ctx, 1 - side)

    def source(step):
        return partner(own, step)

    barrier = pltpu.get_barrier_semaphore()
    for step in range(1, count):
        pl.semaphore_signal(barrier, 1, device_id=(source(step), ctx, side), device_id_type=MESH)
    chip, core = ctx // 2, ctx % 2
    core_peer = (own, chip * 2 + 1 - core, side)
    chip_peer = (own, (1 - chip) * 2 + core, side)
    for device in (peer, core_peer, chip_peer):
        pl.semaphore_signal(barrier, 1, device_id=device, device_id_type=MESH)
    deep = gate_own.shape[0]
    origins = (ctx, (1 - chip) * 2 + core, chip * 2 + 1 - core, (1 - chip) * 2 + 1 - core)
    pieces_of = (
        (gate_w, (gate_own, gate_chip, gate_core, gate_far)),
        (up_w, (up_own, up_chip, up_core, up_far)),
        (down_w, (down_own, down_chip, down_core, down_far)),
    )
    loads = []
    for number, (target, sources) in enumerate(pieces_of):
        for turn, source_ref in enumerate(sources):
            spot = pl.ds(pl.multiple_of(origins[turn] * deep, deep), deep)
            sem = load_sem.at[4 * number + turn]
            loads.append(pltpu.make_async_copy(source_ref, target.at[spot], sem))
    loads.append(pltpu.make_async_copy(upstream_hbm, upstream, load_sem.at[12]))
    for load in loads:
        load.start()
    pl.semaphore_wait(barrier, count + 2)

    my_half = pl.ds(pl.multiple_of(side * half, half), half)
    peer_half = pl.ds(pl.multiple_of((1 - side) * half, half), half)
    cut = half // CUTS

    def lines(which, piece):
        return pl.ds(pl.multiple_of(which * half + piece * cut, cut), cut)


    def picked(expert, start, amount):
        slots = lax.broadcasted_iota(jnp.int32, (amount, tokens), 0) + expert * room + start
        slots = slots.astype(jnp.float32)
        hit = (code_rows[0:1, :] == slots) | (code_rows[1:2, :] == slots)
        return jnp.where(hit, 1.0, 0.0).astype(jnp.bfloat16)

    def slot_gates(expert):
        slots = lax.broadcasted_iota(jnp.int32, (tokens, room), 1) + expert * room
        slots = slots.astype(jnp.float32)
        held = jnp.where(code_cols[:, 0:1] == slots, gates[:, 0:1], 0.0)
        held = held + jnp.where(code_cols[:, 1:2] == slots, gates[:, 1:2], 0.0)
        return jnp.broadcast_to(jnp.sum(held, axis=0, keepdims=True), (8, room))

    def rows_copy(step, piece):
        target = source(step)
        return pltpu.make_async_remote_copy(
            sent.at[step - 1, lines(0, piece)],
            rows.at[own, lines(side, piece)],
            rows_send.at[step - 1, piece],
            rows_recv.at[own, piece],
            device_id=(target, ctx, side),
            device_id_type=MESH,
        )

    def gates_copy(step):
        return pltpu.make_async_remote_copy(
            gates_out.at[step - 1],
            gates_in.at[own],
            gates_send.at[step - 1],
            gates_recv.at[own],
            device_id=(source(step), ctx, side),
            device_id_type=MESH,
        )

    def send_rows(step, unused):
        target = source(step)
        sent[step - 1] = dot32(picked(target, side * half, half), norm[...]).astype(jnp.bfloat16)
        for piece in range(CUTS):
            rows_copy(step, piece).start()
        gates_out[step - 1] = slot_gates(target)
        gates_copy(step).start()
        return unused

    lax.fori_loop(1, count, send_rows, 0)
    rows[own] = dot32(picked(own, 0, room), norm[...]).astype(jnp.bfloat16)
    gates_in[own] = slot_gates(own)
    for load in loads:
        load.wait()

    def landed(buffer, send, recv, origin):
        return pltpu.make_async_remote_copy(
            buffer, buffer, send, recv, device_id=peer, device_id_type=MESH
        )

    def pass_copy(origin, piece):
        spot = rows.at[origin, lines(side, piece)]
        return remote(spot, spot, pass_send.at[origin, piece], pass_recv.at[origin, piece], peer)

    def part_copy(step, piece):
        return remote(
            partial.at[step, lines(1 - side, piece)],
            peer_part.at[step, lines(0, piece)],
            part_send.at[step, piece],
            part_recv.at[step, piece],
            peer,
        )

    def back_copy(step, piece):
        return remote(
            summed.at[step, lines(0, piece)],
            back.at[own, lines(0, piece)],
            back_send.at[step, piece],
            back_recv.at[own, piece],
            (source(step), ctx, side),
        )

    def dots_copy(step):
        return pltpu.make_async_remote_copy(
            dots_out.at[step],
            dots_in.at[own],
            dots_send.at[step],
            dots_recv.at[own],
            device_id=(source(step), ctx, side),
            device_id_type=MESH,
        )

    def send_back(step):
        for piece in range(CUTS):
            part_copy(step, piece).wait_recv()
            summed[step, lines(0, piece), :] = (
                partial[step, lines(side, piece), :].astype(jnp.float32)
                + peer_part[step, lines(0, piece), :].astype(jnp.float32)
            ).astype(jnp.bfloat16)
            back_copy(step, piece).start()

    edge = (hidden // 256 + 1) // 2 * 256
    pieces = (slice(0, edge), slice(edge, hidden))

    def run_chunk(step, unused):
        origin = source(step)

        @pl.when(step > 0)
        def _():
            for piece in range(CUTS):
                spot = rows.at[origin, lines(1 - side, piece)]
                landed(spot, pass_send.at[0, 0], pass_recv.at[origin, piece], 0).wait_recv()
            landed(gates_in.at[origin], gates_send.at[0], gates_recv.at[origin], 0).wait_recv()

        gate_column = jnp.transpose(gates_in[origin])[:, 0:1]
        slot_grad[origin] = (upstream[origin].astype(jnp.float32) * gate_column).astype(
            jnp.bfloat16
        )

        def inside(piece):
            block = rows[origin]
            gate_pre = dot32(block, gate_w[:, piece])
            up_pre = dot32(block, up_w[:, piece])
            inner_grad = dot32(slot_grad[origin], down_w[:, piece])
            active, slope = gelu_parts(gate_pre)
            held = (active * up_pre).astype(jnp.bfloat16)
            inner[origin, :, piece] = held
            gate_grad[origin, :, piece] = (inner_grad * up_pre * slope).astype(jnp.bfloat16)
            up_grad[origin, :, piece] = (inner_grad * active).astype(jnp.bfloat16)
            return jnp.sum(active * up_pre * inner_grad, axis=1, keepdims=True)

        dots = inside(pieces[0])

        @pl.when(step < count - 1)
        def _():
            following = source(step + 1)
            for piece in range(CUTS):
                spot = rows.at[following, lines(side, piece)]
                landed(spot, rows_send.at[0, 0], rows_recv.at[following, piece], 0).wait_recv()
                pass_copy(following, piece).start()

        dots = dots + inside(pieces[1])
        dots_out[step] = jnp.transpose(jnp.broadcast_to(dots, (room, 128)))[0:8, :]

        @pl.when(step > 1)
        def _():
            send_back(step - 1)

        for spot in (peer_half, my_half):
            found = dot_last(gate_grad[origin, spot, :], gate_w[...])
            found = found + dot_last(up_grad[origin, spot, :], up_w[...])
            partial[step, spot, :] = found.astype(jnp.bfloat16)
            if spot is peer_half:

                @pl.when(step > 0)
                def _():
                    for piece in range(CUTS):
                        part_copy(step, piece).start()
                    dots_copy(step).start()

        return unused

    lax.fori_loop(0, count, run_chunk, 0)
    products = ((gate_w, rows, gate_grad), (up_w, rows, up_grad), (down_w, slot_grad, inner))

    def owner(turn):
        return turn % 2 * 2 + (core + 1 + turn // 2) % 2

    def to_core(number, turn):
        spot = pl.ds(pl.multiple_of(owner(turn) * deep, deep), deep)
        return pltpu.make_async_remote_copy(
            products[number][0].at[spot],
            core_in.at[number, turn],
            core_send.at[number, turn],
            core_recv.at[number, turn],
            device_id=core_peer,
            device_id_type=MESH,
        )

    def weigh(number):
        target, left, right = products[number]

        def block(turn, unused):
            spot = pl.ds(pl.multiple_of(owner(turn) * deep, deep), deep)
            lines = left[:, :, spot].reshape(count * room, deep)
            target[spot, :] = lax.dot_general(
                lines,
                right[...].reshape(count * room, hidden),
                (((0,), (0,)), ((), ())),
                preferred_element_type=jnp.float32,
            ).astype(jnp.bfloat16)

            @pl.when(turn < 2)
            def _():
                to_core(number, turn).start()

            return unused

        lax.fori_loop(0, 4, block, 0)

    def run_out(step, unused):
        outs[step] = dot_last(inner[step], down_w[...]).astype(jnp.bfloat16)
        return unused

    def to_chip(number):
        return remote(
            core_in.at[number, 1 - chip],
            chip_in.at[0],
            chip_send.at[number],
            chip_recv.at[number],
            chip_peer,
        )

    def over_chip(number):
        for turn in range(2):
            spot = pl.ds(pl.multiple_of(owner(turn + 2) * deep, deep), deep)
            to_core(number, turn).wait_recv()
            core_in[number, turn] = (
                products[number][0][spot, :].astype(jnp.float32)
                + core_in[number, turn].astype(jnp.float32)
            ).astype(jnp.bfloat16)
        if number == 0:
            to_chip(number).start()

    weigh(0)
    send_back(count - 1)
    lax.fori_loop(0, count, run_out, 0)
    moves = (
        (outs.at[own], own_hbm),
        (outs.at[partner(own, 1), pl.ds(0, half)], out_first),
        (outs.at[partner(own, 1), pl.ds(half, half)], out_one),
        (outs.at[partner(own, 2), pl.ds(0, half)], out_near),
        (outs.at[partner(own, 2), pl.ds(half, half)], out_two),
        (outs.at[partner(own, 3), pl.ds(0, half)], out_three),
        (outs.at[partner(own, 3), pl.ds(half, half)], out_last),
    )
    stores = []
    for number, (source_ref, target) in enumerate(moves):
        sem = store_sem.at[number if number == 0 else 10 + number]
        stores.append(pltpu.make_async_copy(source_ref, target, sem))
    for store in stores:
        store.start()
    weigh(1)
    over_chip(0)

    def dots_landed(step, unused):
        origin = source(step)
        landed(dots_in.at[origin], dots_send.at[0], dots_recv.at[origin], 0).wait_recv()
        return unused

    def back_landed(step, unused):
        origin = source(step)
        for piece in range(CUTS):
            spot = back.at[origin, lines(0, piece)]
            landed(spot, back_send.at[0, 0], back_recv.at[origin, piece], 0).wait_recv()
        return unused

    lax.fori_loop(1, count, dots_landed, 0)
    dots_in[own] = dots_out[0]
    final_dots[0] = jnp.zeros((8, tokens), jnp.float32)
    for expert in range(count):
        column = jnp.transpose(dots_in[expert])[:, 0:1]
        slots = lax.broadcasted_iota(jnp.int32, (room, tokens), 0) + expert * room
        slots = slots.astype(jnp.float32)
        for choice in range(2):
            final_dots[0, choice : choice + 1, :] += jnp.sum(
                jnp.where(code_rows[choice : choice + 1, :] == slots, column, 0.0),
                axis=0,
                keepdims=True,
            )
    lax.fori_loop(1, count, back_landed, 0)
    blocks = final_out.shape[0]
    span = tokens // blocks

    def final_copy(block):
        return pltpu.make_async_remote_copy(
            final_out.at[block],
            final_in.at[block],
            final_send.at[block],
            final_recv.at[block],
            device_id=peer,
            device_id_type=MESH,
        )

    dots_final = pltpu.make_async_remote_copy(
        final_dots.at[0],
        final_dots.at[1],
        final_send.at[blocks],
        final_recv.at[blocks],
        device_id=peer,
        device_id_type=MESH,
    )
    dots_final.start()

    def combine(block, unused):
        spot = pl.ds(pl.multiple_of(block * span, span), span)

        def chosen(start, amount):
            slots = lax.broadcasted_iota(jnp.int32, (span, amount), 1) + start
            slots = slots.astype(jnp.float32)
            hit = (code_cols[spot, 0:1] == slots) | (code_cols[spot, 1:2] == slots)
            return jnp.where(hit, 1.0, 0.0).astype(jnp.bfloat16)

        total = dot32(chosen(own * room, room), partial[0])
        for step in range(1, count):
            origin = source(step)
            total = total + dot32(chosen(origin * room + side * half, half), back[origin])
        final_out[block] = total.astype(jnp.bfloat16)
        final_copy(block).start()
        return unused

    lax.fori_loop(0, blocks, combine, 0)

    weigh(2)

    def finish(block, unused):
        spot = pl.ds(pl.multiple_of(block * span, span), span)
        final_copy(block).wait_recv()
        row_grad[spot, :] = final_out[block].astype(jnp.float32) + final_in[block].astype(
            jnp.float32
        )
        return unused

    lax.fori_loop(0, blocks, finish, 0)
    dots_final.wait_recv()
    dot_rows[...] = final_dots[0] + final_dots[1]
    to_chip(0).wait_recv()
    for number in range(3):
        if number:
            over_chip(number)
        given = core_in.at[number, 1 - chip] if number else chip_in.at[0]
        for place, source_ref in enumerate((core_in.at[number, chip], given)):
            target = (kept_hbm.at[number], pair_given.at[number - 1] if number else gate_given)[place]
            sem = store_sem.at[4 + 2 * number + place]
            store = pltpu.make_async_copy(source_ref, target, sem)
            store.start()
            stores.append(store)

    def drain(step, unused):
        for piece in range(CUTS):
            rows_copy(step, piece).wait_send()
            pass_copy(source(step), piece).wait_send()
            part_copy(step, piece).wait_send()
            back_copy(step, piece).wait_send()
        gates_copy(step).wait_send()
        dots_copy(step).wait_send()
        return unused

    lax.fori_loop(1, count, drain, 0)

    def drain_final(block, unused):
        final_copy(block).wait_send()
        return unused

    lax.fori_loop(0, blocks, drain_final, 0)
    dots_final.wait_send()
    for number in range(3):
        for turn in range(2):
            to_core(number, turn).wait_send()
        if number == 0:
            to_chip(number).wait_send()
    for store in stores:
        store.wait()


def run_experts(count, ctx_size, norm, gates, code_rows, code_cols, upstream, weights):
    tokens, width = norm.shape
    room = upstream.shape[1]
    half = room // 2
    hidden = weights[0].shape[1]
    blocks = 4
    low = jnp.bfloat16
    full = jnp.float32
    dma = pltpu.SemaphoreType.DMA
    return pl.pallas_call(
        partial(expert_exchange, count),
        out_shape=(
            jax.ShapeDtypeStruct((tokens, width), full),
            jax.ShapeDtypeStruct((8, tokens), full),
            jax.ShapeDtypeStruct((room, width), low),
            *[jax.ShapeDtypeStruct((half, width), low)] * 6,
            jax.ShapeDtypeStruct((3, width // ctx_size, hidden), low),
            jax.ShapeDtypeStruct((width // ctx_size, hidden), low),
            jax.ShapeDtypeStruct((2, width // ctx_size, hidden), low),
        ),
        in_specs=in_vmem(4) + [pl.BlockSpec(memory_space=pl.ANY)] * 13,
        out_specs=tuple(in_vmem(2) + [pl.BlockSpec(memory_space=pl.ANY)] * 10),
        scratch_shapes=[
            pltpu.VMEM(upstream.shape, low),
            pltpu.VMEM((width, hidden), low),
            pltpu.VMEM((width, hidden), low),
            pltpu.VMEM((width, hidden), low),
            pltpu.VMEM((count, room, width), low),
            pltpu.VMEM((count - 1, half, width), low),
            pltpu.VMEM((count, 8, room), full),
            pltpu.VMEM((count - 1, 8, room), full),
            pltpu.VMEM((count, room, width), low),
            pltpu.VMEM((count, room, hidden), low),
            pltpu.VMEM((count, room, hidden), low),
            pltpu.VMEM((count, room, hidden), low),
            pltpu.VMEM((count, room, width), low),
            pltpu.VMEM((count, room, width), low),
            pltpu.VMEM((count, half, width), low),
            pltpu.VMEM((count, half, width), low),
            pltpu.VMEM((count, half, width), low),
            pltpu.VMEM((count, 8, room), full),
            pltpu.VMEM((count, 8, room), full),
            pltpu.VMEM((blocks, tokens // blocks, width), low),
            pltpu.VMEM((blocks, tokens // blocks, width), low),
            pltpu.VMEM((2, 8, tokens), full),
            pltpu.VMEM((3, 2, width // ctx_size, hidden), low),
            pltpu.VMEM((1, width // ctx_size, hidden), low),
            dma((13,)),
            dma((18,)),
            dma((count, CUTS)),
            dma((count, CUTS)),
            dma((count, CUTS)),
            dma((count, CUTS)),
            dma((count,)),
            dma((count,)),
            dma((count, CUTS)),
            dma((count, CUTS)),
            dma((count, CUTS)),
            dma((count, CUTS)),
            dma((count,)),
            dma((count,)),
            dma((blocks + 1,)),
            dma((blocks + 1,)),
            dma((3, 2)),
            dma((3, 2)),
            dma((3,)),
            dma((3,)),
        ],
        cost_estimate=estimate(110),
        compiler_params=pltpu.CompilerParams(
            collective_id=3, has_side_effects=True, vmem_limit_bytes=67043328
        ),
        name="expert_exchange",
    )(norm, gates, code_rows, code_cols, upstream, *weights)


def begin(pairs, sems):
    copies = [
        pltpu.make_async_copy(source, target, sems.at[number])
        for number, (source, target) in enumerate(pairs)
    ]
    for copy in copies:
        copy.start()
    return copies


def gather_project(
    count,
    w_query,
    w_key,
    w_value,
    w_out,
    first_gain,
    second_gain,
    router,
    tokens,
    segment_ids,
    cotangent,
    routes,
    live,
    rel_bias,
    gate_hbm,
    up_hbm,
    down_hbm,
    full_hbm,
    packed,
    norm_hbm,
    segments,
    out_hbm,
    upstream_hbm,
    gate_hbm_low,
    up_hbm_low,
    down_hbm_low,
    gate_core,
    up_core,
    down_core,
    gate_chip,
    gate_far,
    codes,
    code_rows,
    extras,
    alive,
    bias_line,
    full,
    norm,
    out_full,
    upstream,
    gate_low,
    up_low,
    down_low,
    weight,
    out_weight,
    segment,
    outgoing,
    sent,
    experts_wide,
    line_send,
    line_recv,
    chip_send,
    chip_recv,
    core_send,
    core_recv,
    packed_send,
    packed_recv,
    segment_send,
    segment_recv,
    out_line_send,
    out_line_recv,
    out_chip_send,
    out_chip_recv,
    out_core_send,
    out_core_recv,
    out_pair_send,
    out_pair_recv,
    rows_send,
    rows_recv,
    pass_send,
    pass_recv,
    expert_send,
    expert_recv,
    load_sem,
    store_sem,
):
    own, ctx, side, chip, core = places()
    rows = weight.shape[0]
    ctx_size, here, share = packed.shape
    room = upstream.shape[1]
    half = room // 2
    chip_peer = (own, (1 - chip) * 2 + core, side)
    core_peer = (own, chip * 2 + 1 - core, side)
    pair = (own, ctx, 1 - side)
    loads = [
        pltpu.make_async_copy(source, experts_wide.at[number], load_sem.at[number])
        for number, source in enumerate((gate_hbm, up_hbm, down_hbm))
    ]
    for load in loads:
        load.start()
    stores = []

    def store(source, target):
        copy = pltpu.make_async_copy(source, target, store_sem.at[len(stores)])
        copy.start()
        stores.append(copy)

    experts = router.shape[0]
    extra = jnp.concatenate(
        [first_gain[...], second_gain[...], router[...], jnp.zeros((6 - experts, rows))], axis=0
    )
    weight[:, ctx_size * share :] = jnp.zeros((rows, LANES), jnp.bfloat16)
    extra_columns = slice(ctx_size * share, ctx_size * share + 8)
    weight[:, extra_columns] = jnp.transpose(extra).astype(jnp.bfloat16)
    for place in range(ctx_size):
        for number, member in enumerate((w_query, w_key, w_value)):
            target = slice(place * share + number * LANES, place * share + (number + 1) * LANES)
            found = member[:, place * LANES : (place + 1) * LANES]
            weight[:, target] = found.astype(jnp.bfloat16)
    out_weight[...] = w_out[...].astype(jnp.bfloat16)
    segment[...] = jnp.broadcast_to(segment_ids[...].astype(jnp.float32), segment.shape)
    greet(
        [(nearest(own, count, step), ctx, side) for step in range(1, count)]
        + [(own, across(chip, core, step), side) for step in range(3)]
        + [pair]
    )

    def block(shard, place):
        return pl.ds(pl.multiple_of((shard * ctx_size + place) * rows, rows), rows)

    def along(origin, forward):
        turn = 2 * forward - 1
        target = own + turn
        there = (target + count) // count * (1 - target // count)
        return (target + count) % count, there

    def onward(origin):
        return 1 - (origin - own + count) // count

    def to_line(origin, forward, source, number):
        target, _ = along(origin, forward)
        spot = full.at[block(origin, ctx)]
        return remote(
            source, spot, line_send.at[number], line_recv.at[origin], (target, ctx, side)
        )

    def in_line(copy_of, origin, forward, source, number, act):
        _, there = along(origin, forward)

        @pl.when(there == 1)
        def _():
            act(copy_of(origin, forward, source, number))

    def to_chip(shard, source):
        target = full.at[block(shard, ctx)]
        return remote(source, target, chip_send.at[shard], chip_recv.at[shard], chip_peer)

    def to_core(shard, place, source):
        index = shard * 2 + place // 2
        target = full.at[block(shard, place)]
        return remote(source, target, core_send.at[index], core_recv.at[index], core_peer)

    def to_segment(step):
        device = (own, across(chip, core, step), side)
        return remote(segment, segments.at[ctx], segment_send.at[step], segment_recv.at[ctx], device)

    def out_to_line(origin, forward, source, number):
        target, _ = along(origin, forward)
        spot = out_full.at[side, block(origin, ctx)]
        return remote(
            source, spot, out_line_send.at[number], out_line_recv.at[origin], (target, ctx, side)
        )

    def start(copy):
        copy.start()

    def sent_off(copy):
        copy.wait_send()

    def out_to_chip(shard, source):
        target = out_full.at[side, block(shard, ctx)]
        return remote(source, target, out_chip_send.at[shard], out_chip_recv.at[shard], chip_peer)

    def out_to_core(which, shard, place, source):
        index = shard * 2 + place // 2
        target = out_full.at[which, block(shard, place)]
        return remote(
            source, target, out_core_send.at[which, index], out_core_recv.at[which, index], core_peer
        )

    def out_to_pair(shard, place, source):
        index = shard * 2 + place // 2
        target = out_full.at[side, block(shard, place)]
        return remote(source, target, out_pair_send.at[index], out_pair_recv.at[index], pair)

    for forward in range(2):
        in_line(to_line, own, forward, weight, forward, start)
    to_chip(own, weight).start()
    to_core(own, ctx, weight).start()
    for step in range(3):
        to_segment(step).start()
    for forward in range(2):
        in_line(out_to_line, own, forward, out_weight, forward, start)
    out_to_core(side, own, ctx, out_weight).start()
    out_to_pair(own, ctx, out_weight).start()
    full[block(own, ctx), :] = weight[...]
    out_full[side, block(own, ctx), :] = out_weight[...]
    segments[ctx] = segment[...]

    index = lax.broadcasted_iota(jnp.int32, (NBUCK, SPAN), 1)
    relative = jnp.where(index < SPAN // 2, -index, SPAN - index)
    bucket = lax.broadcasted_iota(jnp.int32, (NBUCK, SPAN), 0)
    onehot = jnp.where(bucket_ids(relative) == bucket, 1.0, 0.0)
    found = jnp.dot(
        rel_bias[...], onehot, precision=lax.Precision.HIGHEST, preferred_element_type=jnp.float32
    )
    head = lax.broadcasted_iota(jnp.int32, found.shape, 0)
    for number in range(2):
        chosen = jnp.where(head == 2 * ctx + number, found, 0.0)
        bias_line[number : number + 1, :] = jnp.sum(chosen, axis=0, keepdims=True)
    lane = lax.broadcasted_iota(jnp.int32, (here, LANES), 1).astype(jnp.float32)
    named = jnp.concatenate([routes[...].astype(jnp.float32), jnp.zeros((6, here))], axis=0)
    columns = jnp.transpose(named)
    first, second = columns[:, 0:1], columns[:, 1:2]
    codes[:, 2:3] = first
    codes[:, 3:4] = second
    named = jnp.where((first == lane) | (second == lane), 1.0, 0.0).astype(jnp.bfloat16)
    later = lax.broadcasted_iota(jnp.int32, (here, here), 0)
    before = later > lax.broadcasted_iota(jnp.int32, (here, here), 1)
    slots = dot32(jnp.where(before, 1.0, 0.0).astype(jnp.bfloat16), named) + room * lane
    first = jnp.sum(jnp.where(first == lane, slots, 0.0), axis=1, keepdims=True)
    second = jnp.sum(jnp.where(second == lane, slots, 0.0), axis=1, keepdims=True)
    codes[:, 0:1] = first
    codes[:, 1:2] = second
    both = jnp.where(lane == 0.0, first, jnp.where(lane == 1.0, second, -1.0))
    code_rows[...] = jnp.transpose(both)[0:8]
    my_half = pl.ds(pl.multiple_of(side * half, half), half)
    peer_half = pl.ds(pl.multiple_of((1 - side) * half, half), half)

    def picked(expert, start, amount):
        slots = lax.broadcasted_iota(jnp.int32, (amount, here), 0) + expert * room + start
        slots = slots.astype(jnp.float32)
        hit = (code_rows[0:1, :] == slots) | (code_rows[1:2, :] == slots)
        rows_found = jnp.where(hit, 1.0, 0.0).astype(jnp.bfloat16)
        return dot32(rows_found, cotangent[...]).astype(jnp.bfloat16)

    cut = half // CUTS

    def lines(which, piece):
        return pl.ds(pl.multiple_of(which * half + piece * cut, cut), cut)

    def to_expert(step, piece):
        return remote(
            sent.at[step - 1, lines(0, piece)],
            upstream.at[own, lines(side, piece)],
            rows_send.at[step - 1, piece],
            rows_recv.at[own, piece],
            (nearest(own, count, step), ctx, side),
        )

    def pass_rows(shard, piece):
        spot = lines(side, piece)
        source, target = upstream.at[shard, spot], upstream_hbm.at[shard, spot]
        return remote(source, target, pass_send.at[shard, piece], pass_recv.at[shard, piece], pair)

    lows = (gate_low, up_low, down_low)
    near = (gate_core, up_core, down_core)
    for number, load in enumerate(loads):
        load.wait()
        lows[number][...] = experts_wide[number].astype(jnp.bfloat16)
        store(lows[number], (gate_hbm_low, up_hbm_low, down_hbm_low)[number])
    for step in range(1, count):
        sent[step - 1] = picked(nearest(own, count, step), side * half, half)
    upstream[own] = picked(own, 0, room)
    store(upstream.at[own], upstream_hbm.at[own])

    def to_near(number):
        return remote(
            lows[number], near[number], expert_send.at[number], expert_recv.at[number], core_peer
        )

    gate_over = remote(gate_low, gate_chip, expert_send.at[3], expert_recv.at[3], chip_peer)
    gate_far_copy = remote(gate_chip, gate_far, expert_send.at[4], expert_recv.at[4], core_peer)

    other_place = (1 - chip) * 2 + core

    def pass_line(step):
        shard = nearest(own, count, step)
        source = full.at[block(shard, ctx)]
        remote(source, source, line_send.at[0], line_recv.at[shard], core_peer).wait_recv()
        in_line(to_line, shard, onward(shard), source, 1 + step, start)
        to_chip(shard, source).start()
        to_core(shard, ctx, source).start()

    def pass_chip(step):
        shard = nearest(own, count, step)
        source = full.at[block(shard, other_place)]
        remote(source, source, chip_send.at[0], chip_recv.at[shard], core_peer).wait_recv()
        to_core(shard, other_place, source).start()

    pass_chip(0)
    for step in range(1, count):
        pass_line(step)
        pass_chip(step)
    out_to_chip(own, out_weight).start()
    for step in range(1, count):
        shard = nearest(own, count, step)
        source = out_full.at[side, block(shard, ctx)]
        remote(source, source, line_send.at[0], out_line_recv.at[shard], core_peer).wait_recv()
        in_line(out_to_line, shard, onward(shard), source, 1 + step, start)
        out_to_chip(shard, source).start()
        out_to_core(side, shard, ctx, source).start()
        out_to_pair(shard, ctx, source).start()

    for step in range(1, count):
        for piece in range(CUTS):
            to_expert(step, piece).start()
    gate_over.start()
    values = tokens[...].astype(jnp.float32)
    scale = lax.rsqrt(jnp.mean(values * values, axis=1, keepdims=True) + 1e-06)
    for shard in range(count):
        for place in range(2):
            spot = full.at[block(shard, place * 2 + 1 - core)]
            index = shard * 2 + place
            remote(spot, spot, core_send.at[0], core_recv.at[index], core_peer).wait_recv()
    store(full, full_hbm)
    extras[...] = full[:, ctx_size * share :]
    gain = jnp.transpose(extras[...].astype(jnp.float32))[0:1, :]
    norm[...] = (values * scale * gain).astype(jnp.bfloat16)
    store(norm, norm_hbm)

    def project(place):
        spot = pl.ds(pl.multiple_of(place * share, LANES), share)
        return dot32(norm[...], full[:, spot]).astype(jnp.bfloat16)

    def to_packed(step):
        device = (own, across(chip, core, step), side)
        return remote(
            outgoing.at[step], packed.at[ctx], packed_send.at[step], packed_recv.at[ctx], device
        )

    for step in range(3):
        outgoing[step] = project(across(chip, core, step))
        to_packed(step).start()
    packed[ctx] = project(ctx)
    for number in range(3):
        to_near(number).start()
    for step in range(count):
        shard = nearest(own, count, step)
        source = out_full.at[side, block(shard, other_place)]
        remote(source, source, line_send.at[0], out_chip_recv.at[shard], core_peer).wait_recv()
        out_to_core(side, shard, other_place, source).start()
        out_to_pair(shard, other_place, source).start()
    for step in range(1, count):
        shard = nearest(own, count, step)
        for piece in range(CUTS):
            spot = upstream.at[shard, lines(side, piece)]
            remote(spot, spot, line_send.at[0], rows_recv.at[shard, piece], pair).wait_recv()
            pass_rows(shard, piece).start()
        store(upstream.at[shard, my_half], upstream_hbm.at[shard, my_half])
    gate_over.wait_recv()
    gate_far_copy.start()
    for step in range(count):
        shard = nearest(own, count, step)
        for place in (core, 2 + core):
            index = shard * 2 + place // 2
            source = out_full.at[1 - side, block(shard, place)]
            remote(source, source, line_send.at[0], out_pair_recv.at[index], pair).wait_recv()
            out_to_core(1 - side, shard, place, source).start()
    for step in range(3):
        place = across(chip, core, step)
        spot = packed.at[place]
        remote(spot, spot, packed_send.at[step], packed_recv.at[place], core_peer).wait_recv()
        spot = segments.at[place]
        remote(spot, spot, segment_send.at[step], segment_recv.at[place], core_peer).wait_recv()
    for which in (side, 1 - side):
        for shard in range(count):
            for place in range(2):
                spot = out_full.at[which, block(shard, place * 2 + 1 - core)]
                index = shard * 2 + place
                remote(
                    spot, spot, line_send.at[0], out_core_recv.at[which, index], core_peer
                ).wait_recv()
        store(out_full.at[which], out_hbm.at[which])
    for step in range(1, count):
        shard = nearest(own, count, step)
        for piece in range(CUTS):
            spot = upstream_hbm.at[shard, lines(1 - side, piece)]
            remote(spot, spot, line_send.at[0], pass_recv.at[shard, piece], pair).wait_recv()

    shape = alive.shape
    query = lax.broadcasted_iota(jnp.int32, shape, 0)
    keys = lax.broadcasted_iota(jnp.int32, shape, 1)
    ends = [jnp.zeros(shape, jnp.float32)] * 4
    for tile in range(shape[0]):
        place, start = tile * TILE // here, tile * TILE % here
        first = segments[place, 0:1, start : start + 1]
        last = segments[place, 0:1, start + TILE - 1 : start + TILE]
        for number, (which, value) in enumerate(
            ((query, first), (query, last), (keys, first), (keys, last))
        ):
            ends[number] = jnp.where(which == tile, value, ends[number])
    open_blocks = jnp.zeros(shape, jnp.int32)
    ratio = ATT_BLK // TILE
    for row in range(live.shape[0]):
        for column in range(live.shape[1]):
            here_now = (query // ratio == row) & (keys // ratio == column)
            value = live[row : row + 1, column : column + 1]
            open_blocks = jnp.where(here_now, value, open_blocks)
    meets = (ends[0] <= ends[3]) & (ends[2] <= ends[1]) & (open_blocks == 1)
    alive[...] = jnp.where(meets, 1, 0)
    for copy in stores:
        copy.wait()
    for step in range(3):
        to_packed(step).wait_send()
        to_segment(step).wait_send()
        to_near(step).wait()
    gate_over.wait_send()
    gate_far_copy.wait()
    for forward in range(2):
        in_line(to_line, own, forward, weight, forward, sent_off)
        in_line(out_to_line, own, forward, out_weight, forward, sent_off)
    for step in range(count):
        shard = nearest(own, count, step)
        if step:
            in_line(to_line, shard, onward(shard), weight, 1 + step, sent_off)
            in_line(out_to_line, shard, onward(shard), out_weight, 1 + step, sent_off)
            for piece in range(CUTS):
                to_expert(step, piece).wait_send()
                pass_rows(shard, piece).wait_send()
        to_chip(shard, weight).wait_send()
        out_to_chip(shard, out_weight).wait_send()
        for place in (ctx, other_place):
            to_core(shard, place, weight).wait_send()
            out_to_pair(shard, place, out_weight).wait_send()
            out_to_core(side, shard, place, out_weight).wait_send()
            out_to_core(1 - side, shard, place, out_weight).wait_send()


def run_gather(count, ctx_size, room, members, experts):
    rows, head_columns = members[0].shape
    here, width = members[7].shape
    share = 3 * head_columns // ctx_size
    columns = ctx_size * share + LANES
    dma = pltpu.SemaphoreType.DMA
    low = jnp.bfloat16
    deep, hidden = experts[0].shape
    return pl.pallas_call(
        partial(gather_project, count),
        out_shape=(
            jax.ShapeDtypeStruct((rows * count * ctx_size, columns), low),
            jax.ShapeDtypeStruct((ctx_size, here, share), low),
            jax.ShapeDtypeStruct((here, width), low),
            jax.ShapeDtypeStruct((ctx_size, 8, here), jnp.float32),
            jax.ShapeDtypeStruct((2, rows * count * ctx_size, head_columns), low),
            jax.ShapeDtypeStruct((count, room, width), low),
            *[jax.ShapeDtypeStruct((deep, hidden), low)] * 8,
            jax.ShapeDtypeStruct((here, 4), jnp.float32),
            jax.ShapeDtypeStruct((8, here), jnp.float32),
            jax.ShapeDtypeStruct((rows * count * ctx_size, LANES), low),
            jax.ShapeDtypeStruct((ctx_size * here // TILE,) * 2, jnp.int32),
            jax.ShapeDtypeStruct((2, SPAN), jnp.float32),
        ),
        in_specs=in_vmem(13) + [pl.BlockSpec(memory_space=pl.ANY)] * 3,
        out_specs=tuple(
            pl.BlockSpec(memory_space=pltpu.VMEM if number in (1, 3, 14, 15, 16, 17, 18) else pl.ANY)
            for number in range(19)
        ),
        scratch_shapes=[
            pltpu.VMEM((rows * count * ctx_size, columns), low),
            pltpu.VMEM((here, width), low),
            pltpu.VMEM((2, rows * count * ctx_size, head_columns), low),
            pltpu.VMEM((count, room, width), low),
            pltpu.VMEM((deep, hidden), low),
            pltpu.VMEM((deep, hidden), low),
            pltpu.VMEM((deep, hidden), low),
            pltpu.VMEM((rows, columns), low),
            pltpu.VMEM((rows, head_columns), low),
            pltpu.VMEM((8, here), jnp.float32),
            pltpu.VMEM((3, here, share), low),
            pltpu.VMEM((count - 1, room // 2, width), low),
            pltpu.VMEM((3, deep, hidden), jnp.float32),
            dma((count + 1,)),
            dma((count,)),
            dma((count,)),
            dma((count,)),
            dma((2 * count,)),
            dma((2 * count,)),
            dma((3,)),
            dma((ctx_size,)),
            dma((3,)),
            dma((ctx_size,)),
            dma((count + 1,)),
            dma((count,)),
            dma((count,)),
            dma((count,)),
            dma((2, 2 * count)),
            dma((2, 2 * count)),
            dma((2 * count,)),
            dma((2 * count,)),
            dma((count, CUTS)),
            dma((count, CUTS)),
            dma((count, CUTS)),
            dma((count, CUTS)),
            dma((5,)),
            dma((5,)),
            dma((3,)),
            dma((12,)),
        ],
        compiler_params=pltpu.CompilerParams(
            collective_id=1, has_side_effects=True, vmem_limit_bytes=67043328
        ),
        cost_estimate=estimate(60),
        name="gather_project",
    )(*members, *experts)


def attend_out(
    attended,
    tokens_hbm,
    out_hbm,
    extras_hbm,
    codes,
    hidden_hbm,
    norm_hbm,
    gates,
    low_hbm,
    gathered,
    tokens,
    out_w,
    extras,
    hidden_one,
    norm_two,
    send,
    recv,
    load_sem,
    store_sem,
):
    own, ctx, side, chip, core = places()
    here, width = tokens.shape
    heads = attended.shape[2]
    peers = [
        (across(chip, core, step), (side + other) % 2)
        for other in range(2)
        for step in range(4)
        if (other, step) != (0, 3)
    ]
    peers = peers[:2] + peers[3:5] + peers[2:3] + peers[5:]
    columns = pl.ds(pl.multiple_of(ctx * heads, heads), heads)
    loads = begin(
        (
            (attended.at[ctx], gathered.at[side, :, columns]),
            (tokens_hbm, tokens),
            (out_hbm, out_w),
            (extras_hbm, extras),
        ),
        load_sem,
    )
    greet([(own, place, which) for place, which in peers])

    def copy(number):
        place, which = peers[number]
        return remote(
            attended.at[place],
            gathered.at[side, :, columns],
            send.at[number],
            recv.at[side, ctx],
            (own, place, which),
        )

    for number in range(len(peers)):
        copy(number).start()
    for load in loads:
        load.wait()
    for place, which in peers:
        spot = gathered.at[which, :, pl.ds(pl.multiple_of(place * heads, heads), heads)]
        remote(
            spot, spot, send.at[0], recv.at[which, place], (own, place, which)
        ).wait_recv()
    stores = begin(((gathered.at[side], low_hbm),), store_sem)
    hidden = tokens[...].astype(jnp.float32) + (
        dot_last(gathered[0], out_w[0]) + dot_last(gathered[1], out_w[1])
    )
    hidden_one[...] = hidden
    stores += begin(((hidden_one, hidden_hbm),), store_sem.at[pl.ds(1, 1)])
    scale = lax.rsqrt(jnp.mean(hidden * hidden, axis=1, keepdims=True) + 1e-06)
    gain = jnp.transpose(extras[...].astype(jnp.float32))[1:2, :]
    norm = (hidden * scale * gain).astype(jnp.bfloat16)
    norm_two[...] = norm
    stores += begin(((norm_two, norm_hbm),), store_sem.at[pl.ds(2, 1)])
    logits = dot32(norm, extras[...])
    lane = lax.broadcasted_iota(jnp.int32, (here, LANES), 1).astype(jnp.float32)
    first = jnp.sum(jnp.where(lane == codes[:, 2:3] + 2.0, logits, 0.0), axis=1, keepdims=True)
    second = jnp.sum(jnp.where(lane == codes[:, 3:4] + 2.0, logits, 0.0), axis=1, keepdims=True)
    highest = jnp.maximum(first, second)
    first, second = jnp.exp(first - highest), jnp.exp(second - highest)
    gates[:, 0:1] = first / (first + second)
    gates[:, 1:2] = second / (first + second)
    for number in range(len(peers)):
        copy(number).wait_send()
    for store in stores:
        store.wait()


def run_attend_out(attended, tokens, out_w, extras, codes):
    here, width = tokens.shape
    heads = out_w.shape[2]
    low, wide = jnp.bfloat16, jnp.float32
    return pl.pallas_call(
        attend_out,
        out_shape=(
            jax.ShapeDtypeStruct((here, width), wide),
            jax.ShapeDtypeStruct((here, width), low),
            jax.ShapeDtypeStruct((here, 2), wide),
            jax.ShapeDtypeStruct((here, heads), low),
        ),
        in_specs=in_hbm(4) + in_vmem(1),
        out_specs=tuple(in_hbm(2) + in_vmem(1) + in_hbm(1)),
        scratch_shapes=[
            pltpu.VMEM((2, here, heads), low),
            pltpu.VMEM(tokens.shape, low),
            pltpu.VMEM(out_w.shape, low),
            pltpu.VMEM(extras.shape, low),
            pltpu.VMEM((here, width), wide),
            pltpu.VMEM((here, width), low),
            pltpu.SemaphoreType.DMA((7,)),
            pltpu.SemaphoreType.DMA((2, 4)),
            pltpu.SemaphoreType.DMA((4,)),
            pltpu.SemaphoreType.DMA((3,)),
        ],
        compiler_params=pltpu.CompilerParams(
            collective_id=4, has_side_effects=True, vmem_limit_bytes=67043328
        ),
        cost_estimate=estimate(1),
        name="attend_out",
    )(attended, tokens, out_w, extras, codes)


def attend_back(
    rows_hbm,
    dot_rows,
    gates,
    codes,
    extras_hbm,
    one_hbm,
    cotangent_hbm,
    norm_hbm,
    out_hbm,
    hidden_hbm,
    branch_hbm,
    heads_grad,
    small,
    rows_grad,
    extras,
    hidden_one,
    cotangent,
    norm_two,
    out_w,
    hidden_grad,
    branch_grad,
    outgoing,
    send,
    recv,
    load_sem,
    store_sem,
):
    own, ctx, side, chip, core = places()
    here, width = hidden_one.shape
    heads = heads_grad.shape[2]
    loads = begin(
        (
            (rows_hbm, rows_grad),
            (extras_hbm, extras),
            (one_hbm, hidden_one),
            (cotangent_hbm, cotangent),
            (out_hbm.at[side], out_w),
            (norm_hbm, norm_two),
        ),
        load_sem,
    )
    greet([(own, across(chip, core, step), side) for step in range(3)])
    lane = lax.broadcasted_iota(jnp.int32, (here, LANES), 1).astype(jnp.float32)
    dots = jnp.transpose(dot_rows[...])
    total = dots[:, 0:1] + dots[:, 1:2]
    logit_grad = jnp.zeros((here, LANES), jnp.float32)
    for choice in range(TOP):
        shift = dots[:, choice : choice + 1] - gates[:, choice : choice + 1] * total
        logit_grad = jnp.where(lane == codes[:, 2 + choice : 3 + choice] + 2.0, shift, logit_grad)
    for load in loads:
        load.wait()
    extra = extras[...].astype(jnp.float32)
    norm_grad = rows_grad[...] + lax.dot_general(
        logit_grad,
        extra,
        (((1,), (1,)), ((), ())),
        precision=lax.Precision.HIGHEST,
        preferred_element_type=jnp.float32,
    )
    hidden = hidden_one[...]
    scale = lax.rsqrt(jnp.mean(hidden * hidden, axis=1, keepdims=True) + 1e-06)
    normal = hidden * scale
    spread = norm_grad * jnp.transpose(extra)[1:2, :]
    found = cotangent[...].astype(jnp.float32) + scale * (
        spread - normal * jnp.mean(spread * normal, axis=1, keepdims=True)
    )
    hidden_grad[...] = found
    branch_grad[...] = found.astype(jnp.bfloat16)
    stores = begin(((hidden_grad, hidden_hbm), (branch_grad, branch_hbm)), store_sem)

    def project(place):
        columns = pl.ds(pl.multiple_of(place * heads, heads), heads)
        return dot32(branch_grad[...], out_w[:, columns]).astype(jnp.bfloat16)

    def copy(step):
        place = across(chip, core, step)
        return remote(
            outgoing.at[step], heads_grad.at[ctx], send.at[step], recv.at[ctx], (own, place, side)
        )

    for step in range(3):
        outgoing[step] = project(across(chip, core, step))
        copy(step).start()
    outgoing[3] = project(ctx)
    stores += begin(((outgoing.at[3], heads_grad.at[ctx]),), store_sem.at[pl.ds(2, 1)])
    gain_row = jnp.sum(norm_grad * normal, axis=0, keepdims=True)
    routed = jnp.dot(
        jnp.transpose(logit_grad),
        norm_two[...].astype(jnp.float32),
        precision=lax.Precision.HIGHEST,
        preferred_element_type=jnp.float32,
    )
    line = lax.broadcasted_iota(jnp.int32, (8, width), 0)
    small[...] = jnp.where(line == 1, gain_row, routed[0:8])
    for step in range(3):
        place = across(chip, core, step)
        spot = heads_grad.at[place]
        remote(spot, spot, send.at[0], recv.at[place], (own, place, side)).wait_recv()
    for step in range(3):
        copy(step).wait_send()
    for store in stores:
        store.wait()


def run_attend_back(
    rows_grad, dot_rows, gates, codes, extras, hidden_one, cotangent, norm_two, out_w
):
    here, width = hidden_one.shape
    low, wide = jnp.bfloat16, jnp.float32
    heads = out_w.shape[2] // 4
    return pl.pallas_call(
        attend_back,
        out_shape=(
            jax.ShapeDtypeStruct((here, width), wide),
            jax.ShapeDtypeStruct((here, width), low),
            jax.ShapeDtypeStruct((4, here, heads), low),
            jax.ShapeDtypeStruct((8, width), wide),
        ),
        in_specs=in_hbm(1) + in_vmem(3) + in_hbm(5),
        out_specs=tuple(in_hbm(3) + in_vmem(1)),
        scratch_shapes=[
            pltpu.VMEM((here, width), wide),
            pltpu.VMEM(extras.shape, low),
            pltpu.VMEM((here, width), wide),
            pltpu.VMEM((here, width), low),
            pltpu.VMEM((here, width), low),
            pltpu.VMEM(out_w.shape[1:], low),
            pltpu.VMEM((here, width), wide),
            pltpu.VMEM((here, width), low),
            pltpu.VMEM((4, here, heads), low),
            pltpu.SemaphoreType.DMA((3,)),
            pltpu.SemaphoreType.DMA((4,)),
            pltpu.SemaphoreType.DMA((6,)),
            pltpu.SemaphoreType.DMA((3,)),
        ],
        compiler_params=pltpu.CompilerParams(
            collective_id=5, has_side_effects=True, vmem_limit_bytes=67043328
        ),
        cost_estimate=estimate(4),
        name="attend_back",
    )(rows_grad, dot_rows, gates, codes, extras, hidden_one, cotangent, norm_two, out_w)


def gradient_return(
    count,
    packed_grad,
    full_hbm,
    norm,
    tokens,
    bias_line,
    own_hbm,
    first_hbm,
    one_out_hbm,
    near_out_hbm,
    two_out_hbm,
    three_out_hbm,
    last_hbm,
    gates,
    codes,
    branch_grad,
    attended,
    small,
    one_hbm,
    grad_hbm,
    extras,
    mixed,
    input_grad,
    query_grad,
    key_grad,
    value_grad,
    bias_grad,
    gain_grad,
    out_grad,
    mixture,
    mixture_in,
    full,
    outs,
    hidden_one,
    hidden_grad,
    incoming,
    norm_t,
    outgoing,
    side_out,
    side_in,
    spread,
    core_in,
    chip_out,
    chip_in,
    line_out,
    line_in,
    out_going,
    out_core_in,
    out_spread,
    out_chip_out,
    out_chip_in,
    out_line_out,
    out_line_in,
    bias_out,
    bias_in,
    spread_gain,
    grad_send,
    grad_recv,
    side_send,
    side_recv,
    core_send,
    core_recv,
    chip_send,
    chip_recv,
    line_send,
    line_recv,
    bias_send,
    bias_recv,
    mixture_sem,
    mix_sem,
    load_sem,
):
    own, ctx, side, chip, core = places()
    ctx_size, here, share = packed_grad.shape
    width = norm.shape[1]
    halves = HALVES
    part = here // halves
    groups = ctx_size
    pair = (own, ctx, 1 - side)
    chip_peer = (own, (1 - chip) * 2 + core, side)
    core_peer = (own, chip * 2 + 1 - core, side)
    others = [
        (nearest(own, count, step), across(chip, core, turn), side)
        for step in range(count)
        for turn in range(4)
        if (step, turn) != (0, 3)
    ]
    room, half = outs.shape[1], last_hbm.shape[0]
    pairs = (
        (full_hbm, full),
        (own_hbm, outs.at[0]),
        (grad_hbm, hidden_grad),
        (one_hbm, hidden_one),
        (first_hbm, outs.at[1, pl.ds(0, half)]),
        (one_out_hbm, outs.at[1, pl.ds(half, half)]),
        (near_out_hbm, outs.at[2, pl.ds(0, half)]),
        (two_out_hbm, outs.at[2, pl.ds(half, half)]),
        (three_out_hbm, outs.at[3, pl.ds(0, half)]),
    )
    loads = [
        pltpu.make_async_copy(source, target, load_sem.at[number])
        for number, (source, target) in enumerate(pairs)
    ]
    for load in loads:
        load.start()
    greet(others + [pair])

    def to_owner(step, piece):
        place = across(chip, core, step)
        spot = pl.ds(piece * part, part)
        return remote(
            packed_grad.at[place, spot],
            incoming.at[ctx, spot],
            grad_send.at[step, piece],
            grad_recv.at[ctx, piece],
            (own, place, side),
        )

    for piece in range(halves):
        for step in range(3):
            to_owner(step, piece).start()
    incoming[ctx] = packed_grad[ctx]

    mixture_copy = remote(mixture, mixture_in, mixture_sem.at[0], mixture_sem.at[1], pair)

    def mixing(start, amount):
        slots = lax.broadcasted_iota(jnp.int32, (here, amount), 1) + start
        slots = slots.astype(jnp.float32)
        held = jnp.where(codes[:, 0:1] == slots, gates[:, 0:1], 0.0)
        held = held + jnp.where(codes[:, 1:2] == slots, gates[:, 1:2], 0.0)
        return held.astype(jnp.bfloat16)

    last_copy = remote(
        last_hbm,
        outs.at[3, pl.ds(half, half)],
        mix_sem.at[0],
        mix_sem.at[1],
        (partner(own, 3), ctx, side),
    )
    last_copy.start()

    def mix():
        for number in (1, 4, 5, 6, 7, 8):
            loads[number].wait()
        last_copy.wait_recv()
        total = jnp.zeros((here, width), jnp.float32)
        for turn in range(count):
            total = total + dot32(mixing(partner(own, turn) * room, room), outs[turn])
        mixture[...] = total.astype(jnp.bfloat16)
        mixture_copy.start()

    span = bias_line.shape[1]
    index = lax.broadcasted_iota(jnp.int32, (span, LANES), 0)
    relative = jnp.where(index < span // 2, -index, span - index)
    bucket = lax.broadcasted_iota(jnp.int32, (span, LANES), 1)
    onehot = jnp.where(bucket_ids(relative) == bucket, 1.0, 0.0)
    sums = jnp.dot(
        bias_line[...], onehot, precision=lax.Precision.HIGHEST, preferred_element_type=jnp.float32
    )
    far = jnp.sum(bias_line[...], axis=1, keepdims=True)
    lane = lax.broadcasted_iota(jnp.int32, (2, LANES), 1)
    total = sums[0:2] + jnp.where(lane == NBUCK // 2 - 1, far[2:4], 0.0)
    total = total + jnp.where(lane == NBUCK - 1, far[4:6], 0.0)
    bias_sum = jnp.concatenate([total, jnp.zeros((6, LANES), jnp.float32)], axis=0)

    def to_bias(number):
        return remote(
            bias_out.at[number],
            bias_in.at[own, ctx],
            bias_send.at[number],
            bias_recv.at[own, ctx],
            others[number],
        )

    stages = [
        (
            outgoing.at[group],
            core_in.at[group],
            spread.at[group],
            chip_out.at[group],
            chip_in.at[group],
            line_out.at[group],
            line_in.at[group],
            None,
        )
        for group in range(groups)
    ]
    stages.append(
        (
            out_going,
            out_core_in,
            out_spread,
            out_chip_out,
            out_chip_in,
            out_line_out,
            out_line_in,
            None,
        )
    )
    rows = norm_t.shape[0] // (count * ctx_size)

    def to_core(group):
        source, target = stages[group][0].at[:, 1 - core], stages[group][1]
        return remote(source, target, core_send.at[group], core_recv.at[group], core_peer)

    def to_chip(group):
        source, target = stages[group][3], stages[group][4]
        return remote(source, target, chip_send.at[group], chip_recv.at[group], chip_peer)

    def to_line(group, step):
        shard = nearest(own, count, step)
        source, target = stages[group][5].at[shard], stages[group][6].at[own]
        send, recv = line_send.at[group, step], line_recv.at[group, own]
        return remote(source, target, send, recv, (shard, ctx, side))

    def contract(group):
        found = dot32(norm_t[...], incoming[group] if group < groups else attended[...])
        found = found.reshape(count * 2, 2, rows, found.shape[1])
        stages[group][0][...] = found.astype(jnp.bfloat16)
        to_core(group).start()

    def over_chip(group):
        to_core(group).wait_recv()
        source, arrived, summed, target = stages[group][:4]
        found = source[:, core].astype(jnp.float32) + arrived[...].astype(jnp.float32)
        summed[...] = found.reshape(count, 2, rows, found.shape[2])
        target[...] = summed[:, 1 - chip].astype(jnp.bfloat16)
        to_chip(group).start()

    def over_line(group):
        to_chip(group).wait_recv()
        found = stages[group][2][:, chip] + stages[group][4][...].astype(jnp.float32)
        stages[group][5][...] = found.astype(jnp.bfloat16)
        for step in range(1, count):
            to_line(group, step).start()

    def collect(group):
        total = stages[group][5][own].astype(jnp.float32)
        for step in range(1, count):
            shard = nearest(own, count, step)
            spot = stages[group][6].at[shard]
            remote(
                spot, spot, line_send.at[group, 0], line_recv.at[group, shard], pair
            ).wait_recv()
            total = total + spot[...].astype(jnp.float32)
        if group == groups:
            out_grad[...] = total
        else:
            columns = slice(group * LANES, (group + 1) * LANES)
            for number, target in enumerate((query_grad, key_grad, value_grad)):
                target[:, columns] = total[:, number * LANES : (number + 1) * LANES]

    norm_t[...] = jnp.transpose(branch_grad[...].astype(jnp.float32)).astype(jnp.bfloat16)
    contract(groups)
    norm_t[...] = jnp.transpose(norm[...].astype(jnp.float32)).astype(jnp.bfloat16)
    over_chip(groups)

    def to_side(piece):
        return remote(
            side_out.at[piece],
            side_in.at[piece],
            side_send.at[piece],
            side_recv.at[piece],
            pair,
        )

    values = tokens[...].astype(jnp.float32)
    scale = lax.rsqrt(jnp.mean(values * values, axis=1, keepdims=True) + 1e-06)
    normal = values * scale
    first_gain = jnp.transpose(extras[...].astype(jnp.float32))[0:1, :]
    loads[0].wait()

    def landed(piece):
        for step in range(3):
            place = across(chip, core, step)
            target = incoming.at[place, pl.ds(piece * part, part)]
            remote(
                target, target, grad_send.at[0, 0], grad_recv.at[place, piece], pair
            ).wait_recv()

    def send_side(piece):
        spot = pl.ds(piece * part, part)
        total = jnp.zeros((part, width), jnp.float32)
        for place in range(ctx_size):
            columns = slice(place * share, (place + 1) * share)
            total = total + dot_last(incoming[place, spot, :], full[:, columns])
        side_out[piece] = total.astype(jnp.bfloat16)
        to_side(piece).start()

    def finish_sides():
        loads[2].wait()
        gain = jnp.zeros((1, width), jnp.float32)
        for piece in range(halves):
            to_side(piece).wait_recv()
            total = side_out[piece].astype(jnp.float32) + side_in[piece].astype(jnp.float32)
            lines = slice(piece * part, (piece + 1) * part)
            upright = normal[lines]
            gain = gain + jnp.sum(total * upright, axis=0, keepdims=True)
            total = total * first_gain
            total = total - upright * jnp.mean(total * upright, axis=1, keepdims=True)
            input_grad[lines, :] = (hidden_grad[lines, :] + scale[lines] * total).astype(
                jnp.bfloat16
            )
        spread_gain[...] = small[...]
        spread_gain[0:1, :] = gain

        def message(shard, place):
            lanes = pl.ds(pl.multiple_of((shard * 2 + place // 2) * LANES, LANES), LANES)
            return jnp.concatenate([bias_sum, spread_gain[:, lanes]], axis=0)

        for number, (shard, place, _) in enumerate(others):
            bias_out[number] = message(shard, place)
            to_bias(number).start()
        bias_in[own, ctx] = message(own, ctx)

    for piece in range(halves - 1):
        landed(piece)
        send_side(piece)
    landed(halves - 1)
    contract(0)
    send_side(halves - 1)
    over_chip(0)
    contract(1)
    contract(2)
    over_chip(1)
    mix()
    contract(3)
    over_chip(2)
    over_line(groups)
    over_chip(3)
    over_line(0)
    over_line(1)
    over_line(2)
    over_line(3)
    finish_sides()
    for group in (groups, 0, 1, 2, 3):
        collect(group)

    for number, (shard, place, _) in enumerate(others):
        spot = bias_in.at[shard, place]
        remote(spot, spot, bias_send.at[0], bias_recv.at[shard, place], pair).wait_recv()
    for place in range(ctx_size):
        total = bias_in[0, place]
        for shard in range(1, count):
            total = total + bias_in[shard, place]
        bias_grad[place] = total[:8]
        gain_total = total[8:] if place == 0 else gain_total + total[8:]
    gain_grad[...] = gain_total

    mixture_copy.wait()
    loads[3].wait()
    last_copy.wait_send()
    mixed[...] = (
        hidden_one[...] + (mixture[...].astype(jnp.float32) + mixture_in[...].astype(jnp.float32))
    ).astype(jnp.bfloat16)
    for number in range(len(others)):
        to_bias(number).wait_send()
    for piece in range(halves):
        to_side(piece).wait_send()
        for step in range(3):
            to_owner(step, piece).wait_send()
    for group in range(groups + 1):
        to_core(group).wait_send()
        to_chip(group).wait_send()
        for step in range(1, count):
            to_line(group, step).wait_send()


def run_return(
    count,
    packed_grad,
    full,
    norm,
    tokens,
    bias_line,
    outs,
    gates,
    codes,
    branch_grad,
    attended,
    small,
    hidden_one,
    hidden_grad,
    extras,
):
    ctx_size, here, share = packed_grad.shape
    width = norm.shape[1]
    rows = width // (count * ctx_size)
    low, wide = jnp.bfloat16, jnp.float32
    dma = pltpu.SemaphoreType.DMA
    columns = share
    out_columns = attended.shape[1]
    return pl.pallas_call(
        partial(gradient_return, count),
        out_shape=(
            jax.ShapeDtypeStruct((here, width), low),
            jax.ShapeDtypeStruct((here, width), low),
            *[jax.ShapeDtypeStruct((rows, ctx_size * LANES), wide)] * 3,
            jax.ShapeDtypeStruct((ctx_size, 8, LANES), wide),
            jax.ShapeDtypeStruct((8, LANES), wide),
            jax.ShapeDtypeStruct((rows, out_columns), wide),
        ),
        in_specs=[
            pl.BlockSpec(memory_space=pl.ANY if number in (1, 5, 6, 7, 8, 9, 10, 11, 17, 18) else pltpu.VMEM)
            for number in range(20)
        ],
        out_specs=tuple(in_vmem(8)),
        scratch_shapes=[
            pltpu.VMEM((here, width), low),
            pltpu.VMEM((here, width), low),
            pltpu.VMEM(full.shape, low),
            pltpu.VMEM((count,) + outs[0].shape, low),
            pltpu.VMEM((here, width), wide),
            pltpu.VMEM((here, width), wide),
            pltpu.VMEM((ctx_size, here, share), low),
            pltpu.VMEM((width, here), low),
            pltpu.VMEM((ctx_size, count * 2, 2, rows, columns), low),
            pltpu.VMEM((HALVES, here // HALVES, width), low),
            pltpu.VMEM((HALVES, here // HALVES, width), low),
            pltpu.VMEM((ctx_size, count, 2, rows, columns), wide),
            pltpu.VMEM((ctx_size, count * 2, rows, columns), low),
            pltpu.VMEM((ctx_size, count, rows, columns), low),
            pltpu.VMEM((ctx_size, count, rows, columns), low),
            pltpu.VMEM((ctx_size, count, rows, columns), low),
            pltpu.VMEM((ctx_size, count, rows, columns), low),
            pltpu.VMEM((count * 2, 2, rows, out_columns), low),
            pltpu.VMEM((count * 2, rows, out_columns), low),
            pltpu.VMEM((count, 2, rows, out_columns), wide),
            pltpu.VMEM((count, rows, out_columns), low),
            pltpu.VMEM((count, rows, out_columns), low),
            pltpu.VMEM((count, rows, out_columns), low),
            pltpu.VMEM((count, rows, out_columns), low),
            pltpu.VMEM((15, 16, LANES), wide),
            pltpu.VMEM((count, ctx_size, 16, LANES), wide),
            pltpu.VMEM((8, width), wide),
            dma((3, HALVES)),
            dma((ctx_size, HALVES)),
            dma((HALVES,)),
            dma((HALVES,)),
            dma((ctx_size + 1,)),
            dma((ctx_size + 1,)),
            dma((ctx_size + 1,)),
            dma((ctx_size + 1,)),
            dma((ctx_size + 1, count)),
            dma((ctx_size + 1, count)),
            dma((15,)),
            dma((count, ctx_size)),
            dma((2,)),
            dma((2,)),
            dma((9,)),
        ],
        compiler_params=pltpu.CompilerParams(
            collective_id=2, has_side_effects=True, vmem_limit_bytes=67043328
        ),
        cost_estimate=estimate(45),
        name="gradient_return",
    )(
        packed_grad,
        full,
        norm,
        tokens,
        bias_line,
        *outs,
        gates,
        codes,
        branch_grad,
        attended,
        small,
        hidden_one,
        hidden_grad,
        extras,
    )


def swap_sides(member):
    return lax.ppermute(member, "tensor", [(0, 1), (1, 0)])


def exchange(member, axis):
    return lax.all_to_all(member, axis, split_axis=0, concat_axis=0, tiled=True)


def slot_codes(routes, experts, room):
    tokens = routes.shape[0]
    picks = routes[:, :, None] == jnp.arange(experts, dtype=jnp.int32)[None, None, :]
    named = jnp.sum(picks, axis=1).astype(jnp.bfloat16)
    index = jnp.arange(tokens, dtype=jnp.int32)
    before = (index[:, None] > index[None, :]).astype(jnp.bfloat16)
    rank = jnp.dot(before, named, preferred_element_type=jnp.float32)
    slots = rank + room * jnp.arange(experts, dtype=jnp.float32)[None, :]
    return picks, jnp.sum(jnp.where(picks, slots[:, None, :], 0.0), axis=2)


def experts_apart(norm_two, upstream, gates, codes, room, count, weights):
    tokens, width = norm_two.shape
    codes = codes.astype(jnp.int32).reshape(-1)
    shaped = (count, room, width)

    def sent(member):
        slots = jnp.zeros((count * room, width), jnp.bfloat16).at[codes].set(member)
        return exchange(slots.reshape(shaped), "shard").reshape(-1, width)

    slot_rows = sent(jnp.repeat(norm_two, TOP, axis=0))
    slot_grads = sent(
        (gates[:, :, None] * upstream[:, None, :]).reshape(-1, width).astype(jnp.bfloat16)
    )
    gate_mat, up_mat, down_mat = weights
    gate_pre = dot32(slot_rows, gate_mat)
    up_pre = dot32(slot_rows, up_mat)
    activated, slope = gelu_parts(gate_pre)
    inner = (activated * up_pre).astype(jnp.bfloat16)
    expert_out = contract_cols(inner, down_mat)
    inner_grad = dot32(slot_grads, down_mat)
    gate_grad = (inner_grad * up_pre * slope).astype(jnp.bfloat16)
    up_grad = (inner_grad * activated).astype(jnp.bfloat16)
    rows_grad = contract_cols(gate_grad, gate_mat) + contract_cols(up_grad, up_mat)

    def returned(member):
        member = lax.psum(member.astype(jnp.bfloat16), "tensor").reshape(shaped)
        member = exchange(member, "shard").reshape(-1, width)[codes]
        return member.astype(jnp.float32).reshape(tokens, TOP, width)

    per_choice = returned(expert_out)
    mixture = jnp.sum(gates[:, :, None] * per_choice, axis=1)
    dots = gates * jnp.sum(per_choice * upstream[:, None, :], axis=2)
    norm_grad = jnp.sum(returned(rows_grad), axis=1)
    return mixture, dots, norm_grad, slot_rows, slot_grads, inner, gate_grad, up_grad


def local_general(
    tokens_in,
    cotangent,
    segment_ids,
    live_blocks,
    routes,
    w_query,
    w_key,
    w_value,
    w_out,
    rel_bias,
    attn_gain,
    ffn_gain,
    router,
    w_gate,
    w_up,
    w_down,
):
    rows_here, width = tokens_in.shape
    ctx_size = lax.axis_size("ctx")
    side_count = lax.axis_size("tensor")
    ctx_index = lax.axis_index("ctx")
    side = lax.axis_index("tensor")
    head_cols = w_query.shape[1]
    share = head_cols // ctx_size
    experts = router.shape[1]
    room = max(2, 3 * rows_here // experts)

    picks, codes = slot_codes(routes, experts, room)

    def by_owner(member):
        return member.reshape(member.shape[0], ctx_size, share)

    packed_rows = jnp.stack([by_owner(w_query), by_owner(w_key), by_owner(w_value)], axis=2)
    gathered = lax.all_gather(
        jnp.concatenate(
            [
                packed_rows.reshape(w_query.shape[0], -1),
                attn_gain[:, None],
                ffn_gain[:, None],
                router,
            ],
            axis=1,
        ).astype(jnp.bfloat16),
        ("shard", "ctx"),
        axis=0,
        tiled=True,
    )
    packed_w = gathered[:, : 3 * head_cols]
    gain_one = gathered[:, 3 * head_cols]
    gain_two = gathered[:, 3 * head_cols + 1]
    router_w = gathered[:, 3 * head_cols + 2 :]
    out_w = lax.all_gather(w_out.astype(jnp.bfloat16), ("shard", "ctx", "tensor"), axis=0)
    out_w = out_w.reshape(-1, side_count, w_out.shape[0], head_cols)
    out_w = jnp.transpose(out_w, (0, 2, 1, 3)).reshape(width, side_count * head_cols)
    expert_weights = tuple(
        lax.all_gather(member.astype(jnp.bfloat16), "ctx", axis=1, tiled=True)[0]
        for member in (w_gate, w_up, w_down)
    )

    inputs = tokens_in.astype(jnp.float32)
    scale_one = lax.rsqrt(jnp.mean(inputs * inputs, axis=1, keepdims=True) + 1e-06)
    normal_one = inputs * scale_one
    norm_one = (normal_one * gain_one.astype(jnp.float32)).astype(jnp.bfloat16)
    packed = dot32(norm_one, packed_w).astype(jnp.bfloat16)
    packed = jnp.transpose(packed.reshape(rows_here, ctx_size, 3 * share), (1, 0, 2))
    packed = exchange(packed, "ctx").reshape(ctx_size * rows_here, 3 * share)
    segments = lax.all_gather(segment_ids.reshape(-1), "ctx", axis=0, tiled=True)
    alive = live_tiles(segments, live_blocks[0])
    segment_row = segments.astype(jnp.float32)[None]
    pair_heads = share // HEAD
    own_bias = lax.dynamic_slice_in_dim(rel_bias, ctx_index * pair_heads, pair_heads, 1)
    buckets = span_buckets()
    line = jnp.dot(own_bias.T, buckets.T, precision=lax.Precision.HIGHEST)
    attended, attended_t, log_sum = run_forward(alive, packed, segment_row, line)
    attended = attended.reshape(ctx_size, 1, rows_here, share)
    attended = jnp.broadcast_to(attended, (ctx_size, side_count, rows_here, share))
    attended = exchange(attended.reshape(-1, rows_here, share), ("ctx", "tensor"))
    attended = attended.reshape(ctx_size, side_count, rows_here, share)
    attended = jnp.transpose(attended, (2, 1, 0, 3))
    attended_low = lax.dynamic_index_in_dim(attended, side, 1, False).reshape(rows_here, head_cols)
    attended = attended.reshape(rows_here, side_count * head_cols)
    hidden_one = inputs + contract_cols(attended, out_w)
    scale_two = lax.rsqrt(jnp.mean(hidden_one * hidden_one, axis=1, keepdims=True) + 1e-06)
    normal_two = hidden_one * scale_two
    norm_two = (normal_two * gain_two.astype(jnp.float32)).astype(jnp.bfloat16)
    logits = dot32(norm_two, router_w)
    chosen = jnp.sum(jnp.where(picks, logits[:, None, :], 0.0), axis=2)
    gates = jax.nn.softmax(chosen, axis=1)
    upstream = cotangent.astype(jnp.float32)
    results = experts_apart(norm_two, upstream, gates, codes, room, experts, expert_weights)
    mixture, gate_dots, norm_grad, slot_rows, slot_grads, inner, gate_grad, up_grad = results
    weight_grads = lax.psum_scatter(
        jnp.stack(
            [
                contract_rows(slot_rows, gate_grad),
                contract_rows(slot_rows, up_grad),
                contract_rows(slot_grads, inner),
            ],
            axis=1,
        ).astype(jnp.bfloat16),
        "ctx",
        scatter_dimension=0,
        tiled=True,
    ).astype(jnp.float32)
    mixed = (hidden_one + mixture).astype(jnp.bfloat16)
    gate_shift = gate_dots - gates * jnp.sum(gate_dots, axis=1, keepdims=True)
    logit_grad = jnp.sum(jnp.where(picks, gate_shift[:, :, None], 0.0), axis=1)
    router_f = router_w.astype(jnp.float32)
    norm_grad = norm_grad + jnp.dot(logit_grad, router_f.T, precision=lax.Precision.HIGHEST)
    spread_two = norm_grad * gain_two.astype(jnp.float32)
    hidden_grad = upstream + scale_two * (
        spread_two - normal_two * jnp.mean(spread_two * normal_two, axis=1, keepdims=True)
    )
    branch_grad = hidden_grad.astype(jnp.bfloat16)
    own_out_w = lax.dynamic_slice_in_dim(out_w, side * head_cols, head_cols, 1)
    grad_heads = dot32(branch_grad, own_out_w).astype(jnp.bfloat16)
    grad_heads = jnp.transpose(grad_heads.reshape(rows_here, ctx_size, share), (1, 0, 2))
    grad_heads = exchange(grad_heads, "ctx").reshape(-1, share)
    packed_grad, bias_line = run_backward(
        alive, packed, segment_row, line, grad_heads, attended_t, log_sum
    )
    own_grad = jnp.dot(buckets.T, bias_line[:pair_heads].T, precision=lax.Precision.HIGHEST)
    far = jnp.sum(bias_line[pair_heads : 3 * pair_heads], axis=1)
    half = NBUCK // 2
    own_grad = own_grad.at[half - 1].add(far[:pair_heads]).at[NBUCK - 1].add(far[pair_heads:])
    bias_acc = lax.dynamic_update_slice_in_dim(
        jnp.zeros(rel_bias.shape, jnp.float32), own_grad, ctx_index * pair_heads, 1
    )
    packed_grad = exchange(packed_grad.reshape(ctx_size, rows_here, 3 * share), "ctx")
    packed_grad = jnp.transpose(packed_grad, (1, 0, 2)).reshape(rows_here, 3 * head_cols)
    norm_one_grad = contract_cols(packed_grad, packed_w).astype(jnp.bfloat16)
    norm_one_grad = norm_one_grad.astype(jnp.float32) + swap_sides(norm_one_grad).astype(
        jnp.float32
    )
    spread_one = norm_one_grad * gain_one.astype(jnp.float32)
    input_grad = hidden_grad + scale_one * (
        spread_one - normal_one * jnp.mean(spread_one * normal_one, axis=1, keepdims=True)
    )
    first_gain = jnp.sum(norm_one_grad * normal_one, axis=0)[:, None]
    second_gain = jnp.sum(norm_grad * normal_two, axis=0)[:, None]
    router_part = jnp.dot(
        norm_two.astype(jnp.float32).T, logit_grad, precision=lax.Precision.HIGHEST
    )
    reduced = lax.psum_scatter(
        jnp.concatenate(
            [
                contract_rows(norm_one, packed_grad),
                contract_rows(branch_grad, attended_low),
                first_gain,
                second_gain,
                router_part,
            ],
            axis=1,
        ),
        ("shard", "ctx"),
        scatter_dimension=0,
        tiled=True,
    )
    grad_bias = lax.psum(bias_acc, ("shard", "ctx"))
    packed_rows = reduced[:, : 3 * head_cols].reshape(-1, ctx_size, 3, share)
    return (
        mixed,
        input_grad.astype(jnp.bfloat16),
        packed_rows[:, :, 0].reshape(-1, head_cols),
        packed_rows[:, :, 1].reshape(-1, head_cols),
        packed_rows[:, :, 2].reshape(-1, head_cols),
        reduced[:, 3 * head_cols : 4 * head_cols],
        grad_bias,
        reduced[:, 4 * head_cols],
        reduced[:, 4 * head_cols + 1],
        reduced[:, 4 * head_cols + 2 :],
        weight_grads[:, 0][None],
        weight_grads[:, 1][None],
        weight_grads[:, 2][None],
    )


def ppermute_ctx(member, flip):
    return lax.ppermute(member, "ctx", [(place, place ^ flip) for place in range(4)])


def local_fused(
    tokens_in,
    cotangent,
    segment_ids,
    live_blocks,
    routes,
    w_query,
    w_key,
    w_value,
    w_out,
    rel_bias,
    attn_gain,
    ffn_gain,
    router,
    w_gate,
    w_up,
    w_down,
):
    rows_here, width = tokens_in.shape
    count = lax.axis_size("shard")
    ctx_size = lax.axis_size("ctx")
    ctx_index = lax.axis_index("ctx")
    share = w_query.shape[1] // ctx_size
    rows = w_query.shape[0]
    experts = router.shape[1]
    room = max(2, 3 * rows_here // experts)
    members = (
        w_query,
        w_key,
        w_value,
        w_out,
        attn_gain[None],
        ffn_gain[None],
        router.T,
        tokens_in,
        segment_ids,
        cotangent,
        routes.T,
        live_blocks[0],
        rel_bias.T,
    )
    full, packed, norm_one, segments, out_w, up_slots, *lows = run_gather(
        count, ctx_size, room, members, (w_gate[0], w_up[0], w_down[0])
    )
    gate_low, up_low, down_low, gate_core, up_core, down_core, gate_chip, gate_far = lows[:8]
    codes, code_rows, extras, alive, line = lows[8:]
    alive = alive.reshape(-1)
    up_chip, down_chip = ppermute_ctx(up_low, 2), ppermute_ctx(down_low, 2)

    packed = packed.reshape(ctx_size * rows_here, 3 * share)
    segment_row = segments[:, 0].reshape(1, -1)
    pair_heads = share // HEAD
    attended, attended_t, log_sum = run_forward(alive, packed, segment_row, line)
    attended, up_chip = lax.optimization_barrier((attended, up_chip))
    expert_weights = [gate_low, gate_chip, gate_core, gate_far]
    expert_weights += [up_low, up_chip, up_core, ppermute_ctx(up_chip, 1)]
    expert_weights += [down_low, down_chip, down_core, ppermute_ctx(down_chip, 1)]
    hidden_one, norm_two, gates, attended_low = run_attend_out(
        attended.reshape(ctx_size, rows_here, share), tokens_in, out_w, extras, codes
    )
    rows_grad, dots, own_out, *outs, last_out, kept, gate_given, pair_given = run_experts(
        count, ctx_size, norm_two, gates, code_rows, codes, up_slots, expert_weights
    )
    for number, turn in enumerate((1, 1, 2, 2, 3)):
        pairs = [(place, place ^ turn) for place in range(count)]
        outs[number] = lax.ppermute(outs[number], "shard", pairs)
    hidden_grad, branch_grad, heads_grad, small = run_attend_back(
        rows_grad, dots, gates, codes, extras, hidden_one, cotangent, norm_two, out_w
    )
    heads_grad, pair_given, outs[0] = lax.optimization_barrier((heads_grad, pair_given, outs[0]))
    pair_given = ppermute_ctx(pair_given, 2)
    outs = [own_out, *outs, last_out]
    given = [gate_given, pair_given[0], pair_given[1]]
    weight_grads = [
        kept[number].astype(jnp.float32) + given[number].astype(jnp.float32) for number in range(3)
    ]
    packed_grad, bias_line = run_backward(
        alive, packed, segment_row, line, heads_grad.reshape(-1, share), attended_t, log_sum
    )
    returned = run_return(
        count,
        packed_grad.reshape(ctx_size, rows_here, 3 * share),
        full,
        norm_one,
        tokens_in,
        bias_line,
        outs,
        gates,
        codes,
        branch_grad,
        attended_low,
        small,
        hidden_one,
        hidden_grad,
        extras,
    )
    mixed, input_grad, query_grad, key_grad, value_grad, bias_grad, gains_grad, out_grad = returned
    gains_grad = lax.dynamic_slice_in_dim(gains_grad, ctx_index % 2 * rows, rows, 1)
    bias_grad = jnp.transpose(bias_grad[:, :pair_heads, :NBUCK], (2, 0, 1))
    return (
        mixed,
        input_grad,
        query_grad,
        key_grad,
        value_grad,
        out_grad,
        bias_grad.reshape(rel_bias.shape),
        gains_grad[0],
        gains_grad[1],
        jnp.transpose(gains_grad[2 : 2 + experts]),
        weight_grads[0][None],
        weight_grads[1][None],
        weight_grads[2][None],
    )


def solution(mesh):
    placed = (
        P(("shard", "ctx"), None),
        P(("shard", "ctx"), None),
        P("shard", "ctx"),
        P("shard", None, None),
        P(("shard", "ctx"), None),
        P(("shard", "ctx"), "tensor"),
        P(("shard", "ctx"), "tensor"),
        P(("shard", "ctx"), "tensor"),
        P(("shard", "ctx"), "tensor"),
        P(None, "tensor"),
        P(("shard", "ctx")),
        P(("shard", "ctx")),
        P(("shard", "ctx"), None),
        P("shard", "ctx", "tensor"),
        P("shard", "ctx", "tensor"),
        P("shard", "ctx", "tensor"),
    )
    sizes = (mesh.shape["shard"], mesh.shape["ctx"], mesh.shape["tensor"])
    fused = sizes == (4, 4, 2)
    return jax.shard_map(
        local_fused if fused else local_general,
        mesh=mesh,
        in_specs=placed,
        out_specs=(
            P(("shard", "ctx"), None),
            P(("shard", "ctx"), None),
            P(("shard", "ctx"), "tensor"),
            P(("shard", "ctx"), "tensor"),
            P(("shard", "ctx"), "tensor"),
            P(("shard", "ctx"), "tensor"),
            P(None, "tensor"),
            P(("shard", "ctx")),
            P(("shard", "ctx")),
            P(("shard", "ctx"), None),
            P("shard", "ctx", "tensor"),
            P("shard", "ctx", "tensor"),
            P("shard", "ctx", "tensor"),
        ),
        check_vma=False,
    )
```
